32 devices in a mesh: dp: 4 (over z), fsdp: 8 (over y, x, core).
Axes of the slice: x: 2, y: 2, z: 4, core: 2. Of those that a mesh axis runs over, the one named last changes fastest.
Arguments:
- tokens: bfloat16 [32, 512, 1024], P(('dp', 'fsdp')), may hold values from -6 to 6
- memory: bfloat16 [32, 588, 1024], P(('dp', 'fsdp')), may hold values from -6 to 6
- page_lengths: int32 [32], P(('dp', 'fsdp')), may hold values from 256 to 512, as said below
- end_flags: int32 [32], P(('dp', 'fsdp')), may hold values from 0 to 1, as said below
- out_grad: bfloat16 [32, 512, 1024], P(('dp', 'fsdp')), may hold values from -6 to 6
- self_gain: bfloat16 [1024], P(('dp', 'fsdp')), may hold values from 0.25 to 1.75
- self_shift: bfloat16 [1024], P(('dp', 'fsdp')), may hold values from -1.25 to 1.25
- self_query: bfloat16 [1024, 1024], P(('dp', 'fsdp')), may hold values from -0.1875 to 0.1875
- self_query_bias: bfloat16 [1024], P(('dp', 'fsdp')), may hold values from -1.25 to 1.25
- self_key: bfloat16 [1024, 1024], P(('dp', 'fsdp')), may hold values from -0.1875 to 0.1875
- self_value: bfloat16 [1024, 1024], P(('dp', 'fsdp')), may hold values from -0.1875 to 0.1875
- self_value_bias: bfloat16 [1024], P(('dp', 'fsdp')), may hold values from -1.25 to 1.25
- self_out: bfloat16 [1024, 1024], P(('dp', 'fsdp')), may hold values from -1.5 to 1.5
- self_out_bias: bfloat16 [1024], P(('dp', 'fsdp')), may hold values from -1.25 to 1.25
- cross_gain: bfloat16 [1024], P(('dp', 'fsdp')), may hold values from 0.25 to 1.75
- cross_shift: bfloat16 [1024], P(('dp', 'fsdp')), may hold values from -1.25 to 1.25
- cross_query: bfloat16 [1024, 1024], P(('dp', 'fsdp')), may hold values from -0.1875 to 0.1875
- cross_query_bias: bfloat16 [1024], P(('dp', 'fsdp')), may hold values from -1.25 to 1.25
- cross_key: bfloat16 [1024, 1024], P(('dp', 'fsdp')), may hold values from -0.1875 to 0.1875
- cross_value: bfloat16 [1024, 1024], P(('dp', 'fsdp')), may hold values from -0.1875 to 0.1875
- cross_value_bias: bfloat16 [1024], P(('dp', 'fsdp')), may hold values from -1.25 to 1.25
- cross_out: bfloat16 [1024, 1024], P(('dp', 'fsdp')), may hold values from -1.5 to 1.5
- cross_out_bias: bfloat16 [1024], P(('dp', 'fsdp')), may hold values from -1.25 to 1.25
- feed_gain: bfloat16 [1024], P(('dp', 'fsdp')), may hold values from 0.25 to 1.75
- feed_shift: bfloat16 [1024], P(('dp', 'fsdp')), may hold values from -1.25 to 1.25
- feed_in: bfloat16 [1024, 4096], P(('dp', 'fsdp')), may hold values from -0.1875 to 0.1875
- feed_in_bias: bfloat16 [4096], P(('dp', 'fsdp')), may hold values from -1.25 to 1.25
- feed_out: bfloat16 [4096, 1024], P(('dp', 'fsdp')), may hold values from -0.09375 to 0.09375
- feed_out_bias: bfloat16 [1024], P(('dp', 'fsdp')), may hold values from -1.25 to 1.25
Outputs:
- layer_out: bfloat16 [32, 512, 1024], P(('dp', 'fsdp'))
- tokens_grad: float32 [32, 512, 1024], P(('dp', 'fsdp'))
- memory_grad: float32 [32, 588, 1024], P(('dp', 'fsdp'))
- grad_self_gain: float32 [1024], P(('dp', 'fsdp'))
- grad_self_shift: float32 [1024], P(('dp', 'fsdp'))
- grad_self_query: float32 [1024, 1024], P(('dp', 'fsdp'))
- grad_self_query_bias: float32 [1024], P(('dp', 'fsdp'))
- grad_self_key: float32 [1024, 1024], P(('dp', 'fsdp'))
- grad_self_value: float32 [1024, 1024], P(('dp', 'fsdp'))
- grad_self_value_bias: float32 [1024], P(('dp', 'fsdp'))
- grad_self_out: float32 [1024, 1024], P(('dp', 'fsdp'))
- grad_self_out_bias: float32 [1024], P(('dp', 'fsdp'))
- grad_cross_gain: float32 [1024], P(('dp', 'fsdp'))
- grad_cross_shift: float32 [1024], P(('dp', 'fsdp'))
- grad_cross_query: float32 [1024, 1024], P(('dp', 'fsdp'))
- grad_cross_query_bias: float32 [1024], P(('dp', 'fsdp'))
- grad_cross_key: float32 [1024, 1024], P(('dp', 'fsdp'))
- grad_cross_value: float32 [1024, 1024], P(('dp', 'fsdp'))
- grad_cross_value_bias: float32 [1024], P(('dp', 'fsdp'))
- grad_cross_out: float32 [1024, 1024], P(('dp', 'fsdp'))
- grad_cross_out_bias: float32 [1024], P(('dp', 'fsdp'))
- grad_feed_gain: float32 [1024], P(('dp', 'fsdp'))
- grad_feed_shift: float32 [1024], P(('dp', 'fsdp'))
- grad_feed_in: float32 [1024, 4096], P(('dp', 'fsdp'))
- grad_feed_in_bias: float32 [4096], P(('dp', 'fsdp'))
- grad_feed_out: float32 [4096, 1024], P(('dp', 'fsdp'))
- grad_feed_out_bias: float32 [1024], P(('dp', 'fsdp'))
The draws below stay inside these ranges and needn't reach their ends.
Inputs may be any that keep to these rules, and one draw needn't show every extreme that they name: `page_lengths`: lengths lie from 256 to 512; some page that is not an end page has exactly 512. `end_flags`: an end page's entry of page_lengths is not used; some page is an end page.
All inputs are finite; a program needn't handle non-finite values.
Results may differ from the reference program's by a relative error of at most 0.02.
Values may be sent and summed in bfloat16 or wider, within the bound.
A program may use at most 256 MiB of HBM per device.

```python
import jax
import jax.numpy as jnp
from jax import lax

D = 1024
HEADS = 16
HEAD = 64
FF = 4096
MEM = 588
PAGE_LEN = 512
PAGES = 32


def page_draw(key):
    base_key = jax.random.fold_in(key, 11)
    key_len, key_flag, key_full = jax.random.split(base_key, 3)
    slot_index = jnp.arange(PAGES, dtype=jnp.int32)
    full_slot = jax.random.randint(key_full, (), 0, PAGES, dtype=jnp.int32)
    lengths = jax.random.randint(key_len, (PAGES,), PAGE_LEN // 2, PAGE_LEN + 1, dtype=jnp.int32)
    lengths = jnp.where(slot_index == full_slot, PAGE_LEN, lengths)
    end_marks = (jax.random.randint(key_flag, (PAGES,), 0, 8, dtype=jnp.int32) == 0).astype(jnp.int32)
    end_marks = jnp.where(slot_index == full_slot, 0, end_marks)
    end_marks = jnp.where(slot_index == (full_slot + 1) % PAGES, 1, end_marks)
    return (lengths, end_marks)


def draw_page_lengths(key, part):
    return page_draw(key)[0]


def draw_end_flags(key, part):
    return page_draw(key)[1]


def with_spikes(values, rng, source, target, parts, factor):
    def block_of(axis_at):
        return (jnp.arange(values.shape[axis_at]) // (values.shape[axis_at] // parts)).reshape((-1,) + (1,) * (values.ndim - 1 - axis_at))

    first = jax.random.permutation(rng, parts)[block_of(target)]
    second = (block_of(target) + parts // 2) % parts
    return jnp.where((block_of(source) == first) | (block_of(source) == second), factor * values, values)


def level_of(key, extent, pieces, smallest, top_value):
    factor_of = 1.0
    for dim, blocks in pieces:
        steps = jax.random.uniform(jax.random.fold_in(jax.random.fold_in(key, 6), dim), (blocks,), jnp.float32, smallest / len(pieces), top_value / len(pieces))
        factor_of = factor_of * jnp.repeat(jnp.exp(steps), extent[dim] // blocks).reshape((-1,) + (1,) * (len(extent) - 1 - dim))
    return factor_of


def scatter_about(own_key, extent, width, limit, pieces=(), kind=jnp.bfloat16):
    values = jax.random.normal(own_key, extent, jnp.float32) * width
    if len(pieces) > 0:
        values = level_of(own_key, extent, pieces, -0.22, 0.18) * values
    return jnp.clip(values, min=-limit, max=limit).astype(kind)


def gaussian_with(rng, dims, spread, limit, cuts, heavy, held_as=jnp.bfloat16):
    array = spread * jax.random.normal(rng, dims, jnp.float32)
    if cuts:
        array = array * level_of(rng, dims, cuts, -0.22, 0.18)
    return jnp.clip(with_spikes(array, jax.random.fold_in(rng, 3), *heavy), -limit, limit).astype(held_as)


def setup_inputs(seed: int = 0) -> dict:
    streams_of = jax.random.split(jax.random.key(seed), 30)
    tokens = gaussian_with(streams_of[0], (PAGES, PAGE_LEN, D), 1.0, 6.0, ((0, 32),), (0, 2, 32, 2.75))
    memory = scatter_about(streams_of[1], (PAGES, MEM, D), 1.0, 6.0, ((0, 32),))
    page_lengths = draw_page_lengths(jax.random.fold_in(streams_of[29], 71), 0)
    end_flags = draw_end_flags(jax.random.fold_in(streams_of[29], 71), 0)
    out_grad = gaussian_with(streams_of[4], (PAGES, PAGE_LEN, D), 1.0, 6.0, ((0, 32),), (0, 2, 32, 2.75))
    self_gain = jnp.clip(1.0 + 0.15 * jax.random.normal(streams_of[5], (D,), jnp.float32), 0.25, 1.75).astype(jnp.bfloat16)
    self_shift = scatter_about(streams_of[6], (D,), 0.2, 1.25, ((0, 32),))
    self_query = scatter_about(streams_of[7], (D, D), D ** -0.5, 0.1875, ((0, 32),))
    self_query_bias = scatter_about(streams_of[8], (D,), 0.2, 1.25, ((0, 32),))
    self_key = scatter_about(streams_of[9], (D, D), D ** -0.5, 0.1875, ((0, 32),))
    self_value = scatter_about(streams_of[10], (D, D), D ** -0.5, 0.1875, ((0, 32),))
    self_value_bias = scatter_about(streams_of[11], (D,), 0.2, 1.25, ((0, 32),))
    self_out = scatter_about(streams_of[12], (D, D), (max(D // 64, 1)) ** -0.5, 1.5, ((0, 32),))
    self_out_bias = scatter_about(streams_of[13], (D,), 0.2, 1.25, ((0, 32),))
    cross_gain = jnp.clip(1.0 + 0.15 * jax.random.normal(streams_of[14], (D,), jnp.float32), 0.25, 1.75).astype(jnp.bfloat16)
    cross_shift = scatter_about(streams_of[15], (D,), 0.2, 1.25, ((0, 32),))
    cross_query = scatter_about(streams_of[16], (D, D), D ** -0.5, 0.1875, ((0, 32),))
    cross_query_bias = scatter_about(streams_of[17], (D,), 0.2, 1.25, ((0, 32),))
    cross_key = scatter_about(streams_of[18], (D, D), D ** -0.5, 0.1875, ((0, 32),))
    cross_value = scatter_about(streams_of[19], (D, D), D ** -0.5, 0.1875, ((0, 32),))
    cross_value_bias = scatter_about(streams_of[20], (D,), 0.2, 1.25, ((0, 32),))
    cross_out = scatter_about(streams_of[21], (D, D), (max(D // 64, 1)) ** -0.5, 1.5, ((0, 32),))
    cross_out_bias = scatter_about(streams_of[22], (D,), 0.2, 1.25, ((0, 32),))
    feed_gain = jnp.clip(1.0 + 0.15 * jax.random.normal(streams_of[23], (D,), jnp.float32), 0.25, 1.75).astype(jnp.bfloat16)
    feed_shift = scatter_about(streams_of[24], (D,), 0.2, 1.25, ((0, 32),))
    feed_in = scatter_about(streams_of[25], (D, FF), D ** -0.5, 0.1875, ((0, 32),))
    feed_in_bias = scatter_about(streams_of[26], (FF,), 0.2, 1.25, ((0, 32),))
    feed_out = scatter_about(streams_of[27], (FF, D), FF ** -0.5, 0.09375, ((0, 32),))
    feed_out_bias = scatter_about(streams_of[28], (D,), 0.2, 1.25, ((0, 32),))
    return dict(tokens=tokens, memory=memory, page_lengths=page_lengths, end_flags=end_flags, out_grad=out_grad, self_gain=self_gain, self_shift=self_shift, self_query=self_query, self_query_bias=self_query_bias, self_key=self_key, self_value=self_value, self_value_bias=self_value_bias, self_out=self_out, self_out_bias=self_out_bias, cross_gain=cross_gain, cross_shift=cross_shift, cross_query=cross_query, cross_query_bias=cross_query_bias, cross_key=cross_key, cross_value=cross_value, cross_value_bias=cross_value_bias, cross_out=cross_out, cross_out_bias=cross_out_bias, feed_gain=feed_gain, feed_shift=feed_shift, feed_in=feed_in, feed_in_bias=feed_in_bias, feed_out=feed_out, feed_out_bias=feed_out_bias)


@jax.custom_vjp
def low(v):
    return lax.optimization_barrier(v.astype(jnp.bfloat16)).astype(jnp.float32)

@jax.custom_vjp
def low_back(v):
    return v

def low_keep(v):
    return (low(v), None)

def low_pass(kept, grad):
    return (grad,)

def back_keep(v):
    return (v, None)

def back_low(kept, grad):
    return (low(grad),)
low.defvjp(low_keep, low_pass)
low_back.defvjp(back_keep, back_low)
EPSILON = 1e-05
MASKED = -1000000000.0

def matmul(left, right):
    return jnp.dot(left, right, precision=lax.Precision.HIGHEST)

def normalize(rows_in, norm_gain, norm_shift):
    centered = rows_in - lax.optimization_barrier(jnp.mean(rows_in, axis=-1, keepdims=True))
    inv_std = lax.rsqrt(lax.optimization_barrier(jnp.mean(centered * centered, axis=-1, keepdims=True)) + EPSILON)
    return centered * inv_std * norm_gain + norm_shift

def page_mask(length_now, row_count):
    query_pos = lax.broadcasted_iota(jnp.int32, (row_count, row_count), 0)
    key_pos = lax.broadcasted_iota(jnp.int32, (row_count, row_count), 1)
    return (key_pos <= query_pos) & (key_pos < length_now)

def attention(query_rows, key_rows, value_rows, mask_now):
    query_heads = query_rows.reshape(query_rows.shape[0], HEADS, HEAD)
    key_heads = key_rows.reshape(key_rows.shape[0], HEADS, HEAD)
    value_heads = value_rows.reshape(value_rows.shape[0], HEADS, HEAD)
    raw_scores = low_back(jnp.einsum('qhe,khe->hqk', query_heads, key_heads, precision=lax.Precision.HIGHEST))
    scaled = raw_scores * HEAD ** (-0.5)
    if mask_now is not None:
        scaled = jnp.where(mask_now[None], scaled, MASKED)
    weights_low = low(jax.nn.softmax(scaled, axis=-1))
    mixed = jnp.einsum('hqk,khe->qhe', weights_low, value_heads, precision=lax.Precision.HIGHEST)
    return mixed.reshape(query_rows.shape[0], HEADS * HEAD)

def page_forward(weight_set, inputs, mem_rows, length_now):
    gain_one, shift_one, query_mat, query_vec, key_mat, value_mat, value_vec, out_mat, out_vec, gain_two, shift_two, cquery_mat, cquery_vec, ckey_mat, cvalue_mat, cvalue_vec, cout_mat, cout_vec, gain_three, shift_three, hidden_mat, hidden_vec, final_mat, final_vec = weight_set
    first_low = low(normalize(inputs, gain_one, shift_one))
    query_low = low(low_back(matmul(first_low, query_mat) + query_vec))
    key_low = low(low_back(matmul(first_low, key_mat)))
    value_low = low(low_back(matmul(first_low, value_mat) + value_vec))
    mask_now = page_mask(length_now, inputs.shape[0])
    self_low = low(low_back(attention(query_low, key_low, value_low, mask_now)))
    after_self = inputs + low_back(matmul(self_low, out_mat) + out_vec)
    second_low = low(normalize(after_self, gain_two, shift_two))
    cquery_low = low(low_back(matmul(second_low, cquery_mat) + cquery_vec))
    ckey_low = low(low_back(matmul(mem_rows, ckey_mat)))
    cvalue_low = low(low_back(matmul(mem_rows, cvalue_mat) + cvalue_vec))
    cross_low = low(low_back(attention(cquery_low, ckey_low, cvalue_low, None)))
    after_cross = after_self + low_back(matmul(cross_low, cout_mat) + cout_vec)
    third_low = low(normalize(after_cross, gain_three, shift_three))
    hidden_low = low(jax.nn.gelu(low_back(matmul(third_low, hidden_mat) + hidden_vec), approximate=False))
    return after_cross + low_back(matmul(hidden_low, final_mat) + final_vec)

def reference(tokens, memory, page_lengths, end_flags, out_grad, self_gain, self_shift, self_query, self_query_bias, self_key, self_value, self_value_bias, self_out, self_out_bias, cross_gain, cross_shift, cross_query, cross_query_bias, cross_key, cross_value, cross_value_bias, cross_out, cross_out_bias, feed_gain, feed_shift, feed_in, feed_in_bias, feed_out, feed_out_bias):
    shard_set = (self_gain, self_shift, self_query, self_query_bias, self_key, self_value, self_value_bias, self_out, self_out_bias, cross_gain, cross_shift, cross_query, cross_query_bias, cross_key, cross_value, cross_value_bias, cross_out, cross_out_bias, feed_gain, feed_shift, feed_in, feed_in_bias, feed_out, feed_out_bias)
    weight_set = tuple((entry.astype(jnp.float32) for entry in shard_set))
    lengths_now = jnp.where(end_flags == 1, 1, page_lengths).astype(jnp.int32)
    inputs = tokens.astype(jnp.float32)
    mem_all = memory.astype(jnp.float32)

    def forward(inputs, mem_all, weight_set):

        def one_page(page_item):
            return page_forward(weight_set, page_item[0], page_item[1], page_item[2])
        return lax.map(jax.checkpoint(one_page), (inputs, mem_all, lengths_now))
    result, pullback = jax.vjp(forward, inputs, mem_all, weight_set)
    grad_in, grad_mem, grads = pullback(out_grad.astype(jnp.float32))
    return (result.astype(jnp.bfloat16), grad_in, grad_mem, grads[0], grads[1], grads[2], grads[3], grads[4], grads[5], grads[6], grads[7], grads[8], grads[9], grads[10], grads[11], grads[12], grads[13], grads[14], grads[15], grads[16], grads[17], grads[18], grads[19], grads[20], grads[21], grads[22], grads[23])
```

```python
import functools

import jax
import jax.numpy as jnp
from jax import lax
from jax.experimental import pallas as pl
from jax.experimental.pallas import tpu as pltpu
from jax.sharding import PartitionSpec as P

HEADS = 16


EPSILON = 1e-05
MASKED = -1000000000.0
ROOT_HALF = 0.7071067811865476
INV_ROOT_TWO_PI = 0.3989422804014327


def product(left, right):
    return jnp.dot(left, right, preferred_element_type=jnp.float32)


def product_tn(left, right):
    return lax.dot_general(
        left, right, (((0,), (0,)), ((), ())), preferred_element_type=jnp.float32
    )


def product_nt(left, right):
    return lax.dot_general(
        left, right, (((1,), (1,)), ((), ())), preferred_element_type=jnp.float32
    )


def normalize(rows_in, norm_gain, norm_shift):
    centered = rows_in - jnp.mean(rows_in, axis=-1, keepdims=True)
    inv_std = lax.rsqrt(jnp.mean(centered * centered, axis=-1, keepdims=True) + EPSILON)
    unit_rows = centered * inv_std
    return (unit_rows * norm_gain + norm_shift, unit_rows, inv_std)


def normalize_back(grad_norm, unit_rows, inv_std, norm_gain):
    scaled = grad_norm * norm_gain
    inner_part = (
        scaled
        - jnp.mean(scaled, axis=-1, keepdims=True)
        - unit_rows * jnp.mean(scaled * unit_rows, axis=-1, keepdims=True)
    )
    return (
        inner_part * inv_std,
        jnp.sum(grad_norm * unit_rows, axis=0),
        jnp.sum(grad_norm, axis=0),
    )


def gelu_slope(pre_act):
    return 0.5 * (
        1.0 + jax.scipy.special.erf(pre_act * ROOT_HALF)
    ) + pre_act * INV_ROOT_TWO_PI * jnp.exp(-0.5 * pre_act * pre_act)


def page_mask(length_now, row_count):
    query_pos = lax.broadcasted_iota(jnp.int32, (row_count, row_count), 0)
    key_pos = lax.broadcasted_iota(jnp.int32, (row_count, row_count), 1)
    return (key_pos <= query_pos) & (key_pos < length_now)


def split_heads(rows_in):
    return rows_in.reshape(rows_in.shape[0], HEADS, rows_in.shape[1] // HEADS)


def merge_heads(heads_in):
    return heads_in.reshape(heads_in.shape[0], heads_in.shape[1] * heads_in.shape[2])


def scores_of(query_rows, key_rows, mask_now):
    head_size = query_rows.shape[1] // HEADS
    raw_scores = jnp.einsum(
        "qhe,khe->hqk",
        split_heads(query_rows),
        split_heads(key_rows),
        preferred_element_type=jnp.float32,
    )
    scaled = raw_scores * head_size ** (-0.5)
    if mask_now is None:
        return scaled
    return jnp.where(mask_now[None], scaled, MASKED)


def attend_forward(query_rows, key_rows, value_rows, mask_now):
    scaled = scores_of(query_rows, key_rows, mask_now)
    row_top = jnp.max(scaled, axis=-1, keepdims=True)
    expo_rows = jnp.exp(scaled - row_top)
    row_total = jnp.sum(expo_rows, axis=-1, keepdims=True)
    weights_low = (expo_rows / row_total).astype(jnp.bfloat16)
    mixed = jnp.einsum(
        "hqk,khe->qhe", weights_low, split_heads(value_rows), preferred_element_type=jnp.float32
    )
    return (merge_heads(mixed), row_top + jnp.log(row_total))


def attend_backward(query_rows, key_rows, value_rows, mixed_grad, log_total, mask_now):
    head_size = query_rows.shape[1] // HEADS
    probs = jnp.exp(scores_of(query_rows, key_rows, mask_now) - log_total)
    grad_heads = split_heads(mixed_grad)
    query_heads = split_heads(query_rows)
    key_heads = split_heads(key_rows)
    prob_grad = jnp.einsum(
        "qhe,khe->hqk", grad_heads, split_heads(value_rows), preferred_element_type=jnp.float32
    )
    value_grad = jnp.einsum(
        "hqk,qhe->khe", probs.astype(jnp.bfloat16), grad_heads, preferred_element_type=jnp.float32
    )
    row_dot = jnp.sum(probs * prob_grad, axis=-1, keepdims=True)
    score_grad = (probs * (prob_grad - row_dot) * head_size ** (-0.5)).astype(jnp.bfloat16)
    query_grad = jnp.einsum(
        "hqk,khe->qhe", score_grad, key_heads, preferred_element_type=jnp.float32
    )
    key_grad = jnp.einsum(
        "hqk,qhe->khe", score_grad, query_heads, preferred_element_type=jnp.float32
    )
    return (merge_heads(query_grad), merge_heads(key_grad), merge_heads(value_grad))


def self_forward(query_pages, key_pages, value_pages, lengths_now):

    def one_page(page_item):
        mask_now = page_mask(page_item[3], page_item[0].shape[0])
        return attend_forward(page_item[0], page_item[1], page_item[2], mask_now)

    return lax.map(one_page, (query_pages, key_pages, value_pages, lengths_now))


def self_backward(query_pages, key_pages, value_pages, grad_pages, total_pages, lengths_now):

    def one_page(page_item):
        mask_now = page_mask(page_item[5], page_item[0].shape[0])
        return attend_backward(
            page_item[0], page_item[1], page_item[2], page_item[3], page_item[4], mask_now
        )

    return lax.map(
        one_page, (query_pages, key_pages, value_pages, grad_pages, total_pages, lengths_now)
    )


def cross_forward(query_pages, key_pages, value_pages):

    def one_page(page_item):
        return attend_forward(page_item[0], page_item[1], page_item[2], None)

    return lax.map(one_page, (query_pages, key_pages, value_pages))


def cross_backward(query_pages, key_pages, value_pages, grad_pages, total_pages):

    def one_page(page_item):
        return attend_backward(
            page_item[0], page_item[1], page_item[2], page_item[3], page_item[4], None
        )

    return lax.map(one_page, (query_pages, key_pages, value_pages, grad_pages, total_pages))


MESH_ID = pl.DeviceIdType.MESH
BOTH = ("dp", "fsdp")
CORE_RATE = 500e3
LINK_RATE = 96e3
HOP = 2.5
VEC_ROWS = 8
VEC_LANES = 128


def bit_table(mesh):
    bits = []
    for axis, name in enumerate(BOTH):
        step = mesh.shape[name] // 2
        while step >= 1:
            bits.append((axis, step))
            step //= 2
    return bits


def can_route(mesh, rows):
    sizes = [mesh.shape[name] for name in BOTH]
    return all(s & (s - 1) == 0 for s in sizes) and rows % 16 == 0


def route_orders(bits):
    outer = [i for i, (axis, _) in enumerate(bits) if axis == 0]
    inner = [i for i, (axis, _) in enumerate(bits) if axis == 1]
    return (outer + inner, outer + inner[:-1][::-1] + inner[-1:])


def loads_of(bits, at, size):
    axis, step = bits[at]
    if axis == 1 and step == 1:
        return {"core": size / CORE_RATE}
    if axis == 1:
        return {f"inner{step}": 2 * size / LINK_RATE}
    loads = {"outer1": 2 * size / LINK_RATE}
    if step > 1:
        loads["outer2"] = 2 * size * step / LINK_RATE
    return loads


def plan_sends(bits, orders, sizes, growing, add_rate):
    count = len(bits)
    ready = [(0.0, unit, 0) for unit in range(len(orders))]
    free = {}
    plan = []
    while ready:
        choices = []
        for when, unit, stage in ready:
            scale = 2**stage if growing else 2 ** (count - 1 - stage)
            loads = loads_of(bits, orders[unit][stage], sizes[unit] * scale)
            start = max([when] + [free.get(link, 0.0) for link in loads])
            choices.append((round(start, 3), unit, -stage, when, scale))
        start, unit, stage, when, scale = min(choices)
        stage = -stage
        ready.remove((when, unit, stage))
        loads = loads_of(bits, orders[unit][stage], sizes[unit] * scale)
        for link, took in loads.items():
            free[link] = start + took
        plan.append((start, unit, stage))
        if stage + 1 < count:
            after = start + max(loads.values()) + HOP
            if add_rate:
                after += sizes[unit] * scale / add_rate
            ready.append((after, unit, stage + 1))
    return [(unit, stage) for _, unit, stage in sorted(plan)]


def my_bits(bits):
    place = (lax.axis_index("dp"), lax.axis_index("fsdp"))
    return [(place[axis] // step) % 2 for axis, step in bits]


def partner(bits, mine, at):
    place = [lax.axis_index("dp"), lax.axis_index("fsdp")]
    axis, step = bits[at]
    place[axis] = place[axis] + step * (1 - 2 * mine[at])
    return tuple(place)


def greet(bits, mine):
    barrier = pltpu.get_barrier_semaphore()
    for at in range(len(bits)):
        pl.semaphore_signal(
            barrier, inc=1, device_id=partner(bits, mine, at), device_id_type=MESH_ID
        )
    pl.semaphore_wait(barrier, len(bits))


def unit_shape(blocks, unit):
    array, rows, cols = unit
    block = blocks[array]
    return (len(range(*rows.indices(block[0]))), len(range(*cols.indices(block[1]))))


def gather_kernel(bits, units, orders, plan, n_arrays, *refs):
    count = len(bits)
    sources = refs[:n_arrays]
    targets = refs[n_arrays : 2 * n_arrays]
    send_sem, recv_sem, own_sem = refs[2 * n_arrays :]
    mine = my_bits(bits)
    own = [
        pltpu.make_async_copy(sources[i], targets[i].at[tuple(mine)], own_sem.at[i])
        for i in range(n_arrays)
    ]
    for copy in own:
        copy.start()
    greet(bits, mine)

    def message(unit, stage):
        array, rows, cols = units[unit]
        order = orders[unit]
        where = tuple(slice(None) if b in order[:stage] else mine[b] for b in range(count))
        place = targets[array].at[where + (rows, cols)]
        source = sources[array].at[rows, cols] if stage == 0 else place
        return pltpu.make_async_remote_copy(
            src_ref=source,
            dst_ref=place,
            send_sem=send_sem.at[unit, stage],
            recv_sem=recv_sem.at[unit, stage],
            device_id=partner(bits, mine, order[stage]),
            device_id_type=MESH_ID,
        )

    settled = set()
    for unit, stage in plan:
        array = units[unit][0]
        if stage > 0:
            if array not in settled:
                settled.add(array)
                own[array].wait()
            message(unit, stage - 1).wait_recv()
        message(unit, stage).start()
    for array in range(n_arrays):
        if array not in settled:
            own[array].wait()
    for unit in range(len(units)):
        message(unit, count - 1).wait_recv()
    for unit in range(len(units)):
        for stage in range(count):
            message(unit, stage).wait_send()


def gather_all(mesh, shards, units, collective_id):
    bits = bit_table(mesh)
    routes = route_orders(bits)
    orders = [routes[u % 2] for u in range(len(units))]
    shapes = [unit_shape([s.shape for s in shards], unit) for unit in units]
    sizes = [
        shape[0] * shape[1] * shards[unit[0]].dtype.itemsize for shape, unit in zip(shapes, units)
    ]
    plan = plan_sends(bits, orders, sizes, True, None)
    n = len(shards)
    sems = (len(units), len(bits))
    return pl.pallas_call(
        functools.partial(gather_kernel, bits, units, orders, plan, n),
        out_shape=[
            jax.ShapeDtypeStruct((2,) * len(bits) + s.shape, s.dtype) for s in shards
        ],
        in_specs=[pl.BlockSpec(memory_space=pltpu.HBM)] * n,
        out_specs=[pl.BlockSpec(memory_space=pltpu.HBM)] * n,
        scratch_shapes=[
            pltpu.SemaphoreType.DMA(sems),
            pltpu.SemaphoreType.DMA(sems),
            pltpu.SemaphoreType.DMA((n,)),
        ],
        compiler_params=pltpu.CompilerParams(
            collective_id=collective_id, has_side_effects=True
        ),
        name="gather_weights",
    )(*shards)


def scatter_kernel(bits, units, orders, plan, n_arrays, n_units, *refs):
    count = len(bits)
    sources = refs[:n_arrays]
    results = refs[n_arrays : 2 * n_arrays]
    held = refs[2 * n_arrays : 2 * n_arrays + n_units]
    boxes = refs[2 * n_arrays + n_units : 2 * n_arrays + n_units + n_units * count]
    totals = refs[2 * n_arrays + n_units + n_units * count : -4]
    send_sem, recv_sem, load_sem, store_sem = refs[-4:]
    mine = my_bits(bits)

    def load(unit):
        array, rows, cols = units[unit]
        first = orders[unit][0]
        where = tuple(mine[b] if b == first else slice(None) for b in range(count))
        return pltpu.make_async_copy(
            sources[array].at[where + (rows, cols)], held[unit], load_sem.at[unit]
        )

    for unit in range(n_units):
        load(unit).start()
    greet(bits, mine)

    def message(unit, stage):
        array, rows, cols = units[unit]
        order = orders[unit]
        now = order[stage]
        where = []
        for b in range(count):
            if b == now:
                where.append(1 - mine[b])
            elif b in order[:stage]:
                where.append(mine[b])
            else:
                where.append(slice(None))
        if stage == 0:
            source = sources[array].at[tuple(where) + (rows, cols)]
        else:
            source = held[unit].at[tuple(w for b, w in enumerate(where) if b != order[0])]
        return pltpu.make_async_remote_copy(
            src_ref=source,
            dst_ref=boxes[unit * count + stage],
            send_sem=send_sem.at[unit, stage],
            recv_sem=recv_sem.at[unit, stage],
            device_id=partner(bits, mine, now),
            device_id_type=MESH_ID,
        )

    def add(unit, stage):
        order = orders[unit]
        message(unit, stage).wait_recv()
        if stage == 0:
            load(unit).wait()
        box = boxes[unit * count + stage]
        open_bits = [b for b in range(count) if b not in order[: stage + 1]]
        blocks = 2 ** len(open_bits)

        def one(block, carry):
            where = []
            spot = []
            for b in range(count):
                if b == order[0]:
                    continue
                if b in open_bits:
                    digit = (block // 2 ** (len(open_bits) - 1 - open_bits.index(b))) % 2
                    where.append(digit)
                    spot.append(digit)
                else:
                    where.append(mine[b])
            where, spot = tuple(where), tuple(spot)
            total = held[unit][where].astype(jnp.float32) + box[spot].astype(jnp.float32)
            if stage == count - 1:
                totals[unit][...] = total
            else:
                held[unit][where] = total.astype(held[unit].dtype)
            return carry

        if blocks == 1:
            one(0, 0)
        else:
            lax.fori_loop(0, blocks, one, 0)

    def store(unit):
        array, rows, cols = units[unit]
        return pltpu.make_async_copy(
            totals[unit], results[array].at[rows, cols], store_sem.at[unit]
        )

    for unit, stage in plan:
        if stage > 0:
            add(unit, stage - 1)
        message(unit, stage).start()
    for unit in range(n_units):
        add(unit, count - 1)
        store(unit).start()
    for unit in range(n_units):
        store(unit).wait()
        for stage in range(count):
            message(unit, stage).wait_send()


def scatter_all(mesh, terms, units, collective_id):
    bits = bit_table(mesh)
    routes = route_orders(bits)
    count = len(bits)
    orders = [routes[u % 2][::-1] for u in range(len(units))]
    shapes = [unit_shape([t.shape[count:] for t in terms], unit) for unit in units]
    kinds = [terms[array].dtype for array, _, _ in units]
    sizes = [s[0] * s[1] * kind.itemsize for s, kind in zip(shapes, kinds)]
    plan = plan_sends(bits, orders, sizes, False, 1000e3)
    n = len(terms)
    n_units = len(units)
    sems = (n_units, count)
    scratch = [
        pltpu.VMEM((2,) * (count - 1) + shapes[u], kinds[u]) for u in range(n_units)
    ]
    for u in range(n_units):
        for stage in range(count):
            scratch.append(pltpu.VMEM((2,) * (count - 1 - stage) + shapes[u], kinds[u]))
    scratch += [pltpu.VMEM(shapes[u], jnp.float32) for u in range(n_units)]
    scratch += [
        pltpu.SemaphoreType.DMA(sems),
        pltpu.SemaphoreType.DMA(sems),
        pltpu.SemaphoreType.DMA((n_units,)),
        pltpu.SemaphoreType.DMA((n_units,)),
    ]
    return pl.pallas_call(
        functools.partial(scatter_kernel, bits, units, orders, plan, n, n_units),
        out_shape=[jax.ShapeDtypeStruct(t.shape[count:], jnp.float32) for t in terms],
        in_specs=[pl.BlockSpec(memory_space=pltpu.HBM)] * n,
        out_specs=[pl.BlockSpec(memory_space=pltpu.HBM)] * n,
        scratch_shapes=scratch,
        compiler_params=pltpu.CompilerParams(
            collective_id=collective_id,
            has_side_effects=True,
            vmem_limit_bytes=60 * 1024 * 1024,
        ),
        name="scatter_grads",
    )(*terms)


MATS = (2, 4, 5, 7, 11, 13, 14, 16, 20, 22)
VECS = (0, 1, 3, 6, 8, 9, 10, 12, 15, 17, 18, 19, 23, 21)


def split_units(blocks):
    units = [(0, slice(None), slice(None))]
    for i, (rows, cols) in enumerate(blocks):
        base_rows, base_cols = min(rows, blocks[0][0]), min(cols, blocks[0][1])
        for top in range(0, rows, base_rows):
            for left in range(0, cols, base_cols):
                units.append(
                    (i + 1, slice(top, top + base_rows), slice(left, left + base_cols))
                )
    return units


def collect(mesh, *shards):
    mats = [shards[i] for i in MATS]
    if not can_route(mesh, mats[0].shape[0]):
        return tuple(lax.all_gather(s, BOTH, axis=0, tiled=True) for s in shards)
    per = shards[0].shape[0]
    packed = jnp.concatenate([shards[i].astype(jnp.float32) for i in VECS])
    spare = VEC_ROWS * VEC_LANES - packed.shape[0]
    packed = jnp.pad(packed, (0, spare)).reshape(VEC_ROWS, VEC_LANES)
    units = split_units([m.shape for m in mats])
    got = gather_all(mesh, [packed] + mats, units, 0)
    devices = mesh.shape["dp"] * mesh.shape["fsdp"]
    table = got[0].reshape(devices, VEC_ROWS * VEC_LANES)
    full = [None] * len(shards)
    start = 0
    for i in VECS:
        size = shards[i].shape[0]
        full[i] = table[:, start : start + size].reshape(devices * size)
        start += size
    for i, value in zip(MATS, got[1:]):
        full[i] = value.reshape(devices * shards[i].shape[0], shards[i].shape[1])
    return tuple(full)


def spread(mesh, *grads):
    devices = mesh.shape["dp"] * mesh.shape["fsdp"]
    mats = [grads[i] for i in MATS]
    if not can_route(mesh, mats[0].shape[0] // devices):
        return tuple(
            lax.psum_scatter(g.astype(jnp.float32), BOTH, scatter_dimension=0, tiled=True)
            for g in grads
        )
    spots = (2,) * len(bit_table(mesh))
    table = jnp.concatenate([grads[i].reshape(devices, -1) for i in VECS], axis=1)
    spare = VEC_ROWS * VEC_LANES - table.shape[1]
    table = jnp.pad(table, ((0, 0), (0, spare))).reshape(spots + (VEC_ROWS, VEC_LANES))
    terms = [m.reshape(spots + (m.shape[0] // devices, m.shape[1])) for m in mats]
    units = split_units([t.shape[-2:] for t in terms])
    got = scatter_all(mesh, [table] + terms, units, 1)
    flat = got[0].reshape(-1)
    owned = [None] * len(grads)
    start = 0
    for i in VECS:
        size = grads[i].shape[0] // devices
        owned[i] = flat[start : start + size]
        start += size
    for i, value in zip(MATS, got[1:]):
        owned[i] = value
    return tuple(owned)


def on_device(
    mesh,
    tokens,
    memory,
    page_lengths,
    end_flags,
    out_grad,
    self_gain,
    self_shift,
    self_query,
    self_query_bias,
    self_key,
    self_value,
    self_value_bias,
    self_out,
    self_out_bias,
    cross_gain,
    cross_shift,
    cross_query,
    cross_query_bias,
    cross_key,
    cross_value,
    cross_value_bias,
    cross_out,
    cross_out_bias,
    feed_gain,
    feed_shift,
    feed_in,
    feed_in_bias,
    feed_out,
    feed_out_bias,
):
    page_count, page_len, width = tokens.shape
    mem_len = memory.shape[1]
    row_count = page_count * page_len
    lengths_now = jnp.where(end_flags == 1, 1, page_lengths)
    inputs = tokens.reshape(row_count, width).astype(jnp.float32)
    mem_rows = memory.reshape(page_count * mem_len, width)
    full_set = collect(
        mesh,
        self_gain,
        self_shift,
        self_query,
        self_query_bias,
        self_key,
        self_value,
        self_value_bias,
        self_out,
        self_out_bias,
        cross_gain,
        cross_shift,
        cross_query,
        cross_query_bias,
        cross_key,
        cross_value,
        cross_value_bias,
        cross_out,
        cross_out_bias,
        feed_gain,
        feed_shift,
        feed_in,
        feed_in_bias,
        feed_out,
        feed_out_bias,
    )
    (
        gain_one,
        shift_one,
        query_mat,
        query_vec,
        key_mat,
        value_mat,
        value_vec,
        out_mat,
        out_vec,
        gain_two,
        shift_two,
        cquery_mat,
        cquery_vec,
        ckey_mat,
        cvalue_mat,
        cvalue_vec,
        cout_mat,
        cout_vec,
        gain_three,
        shift_three,
        hidden_mat,
        hidden_vec,
        final_mat,
        final_vec,
    ) = full_set
    first_norm, first_unit, first_std = normalize(
        inputs, gain_one.astype(jnp.float32), shift_one.astype(jnp.float32)
    )
    first_low = first_norm.astype(jnp.bfloat16)
    query_low = (product(first_low, query_mat) + query_vec.astype(jnp.float32)).astype(jnp.bfloat16)
    key_low = product(first_low, key_mat).astype(jnp.bfloat16)
    value_low = (product(first_low, value_mat) + value_vec.astype(jnp.float32)).astype(jnp.bfloat16)
    query_pages = query_low.reshape(page_count, page_len, width)
    key_pages = key_low.reshape(page_count, page_len, width)
    value_pages = value_low.reshape(page_count, page_len, width)
    self_mixed, self_total = self_forward(query_pages, key_pages, value_pages, lengths_now)
    self_low = self_mixed.reshape(row_count, width).astype(jnp.bfloat16)
    after_self = inputs + product(self_low, out_mat) + out_vec.astype(jnp.float32)
    second_norm, second_unit, second_std = normalize(
        after_self, gain_two.astype(jnp.float32), shift_two.astype(jnp.float32)
    )
    second_low = second_norm.astype(jnp.bfloat16)
    cquery_low = (product(second_low, cquery_mat) + cquery_vec.astype(jnp.float32)).astype(
        jnp.bfloat16
    )
    ckey_low = product(mem_rows, ckey_mat).astype(jnp.bfloat16)
    cvalue_low = (product(mem_rows, cvalue_mat) + cvalue_vec.astype(jnp.float32)).astype(
        jnp.bfloat16
    )
    cquery_pages = cquery_low.reshape(page_count, page_len, width)
    ckey_pages = ckey_low.reshape(page_count, mem_len, width)
    cvalue_pages = cvalue_low.reshape(page_count, mem_len, width)
    cross_mixed, cross_total = cross_forward(cquery_pages, ckey_pages, cvalue_pages)
    cross_low = cross_mixed.reshape(row_count, width).astype(jnp.bfloat16)
    after_cross = after_self + product(cross_low, cout_mat) + cout_vec.astype(jnp.float32)
    third_norm, third_unit, third_std = normalize(
        after_cross, gain_three.astype(jnp.float32), shift_three.astype(jnp.float32)
    )
    third_low = third_norm.astype(jnp.bfloat16)
    hidden_pre = product(third_low, hidden_mat) + hidden_vec.astype(jnp.float32)
    hidden_low = jax.nn.gelu(hidden_pre, approximate=False).astype(jnp.bfloat16)
    result = after_cross + product(hidden_low, final_mat) + final_vec.astype(jnp.float32)
    layer_out = result.astype(jnp.bfloat16).reshape(page_count, page_len, width)
    grad_rows = out_grad.reshape(row_count, width).astype(jnp.float32)
    final_grad = out_grad.reshape(row_count, width)
    grad_final_mat = product_tn(hidden_low, final_grad).astype(jnp.bfloat16)
    grad_final_vec = jnp.sum(final_grad.astype(jnp.float32), axis=0)
    hidden_grad = (product_nt(final_grad, final_mat) * gelu_slope(hidden_pre)).astype(jnp.bfloat16)
    grad_hidden_mat = product_tn(third_low, hidden_grad).astype(jnp.bfloat16)
    grad_hidden_vec = jnp.sum(hidden_grad.astype(jnp.float32), axis=0)
    third_back, grad_gain_three, grad_shift_three = normalize_back(
        product_nt(hidden_grad, hidden_mat), third_unit, third_std, gain_three.astype(jnp.float32)
    )
    cross_grad_total = grad_rows + third_back
    cout_grad = cross_grad_total.astype(jnp.bfloat16)
    grad_cout_mat = product_tn(cross_low, cout_grad).astype(jnp.bfloat16)
    grad_cout_vec = jnp.sum(cout_grad.astype(jnp.float32), axis=0)
    cmix_grad = (
        product_nt(cout_grad, cout_mat).astype(jnp.bfloat16).reshape(page_count, page_len, width)
    )
    cquery_grad, ckey_grad, cvalue_grad = cross_backward(
        cquery_pages, ckey_pages, cvalue_pages, cmix_grad, cross_total
    )
    cquery_grad = cquery_grad.reshape(row_count, width).astype(jnp.bfloat16)
    ckey_grad = ckey_grad.reshape(page_count * mem_len, width).astype(jnp.bfloat16)
    cvalue_grad = cvalue_grad.reshape(page_count * mem_len, width).astype(jnp.bfloat16)
    grad_cquery_mat = product_tn(second_low, cquery_grad).astype(jnp.bfloat16)
    grad_cquery_vec = jnp.sum(cquery_grad.astype(jnp.float32), axis=0)
    grad_ckey_mat = product_tn(mem_rows, ckey_grad).astype(jnp.bfloat16)
    grad_cvalue_mat = product_tn(mem_rows, cvalue_grad).astype(jnp.bfloat16)
    grad_cvalue_vec = jnp.sum(cvalue_grad.astype(jnp.float32), axis=0)
    memory_grad = (product_nt(ckey_grad, ckey_mat) + product_nt(cvalue_grad, cvalue_mat)).reshape(
        page_count, mem_len, width
    )
    second_back, grad_gain_two, grad_shift_two = normalize_back(
        product_nt(cquery_grad, cquery_mat), second_unit, second_std, gain_two.astype(jnp.float32)
    )
    self_grad_total = cross_grad_total + second_back
    sout_grad = self_grad_total.astype(jnp.bfloat16)
    grad_out_mat = product_tn(self_low, sout_grad).astype(jnp.bfloat16)
    grad_out_vec = jnp.sum(sout_grad.astype(jnp.float32), axis=0)
    smix_grad = (
        product_nt(sout_grad, out_mat).astype(jnp.bfloat16).reshape(page_count, page_len, width)
    )
    query_grad, key_grad, value_grad = self_backward(
        query_pages, key_pages, value_pages, smix_grad, self_total, lengths_now
    )
    query_grad = query_grad.reshape(row_count, width).astype(jnp.bfloat16)
    key_grad = key_grad.reshape(row_count, width).astype(jnp.bfloat16)
    value_grad = value_grad.reshape(row_count, width).astype(jnp.bfloat16)
    grad_query_mat = product_tn(first_low, query_grad).astype(jnp.bfloat16)
    grad_query_vec = jnp.sum(query_grad.astype(jnp.float32), axis=0)
    grad_key_mat = product_tn(first_low, key_grad).astype(jnp.bfloat16)
    grad_value_mat = product_tn(first_low, value_grad).astype(jnp.bfloat16)
    grad_value_vec = jnp.sum(value_grad.astype(jnp.float32), axis=0)
    first_in = (
        product_nt(query_grad, query_mat)
        + product_nt(key_grad, key_mat)
        + product_nt(value_grad, value_mat)
    )
    first_back, grad_gain_one, grad_shift_one = normalize_back(
        first_in, first_unit, first_std, gain_one.astype(jnp.float32)
    )
    tokens_grad = (self_grad_total + first_back).reshape(page_count, page_len, width)
    owned = spread(
        mesh,
        grad_gain_one,
        grad_shift_one,
        grad_query_mat,
        grad_query_vec,
        grad_key_mat,
        grad_value_mat,
        grad_value_vec,
        grad_out_mat,
        grad_out_vec,
        grad_gain_two,
        grad_shift_two,
        grad_cquery_mat,
        grad_cquery_vec,
        grad_ckey_mat,
        grad_cvalue_mat,
        grad_cvalue_vec,
        grad_cout_mat,
        grad_cout_vec,
        grad_gain_three,
        grad_shift_three,
        grad_hidden_mat,
        grad_hidden_vec,
        grad_final_mat,
        grad_final_vec,
    )
    return (layer_out, tokens_grad, memory_grad) + tuple(owned)


def solution(mesh):
    placed = (
        P(("dp", "fsdp"), None, None),
        P(("dp", "fsdp"), None, None),
        P(("dp", "fsdp")),
        P(("dp", "fsdp")),
        P(("dp", "fsdp"), None, None),
        P(("dp", "fsdp")),
        P(("dp", "fsdp")),
        P(("dp", "fsdp"), None),
        P(("dp", "fsdp")),
        P(("dp", "fsdp"), None),
        P(("dp", "fsdp"), None),
        P(("dp", "fsdp")),
        P(("dp", "fsdp"), None),
        P(("dp", "fsdp")),
        P(("dp", "fsdp")),
        P(("dp", "fsdp")),
        P(("dp", "fsdp"), None),
        P(("dp", "fsdp")),
        P(("dp", "fsdp"), None),
        P(("dp", "fsdp"), None),
        P(("dp", "fsdp")),
        P(("dp", "fsdp"), None),
        P(("dp", "fsdp")),
        P(("dp", "fsdp")),
        P(("dp", "fsdp")),
        P(("dp", "fsdp"), None),
        P(("dp", "fsdp")),
        P(("dp", "fsdp"), None),
        P(("dp", "fsdp")),
    )
    return jax.shard_map(
        functools.partial(on_device, mesh),
        mesh=mesh,
        in_specs=placed,
        out_specs=(
            P(("dp", "fsdp"), None, None),
            P(("dp", "fsdp"), None, None),
            P(("dp", "fsdp"), None, None),
            P(("dp", "fsdp")),
            P(("dp", "fsdp")),
            P(("dp", "fsdp"), None),
            P(("dp", "fsdp")),
            P(("dp", "fsdp"), None),
            P(("dp", "fsdp"), None),
            P(("dp", "fsdp")),
            P(("dp", "fsdp"), None),
            P(("dp", "fsdp")),
            P(("dp", "fsdp")),
            P(("dp", "fsdp")),
            P(("dp", "fsdp"), None),
            P(("dp", "fsdp")),
            P(("dp", "fsdp"), None),
            P(("dp", "fsdp"), None),
            P(("dp", "fsdp")),
            P(("dp", "fsdp"), None),
            P(("dp", "fsdp")),
            P(("dp", "fsdp")),
            P(("dp", "fsdp")),
            P(("dp", "fsdp"), None),
            P(("dp", "fsdp")),
            P(("dp", "fsdp"), None),
            P(("dp", "fsdp")),
        ),
        check_vma=False,
    )
```

```python
import functools

import jax
import jax.numpy as jnp
from jax import lax
from jax.experimental import pallas as pl
from jax.experimental.pallas import tpu as pltpu
from jax.sharding import PartitionSpec as P

HEADS = 16


EPSILON = 1e-05
ROOT_HALF = 0.7071067811865476
INV_ROOT_TWO_PI = 0.3989422804014327


def product(left, right):
    return jnp.dot(left, right, preferred_element_type=jnp.float32)


def product_tn(left, right):
    return lax.dot_general(
        left, right, (((0,), (0,)), ((), ())), preferred_element_type=jnp.float32
    )


def product_nt(left, right):
    return lax.dot_general(
        left, right, (((1,), (1,)), ((), ())), preferred_element_type=jnp.float32
    )


def normalize(rows_in, norm_gain, norm_shift):
    centered = rows_in - jnp.mean(rows_in, axis=-1, keepdims=True)
    inv_std = lax.rsqrt(jnp.mean(centered * centered, axis=-1, keepdims=True) + EPSILON)
    unit_rows = centered * inv_std
    return (unit_rows * norm_gain + norm_shift, unit_rows, inv_std)


def normalize_back(grad_norm, unit_rows, inv_std, norm_gain):
    scaled = grad_norm * norm_gain
    inner_part = (
        scaled
        - jnp.mean(scaled, axis=-1, keepdims=True)
        - unit_rows * jnp.mean(scaled * unit_rows, axis=-1, keepdims=True)
    )
    return (
        inner_part * inv_std,
        jnp.sum(grad_norm * unit_rows, axis=0),
        jnp.sum(grad_norm, axis=0),
    )


def gelu_slope(pre_act):
    return 0.5 * (
        1.0 + jax.scipy.special.erf(pre_act * ROOT_HALF)
    ) + pre_act * INV_ROOT_TWO_PI * jnp.exp(-0.5 * pre_act * pre_act)


LOG2E = 1.4426950408889634
LN2 = 0.6931471805599453


def dot_nn(a, b):
    return jnp.dot(a, b, preferred_element_type=jnp.float32)


def dot_nt(a, b):
    return lax.dot_general(a, b, (((1,), (1,)), ((), ())), preferred_element_type=jnp.float32)


def dot_tn(a, b):
    return lax.dot_general(a, b, (((0,), (0,)), ((), ())), preferred_element_type=jnp.float32)


def lane_half(x, head, half):
    lane = lax.broadcasted_iota(jnp.int32, (1, x.shape[1]), 1)
    keep = (lane < half) if head == 0 else (lane >= half)
    return jnp.where(keep, x, jnp.zeros_like(x))


def causal_spans(rows, chunk):
    return [(start, chunk, start + chunk) for start in range(0, rows, chunk)]


def limit_row(start, width, length):
    pos = start + lax.broadcasted_iota(jnp.int32, (1, width), 1)
    return jnp.minimum(pos, length - 1)


def forward_pair(load_q, load_k, load_v, write, spans, length, scale):
    for start, size, keys in spans:
        q2 = load_q(start, size)
        k2 = load_k(0, keys)
        v2 = load_v(0, keys)
        half = q2.shape[1] // 2
        vt = v2.T
        outs, totals = [], []
        for head in (0, 1):
            raw = dot_nt(k2, lane_half(q2, head, half))
            if length is not None:
                key_pos = lax.broadcasted_iota(jnp.int32, raw.shape, 0)
                raw = jnp.where(key_pos <= limit_row(start, size, length), raw, -1e30)
            top = jnp.max(raw, axis=0, keepdims=True)
            expo = jnp.exp2((raw - top) * (scale * LOG2E))
            total = jnp.sum(expo, axis=0, keepdims=True)
            mixed = dot_nn(vt[head * half : (head + 1) * half], expo.astype(jnp.bfloat16))
            outs.append(mixed / total)
            totals.append(top * (scale * LOG2E) + jnp.log2(total))
        write(start, size, jnp.concatenate(outs, axis=0).T.astype(jnp.bfloat16), totals)


def fwd_kernel(masked, scale, chunk, *refs):
    if masked:
        len_ref, q_ref, k_ref, v_ref, a_ref, t_ref = refs
        length = len_ref[pl.program_id(0)]
    else:
        q_ref, k_ref, v_ref, a_ref, t_ref = refs
        length = None
    rows, keys = q_ref.shape[1], k_ref.shape[1]
    if masked:
        spans = causal_spans(rows, chunk)
    else:
        spans = [(s, chunk, keys) for s in range(0, rows, chunk)]

    def write(start, size, out, totals):
        a_ref[0, pl.ds(start, size), :] = out
        for head in (0, 1):
            t_ref[0, 0, pl.ds(head, 1), pl.ds(start, size)] = totals[head]

    forward_pair(
        lambda s, n: q_ref[0, pl.ds(s, n), :],
        lambda s, n: k_ref[0, pl.ds(s, n), :],
        lambda s, n: v_ref[0, pl.ds(s, n), :],
        write, spans, length, scale,
    )


def attend_fwd(q, k, v, lengths, heads, chunk=256):
    pages, rows, width = q.shape
    keys = k.shape[1]
    head = width // heads
    pairs = heads // 2
    masked = lengths is not None
    row_spec = pl.BlockSpec((1, rows, 2 * head), lambda p, h: (p, 0, h))
    key_spec = pl.BlockSpec((1, keys, 2 * head), lambda p, h: (p, 0, h))
    in_specs = [row_spec, key_spec, key_spec]
    args = [q, k, v]
    if masked:
        in_specs = [pl.BlockSpec(memory_space=pltpu.SMEM)] + in_specs
        args = [lengths] + args
    return pl.pallas_call(
        functools.partial(fwd_kernel, masked, head**-0.5, chunk),
        grid=(pages, pairs),
        in_specs=in_specs,
        out_specs=[row_spec, pl.BlockSpec((1, 1, 2, rows), lambda p, h: (p, h, 0, 0))],
        out_shape=[
            jax.ShapeDtypeStruct(q.shape, jnp.bfloat16),
            jax.ShapeDtypeStruct((pages, pairs, 2, rows), jnp.float32),
        ],
        compiler_params=pltpu.CompilerParams(vmem_limit_bytes=48 * 1024 * 1024),
        name="attend_forward",
    )(*args)


def bwd_kernel(masked, scale, chunk, *refs):
    if masked:
        len_ref, q_ref, k_ref, v_ref, g_ref, t_ref, dq_ref, dk_ref, dv_ref, dk_acc, dv_acc = refs
        length = len_ref[pl.program_id(0)]
    else:
        q_ref, k_ref, v_ref, g_ref, t_ref, dq_ref, dk_ref, dv_ref, dk_acc, dv_acc = refs
        length = None
    rows, keys_all = q_ref.shape[1], k_ref.shape[1]
    if masked:
        spans = causal_spans(rows, chunk)[::-1]
    else:
        spans = [(s, chunk, keys_all) for s in range(0, rows, chunk)]
    half = q_ref.shape[2] // 2
    for step, (start, size, keys) in enumerate(spans):
        q2 = q_ref[0, pl.ds(start, size), :]
        g2 = g_ref[0, pl.ds(start, size), :]
        k2 = k_ref[0, pl.ds(0, keys), :]
        v2 = v_ref[0, pl.ds(0, keys), :]
        kt = k2.T
        dk, dv, dqt = None, None, []
        for head in (0, 1):
            qm = lane_half(q2, head, half)
            gm = lane_half(g2, head, half)
            raw = dot_nt(k2, qm)
            total = t_ref[0, 0, pl.ds(head, 1), pl.ds(start, size)]
            probs = jnp.exp2(raw * (scale * LOG2E) - total)
            if length is not None:
                key_pos = lax.broadcasted_iota(jnp.int32, raw.shape, 0)
                probs = jnp.where(key_pos <= limit_row(start, size, length), probs, 0.0)
            grad = dot_nt(v2, gm)
            part = probs * grad
            dot_row = jnp.sum(part, axis=0, keepdims=True)
            score = ((part - probs * dot_row) * scale).astype(jnp.bfloat16)
            dvh = dot_nn(probs.astype(jnp.bfloat16), gm)
            dkh = dot_nn(score, qm)
            dv = dvh if dv is None else dv + dvh
            dk = dkh if dk is None else dk + dkh
            dqt.append(dot_nn(kt[head * half : (head + 1) * half], score))
        dq_ref[0, pl.ds(start, size), :] = jnp.concatenate(dqt, axis=0).T.astype(jnp.bfloat16)
        if step == 0:
            dk_acc[pl.ds(0, keys), :] = dk
            dv_acc[pl.ds(0, keys), :] = dv
        else:
            dk_acc[pl.ds(0, keys), :] += dk
            dv_acc[pl.ds(0, keys), :] += dv
    dk_ref[0] = dk_acc[...].astype(jnp.bfloat16)
    dv_ref[0] = dv_acc[...].astype(jnp.bfloat16)


def attend_bwd(q, k, v, g, totals, lengths, heads, chunk=256):
    pages, rows, width = q.shape
    keys = k.shape[1]
    head = width // heads
    pairs = heads // 2
    masked = lengths is not None
    row_spec = pl.BlockSpec((1, rows, 2 * head), lambda p, h: (p, 0, h))
    key_spec = pl.BlockSpec((1, keys, 2 * head), lambda p, h: (p, 0, h))
    total_spec = pl.BlockSpec((1, 1, 2, rows), lambda p, h: (p, h, 0, 0))
    in_specs = [row_spec, key_spec, key_spec, row_spec, total_spec]
    args = [q, k, v, g, totals]
    if masked:
        in_specs = [pl.BlockSpec(memory_space=pltpu.SMEM)] + in_specs
        args = [lengths] + args
    return pl.pallas_call(
        functools.partial(bwd_kernel, masked, head**-0.5, chunk),
        grid=(pages, pairs),
        in_specs=in_specs,
        out_specs=[row_spec, key_spec, key_spec],
        out_shape=[jax.ShapeDtypeStruct(a.shape, jnp.bfloat16) for a in (q, k, v)],
        scratch_shapes=[pltpu.VMEM((keys, 2 * head), jnp.float32)] * 2,
        compiler_params=pltpu.CompilerParams(vmem_limit_bytes=48 * 1024 * 1024),
        name="attend_backward",
    )(*args)


MESH_ID = pl.DeviceIdType.MESH
BOTH = ("dp", "fsdp")
CORE_RATE = 500e3
LINK_RATE = 96e3
HOP = 2.5
VEC_ROWS = 8
VEC_LANES = 128


def bit_table(mesh):
    bits = []
    for axis, name in enumerate(BOTH):
        step = mesh.shape[name] // 2
        while step >= 1:
            bits.append((axis, step))
            step //= 2
    return bits


def can_route(mesh, rows):
    sizes = [mesh.shape[name] for name in BOTH]
    return all(s & (s - 1) == 0 for s in sizes) and rows % 16 == 0


def route_orders(bits):
    outer = [i for i, (axis, _) in enumerate(bits) if axis == 0]
    inner = [i for i, (axis, _) in enumerate(bits) if axis == 1]
    return (outer + inner, outer + inner[:-1][::-1] + inner[-1:])


def loads_of(bits, at, size):
    axis, step = bits[at]
    if axis == 1 and step == 1:
        return {"core": size / CORE_RATE}
    if axis == 1:
        return {f"inner{step}": 2 * size / LINK_RATE}
    loads = {"outer1": 2 * size / LINK_RATE}
    if step > 1:
        loads["outer2"] = 2 * size * step / LINK_RATE
    return loads


def plan_sends(bits, orders, sizes, growing, add_rate):
    count = len(bits)
    ready = [(0.0, unit, 0) for unit in range(len(orders))]
    free = {}
    plan = []
    while ready:
        choices = []
        for when, unit, stage in ready:
            scale = 2**stage if growing else 2 ** (count - 1 - stage)
            loads = loads_of(bits, orders[unit][stage], sizes[unit] * scale)
            start = max([when] + [free.get(link, 0.0) for link in loads])
            choices.append((round(start, 3), unit, -stage, when, scale))
        start, unit, stage, when, scale = min(choices)
        stage = -stage
        ready.remove((when, unit, stage))
        loads = loads_of(bits, orders[unit][stage], sizes[unit] * scale)
        for link, took in loads.items():
            free[link] = start + took
        plan.append((start, unit, stage))
        if stage + 1 < count:
            after = start + max(loads.values()) + HOP
            if add_rate:
                after += sizes[unit] * scale / add_rate
            ready.append((after, unit, stage + 1))
    return [(unit, stage) for _, unit, stage in sorted(plan)]


def my_bits(bits):
    place = (lax.axis_index("dp"), lax.axis_index("fsdp"))
    return [(place[axis] // step) % 2 for axis, step in bits]


def partner(bits, mine, at):
    place = [lax.axis_index("dp"), lax.axis_index("fsdp")]
    axis, step = bits[at]
    place[axis] = place[axis] + step * (1 - 2 * mine[at])
    return tuple(place)


def greet(bits, mine):
    barrier = pltpu.get_barrier_semaphore()
    for at in range(len(bits)):
        pl.semaphore_signal(
            barrier, inc=1, device_id=partner(bits, mine, at), device_id_type=MESH_ID
        )
    pl.semaphore_wait(barrier, len(bits))


def unit_shape(blocks, unit):
    array, rows, cols = unit
    block = blocks[array]
    return (len(range(*rows.indices(block[0]))), len(range(*cols.indices(block[1]))))


def gather_kernel(bits, units, orders, plan, n_arrays, *refs):
    count = len(bits)
    sources = refs[:n_arrays]
    targets = refs[n_arrays : 2 * n_arrays]
    send_sem, recv_sem, own_sem = refs[2 * n_arrays :]
    mine = my_bits(bits)
    own = [
        pltpu.make_async_copy(sources[i], targets[i].at[tuple(mine)], own_sem.at[i])
        for i in range(n_arrays)
    ]
    for copy in own:
        copy.start()
    greet(bits, mine)

    def message(unit, stage):
        array, rows, cols = units[unit]
        order = orders[unit]
        where = tuple(slice(None) if b in order[:stage] else mine[b] for b in range(count))
        place = targets[array].at[where + (rows, cols)]
        source = sources[array].at[rows, cols] if stage == 0 else place
        return pltpu.make_async_remote_copy(
            src_ref=source,
            dst_ref=place,
            send_sem=send_sem.at[unit, stage],
            recv_sem=recv_sem.at[unit, stage],
            device_id=partner(bits, mine, order[stage]),
            device_id_type=MESH_ID,
        )

    settled = set()
    for unit, stage in plan:
        array = units[unit][0]
        if stage > 0:
            if array not in settled:
                settled.add(array)
                own[array].wait()
            message(unit, stage - 1).wait_recv()
        message(unit, stage).start()
    for array in range(n_arrays):
        if array not in settled:
            own[array].wait()
    for unit in range(len(units)):
        message(unit, count - 1).wait_recv()
    for unit in range(len(units)):
        for stage in range(count):
            message(unit, stage).wait_send()


def gather_all(mesh, shards, units, collective_id):
    bits = bit_table(mesh)
    routes = route_orders(bits)
    orders = [routes[u % 2] for u in range(len(units))]
    shapes = [unit_shape([s.shape for s in shards], unit) for unit in units]
    sizes = [
        shape[0] * shape[1] * shards[unit[0]].dtype.itemsize for shape, unit in zip(shapes, units)
    ]
    plan = plan_sends(bits, orders, sizes, True, None)
    n = len(shards)
    sems = (len(units), len(bits))
    return pl.pallas_call(
        functools.partial(gather_kernel, bits, units, orders, plan, n),
        out_shape=[
            jax.ShapeDtypeStruct((2,) * len(bits) + s.shape, s.dtype) for s in shards
        ],
        in_specs=[pl.BlockSpec(memory_space=pltpu.HBM)] * n,
        out_specs=[pl.BlockSpec(memory_space=pltpu.HBM)] * n,
        scratch_shapes=[
            pltpu.SemaphoreType.DMA(sems),
            pltpu.SemaphoreType.DMA(sems),
            pltpu.SemaphoreType.DMA((n,)),
        ],
        compiler_params=pltpu.CompilerParams(
            collective_id=collective_id, has_side_effects=True
        ),
        name="gather_weights",
    )(*shards)


def scatter_kernel(bits, units, orders, plan, n_arrays, n_units, *refs):
    count = len(bits)
    sources = refs[:n_arrays]
    results = refs[n_arrays : 2 * n_arrays]
    held = refs[2 * n_arrays : 2 * n_arrays + n_units]
    boxes = refs[2 * n_arrays + n_units : 2 * n_arrays + n_units + n_units * count]
    totals = refs[2 * n_arrays + n_units + n_units * count : -4]
    send_sem, recv_sem, load_sem, store_sem = refs[-4:]
    mine = my_bits(bits)

    def load(unit):
        array, rows, cols = units[unit]
        first = orders[unit][0]
        where = tuple(mine[b] if b == first else slice(None) for b in range(count))
        return pltpu.make_async_copy(
            sources[array].at[where + (rows, cols)], held[unit], load_sem.at[unit]
        )

    for unit in range(n_units):
        load(unit).start()
    greet(bits, mine)

    def message(unit, stage):
        array, rows, cols = units[unit]
        order = orders[unit]
        now = order[stage]
        where = []
        for b in range(count):
            if b == now:
                where.append(1 - mine[b])
            elif b in order[:stage]:
                where.append(mine[b])
            else:
                where.append(slice(None))
        if stage == 0:
            source = sources[array].at[tuple(where) + (rows, cols)]
        else:
            source = held[unit].at[tuple(w for b, w in enumerate(where) if b != order[0])]
        return pltpu.make_async_remote_copy(
            src_ref=source,
            dst_ref=boxes[unit * count + stage],
            send_sem=send_sem.at[unit, stage],
            recv_sem=recv_sem.at[unit, stage],
            device_id=partner(bits, mine, now),
            device_id_type=MESH_ID,
        )

    def add(unit, stage):
        order = orders[unit]
        message(unit, stage).wait_recv()
        if stage == 0:
            load(unit).wait()
        box = boxes[unit * count + stage]
        open_bits = [b for b in range(count) if b not in order[: stage + 1]]
        blocks = 2 ** len(open_bits)

        def one(block, carry):
            where = []
            spot = []
            for b in range(count):
                if b == order[0]:
                    continue
                if b in open_bits:
                    digit = (block // 2 ** (len(open_bits) - 1 - open_bits.index(b))) % 2
                    where.append(digit)
                    spot.append(digit)
                else:
                    where.append(mine[b])
            where, spot = tuple(where), tuple(spot)
            total = held[unit][where].astype(jnp.float32) + box[spot].astype(jnp.float32)
            if stage == count - 1:
                totals[unit][...] = total
            else:
                held[unit][where] = total.astype(held[unit].dtype)
            return carry

        if blocks == 1:
            one(0, 0)
        else:
            lax.fori_loop(0, blocks, one, 0)

    def store(unit):
        array, rows, cols = units[unit]
        return pltpu.make_async_copy(
            totals[unit], results[array].at[rows, cols], store_sem.at[unit]
        )

    for unit, stage in plan:
        if stage > 0:
            add(unit, stage - 1)
        message(unit, stage).start()
    for unit in range(n_units):
        add(unit, count - 1)
        store(unit).start()
    for unit in range(n_units):
        store(unit).wait()
        for stage in range(count):
            message(unit, stage).wait_send()


def scatter_all(mesh, terms, units, collective_id):
    bits = bit_table(mesh)
    routes = route_orders(bits)
    count = len(bits)
    orders = [routes[u % 2][::-1] for u in range(len(units))]
    shapes = [unit_shape([t.shape[count:] for t in terms], unit) for unit in units]
    kinds = [terms[array].dtype for array, _, _ in units]
    sizes = [s[0] * s[1] * kind.itemsize for s, kind in zip(shapes, kinds)]
    plan = plan_sends(bits, orders, sizes, False, 1000e3)
    n = len(terms)
    n_units = len(units)
    sems = (n_units, count)
    scratch = [
        pltpu.VMEM((2,) * (count - 1) + shapes[u], kinds[u]) for u in range(n_units)
    ]
    for u in range(n_units):
        for stage in range(count):
            scratch.append(pltpu.VMEM((2,) * (count - 1 - stage) + shapes[u], kinds[u]))
    scratch += [pltpu.VMEM(shapes[u], jnp.float32) for u in range(n_units)]
    scratch += [
        pltpu.SemaphoreType.DMA(sems),
        pltpu.SemaphoreType.DMA(sems),
        pltpu.SemaphoreType.DMA((n_units,)),
        pltpu.SemaphoreType.DMA((n_units,)),
    ]
    return pl.pallas_call(
        functools.partial(scatter_kernel, bits, units, orders, plan, n, n_units),
        out_shape=[jax.ShapeDtypeStruct(t.shape[count:], jnp.float32) for t in terms],
        in_specs=[pl.BlockSpec(memory_space=pltpu.HBM)] * n,
        out_specs=[pl.BlockSpec(memory_space=pltpu.HBM)] * n,
        scratch_shapes=scratch,
        compiler_params=pltpu.CompilerParams(
            collective_id=collective_id,
            has_side_effects=True,
            vmem_limit_bytes=60 * 1024 * 1024,
        ),
        name="scatter_grads",
    )(*terms)


MATS = (2, 4, 5, 7, 11, 13, 14, 16, 20, 22)
VECS = (0, 1, 3, 6, 8, 9, 10, 12, 15, 17, 18, 19, 23, 21)


def split_units(blocks):
    units = [(0, slice(None), slice(None))]
    for i, (rows, cols) in enumerate(blocks):
        base_rows, base_cols = min(rows, blocks[0][0]), min(cols, blocks[0][1])
        for top in range(0, rows, base_rows):
            for left in range(0, cols, base_cols):
                units.append(
                    (i + 1, slice(top, top + base_rows), slice(left, left + base_cols))
                )
    return units


def collect(mesh, *shards):
    mats = [shards[i] for i in MATS]
    if not can_route(mesh, mats[0].shape[0]):
        return tuple(lax.all_gather(s, BOTH, axis=0, tiled=True) for s in shards)
    per = shards[0].shape[0]
    packed = jnp.concatenate([shards[i].astype(jnp.float32) for i in VECS])
    spare = VEC_ROWS * VEC_LANES - packed.shape[0]
    packed = jnp.pad(packed, (0, spare)).reshape(VEC_ROWS, VEC_LANES)
    units = split_units([m.shape for m in mats])
    got = gather_all(mesh, [packed] + mats, units, 0)
    devices = mesh.shape["dp"] * mesh.shape["fsdp"]
    table = got[0].reshape(devices, VEC_ROWS * VEC_LANES)
    full = [None] * len(shards)
    start = 0
    for i in VECS:
        size = shards[i].shape[0]
        full[i] = table[:, start : start + size].reshape(devices * size)
        start += size
    for i, value in zip(MATS, got[1:]):
        full[i] = value.reshape(devices * shards[i].shape[0], shards[i].shape[1])
    return tuple(full)


def spread(mesh, *grads):
    devices = mesh.shape["dp"] * mesh.shape["fsdp"]
    mats = [grads[i] for i in MATS]
    if not can_route(mesh, mats[0].shape[0] // devices):
        return tuple(
            lax.psum_scatter(g.astype(jnp.float32), BOTH, scatter_dimension=0, tiled=True)
            for g in grads
        )
    spots = (2,) * len(bit_table(mesh))
    table = jnp.concatenate([grads[i].reshape(devices, -1) for i in VECS], axis=1)
    spare = VEC_ROWS * VEC_LANES - table.shape[1]
    table = jnp.pad(table, ((0, 0), (0, spare))).reshape(spots + (VEC_ROWS, VEC_LANES))
    terms = [m.reshape(spots + (m.shape[0] // devices, m.shape[1])) for m in mats]
    units = split_units([t.shape[-2:] for t in terms])
    got = scatter_all(mesh, [table] + terms, units, 1)
    flat = got[0].reshape(-1)
    owned = [None] * len(grads)
    start = 0
    for i in VECS:
        size = grads[i].shape[0] // devices
        owned[i] = flat[start : start + size]
        start += size
    for i, value in zip(MATS, got[1:]):
        owned[i] = value
    return tuple(owned)


def on_device(
    mesh,
    tokens,
    memory,
    page_lengths,
    end_flags,
    out_grad,
    self_gain,
    self_shift,
    self_query,
    self_query_bias,
    self_key,
    self_value,
    self_value_bias,
    self_out,
    self_out_bias,
    cross_gain,
    cross_shift,
    cross_query,
    cross_query_bias,
    cross_key,
    cross_value,
    cross_value_bias,
    cross_out,
    cross_out_bias,
    feed_gain,
    feed_shift,
    feed_in,
    feed_in_bias,
    feed_out,
    feed_out_bias,
):
    page_count, page_len, width = tokens.shape
    mem_len = memory.shape[1]
    row_count = page_count * page_len
    lengths_now = jnp.where(end_flags == 1, 1, page_lengths)
    inputs = tokens.reshape(row_count, width).astype(jnp.float32)
    mem_rows = memory.reshape(page_count * mem_len, width)
    full_set = collect(
        mesh,
        self_gain,
        self_shift,
        self_query,
        self_query_bias,
        self_key,
        self_value,
        self_value_bias,
        self_out,
        self_out_bias,
        cross_gain,
        cross_shift,
        cross_query,
        cross_query_bias,
        cross_key,
        cross_value,
        cross_value_bias,
        cross_out,
        cross_out_bias,
        feed_gain,
        feed_shift,
        feed_in,
        feed_in_bias,
        feed_out,
        feed_out_bias,
    )
    (
        gain_one,
        shift_one,
        query_mat,
        query_vec,
        key_mat,
        value_mat,
        value_vec,
        out_mat,
        out_vec,
        gain_two,
        shift_two,
        cquery_mat,
        cquery_vec,
        ckey_mat,
        cvalue_mat,
        cvalue_vec,
        cout_mat,
        cout_vec,
        gain_three,
        shift_three,
        hidden_mat,
        hidden_vec,
        final_mat,
        final_vec,
    ) = full_set
    first_norm, first_unit, first_std = normalize(
        inputs, gain_one.astype(jnp.float32), shift_one.astype(jnp.float32)
    )
    first_low = first_norm.astype(jnp.bfloat16)
    query_low = (product(first_low, query_mat) + query_vec.astype(jnp.float32)).astype(jnp.bfloat16)
    key_low = product(first_low, key_mat).astype(jnp.bfloat16)
    value_low = (product(first_low, value_mat) + value_vec.astype(jnp.float32)).astype(jnp.bfloat16)
    query_pages = query_low.reshape(page_count, page_len, width)
    key_pages = key_low.reshape(page_count, page_len, width)
    value_pages = value_low.reshape(page_count, page_len, width)
    self_mixed, self_total = attend_fwd(
        query_pages, key_pages, value_pages, lengths_now, HEADS, 512
    )
    self_low = self_mixed.reshape(row_count, width)
    after_self = inputs + product(self_low, out_mat) + out_vec.astype(jnp.float32)
    second_norm, second_unit, second_std = normalize(
        after_self, gain_two.astype(jnp.float32), shift_two.astype(jnp.float32)
    )
    second_low = second_norm.astype(jnp.bfloat16)
    cquery_low = (product(second_low, cquery_mat) + cquery_vec.astype(jnp.float32)).astype(
        jnp.bfloat16
    )
    ckey_low = product(mem_rows, ckey_mat).astype(jnp.bfloat16)
    cvalue_low = (product(mem_rows, cvalue_mat) + cvalue_vec.astype(jnp.float32)).astype(
        jnp.bfloat16
    )
    cquery_pages = cquery_low.reshape(page_count, page_len, width)
    ckey_pages = ckey_low.reshape(page_count, mem_len, width)
    cvalue_pages = cvalue_low.reshape(page_count, mem_len, width)
    cross_mixed, cross_total = attend_fwd(
        cquery_pages, ckey_pages, cvalue_pages, None, HEADS, 512
    )
    cross_low = cross_mixed.reshape(row_count, width)
    after_cross = after_self + product(cross_low, cout_mat) + cout_vec.astype(jnp.float32)
    third_norm, third_unit, third_std = normalize(
        after_cross, gain_three.astype(jnp.float32), shift_three.astype(jnp.float32)
    )
    third_low = third_norm.astype(jnp.bfloat16)
    hidden_pre = product(third_low, hidden_mat) + hidden_vec.astype(jnp.float32)
    hidden_low = jax.nn.gelu(hidden_pre, approximate=False).astype(jnp.bfloat16)
    result = after_cross + product(hidden_low, final_mat) + final_vec.astype(jnp.float32)
    layer_out = result.astype(jnp.bfloat16).reshape(page_count, page_len, width)
    grad_rows = out_grad.reshape(row_count, width).astype(jnp.float32)
    final_grad = out_grad.reshape(row_count, width)
    grad_final_mat = product_tn(hidden_low, final_grad).astype(jnp.bfloat16)
    grad_final_vec = jnp.sum(final_grad.astype(jnp.float32), axis=0)
    hidden_grad = (product_nt(final_grad, final_mat) * gelu_slope(hidden_pre)).astype(jnp.bfloat16)
    grad_hidden_mat = product_tn(third_low, hidden_grad).astype(jnp.bfloat16)
    grad_hidden_vec = jnp.sum(hidden_grad.astype(jnp.float32), axis=0)
    third_back, grad_gain_three, grad_shift_three = normalize_back(
        product_nt(hidden_grad, hidden_mat), third_unit, third_std, gain_three.astype(jnp.float32)
    )
    cross_grad_total = grad_rows + third_back
    cout_grad = cross_grad_total.astype(jnp.bfloat16)
    grad_cout_mat = product_tn(cross_low, cout_grad).astype(jnp.bfloat16)
    grad_cout_vec = jnp.sum(cout_grad.astype(jnp.float32), axis=0)
    cmix_grad = (
        product_nt(cout_grad, cout_mat).astype(jnp.bfloat16).reshape(page_count, page_len, width)
    )
    cquery_grad, ckey_grad, cvalue_grad = attend_bwd(
        cquery_pages, ckey_pages, cvalue_pages, cmix_grad, cross_total, None, HEADS, 512
    )
    cquery_grad = cquery_grad.reshape(row_count, width)
    ckey_grad = ckey_grad.reshape(page_count * mem_len, width)
    cvalue_grad = cvalue_grad.reshape(page_count * mem_len, width)
    grad_cquery_mat = product_tn(second_low, cquery_grad).astype(jnp.bfloat16)
    grad_cquery_vec = jnp.sum(cquery_grad.astype(jnp.float32), axis=0)
    grad_ckey_mat = product_tn(mem_rows, ckey_grad).astype(jnp.bfloat16)
    grad_cvalue_mat = product_tn(mem_rows, cvalue_grad).astype(jnp.bfloat16)
    grad_cvalue_vec = jnp.sum(cvalue_grad.astype(jnp.float32), axis=0)
    memory_grad = (product_nt(ckey_grad, ckey_mat) + product_nt(cvalue_grad, cvalue_mat)).reshape(
        page_count, mem_len, width
    )
    second_back, grad_gain_two, grad_shift_two = normalize_back(
        product_nt(cquery_grad, cquery_mat), second_unit, second_std, gain_two.astype(jnp.float32)
    )
    self_grad_total = cross_grad_total + second_back
    sout_grad = self_grad_total.astype(jnp.bfloat16)
    grad_out_mat = product_tn(self_low, sout_grad).astype(jnp.bfloat16)
    grad_out_vec = jnp.sum(sout_grad.astype(jnp.float32), axis=0)
    smix_grad = (
        product_nt(sout_grad, out_mat).astype(jnp.bfloat16).reshape(page_count, page_len, width)
    )
    query_grad, key_grad, value_grad = attend_bwd(
        query_pages, key_pages, value_pages, smix_grad, self_total, lengths_now, HEADS, 256
    )
    query_grad = query_grad.reshape(row_count, width)
    key_grad = key_grad.reshape(row_count, width)
    value_grad = value_grad.reshape(row_count, width)
    grad_query_mat = product_tn(first_low, query_grad).astype(jnp.bfloat16)
    grad_query_vec = jnp.sum(query_grad.astype(jnp.float32), axis=0)
    grad_key_mat = product_tn(first_low, key_grad).astype(jnp.bfloat16)
    grad_value_mat = product_tn(first_low, value_grad).astype(jnp.bfloat16)
    grad_value_vec = jnp.sum(value_grad.astype(jnp.float32), axis=0)
    first_in = (
        product_nt(query_grad, query_mat)
        + product_nt(key_grad, key_mat)
        + product_nt(value_grad, value_mat)
    )
    first_back, grad_gain_one, grad_shift_one = normalize_back(
        first_in, first_unit, first_std, gain_one.astype(jnp.float32)
    )
    tokens_grad = (self_grad_total + first_back).reshape(page_count, page_len, width)
    owned = spread(
        mesh,
        grad_gain_one,
        grad_shift_one,
        grad_query_mat,
        grad_query_vec,
        grad_key_mat,
        grad_value_mat,
        grad_value_vec,
        grad_out_mat,
        grad_out_vec,
        grad_gain_two,
        grad_shift_two,
        grad_cquery_mat,
        grad_cquery_vec,
        grad_ckey_mat,
        grad_cvalue_mat,
        grad_cvalue_vec,
        grad_cout_mat,
        grad_cout_vec,
        grad_gain_three,
        grad_shift_three,
        grad_hidden_mat,
        grad_hidden_vec,
        grad_final_mat,
        grad_final_vec,
    )
    return (layer_out, tokens_grad, memory_grad) + tuple(owned)


def solution(mesh):
    placed = (
        P(("dp", "fsdp"), None, None),
        P(("dp", "fsdp"), None, None),
        P(("dp", "fsdp")),
        P(("dp", "fsdp")),
        P(("dp", "fsdp"), None, None),
        P(("dp", "fsdp")),
        P(("dp", "fsdp")),
        P(("dp", "fsdp"), None),
        P(("dp", "fsdp")),
        P(("dp", "fsdp"), None),
        P(("dp", "fsdp"), None),
        P(("dp", "fsdp")),
        P(("dp", "fsdp"), None),
        P(("dp", "fsdp")),
        P(("dp", "fsdp")),
        P(("dp", "fsdp")),
        P(("dp", "fsdp"), None),
        P(("dp", "fsdp")),
        P(("dp", "fsdp"), None),
        P(("dp", "fsdp"), None),
        P(("dp", "fsdp")),
        P(("dp", "fsdp"), None),
        P(("dp", "fsdp")),
        P(("dp", "fsdp")),
        P(("dp", "fsdp")),
        P(("dp", "fsdp"), None),
        P(("dp", "fsdp")),
        P(("dp", "fsdp"), None),
        P(("dp", "fsdp")),
    )
    return jax.shard_map(
        functools.partial(on_device, mesh),
        mesh=mesh,
        in_specs=placed,
        out_specs=(
            P(("dp", "fsdp"), None, None),
            P(("dp", "fsdp"), None, None),
            P(("dp", "fsdp"), None, None),
            P(("dp", "fsdp")),
            P(("dp", "fsdp")),
            P(("dp", "fsdp"), None),
            P(("dp", "fsdp")),
            P(("dp", "fsdp"), None),
            P(("dp", "fsdp"), None),
            P(("dp", "fsdp")),
            P(("dp", "fsdp"), None),
            P(("dp", "fsdp")),
            P(("dp", "fsdp")),
            P(("dp", "fsdp")),
            P(("dp", "fsdp"), None),
            P(("dp", "fsdp")),
            P(("dp", "fsdp"), None),
            P(("dp", "fsdp"), None),
            P(("dp", "fsdp")),
            P(("dp", "fsdp"), None),
            P(("dp", "fsdp")),
            P(("dp", "fsdp")),
            P(("dp", "fsdp")),
            P(("dp", "fsdp"), None),
            P(("dp", "fsdp")),
            P(("dp", "fsdp"), None),
            P(("dp", "fsdp")),
        ),
        check_vma=False,
    )
```

```python
import functools

import jax
import jax.numpy as jnp
from jax import lax
from jax.experimental import pallas as pl
from jax.experimental.pallas import tpu as pltpu
from jax.sharding import PartitionSpec as P

HEADS = 16


EPSILON = 1e-05
ROOT_HALF = 0.7071067811865476
INV_ROOT_TWO_PI = 0.3989422804014327


def product(left, right):
    return jnp.dot(left, right, preferred_element_type=jnp.float32)


def product_tn(left, right):
    return lax.dot_general(
        left, right, (((0,), (0,)), ((), ())), preferred_element_type=jnp.float32
    )


def product_nt(left, right):
    return lax.dot_general(
        left, right, (((1,), (1,)), ((), ())), preferred_element_type=jnp.float32
    )


def normalize(rows_in, norm_gain, norm_shift):
    centered = rows_in - jnp.mean(rows_in, axis=-1, keepdims=True)
    inv_std = lax.rsqrt(jnp.mean(centered * centered, axis=-1, keepdims=True) + EPSILON)
    unit_rows = centered * inv_std
    return (unit_rows * norm_gain + norm_shift, unit_rows, inv_std)


def normalize_back(grad_norm, unit_rows, inv_std, norm_gain):
    scaled = grad_norm * norm_gain
    inner_part = (
        scaled
        - jnp.mean(scaled, axis=-1, keepdims=True)
        - unit_rows * jnp.mean(scaled * unit_rows, axis=-1, keepdims=True)
    )
    return (
        inner_part * inv_std,
        jnp.sum(grad_norm * unit_rows, axis=0),
        jnp.sum(grad_norm, axis=0),
    )


LOG2E = 1.4426950408889634
LN2 = 0.6931471805599453


def dot_nn(a, b):
    return jnp.dot(a, b, preferred_element_type=jnp.float32)


def dot_nt(a, b):
    return lax.dot_general(a, b, (((1,), (1,)), ((), ())), preferred_element_type=jnp.float32)


def dot_tn(a, b):
    return lax.dot_general(a, b, (((0,), (0,)), ((), ())), preferred_element_type=jnp.float32)


def lane_half(x, head, half):
    lane = lax.broadcasted_iota(jnp.int32, (1, x.shape[1]), 1)
    keep = (lane < half) if head == 0 else (lane >= half)
    return jnp.where(keep, x, jnp.zeros_like(x))


def causal_spans(rows, chunk):
    return [(start, chunk, start + chunk) for start in range(0, rows, chunk)]


def limit_row(start, width, length):
    pos = start + lax.broadcasted_iota(jnp.int32, (1, width), 1)
    return jnp.minimum(pos, length - 1)


def forward_pair(load_q, load_k, load_v, write, spans, length, scale):
    for start, size, keys in spans:
        q2 = load_q(start, size)
        k2 = load_k(0, keys)
        v2 = load_v(0, keys)
        half = q2.shape[1] // 2
        vt = v2.T
        outs, totals = [], []
        for head in (0, 1):
            raw = dot_nt(k2, lane_half(q2, head, half))
            if length is not None:
                key_pos = lax.broadcasted_iota(jnp.int32, raw.shape, 0)
                raw = jnp.where(key_pos <= limit_row(start, size, length), raw, -1e30)
            top = jnp.max(raw, axis=0, keepdims=True)
            expo = jnp.exp2((raw - top) * (scale * LOG2E))
            total = jnp.sum(expo, axis=0, keepdims=True)
            mixed = dot_nn(vt[head * half : (head + 1) * half], expo.astype(jnp.bfloat16))
            outs.append(mixed / total)
            totals.append(top * (scale * LOG2E) + jnp.log2(total))
        write(start, size, jnp.concatenate(outs, axis=0).T.astype(jnp.bfloat16), totals)


def fwd_kernel(masked, scale, chunk, *refs):
    if masked:
        len_ref, q_ref, k_ref, v_ref, a_ref, t_ref = refs
        length = len_ref[pl.program_id(0)]
    else:
        q_ref, k_ref, v_ref, a_ref, t_ref = refs
        length = None
    rows, keys = q_ref.shape[1], k_ref.shape[1]
    if masked:
        spans = causal_spans(rows, chunk)
    else:
        spans = [(s, chunk, keys) for s in range(0, rows, chunk)]

    def write(start, size, out, totals):
        a_ref[0, pl.ds(start, size), :] = out
        for head in (0, 1):
            t_ref[0, 0, pl.ds(head, 1), pl.ds(start, size)] = totals[head]

    forward_pair(
        lambda s, n: q_ref[0, pl.ds(s, n), :],
        lambda s, n: k_ref[0, pl.ds(s, n), :],
        lambda s, n: v_ref[0, pl.ds(s, n), :],
        write, spans, length, scale,
    )


def attend_fwd(q, k, v, lengths, heads, chunk=256):
    pages, rows, width = q.shape
    keys = k.shape[1]
    head = width // heads
    pairs = heads // 2
    masked = lengths is not None
    row_spec = pl.BlockSpec((1, rows, 2 * head), lambda p, h: (p, 0, h))
    key_spec = pl.BlockSpec((1, keys, 2 * head), lambda p, h: (p, 0, h))
    in_specs = [row_spec, key_spec, key_spec]
    args = [q, k, v]
    if masked:
        in_specs = [pl.BlockSpec(memory_space=pltpu.SMEM)] + in_specs
        args = [lengths] + args
    return pl.pallas_call(
        functools.partial(fwd_kernel, masked, head**-0.5, chunk),
        grid=(pages, pairs),
        in_specs=in_specs,
        out_specs=[row_spec, pl.BlockSpec((1, 1, 2, rows), lambda p, h: (p, h, 0, 0))],
        out_shape=[
            jax.ShapeDtypeStruct(q.shape, jnp.bfloat16),
            jax.ShapeDtypeStruct((pages, pairs, 2, rows), jnp.float32),
        ],
        compiler_params=pltpu.CompilerParams(vmem_limit_bytes=48 * 1024 * 1024),
        name="attend_forward",
    )(*args)


def bwd_kernel(masked, scale, chunk, *refs):
    if masked:
        len_ref, q_ref, k_ref, v_ref, g_ref, t_ref, dq_ref, dk_ref, dv_ref, dk_acc, dv_acc = refs
        length = len_ref[pl.program_id(0)]
    else:
        q_ref, k_ref, v_ref, g_ref, t_ref, dq_ref, dk_ref, dv_ref, dk_acc, dv_acc = refs
        length = None
    rows, keys_all = q_ref.shape[1], k_ref.shape[1]
    if masked:
        spans = causal_spans(rows, chunk)[::-1]
    else:
        spans = [(s, chunk, keys_all) for s in range(0, rows, chunk)]
    half = q_ref.shape[2] // 2
    for step, (start, size, keys) in enumerate(spans):
        q2 = q_ref[0, pl.ds(start, size), :]
        g2 = g_ref[0, pl.ds(start, size), :]
        k2 = k_ref[0, pl.ds(0, keys), :]
        v2 = v_ref[0, pl.ds(0, keys), :]
        kt = k2.T
        dk, dv, dqt = None, None, []
        for head in (0, 1):
            qm = lane_half(q2, head, half)
            gm = lane_half(g2, head, half)
            raw = dot_nt(k2, qm)
            total = t_ref[0, 0, pl.ds(head, 1), pl.ds(start, size)]
            probs = jnp.exp2(raw * (scale * LOG2E) - total)
            if length is not None:
                key_pos = lax.broadcasted_iota(jnp.int32, raw.shape, 0)
                probs = jnp.where(key_pos <= limit_row(start, size, length), probs, 0.0)
            grad = dot_nt(v2, gm)
            part = probs * grad
            dot_row = jnp.sum(part, axis=0, keepdims=True)
            score = ((part - probs * dot_row) * scale).astype(jnp.bfloat16)
            dvh = dot_nn(probs.astype(jnp.bfloat16), gm)
            dkh = dot_nn(score, qm)
            dv = dvh if dv is None else dv + dvh
            dk = dkh if dk is None else dk + dkh
            dqt.append(dot_nn(kt[head * half : (head + 1) * half], score))
        dq_ref[0, pl.ds(start, size), :] = jnp.concatenate(dqt, axis=0).T.astype(jnp.bfloat16)
        if step == 0:
            dk_acc[pl.ds(0, keys), :] = dk
            dv_acc[pl.ds(0, keys), :] = dv
        else:
            dk_acc[pl.ds(0, keys), :] += dk
            dv_acc[pl.ds(0, keys), :] += dv
    dk_ref[0] = dk_acc[...].astype(jnp.bfloat16)
    dv_ref[0] = dv_acc[...].astype(jnp.bfloat16)


def attend_bwd(q, k, v, g, totals, lengths, heads, chunk=256):
    pages, rows, width = q.shape
    keys = k.shape[1]
    head = width // heads
    pairs = heads // 2
    masked = lengths is not None
    row_spec = pl.BlockSpec((1, rows, 2 * head), lambda p, h: (p, 0, h))
    key_spec = pl.BlockSpec((1, keys, 2 * head), lambda p, h: (p, 0, h))
    total_spec = pl.BlockSpec((1, 1, 2, rows), lambda p, h: (p, h, 0, 0))
    in_specs = [row_spec, key_spec, key_spec, row_spec, total_spec]
    args = [q, k, v, g, totals]
    if masked:
        in_specs = [pl.BlockSpec(memory_space=pltpu.SMEM)] + in_specs
        args = [lengths] + args
    return pl.pallas_call(
        functools.partial(bwd_kernel, masked, head**-0.5, chunk),
        grid=(pages, pairs),
        in_specs=in_specs,
        out_specs=[row_spec, key_spec, key_spec],
        out_shape=[jax.ShapeDtypeStruct(a.shape, jnp.bfloat16) for a in (q, k, v)],
        scratch_shapes=[pltpu.VMEM((keys, 2 * head), jnp.float32)] * 2,
        compiler_params=pltpu.CompilerParams(vmem_limit_bytes=48 * 1024 * 1024),
        name="attend_backward",
    )(*args)


MESH_ID = pl.DeviceIdType.MESH
BOTH = ("dp", "fsdp")
CORE_RATE = 500e3
LINK_RATE = 96e3
HOP = 2.5


def bit_table(mesh):
    bits = []
    for axis, name in enumerate(BOTH):
        step = mesh.shape[name] // 2
        while step >= 1:
            bits.append((axis, step))
            step //= 2
    return bits


def can_route(mesh, rows):
    sizes = [mesh.shape[name] for name in BOTH]
    return all(s & (s - 1) == 0 for s in sizes) and rows % 16 == 0


def route_orders(bits):
    outer = [i for i, (axis, _) in enumerate(bits) if axis == 0]
    inner = [i for i, (axis, _) in enumerate(bits) if axis == 1]
    return (outer + inner, outer + inner[:-1][::-1] + inner[-1:])


def loads_of(bits, at, size):
    axis, step = bits[at]
    if axis == 1 and step == 1:
        return {"core": size / CORE_RATE}
    if axis == 1:
        return {f"inner{step}": 2 * size / LINK_RATE}
    loads = {"outer1": 2 * size / LINK_RATE}
    if step > 1:
        loads["outer2"] = 2 * size * step / LINK_RATE
    return loads


def plan_sends(bits, orders, sizes, growing, add_rate):
    count = len(bits)
    ready = [(0.0, unit, 0) for unit in range(len(orders))]
    free = {}
    plan = []
    arrive = {}
    while ready:
        choices = []
        for when, unit, stage in ready:
            scale = 2**stage if growing else 2 ** (count - 1 - stage)
            loads = loads_of(bits, orders[unit][stage], sizes[unit] * scale)
            start = max([when] + [free.get(link, 0.0) for link in loads])
            choices.append((round(start, 3), unit, -stage, when, scale))
        start, unit, stage, when, scale = min(choices)
        stage = -stage
        ready.remove((when, unit, stage))
        loads = loads_of(bits, orders[unit][stage], sizes[unit] * scale)
        for link, took in loads.items():
            free[link] = start + took
        plan.append((start, unit, stage))
        after = start + max(loads.values()) + HOP
        if add_rate:
            after += sizes[unit] * scale / add_rate
        if stage + 1 < count:
            ready.append((after, unit, stage + 1))
        else:
            arrive[unit] = after
    return sorted(plan), arrive


def my_bits(bits):
    place = (lax.axis_index("dp"), lax.axis_index("fsdp"))
    return [(place[axis] // step) % 2 for axis, step in bits]


def partner(bits, mine, at):
    place = [lax.axis_index("dp"), lax.axis_index("fsdp")]
    axis, step = bits[at]
    place[axis] = place[axis] + step * (1 - 2 * mine[at])
    return tuple(place)


def greet(bits, mine):
    barrier = pltpu.get_barrier_semaphore()
    for at in range(len(bits)):
        pl.semaphore_signal(
            barrier, inc=1, device_id=partner(bits, mine, at), device_id_type=MESH_ID
        )
    pl.semaphore_wait(barrier, len(bits))


def unit_shape(blocks, unit):
    array, rows, cols = unit
    block = blocks[array]
    return (len(range(*rows.indices(block[0]))), len(range(*cols.indices(block[1]))))


def scatter_kernel(bits, units, orders, plan, n_arrays, n_units, *refs):
    count = len(bits)
    sources = refs[:n_arrays]
    results = refs[n_arrays : 2 * n_arrays]
    held = refs[2 * n_arrays : 2 * n_arrays + n_units]
    boxes = refs[2 * n_arrays + n_units : 2 * n_arrays + n_units + n_units * count]
    totals = refs[2 * n_arrays + n_units + n_units * count : -4]
    send_sem, recv_sem, load_sem, store_sem = refs[-4:]
    mine = my_bits(bits)

    def load(unit):
        array, rows, cols = units[unit]
        first = orders[unit][0]
        where = tuple(mine[b] if b == first else slice(None) for b in range(count))
        return pltpu.make_async_copy(
            sources[array].at[where + (rows, cols)], held[unit], load_sem.at[unit]
        )

    for unit in range(n_units):
        load(unit).start()
    greet(bits, mine)

    def message(unit, stage):
        array, rows, cols = units[unit]
        order = orders[unit]
        now = order[stage]
        where = []
        for b in range(count):
            if b == now:
                where.append(1 - mine[b])
            elif b in order[:stage]:
                where.append(mine[b])
            else:
                where.append(slice(None))
        if stage == 0:
            source = sources[array].at[tuple(where) + (rows, cols)]
        else:
            source = held[unit].at[tuple(w for b, w in enumerate(where) if b != order[0])]
        return pltpu.make_async_remote_copy(
            src_ref=source,
            dst_ref=boxes[unit * count + stage],
            send_sem=send_sem.at[unit, stage],
            recv_sem=recv_sem.at[unit, stage],
            device_id=partner(bits, mine, now),
            device_id_type=MESH_ID,
        )

    def add(unit, stage):
        order = orders[unit]
        message(unit, stage).wait_recv()
        if stage == 0:
            load(unit).wait()
        box = boxes[unit * count + stage]
        open_bits = [b for b in range(count) if b not in order[: stage + 1]]
        blocks = 2 ** len(open_bits)

        def one(block, carry):
            where = []
            spot = []
            for b in range(count):
                if b == order[0]:
                    continue
                if b in open_bits:
                    digit = (block // 2 ** (len(open_bits) - 1 - open_bits.index(b))) % 2
                    where.append(digit)
                    spot.append(digit)
                else:
                    where.append(mine[b])
            where, spot = tuple(where), tuple(spot)
            total = held[unit][where].astype(jnp.float32) + box[spot].astype(jnp.float32)
            if stage == count - 1:
                totals[unit][...] = total
            else:
                held[unit][where] = total.astype(held[unit].dtype)
            return carry

        if blocks == 1:
            one(0, 0)
        else:
            lax.fori_loop(0, blocks, one, 0)

    def store(unit):
        array, rows, cols = units[unit]
        return pltpu.make_async_copy(
            totals[unit], results[array].at[rows, cols], store_sem.at[unit]
        )

    for _, unit, stage in plan:
        if stage > 0:
            add(unit, stage - 1)
        message(unit, stage).start()
    for unit in range(n_units):
        add(unit, count - 1)
        store(unit).start()
    for unit in range(n_units):
        store(unit).wait()
        for stage in range(count):
            message(unit, stage).wait_send()


def scatter_all(mesh, terms, units, collective_id):
    bits = bit_table(mesh)
    routes = route_orders(bits)
    count = len(bits)
    orders = [routes[u % 2][::-1] for u in range(len(units))]
    shapes = [unit_shape([t.shape[count:] for t in terms], unit) for unit in units]
    kinds = [terms[array].dtype for array, _, _ in units]
    sizes = [s[0] * s[1] * kind.itemsize for s, kind in zip(shapes, kinds)]
    plan, _ = plan_sends(bits, orders, sizes, False, 1000e3)
    n = len(terms)
    n_units = len(units)
    sems = (n_units, count)
    scratch = [
        pltpu.VMEM((2,) * (count - 1) + shapes[u], kinds[u]) for u in range(n_units)
    ]
    for u in range(n_units):
        for stage in range(count):
            scratch.append(pltpu.VMEM((2,) * (count - 1 - stage) + shapes[u], kinds[u]))
    scratch += [pltpu.VMEM(shapes[u], jnp.float32) for u in range(n_units)]
    scratch += [
        pltpu.SemaphoreType.DMA(sems),
        pltpu.SemaphoreType.DMA(sems),
        pltpu.SemaphoreType.DMA((n_units,)),
        pltpu.SemaphoreType.DMA((n_units,)),
    ]
    return pl.pallas_call(
        functools.partial(scatter_kernel, bits, units, orders, plan, n, n_units),
        out_shape=[jax.ShapeDtypeStruct(t.shape[count:], jnp.float32) for t in terms],
        in_specs=[pl.BlockSpec(memory_space=pltpu.HBM)] * n,
        out_specs=[pl.BlockSpec(memory_space=pltpu.HBM)] * n,
        scratch_shapes=scratch,
        compiler_params=pltpu.CompilerParams(
            collective_id=collective_id,
            has_side_effects=True,
            vmem_limit_bytes=60 * 1024 * 1024,
        ),
        name="scatter_grads",
    )(*terms)


ERF_RATE = 0.3275911
ERF_TERMS = (0.254829592, -0.284496736, 1.421413741, -1.453152027, 1.061405429)


def gelu_parts(pre):
    bell = jnp.exp2(pre * pre * (-0.5 * LOG2E))
    arm = 1.0 / (1.0 + jnp.abs(pre) * (ERF_RATE * ROOT_HALF))
    series = ERF_TERMS[4]
    for term in ERF_TERMS[3::-1]:
        series = series * arm + term
    tail = 0.5 * series * arm * bell
    below = jnp.where(pre >= 0.0, 1.0 - tail, tail)
    return pre * below, below + pre * bell * INV_ROOT_TWO_PI


class Schedule:
    def __init__(self, plan, issue):
        self.plan = plan
        self.issue = issue
        self.at = 0
        self.now = 0.0

    def due(self):
        items = []
        while self.at < len(self.plan) and self.plan[self.at][0] <= self.now:
            items.append(self.plan[self.at][1:])
            self.at += 1
        return items

    def spend(self, took):
        self.now += took
        for unit, stage in self.due():
            self.issue(unit, stage)

    def until(self, when):
        self.now = max(self.now, when)
        for unit, stage in self.due():
            self.issue(unit, stage)

    def loop(self, count, took, body):
        buckets = []
        for _ in range(count):
            self.now += took
            buckets.append(self.due())

        def step(i, carry):
            body(i)
            for k, items in enumerate(buckets):
                if items:

                    @pl.when(i == k)
                    def _(items=items):
                        for unit, stage in items:
                            self.issue(unit, stage)

            return carry

        lax.fori_loop(0, count, step, 0)


ROWS_STEP = 128


N_VECS = 14
VEC_ROWS = 16
VEC_LANES = 128


def device_index(bits, mine):
    count = len(bits)
    return sum(mine[b] * 2 ** (count - 1 - b) for b in range(count))


def pack_vectors(loose, pack, spot, size):
    row = lax.broadcasted_iota(jnp.int32, (size, VEC_LANES), 0)
    lane = lax.broadcasted_iota(jnp.int32, (size, VEC_LANES), 1)
    place = (lane == row + size * spot).astype(jnp.float32)
    pieces = []
    for ref in loose[:-1]:
        pieces.append(dot_nn(ref[...].astype(jnp.float32).reshape(1, size), place))
    pieces.append(loose[-1][...].astype(jnp.float32).reshape(1, VEC_LANES))
    pieces.append(jnp.zeros((VEC_ROWS - len(pieces), VEC_LANES), jnp.float32))
    pack[...] = jnp.concatenate(pieces, axis=0).astype(pack.dtype)


def forward_kernel(bits, units, orders, plan, arrive, n_arrays, heads, *refs):
    count = len(bits)
    (tokens, memory, lengths), refs = refs[:3], refs[3:]
    loose, refs = refs[:N_VECS], refs[N_VECS:]
    sources, refs = refs[: n_arrays - 1], refs[n_arrays - 1 :]
    targets, refs = refs[:n_arrays], refs[n_arrays:]
    saved_names = ("q", "k", "v", "a", "total", "h1")
    saved_names += ("cq", "ck", "cv", "ca", "ctotal", "h2", "g", "slope", "out")
    saved = dict(zip(saved_names, refs[: len(saved_names)]))
    refs = refs[len(saved_names) :]
    x, mem, n, q, k, v, a, h, ck, cv, g, slope, tot, ctot = refs[:14]
    wide, tall, pack, vecs, table, hidden_row = refs[14:-6]
    send_sem, recv_sem, own_sem, in_sem, w_sem, out_sem = refs[-6:]
    mine = my_bits(bits)
    rows, width = x.shape
    devices = 2**count
    lanes_each = width // devices
    pack_vectors(loose, pack, device_index(bits, mine) % (VEC_LANES // lanes_each), lanes_each)
    sources = (pack,) + tuple(sources)
    own = [
        pltpu.make_async_copy(sources[i], targets[i].at[tuple(mine)], own_sem.at[i])
        for i in range(n_arrays)
    ]
    for copy in own:
        copy.start()
    load_x = pltpu.make_async_copy(tokens, x, in_sem.at[0])
    load_mem = pltpu.make_async_copy(memory, mem, in_sem.at[1])
    load_x.start()
    load_mem.start()
    greet(bits, mine)

    def message(unit, stage):
        array, top, left = units[unit]
        order = orders[unit]
        where = tuple(slice(None) if b in order[:stage] else mine[b] for b in range(count))
        place = targets[array].at[where + (top, left)]
        source = sources[array].at[top, left] if stage == 0 else place
        return pltpu.make_async_remote_copy(
            src_ref=source,
            dst_ref=place,
            send_sem=send_sem.at[unit, stage],
            recv_sem=recv_sem.at[unit, stage],
            device_id=partner(bits, mine, order[stage]),
            device_id_type=MESH_ID,
        )

    settled = set()

    def issue(unit, stage):
        array = units[unit][0]
        if stage > 0:
            if array not in settled:
                settled.add(array)
                own[array].wait()
            message(unit, stage - 1).wait_recv()
        message(unit, stage).start()

    clock = Schedule(plan, issue)
    every = (slice(None),) * count

    def fetch(unit, slot, sem):
        clock.until(arrive[unit])
        message(unit, count - 1).wait_recv()
        array, top, left = units[unit]
        if array not in settled:
            settled.add(array)
            own[array].wait()
        copy = pltpu.make_async_copy(targets[array].at[every + (top, left)], slot, w_sem.at[sem])
        copy.start()
        copy.wait()

    def times(lhs, slot, tile, write, took=1.4):
        depth = lhs.shape[1]
        tiles = slot.shape[-1] // tile

        def body(j):
            cols = pl.ds(pl.multiple_of(j * tile, tile), tile)
            weight = slot[every + (slice(None), cols)].reshape(depth, tile)
            write(cols, dot_nn(lhs[...], weight))

        clock.loop(tiles, took / tiles, body)

    def norm_into(gain, shift, source):
        def body(i):
            part = pl.ds(pl.multiple_of(i * ROWS_STEP, ROWS_STEP), ROWS_STEP)
            r = source[part, :].astype(jnp.float32)
            n[part, :] = normalize(r, gain, shift)[0].astype(jnp.bfloat16)

        clock.loop(rows // ROWS_STEP, 0.4, body)

    pending = []

    def save(source, name, index):
        copy = pltpu.make_async_copy(source, saved[name], out_sem.at[index])
        copy.start()
        pending.append(copy)
        return copy

    def vec(i):
        return table[pl.ds(i, 1), :]

    clock.until(0.0)
    fetch(0, vecs, 0)
    for group in range(width // VEC_LANES):
        share = VEC_LANES // lanes_each
        total = None
        for d in range(group * share, (group + 1) * share):
            where = tuple((d >> (count - 1 - b)) & 1 for b in range(count))
            block = vecs[where].astype(jnp.float32)
            total = block if total is None else total + block
        table[:, pl.ds(group * VEC_LANES, VEC_LANES)] = total
    for d in range(devices):
        where = tuple((d >> (count - 1 - b)) & 1 for b in range(count))
        block = vecs[where].astype(jnp.float32)
        hidden_row[pl.ds(0, 1), pl.ds(d * VEC_LANES, VEC_LANES)] = block[13:14]
    load_x.wait()
    load_mem.wait()
    norm_into(vec(0), vec(1), x)
    length = lengths[0]

    def project(bias, target, extra=0):
        def write(cols, acc):
            if bias is not None:
                acc = acc + table[pl.ds(bias, 1), cols]
            target[:, cols] = acc.astype(target.dtype)

        return write

    def residual(bias, source):
        def write(cols, acc):
            h[:, cols] = source[:, cols].astype(jnp.float32) + acc + table[pl.ds(bias, 1), cols]

        return write

    def attend(q_ref, k_ref, v_ref, tot_ref, masked):
        keys = k_ref.shape[0]
        pair = 2 * (width // heads)

        def body(p):
            lanes = pl.ds(pl.multiple_of(p * pair, pair), pair)

            def write(start, size, out, totals):
                a[pl.ds(start, size), lanes] = out
                for head in (0, 1):
                    tot_ref[p, pl.ds(head, 1), pl.ds(start, size)] = totals[head]

            forward_pair(
                lambda s, m: q_ref[pl.ds(s, m), lanes],
                lambda s, m: k_ref[pl.ds(s, m), lanes],
                lambda s, m: v_ref[pl.ds(s, m), lanes],
                write,
                [(0, rows, keys)],
                length if masked else None,
                (width // heads) ** -0.5,
            )

        clock.loop(heads // 2, 1.6, body)

    for unit, target, bias in ((1, q, 2), (2, k, None), (3, v, 3)):
        fetch(unit, wide, 1)
        times(n, wide, 256, project(bias, target))
    save(q, "q", 0)
    save(k, "k", 1)
    save(v, "v", 2)
    attend(q, k, v, tot, True)
    save(a, "a", 3)
    save(tot, "total", 4)
    for unit, target, bias in ((4, ck, None), (5, cv, 8)):
        fetch(unit, wide, 1)
        times(mem, wide, 256, project(bias, target), 1.6)
    save(ck, "ck", 5)
    save(cv, "cv", 6)
    fetch(6, wide, 1)
    times(a, wide, 256, residual(4, x))
    save(h, "h1", 7)
    norm_into(vec(5), vec(6), h)
    fetch(7, wide, 1)
    pending[0].wait()
    times(n, wide, 256, project(7, q))
    save(q, "cq", 8)
    pending[3].wait()
    attend(q, ck, cv, ctot, False)
    save(a, "ca", 9)
    save(ctot, "ctotal", 10)
    fetch(8, wide, 1)
    pending[7].wait()
    times(a, wide, 256, residual(9, h))
    save(h, "h2", 11)
    norm_into(vec(10), vec(11), h)
    block = wide.shape[-1]
    blocks = g.shape[1] // block
    for j in range(blocks):
        fetch(9 + j, wide, 1)
        tile = 256

        def body(i, j=j):
            cols = pl.ds(pl.multiple_of(i * tile, tile), tile)
            spot = pl.ds(pl.multiple_of(j * block + i * tile, tile), tile)
            weight = wide[every + (slice(None), cols)].reshape(width, tile)
            for r in range(0, rows, ROWS_STEP):
                part = pl.ds(r, ROWS_STEP)
                pre = dot_nn(n[part, :], weight) + hidden_row[:, spot]
                low, rate = gelu_parts(pre)
                g[part, spot] = low.astype(jnp.bfloat16)
                slope[part, spot] = rate.astype(jnp.bfloat16)

        clock.loop(block // tile, 0.8, body)
    save(g, "g", 12)
    save(slope, "slope", 13)
    for j in range(width // tall.shape[-1]):
        fetch(9 + blocks + j, tall, 2)
        cols = pl.ds(j * tall.shape[-1], tall.shape[-1])
        weight = tall[...].reshape(g.shape[1], tall.shape[-1])
        acc = dot_nn(g[...], weight)
        x[:, cols] = (h[:, cols] + acc + table[pl.ds(12, 1), cols]).astype(jnp.bfloat16)
        clock.spend(1.6)
    save(x, "out", 14)
    clock.until(1e9)
    for i, copy in enumerate(pending):
        if i not in (0, 3, 7):
            copy.wait()
    for unit in range(len(units)):
        for stage in range(count):
            message(unit, stage).wait_send()


def fused_forward(mesh, tokens, memory, lengths, mats, vecs, heads, collective_id):
    bits = bit_table(mesh)
    routes = route_orders(bits)
    rows, width = tokens.shape
    keys = memory.shape[0]
    block = mats[0].shape
    pack = (VEC_ROWS, VEC_LANES)
    every = slice(None)
    units = [(0, every, every)] + [(i, every, every) for i in range(1, 9)]
    hidden = mats[8].shape[1]
    for left in range(0, hidden, width):
        units.append((9, every, slice(left, left + width)))
    tall_rows = mats[9].shape[0]
    tall_cols = width * block[0] // tall_rows
    for left in range(0, width, tall_cols):
        units.append((10, every, slice(left, left + tall_cols)))
    blocks = [pack] + [m.shape for m in mats]
    shapes = [unit_shape(blocks, unit) for unit in units]
    sizes = [2 * s[0] * s[1] for s in shapes]
    orders = [routes[u % 2] for u in range(len(units))]
    plan, arrive = plan_sends(bits, orders, sizes, True, None)
    n = len(blocks)
    spots = (2,) * len(bits)
    low = jnp.bfloat16
    wide_rows = jax.ShapeDtypeStruct((rows, width), low)
    wide_keys = jax.ShapeDtypeStruct((keys, width), low)
    full = jax.ShapeDtypeStruct((rows, width), jnp.float32)
    totals = jax.ShapeDtypeStruct((heads // 2, 2, rows), jnp.float32)
    ff = jax.ShapeDtypeStruct((rows, hidden), low)
    saved = [
        wide_rows, wide_rows, wide_rows, wide_rows, totals, full,
        wide_rows, wide_keys, wide_keys, wide_rows, totals, full, ff, ff, wide_rows,
    ]
    vm = lambda s: pltpu.VMEM(s.shape, s.dtype)
    sems = (len(units), len(bits))
    hbm = pl.BlockSpec(memory_space=pltpu.HBM)
    got = pl.pallas_call(
        functools.partial(forward_kernel, bits, units, orders, plan, arrive, n, heads),
        out_shape=[jax.ShapeDtypeStruct(spots + b, low) for b in blocks] + saved,
        in_specs=[hbm, hbm, pl.BlockSpec(memory_space=pltpu.SMEM)]
        + [pl.BlockSpec(memory_space=pltpu.VMEM)] * len(vecs)
        + [hbm] * len(mats),
        out_specs=[hbm] * (n + len(saved)),
        scratch_shapes=[
            vm(wide_rows), vm(wide_keys), vm(wide_rows), vm(wide_rows), vm(wide_rows),
            vm(wide_rows), vm(wide_rows), vm(full), vm(wide_keys), vm(wide_keys),
            vm(ff), vm(ff), vm(totals), vm(totals),
            pltpu.VMEM(spots + block, low),
            pltpu.VMEM(spots + (tall_rows, tall_cols), low),
            pltpu.VMEM(pack, low),
            pltpu.VMEM(spots + pack, low),
            pltpu.VMEM((VEC_ROWS, width), jnp.float32),
            pltpu.VMEM((1, hidden), jnp.float32),
            pltpu.SemaphoreType.DMA(sems),
            pltpu.SemaphoreType.DMA(sems),
            pltpu.SemaphoreType.DMA((n,)),
            pltpu.SemaphoreType.DMA((2,)),
            pltpu.SemaphoreType.DMA((3,)),
            pltpu.SemaphoreType.DMA((len(saved),)),
        ],
        compiler_params=pltpu.CompilerParams(
            collective_id=collective_id,
            has_side_effects=True,
            vmem_limit_bytes=60 * 1024 * 1024,
        ),
        name="forward_layer",
    )(tokens, memory, lengths, *vecs, *mats)
    return got[:n], got[n:]


MATS = (2, 4, 5, 7, 11, 13, 14, 16, 20, 22)
MATS_ORDER = (2, 4, 5, 13, 14, 7, 11, 16, 20, 22)
GRAD_ROWS = 8
GRAD_LANES = 128
VECS = (0, 1, 3, 6, 8, 9, 10, 12, 15, 17, 18, 19, 23, 21)


def split_units(blocks):
    units = [(0, slice(None), slice(None))]
    for i, (rows, cols) in enumerate(blocks):
        base_rows, base_cols = min(rows, blocks[0][0]), min(cols, blocks[0][1])
        for top in range(0, rows, base_rows):
            for left in range(0, cols, base_cols):
                units.append(
                    (i + 1, slice(top, top + base_rows), slice(left, left + base_cols))
                )
    return units


def collect(*shards):
    return tuple(lax.all_gather(s, BOTH, axis=0, tiled=True) for s in shards)


def unpack_vectors(table, shards):
    devices = table.size // (VEC_ROWS * VEC_LANES)
    table = table.reshape(devices, VEC_ROWS, VEC_LANES)
    size = shards[0].shape[0]
    share = VEC_LANES // size
    narrow = table.reshape(devices // share, share, VEC_ROWS, VEC_LANES).astype(jnp.float32)
    narrow = jnp.sum(narrow, axis=1).transpose(1, 0, 2).reshape(VEC_ROWS, devices * size)
    full = [None] * len(shards)
    for row, i in enumerate(VECS[:-1]):
        full[i] = narrow[row]
    full[VECS[-1]] = table[:, len(VECS) - 1].reshape(-1)
    return full


def spread(mesh, *grads):
    devices = mesh.shape["dp"] * mesh.shape["fsdp"]
    mats = [grads[i] for i in MATS]
    if not can_route(mesh, mats[0].shape[0] // devices):
        return tuple(
            lax.psum_scatter(g.astype(jnp.float32), BOTH, scatter_dimension=0, tiled=True)
            for g in grads
        )
    spots = (2,) * len(bit_table(mesh))
    table = jnp.concatenate([grads[i].reshape(devices, -1) for i in VECS], axis=1)
    spare = GRAD_ROWS * GRAD_LANES - table.shape[1]
    table = jnp.pad(table, ((0, 0), (0, spare))).reshape(spots + (GRAD_ROWS, GRAD_LANES))
    terms = [m.reshape(spots + (m.shape[0] // devices, m.shape[1])) for m in mats]
    units = split_units([t.shape[-2:] for t in terms])
    got = scatter_all(mesh, [table] + terms, units, 1)
    flat = got[0].reshape(-1)
    owned = [None] * len(grads)
    start = 0
    for i in VECS:
        size = grads[i].shape[0] // devices
        owned[i] = flat[start : start + size]
        start += size
    for i, value in zip(MATS, got[1:]):
        owned[i] = value
    return tuple(owned)


def on_device(
    mesh,
    tokens,
    memory,
    page_lengths,
    end_flags,
    out_grad,
    self_gain,
    self_shift,
    self_query,
    self_query_bias,
    self_key,
    self_value,
    self_value_bias,
    self_out,
    self_out_bias,
    cross_gain,
    cross_shift,
    cross_query,
    cross_query_bias,
    cross_key,
    cross_value,
    cross_value_bias,
    cross_out,
    cross_out_bias,
    feed_gain,
    feed_shift,
    feed_in,
    feed_in_bias,
    feed_out,
    feed_out_bias,
):
    page_count, page_len, width = tokens.shape
    mem_len = memory.shape[1]
    row_count = page_count * page_len
    lengths_now = jnp.where(end_flags == 1, 1, page_lengths)
    inputs = tokens.reshape(row_count, width).astype(jnp.float32)
    mem_rows = memory.reshape(page_count * mem_len, width)
    shard_set = (
        self_gain,
        self_shift,
        self_query,
        self_query_bias,
        self_key,
        self_value,
        self_value_bias,
        self_out,
        self_out_bias,
        cross_gain,
        cross_shift,
        cross_query,
        cross_query_bias,
        cross_key,
        cross_value,
        cross_value_bias,
        cross_out,
        cross_out_bias,
        feed_gain,
        feed_shift,
        feed_in,
        feed_in_bias,
        feed_out,
        feed_out_bias,
    )
    if can_route(mesh, self_query.shape[0]):
        mats = [shard_set[i] for i in MATS_ORDER]
        got, saved = fused_forward(
            mesh, tokens[0], memory[0], lengths_now, mats, [shard_set[i] for i in VECS], HEADS, 0
        )
        full_set = unpack_vectors(got[0], shard_set)
        for i, value in zip(MATS_ORDER, got[1:]):
            full_set[i] = value.reshape(-1, value.shape[-1])
        (
            query_low, key_low, value_low, self_low, self_total, after_self,
            cquery_low, ckey_low, cvalue_low, cross_low, cross_total, after_cross,
            hidden_low, hidden_rate, layer_out,
        ) = saved
        self_total, cross_total = self_total[None], cross_total[None]
        layer_out = layer_out[None]
        query_pages, key_pages, value_pages = query_low[None], key_low[None], value_low[None]
        cquery_pages, ckey_pages, cvalue_pages = cquery_low[None], ckey_low[None], cvalue_low[None]
    else:
        full_set = collect(*shard_set)
    (
        gain_one,
        shift_one,
        query_mat,
        query_vec,
        key_mat,
        value_mat,
        value_vec,
        out_mat,
        out_vec,
        gain_two,
        shift_two,
        cquery_mat,
        cquery_vec,
        ckey_mat,
        cvalue_mat,
        cvalue_vec,
        cout_mat,
        cout_vec,
        gain_three,
        shift_three,
        hidden_mat,
        hidden_vec,
        final_mat,
        final_vec,
    ) = full_set
    norm_of = lambda r, g, b: normalize(r, g.astype(jnp.float32), b.astype(jnp.float32))
    first_norm, first_unit, first_std = norm_of(inputs, gain_one, shift_one)
    first_low = first_norm.astype(jnp.bfloat16)
    if not can_route(mesh, self_query.shape[0]):
        query_low = (product(first_low, query_mat) + query_vec.astype(jnp.float32)).astype(jnp.bfloat16)
        key_low = product(first_low, key_mat).astype(jnp.bfloat16)
        value_low = (product(first_low, value_mat) + value_vec.astype(jnp.float32)).astype(jnp.bfloat16)
        query_pages = query_low.reshape(page_count, page_len, width)
        key_pages = key_low.reshape(page_count, page_len, width)
        value_pages = value_low.reshape(page_count, page_len, width)
        self_mixed, self_total = attend_fwd(
            query_pages, key_pages, value_pages, lengths_now, HEADS, 512
        )
        self_low = self_mixed.reshape(row_count, width)
        after_self = inputs + product(self_low, out_mat) + out_vec.astype(jnp.float32)
        second_norm, second_unit, second_std = normalize(
            after_self, gain_two.astype(jnp.float32), shift_two.astype(jnp.float32)
        )
        second_low = second_norm.astype(jnp.bfloat16)
        cquery_low = (product(second_low, cquery_mat) + cquery_vec.astype(jnp.float32)).astype(
            jnp.bfloat16
        )
        ckey_low = product(mem_rows, ckey_mat).astype(jnp.bfloat16)
        cvalue_low = (product(mem_rows, cvalue_mat) + cvalue_vec.astype(jnp.float32)).astype(
            jnp.bfloat16
        )
        cquery_pages = cquery_low.reshape(page_count, page_len, width)
        ckey_pages = ckey_low.reshape(page_count, mem_len, width)
        cvalue_pages = cvalue_low.reshape(page_count, mem_len, width)
        cross_mixed, cross_total = attend_fwd(
            cquery_pages, ckey_pages, cvalue_pages, None, HEADS, 512
        )
        cross_low = cross_mixed.reshape(row_count, width)
        after_cross = after_self + product(cross_low, cout_mat) + cout_vec.astype(jnp.float32)
        third_norm, third_unit, third_std = normalize(
            after_cross, gain_three.astype(jnp.float32), shift_three.astype(jnp.float32)
        )
        third_low = third_norm.astype(jnp.bfloat16)
        hidden_pre = product(third_low, hidden_mat) + hidden_vec.astype(jnp.float32)
        hidden_low, hidden_rate = gelu_parts(hidden_pre)
        hidden_low = hidden_low.astype(jnp.bfloat16)
        hidden_rate = hidden_rate.astype(jnp.bfloat16)
        result = after_cross + product(hidden_low, final_mat) + final_vec.astype(jnp.float32)
        layer_out = result.astype(jnp.bfloat16).reshape(page_count, page_len, width)
    second_norm, second_unit, second_std = norm_of(after_self, gain_two, shift_two)
    second_low = second_norm.astype(jnp.bfloat16)
    third_norm, third_unit, third_std = norm_of(after_cross, gain_three, shift_three)
    third_low = third_norm.astype(jnp.bfloat16)
    grad_rows = out_grad.reshape(row_count, width).astype(jnp.float32)
    final_grad = out_grad.reshape(row_count, width)
    grad_final_mat = product_tn(hidden_low, final_grad).astype(jnp.bfloat16)
    grad_final_vec = jnp.sum(final_grad.astype(jnp.float32), axis=0)
    hidden_grad = (product_nt(final_grad, final_mat) * hidden_rate.astype(jnp.float32)).astype(jnp.bfloat16)
    grad_hidden_mat = product_tn(third_low, hidden_grad).astype(jnp.bfloat16)
    grad_hidden_vec = jnp.sum(hidden_grad.astype(jnp.float32), axis=0)
    third_back, grad_gain_three, grad_shift_three = normalize_back(
        product_nt(hidden_grad, hidden_mat), third_unit, third_std, gain_three.astype(jnp.float32)
    )
    cross_grad_total = grad_rows + third_back
    cout_grad = cross_grad_total.astype(jnp.bfloat16)
    grad_cout_mat = product_tn(cross_low, cout_grad).astype(jnp.bfloat16)
    grad_cout_vec = jnp.sum(cout_grad.astype(jnp.float32), axis=0)
    cmix_grad = (
        product_nt(cout_grad, cout_mat).astype(jnp.bfloat16).reshape(page_count, page_len, width)
    )
    cquery_grad, ckey_grad, cvalue_grad = attend_bwd(
        cquery_pages, ckey_pages, cvalue_pages, cmix_grad, cross_total, None, HEADS, 512
    )
    cquery_grad = cquery_grad.reshape(row_count, width)
    ckey_grad = ckey_grad.reshape(page_count * mem_len, width)
    cvalue_grad = cvalue_grad.reshape(page_count * mem_len, width)
    grad_cquery_mat = product_tn(second_low, cquery_grad).astype(jnp.bfloat16)
    grad_cquery_vec = jnp.sum(cquery_grad.astype(jnp.float32), axis=0)
    grad_ckey_mat = product_tn(mem_rows, ckey_grad).astype(jnp.bfloat16)
    grad_cvalue_mat = product_tn(mem_rows, cvalue_grad).astype(jnp.bfloat16)
    grad_cvalue_vec = jnp.sum(cvalue_grad.astype(jnp.float32), axis=0)
    memory_grad = (product_nt(ckey_grad, ckey_mat) + product_nt(cvalue_grad, cvalue_mat)).reshape(
        page_count, mem_len, width
    )
    second_back, grad_gain_two, grad_shift_two = normalize_back(
        product_nt(cquery_grad, cquery_mat), second_unit, second_std, gain_two.astype(jnp.float32)
    )
    self_grad_total = cross_grad_total + second_back
    sout_grad = self_grad_total.astype(jnp.bfloat16)
    grad_out_mat = product_tn(self_low, sout_grad).astype(jnp.bfloat16)
    grad_out_vec = jnp.sum(sout_grad.astype(jnp.float32), axis=0)
    smix_grad = (
        product_nt(sout_grad, out_mat).astype(jnp.bfloat16).reshape(page_count, page_len, width)
    )
    query_grad, key_grad, value_grad = attend_bwd(
        query_pages, key_pages, value_pages, smix_grad, self_total, lengths_now, HEADS, 256
    )
    query_grad = query_grad.reshape(row_count, width)
    key_grad = key_grad.reshape(row_count, width)
    value_grad = value_grad.reshape(row_count, width)
    grad_query_mat = product_tn(first_low, query_grad).astype(jnp.bfloat16)
    grad_query_vec = jnp.sum(query_grad.astype(jnp.float32), axis=0)
    grad_key_mat = product_tn(first_low, key_grad).astype(jnp.bfloat16)
    grad_value_mat = product_tn(first_low, value_grad).astype(jnp.bfloat16)
    grad_value_vec = jnp.sum(value_grad.astype(jnp.float32), axis=0)
    first_in = (
        product_nt(query_grad, query_mat)
        + product_nt(key_grad, key_mat)
        + product_nt(value_grad, value_mat)
    )
    first_back, grad_gain_one, grad_shift_one = normalize_back(
        first_in, first_unit, first_std, gain_one.astype(jnp.float32)
    )
    tokens_grad = (self_grad_total + first_back).reshape(page_count, page_len, width)
    owned = spread(
        mesh,
        grad_gain_one,
        grad_shift_one,
        grad_query_mat,
        grad_query_vec,
        grad_key_mat,
        grad_value_mat,
        grad_value_vec,
        grad_out_mat,
        grad_out_vec,
        grad_gain_two,
        grad_shift_two,
        grad_cquery_mat,
        grad_cquery_vec,
        grad_ckey_mat,
        grad_cvalue_mat,
        grad_cvalue_vec,
        grad_cout_mat,
        grad_cout_vec,
        grad_gain_three,
        grad_shift_three,
        grad_hidden_mat,
        grad_hidden_vec,
        grad_final_mat,
        grad_final_vec,
    )
    return (layer_out, tokens_grad, memory_grad) + tuple(owned)


def solution(mesh):
    placed = (
        P(("dp", "fsdp"), None, None),
        P(("dp", "fsdp"), None, None),
        P(("dp", "fsdp")),
        P(("dp", "fsdp")),
        P(("dp", "fsdp"), None, None),
        P(("dp", "fsdp")),
        P(("dp", "fsdp")),
        P(("dp", "fsdp"), None),
        P(("dp", "fsdp")),
        P(("dp", "fsdp"), None),
        P(("dp", "fsdp"), None),
        P(("dp", "fsdp")),
        P(("dp", "fsdp"), None),
        P(("dp", "fsdp")),
        P(("dp", "fsdp")),
        P(("dp", "fsdp")),
        P(("dp", "fsdp"), None),
        P(("dp", "fsdp")),
        P(("dp", "fsdp"), None),
        P(("dp", "fsdp"), None),
        P(("dp", "fsdp")),
        P(("dp", "fsdp"), None),
        P(("dp", "fsdp")),
        P(("dp", "fsdp")),
        P(("dp", "fsdp")),
        P(("dp", "fsdp"), None),
        P(("dp", "fsdp")),
        P(("dp", "fsdp"), None),
        P(("dp", "fsdp")),
    )
    return jax.shard_map(
        functools.partial(on_device, mesh),
        mesh=mesh,
        in_specs=placed,
        out_specs=(
            P(("dp", "fsdp"), None, None),
            P(("dp", "fsdp"), None, None),
            P(("dp", "fsdp"), None, None),
            P(("dp", "fsdp")),
            P(("dp", "fsdp")),
            P(("dp", "fsdp"), None),
            P(("dp", "fsdp")),
            P(("dp", "fsdp"), None),
            P(("dp", "fsdp"), None),
            P(("dp", "fsdp")),
            P(("dp", "fsdp"), None),
            P(("dp", "fsdp")),
            P(("dp", "fsdp")),
            P(("dp", "fsdp")),
            P(("dp", "fsdp"), None),
            P(("dp", "fsdp")),
            P(("dp", "fsdp"), None),
            P(("dp", "fsdp"), None),
            P(("dp", "fsdp")),
            P(("dp", "fsdp"), None),
            P(("dp", "fsdp")),
            P(("dp", "fsdp")),
            P(("dp", "fsdp")),
            P(("dp", "fsdp"), None),
            P(("dp", "fsdp")),
            P(("dp", "fsdp"), None),
            P(("dp", "fsdp")),
        ),
        check_vma=False,
    )
```

```python
import functools

import jax
import jax.numpy as jnp
from jax import lax
from jax.experimental import pallas as pl
from jax.experimental.pallas import tpu as pltpu
from jax.sharding import PartitionSpec as P

HEADS = 16


EPSILON = 1e-05
ROOT_HALF = 0.7071067811865476
INV_ROOT_TWO_PI = 0.3989422804014327


def product(left, right):
    return jnp.dot(left, right, preferred_element_type=jnp.float32)


def product_tn(left, right):
    return lax.dot_general(
        left, right, (((0,), (0,)), ((), ())), preferred_element_type=jnp.float32
    )


def product_nt(left, right):
    return lax.dot_general(
        left, right, (((1,), (1,)), ((), ())), preferred_element_type=jnp.float32
    )


def normalize(rows_in, norm_gain, norm_shift):
    centered = rows_in - jnp.mean(rows_in, axis=-1, keepdims=True)
    inv_std = lax.rsqrt(jnp.mean(centered * centered, axis=-1, keepdims=True) + EPSILON)
    unit_rows = centered * inv_std
    return (unit_rows * norm_gain + norm_shift, unit_rows, inv_std)


def normalize_back(grad_norm, unit_rows, inv_std, norm_gain):
    scaled = grad_norm * norm_gain
    inner_part = (
        scaled
        - jnp.mean(scaled, axis=-1, keepdims=True)
        - unit_rows * jnp.mean(scaled * unit_rows, axis=-1, keepdims=True)
    )
    return (
        inner_part * inv_std,
        jnp.sum(grad_norm * unit_rows, axis=0, keepdims=True),
        jnp.sum(grad_norm, axis=0, keepdims=True),
    )


LOG2E = 1.4426950408889634
LN2 = 0.6931471805599453


def dot_nn(a, b):
    return jnp.dot(a, b, preferred_element_type=jnp.float32)


def dot_nt(a, b):
    return lax.dot_general(a, b, (((1,), (1,)), ((), ())), preferred_element_type=jnp.float32)


def dot_tn(a, b):
    return lax.dot_general(a, b, (((0,), (0,)), ((), ())), preferred_element_type=jnp.float32)


def lane_half(x, head, half):
    lane = lax.broadcasted_iota(jnp.int32, (1, x.shape[1]), 1)
    keep = (lane < half) if head == 0 else (lane >= half)
    return jnp.where(keep, x, jnp.zeros_like(x))


def causal_spans(rows, chunk):
    return [(start, chunk, start + chunk) for start in range(0, rows, chunk)]


def limit_row(start, width, length):
    pos = start + lax.broadcasted_iota(jnp.int32, (1, width), 1)
    return jnp.minimum(pos, length - 1)


def forward_pair(load_q, load_k, load_v, write, spans, length, scale):
    for start, size, keys in spans:
        q2 = load_q(start, size)
        k2 = load_k(0, keys)
        v2 = load_v(0, keys)
        half = q2.shape[1] // 2
        vt = v2.T
        outs, totals = [], []
        for head in (0, 1):
            raw = dot_nt(k2, lane_half(q2, head, half))
            if length is not None:
                key_pos = lax.broadcasted_iota(jnp.int32, raw.shape, 0)
                raw = jnp.where(key_pos <= limit_row(start, size, length), raw, -1e30)
            top = jnp.max(raw, axis=0, keepdims=True)
            expo = jnp.exp2((raw - top) * (scale * LOG2E))
            total = jnp.sum(expo, axis=0, keepdims=True)
            mixed = dot_nn(vt[head * half : (head + 1) * half], expo.astype(jnp.bfloat16))
            outs.append(mixed / total)
            totals.append(top * (scale * LOG2E) + jnp.log2(total))
        write(start, size, jnp.concatenate(outs, axis=0).T.astype(jnp.bfloat16), totals)


def fwd_kernel(masked, scale, chunk, *refs):
    if masked:
        len_ref, q_ref, k_ref, v_ref, a_ref, t_ref = refs
        length = len_ref[pl.program_id(0)]
    else:
        q_ref, k_ref, v_ref, a_ref, t_ref = refs
        length = None
    rows, keys = q_ref.shape[1], k_ref.shape[1]
    if masked:
        spans = causal_spans(rows, chunk)
    else:
        spans = [(s, chunk, keys) for s in range(0, rows, chunk)]

    def write(start, size, out, totals):
        a_ref[0, pl.ds(start, size), :] = out
        for head in (0, 1):
            t_ref[0, 0, pl.ds(head, 1), pl.ds(start, size)] = totals[head]

    forward_pair(
        lambda s, n: q_ref[0, pl.ds(s, n), :],
        lambda s, n: k_ref[0, pl.ds(s, n), :],
        lambda s, n: v_ref[0, pl.ds(s, n), :],
        write, spans, length, scale,
    )


def attend_fwd(q, k, v, lengths, heads, chunk=256):
    pages, rows, width = q.shape
    keys = k.shape[1]
    head = width // heads
    pairs = heads // 2
    masked = lengths is not None
    row_spec = pl.BlockSpec((1, rows, 2 * head), lambda p, h: (p, 0, h))
    key_spec = pl.BlockSpec((1, keys, 2 * head), lambda p, h: (p, 0, h))
    in_specs = [row_spec, key_spec, key_spec]
    args = [q, k, v]
    if masked:
        in_specs = [pl.BlockSpec(memory_space=pltpu.SMEM)] + in_specs
        args = [lengths] + args
    return pl.pallas_call(
        functools.partial(fwd_kernel, masked, head**-0.5, chunk),
        grid=(pages, pairs),
        in_specs=in_specs,
        out_specs=[row_spec, pl.BlockSpec((1, 1, 2, rows), lambda p, h: (p, h, 0, 0))],
        out_shape=[
            jax.ShapeDtypeStruct(q.shape, jnp.bfloat16),
            jax.ShapeDtypeStruct((pages, pairs, 2, rows), jnp.float32),
        ],
        compiler_params=pltpu.CompilerParams(vmem_limit_bytes=48 * 1024 * 1024),
        name="attend_forward",
    )(*args)


def bwd_kernel(masked, scale, chunk, *refs):
    if masked:
        len_ref, q_ref, k_ref, v_ref, g_ref, t_ref, dq_ref, dk_ref, dv_ref, dk_acc, dv_acc = refs
        length = len_ref[pl.program_id(0)]
    else:
        q_ref, k_ref, v_ref, g_ref, t_ref, dq_ref, dk_ref, dv_ref, dk_acc, dv_acc = refs
        length = None
    rows, keys_all = q_ref.shape[1], k_ref.shape[1]
    if masked:
        spans = causal_spans(rows, chunk)[::-1]
    else:
        spans = [(s, chunk, keys_all) for s in range(0, rows, chunk)]
    half = q_ref.shape[2] // 2
    for step, (start, size, keys) in enumerate(spans):
        q2 = q_ref[0, pl.ds(start, size), :]
        g2 = g_ref[0, pl.ds(start, size), :]
        k2 = k_ref[0, pl.ds(0, keys), :]
        v2 = v_ref[0, pl.ds(0, keys), :]
        kt = k2.T
        dk, dv, dqt = None, None, []
        for head in (0, 1):
            qm = lane_half(q2, head, half)
            gm = lane_half(g2, head, half)
            raw = dot_nt(k2, qm)
            total = t_ref[0, 0, pl.ds(head, 1), pl.ds(start, size)]
            probs = jnp.exp2(raw * (scale * LOG2E) - total)
            if length is not None:
                key_pos = lax.broadcasted_iota(jnp.int32, raw.shape, 0)
                probs = jnp.where(key_pos <= limit_row(start, size, length), probs, 0.0)
            grad = dot_nt(v2, gm)
            part = probs * grad
            dot_row = jnp.sum(part, axis=0, keepdims=True)
            score = ((part - probs * dot_row) * scale).astype(jnp.bfloat16)
            dvh = dot_nn(probs.astype(jnp.bfloat16), gm)
            dkh = dot_nn(score, qm)
            dv = dvh if dv is None else dv + dvh
            dk = dkh if dk is None else dk + dkh
            dqt.append(dot_nn(kt[head * half : (head + 1) * half], score))
        dq_ref[0, pl.ds(start, size), :] = jnp.concatenate(dqt, axis=0).T.astype(jnp.bfloat16)
        if step == 0:
            dk_acc[pl.ds(0, keys), :] = dk
            dv_acc[pl.ds(0, keys), :] = dv
        else:
            dk_acc[pl.ds(0, keys), :] += dk
            dv_acc[pl.ds(0, keys), :] += dv
    dk_ref[0] = dk_acc[...].astype(jnp.bfloat16)
    dv_ref[0] = dv_acc[...].astype(jnp.bfloat16)


def attend_bwd(q, k, v, g, totals, lengths, heads, chunk=256):
    pages, rows, width = q.shape
    keys = k.shape[1]
    head = width // heads
    pairs = heads // 2
    masked = lengths is not None
    row_spec = pl.BlockSpec((1, rows, 2 * head), lambda p, h: (p, 0, h))
    key_spec = pl.BlockSpec((1, keys, 2 * head), lambda p, h: (p, 0, h))
    total_spec = pl.BlockSpec((1, 1, 2, rows), lambda p, h: (p, h, 0, 0))
    in_specs = [row_spec, key_spec, key_spec, row_spec, total_spec]
    args = [q, k, v, g, totals]
    if masked:
        in_specs = [pl.BlockSpec(memory_space=pltpu.SMEM)] + in_specs
        args = [lengths] + args
    return pl.pallas_call(
        functools.partial(bwd_kernel, masked, head**-0.5, chunk),
        grid=(pages, pairs),
        in_specs=in_specs,
        out_specs=[row_spec, key_spec, key_spec],
        out_shape=[jax.ShapeDtypeStruct(a.shape, jnp.bfloat16) for a in (q, k, v)],
        scratch_shapes=[pltpu.VMEM((keys, 2 * head), jnp.float32)] * 2,
        compiler_params=pltpu.CompilerParams(vmem_limit_bytes=48 * 1024 * 1024),
        name="attend_backward",
    )(*args)


MESH_ID = pl.DeviceIdType.MESH
BOTH = ("dp", "fsdp")
CORE_RATE = 500e3
LINK_RATE = 96e3
HOP = 2.5


def bit_table(mesh):
    bits = []
    for axis, name in enumerate(BOTH):
        step = mesh.shape[name] // 2
        while step >= 1:
            bits.append((axis, step))
            step //= 2
    return bits


def can_route(mesh, rows):
    sizes = [mesh.shape[name] for name in BOTH]
    return all(s & (s - 1) == 0 for s in sizes) and rows % 16 == 0


def route_orders(bits):
    outer = [i for i, (axis, _) in enumerate(bits) if axis == 0]
    inner = [i for i, (axis, _) in enumerate(bits) if axis == 1]
    return (outer + inner, outer + inner[:-1][::-1] + inner[-1:])


def loads_of(bits, at, size):
    axis, step = bits[at]
    if axis == 1 and step == 1:
        return {"core": size / CORE_RATE}
    if axis == 1:
        return {f"inner{step}": 2 * size / LINK_RATE}
    loads = {"outer1": 2 * size / LINK_RATE}
    if step > 1:
        loads["outer2"] = 2 * size * step / LINK_RATE
    return loads


def plan_sends(bits, orders, sizes, growing, add_rate, begin=None):
    count = len(bits)
    ready = [(begin[unit] if begin else 0.0, unit, 0) for unit in range(len(orders))]
    free = {}
    plan = []
    arrive = {}
    while ready:
        choices = []
        for when, unit, stage in ready:
            scale = 2**stage if growing else 2 ** (count - 1 - stage)
            loads = loads_of(bits, orders[unit][stage], sizes[unit] * scale)
            start = max([when] + [free.get(link, 0.0) for link in loads])
            choices.append((round(start, 3), unit, -stage, when, scale))
        start, unit, stage, when, scale = min(choices)
        stage = -stage
        ready.remove((when, unit, stage))
        loads = loads_of(bits, orders[unit][stage], sizes[unit] * scale)
        for link, took in loads.items():
            free[link] = start + took
        plan.append((start, unit, stage))
        after = start + max(loads.values()) + HOP
        if add_rate:
            after += sizes[unit] * scale / add_rate
        if stage + 1 < count:
            ready.append((after, unit, stage + 1))
        else:
            arrive[unit] = after
    return sorted(plan), arrive


def my_bits(bits):
    place = (lax.axis_index("dp"), lax.axis_index("fsdp"))
    return [(place[axis] // step) % 2 for axis, step in bits]


def partner(bits, mine, at):
    place = [lax.axis_index("dp"), lax.axis_index("fsdp")]
    axis, step = bits[at]
    place[axis] = place[axis] + step * (1 - 2 * mine[at])
    return tuple(place)


def greet(bits, mine):
    barrier = pltpu.get_barrier_semaphore()
    for at in range(len(bits)):
        pl.semaphore_signal(
            barrier, inc=1, device_id=partner(bits, mine, at), device_id_type=MESH_ID
        )
    pl.semaphore_wait(barrier, len(bits))


def unit_shape(blocks, unit):
    array, rows, cols = unit
    block = blocks[array]
    return (len(range(*rows.indices(block[0]))), len(range(*cols.indices(block[1]))))


ERF_RATE = 0.3275911
ERF_TERMS = (0.254829592, -0.284496736, 1.421413741, -1.453152027, 1.061405429)


def gelu_parts(pre):
    bell = jnp.exp2(pre * pre * (-0.5 * LOG2E))
    arm = 1.0 / (1.0 + jnp.abs(pre) * (ERF_RATE * ROOT_HALF))
    series = ERF_TERMS[4]
    for term in ERF_TERMS[3::-1]:
        series = series * arm + term
    tail = 0.5 * series * arm * bell
    below = jnp.where(pre >= 0.0, 1.0 - tail, tail)
    return pre * below, below + pre * bell * INV_ROOT_TWO_PI


class Schedule:
    def __init__(self, plan, issue):
        self.plan = plan
        self.issue = issue
        self.at = 0
        self.now = 0.0

    def due(self):
        items = []
        while self.at < len(self.plan) and self.plan[self.at][0] <= self.now:
            items.append(self.plan[self.at][1:])
            self.at += 1
        return items

    def spend(self, took):
        self.now += took
        for unit, stage in self.due():
            self.issue(unit, stage)

    def until(self, when):
        self.now = max(self.now, when)
        for unit, stage in self.due():
            self.issue(unit, stage)

    def loop(self, count, took, body):
        buckets = []
        for _ in range(count):
            self.now += took
            buckets.append(self.due())

        def step(i, carry):
            body(i)
            for k, items in enumerate(buckets):
                if items:

                    @pl.when(i == k)
                    def _(items=items):
                        for unit, stage in items:
                            self.issue(unit, stage)

            return carry

        lax.fori_loop(0, count, step, 0)


ROWS_STEP = 128


N_VECS = 14
VEC_ROWS = 16
VEC_LANES = 128


def device_index(bits, mine):
    count = len(bits)
    return sum(mine[b] * 2 ** (count - 1 - b) for b in range(count))


def pack_vectors(loose, pack, spot, size):
    row = lax.broadcasted_iota(jnp.int32, (size, VEC_LANES), 0)
    lane = lax.broadcasted_iota(jnp.int32, (size, VEC_LANES), 1)
    place = (lane == row + size * spot).astype(jnp.float32)
    pieces = []
    for ref in loose[:-1]:
        pieces.append(dot_nn(ref[...].astype(jnp.float32).reshape(1, size), place))
    pieces.append(loose[-1][...].astype(jnp.float32).reshape(1, VEC_LANES))
    pieces.append(jnp.zeros((VEC_ROWS - len(pieces), VEC_LANES), jnp.float32))
    pack[...] = jnp.concatenate(pieces, axis=0).astype(pack.dtype)


def unpack_table(vecs, table, bits, width, hidden_row=None):
    count = len(bits)
    devices = 2**count
    share = devices * VEC_LANES // width
    spots = [tuple((d >> (count - 1 - b)) & 1 for b in range(count)) for d in range(devices)]
    for group in range(width // VEC_LANES):
        total = None
        for d in range(group * share, (group + 1) * share):
            block = vecs[spots[d]].astype(jnp.float32)
            total = block if total is None else total + block
        table[:, pl.ds(group * VEC_LANES, VEC_LANES)] = total
    if hidden_row is not None:
        for d in range(devices):
            block = vecs[spots[d]].astype(jnp.float32)
            hidden_row[pl.ds(0, 1), pl.ds(d * VEC_LANES, VEC_LANES)] = block[N_VECS - 1 : N_VECS]


def forward_kernel(bits, units, orders, plan, arrive, n_arrays, heads, *refs):
    count = len(bits)
    (tokens, memory, lengths), refs = refs[:3], refs[3:]
    loose, refs = refs[:N_VECS], refs[N_VECS:]
    sources, refs = refs[: n_arrays - 1], refs[n_arrays - 1 :]
    targets, refs = refs[:n_arrays], refs[n_arrays:]
    saved_names = ("q", "k", "v", "a", "total", "h1")
    saved_names += ("cq", "ck", "cv", "ca", "ctotal", "h2", "g", "slope", "out")
    saved = dict(zip(saved_names, refs[: len(saved_names)]))
    refs = refs[len(saved_names) :]
    x, mem, n, q, k, v, a, h, ck, cv, g, slope, tot, ctot = refs[:14]
    wide, tall, pack, vecs, table, hidden_row = refs[14:-6]
    send_sem, recv_sem, own_sem, in_sem, w_sem, out_sem = refs[-6:]
    mine = my_bits(bits)
    rows, width = x.shape
    devices = 2**count
    lanes_each = width // devices
    pack_vectors(loose, pack, device_index(bits, mine) % (VEC_LANES // lanes_each), lanes_each)
    sources = (pack,) + tuple(sources)
    own = [
        pltpu.make_async_copy(sources[i], targets[i].at[tuple(mine)], own_sem.at[i])
        for i in range(n_arrays)
    ]
    for copy in own:
        copy.start()
    load_x = pltpu.make_async_copy(tokens, x, in_sem.at[0])
    load_mem = pltpu.make_async_copy(memory, mem, in_sem.at[1])
    load_x.start()
    load_mem.start()
    greet(bits, mine)

    def message(unit, stage):
        array, top, left = units[unit]
        order = orders[unit]
        where = tuple(slice(None) if b in order[:stage] else mine[b] for b in range(count))
        place = targets[array].at[where + (top, left)]
        source = sources[array].at[top, left] if stage == 0 else place
        return pltpu.make_async_remote_copy(
            src_ref=source,
            dst_ref=place,
            send_sem=send_sem.at[unit, stage],
            recv_sem=recv_sem.at[unit, stage],
            device_id=partner(bits, mine, order[stage]),
            device_id_type=MESH_ID,
        )

    settled = set()

    def issue(unit, stage):
        array = units[unit][0]
        if stage > 0:
            if array not in settled:
                settled.add(array)
                own[array].wait()
            message(unit, stage - 1).wait_recv()
        message(unit, stage).start()

    clock = Schedule(plan, issue)
    every = (slice(None),) * count

    def fetch(unit, slot, sem):
        clock.until(arrive[unit])
        message(unit, count - 1).wait_recv()
        array, top, left = units[unit]
        if array not in settled:
            settled.add(array)
            own[array].wait()
        copy = pltpu.make_async_copy(targets[array].at[every + (top, left)], slot, w_sem.at[sem])
        copy.start()
        copy.wait()

    def times(lhs, slot, tile, write, took=1.4):
        depth = lhs.shape[1]
        tiles = slot.shape[-1] // tile

        def body(j):
            cols = pl.ds(pl.multiple_of(j * tile, tile), tile)
            weight = slot[every + (slice(None), cols)].reshape(depth, tile)
            write(cols, dot_nn(lhs[...], weight))

        clock.loop(tiles, took / tiles, body)

    def norm_into(gain, shift, source):
        def body(i):
            part = pl.ds(pl.multiple_of(i * ROWS_STEP, ROWS_STEP), ROWS_STEP)
            r = source[part, :].astype(jnp.float32)
            n[part, :] = normalize(r, gain, shift)[0].astype(jnp.bfloat16)

        clock.loop(rows // ROWS_STEP, 0.4, body)

    pending = []

    def save(source, name, index):
        copy = pltpu.make_async_copy(source, saved[name], out_sem.at[index])
        copy.start()
        pending.append(copy)
        return copy

    def vec(i):
        return table[pl.ds(i, 1), :]

    clock.until(0.0)
    fetch(0, vecs, 0)
    unpack_table(vecs, table, bits, width, hidden_row)
    load_x.wait()
    load_mem.wait()
    norm_into(vec(0), vec(1), x)
    length = lengths[0]

    def project(bias, target, extra=0):
        def write(cols, acc):
            if bias is not None:
                acc = acc + table[pl.ds(bias, 1), cols]
            target[:, cols] = acc.astype(target.dtype)

        return write

    def residual(bias, source):
        def write(cols, acc):
            h[:, cols] = source[:, cols].astype(jnp.float32) + acc + table[pl.ds(bias, 1), cols]

        return write

    def attend(q_ref, k_ref, v_ref, tot_ref, masked):
        keys = k_ref.shape[0]
        pair = 2 * (width // heads)

        def body(p):
            lanes = pl.ds(pl.multiple_of(p * pair, pair), pair)

            def write(start, size, out, totals):
                a[pl.ds(start, size), lanes] = out
                for head in (0, 1):
                    tot_ref[p, pl.ds(head, 1), pl.ds(start, size)] = totals[head]

            forward_pair(
                lambda s, m: q_ref[pl.ds(s, m), lanes],
                lambda s, m: k_ref[pl.ds(s, m), lanes],
                lambda s, m: v_ref[pl.ds(s, m), lanes],
                write,
                [(0, rows, keys)],
                length if masked else None,
                (width // heads) ** -0.5,
            )

        clock.loop(heads // 2, 1.6, body)

    for unit, target, bias in ((1, q, 2), (2, k, None), (3, v, 3)):
        fetch(unit, wide, 1)
        times(n, wide, 256, project(bias, target))
    save(q, "q", 0)
    save(k, "k", 1)
    save(v, "v", 2)
    attend(q, k, v, tot, True)
    save(a, "a", 3)
    save(tot, "total", 4)
    for unit, target, bias in ((4, ck, None), (5, cv, 8)):
        fetch(unit, wide, 1)
        times(mem, wide, 256, project(bias, target), 1.6)
    save(ck, "ck", 5)
    save(cv, "cv", 6)
    fetch(6, wide, 1)
    times(a, wide, 256, residual(4, x))
    save(h, "h1", 7)
    norm_into(vec(5), vec(6), h)
    fetch(7, wide, 1)
    pending[0].wait()
    times(n, wide, 256, project(7, q))
    save(q, "cq", 8)
    pending[3].wait()
    attend(q, ck, cv, ctot, False)
    save(a, "ca", 9)
    save(ctot, "ctotal", 10)
    fetch(8, wide, 1)
    pending[7].wait()
    times(a, wide, 256, residual(9, h))
    save(h, "h2", 11)
    norm_into(vec(10), vec(11), h)
    block = wide.shape[-1]
    blocks = g.shape[1] // block
    for j in range(blocks):
        fetch(9 + j, wide, 1)
        tile = 256

        def body(i, j=j):
            cols = pl.ds(pl.multiple_of(i * tile, tile), tile)
            spot = pl.ds(pl.multiple_of(j * block + i * tile, tile), tile)
            weight = wide[every + (slice(None), cols)].reshape(width, tile)
            for r in range(0, rows, ROWS_STEP):
                part = pl.ds(r, ROWS_STEP)
                pre = dot_nn(n[part, :], weight) + hidden_row[:, spot]
                low, rate = gelu_parts(pre)
                g[part, spot] = low.astype(jnp.bfloat16)
                slope[part, spot] = rate.astype(jnp.bfloat16)

        clock.loop(block // tile, 0.8, body)
    save(g, "g", 12)
    save(slope, "slope", 13)
    for j in range(width // tall.shape[-1]):
        fetch(9 + blocks + j, tall, 2)
        cols = pl.ds(j * tall.shape[-1], tall.shape[-1])
        weight = tall[...].reshape(g.shape[1], tall.shape[-1])
        acc = dot_nn(g[...], weight)
        x[:, cols] = (h[:, cols] + acc + table[pl.ds(12, 1), cols]).astype(jnp.bfloat16)
        clock.spend(1.6)
    save(x, "out", 14)
    clock.until(1e9)
    for i, copy in enumerate(pending):
        if i not in (0, 3, 7):
            copy.wait()
    for unit in range(len(units)):
        for stage in range(count):
            message(unit, stage).wait_send()


def fused_forward(mesh, tokens, memory, lengths, mats, vecs, heads, collective_id):
    bits = bit_table(mesh)
    routes = route_orders(bits)
    rows, width = tokens.shape
    keys = memory.shape[0]
    block = mats[0].shape
    pack = (VEC_ROWS, VEC_LANES)
    every = slice(None)
    units = [(0, every, every)] + [(i, every, every) for i in range(1, 9)]
    hidden = mats[8].shape[1]
    for left in range(0, hidden, width):
        units.append((9, every, slice(left, left + width)))
    tall_rows = mats[9].shape[0]
    tall_cols = width * block[0] // tall_rows
    for left in range(0, width, tall_cols):
        units.append((10, every, slice(left, left + tall_cols)))
    blocks = [pack] + [m.shape for m in mats]
    shapes = [unit_shape(blocks, unit) for unit in units]
    sizes = [2 * s[0] * s[1] for s in shapes]
    orders = [routes[u % 2] for u in range(len(units))]
    plan, arrive = plan_sends(bits, orders, sizes, True, None)
    n = len(blocks)
    spots = (2,) * len(bits)
    low = jnp.bfloat16
    wide_rows = jax.ShapeDtypeStruct((rows, width), low)
    wide_keys = jax.ShapeDtypeStruct((keys, width), low)
    full = jax.ShapeDtypeStruct((rows, width), jnp.float32)
    totals = jax.ShapeDtypeStruct((heads // 2, 2, rows), jnp.float32)
    ff = jax.ShapeDtypeStruct((rows, hidden), low)
    saved = [
        wide_rows, wide_rows, wide_rows, wide_rows, totals, full,
        wide_rows, wide_keys, wide_keys, wide_rows, totals, full, ff, ff, wide_rows,
    ]
    vm = lambda s: pltpu.VMEM(s.shape, s.dtype)
    sems = (len(units), len(bits))
    hbm = pl.BlockSpec(memory_space=pltpu.HBM)
    got = pl.pallas_call(
        functools.partial(forward_kernel, bits, units, orders, plan, arrive, n, heads),
        out_shape=[jax.ShapeDtypeStruct(spots + b, low) for b in blocks] + saved,
        in_specs=[hbm, hbm, pl.BlockSpec(memory_space=pltpu.SMEM)]
        + [pl.BlockSpec(memory_space=pltpu.VMEM)] * len(vecs)
        + [hbm] * len(mats),
        out_specs=[hbm] * (n + len(saved)),
        scratch_shapes=[
            vm(wide_rows), vm(wide_keys), vm(wide_rows), vm(wide_rows), vm(wide_rows),
            vm(wide_rows), vm(wide_rows), vm(full), vm(wide_keys), vm(wide_keys),
            vm(ff), vm(ff), vm(totals), vm(totals),
            pltpu.VMEM(spots + block, low),
            pltpu.VMEM(spots + (tall_rows, tall_cols), low),
            pltpu.VMEM(pack, low),
            pltpu.VMEM(spots + pack, low),
            pltpu.VMEM((VEC_ROWS, width), jnp.float32),
            pltpu.VMEM((1, hidden), jnp.float32),
            pltpu.SemaphoreType.DMA(sems),
            pltpu.SemaphoreType.DMA(sems),
            pltpu.SemaphoreType.DMA((n,)),
            pltpu.SemaphoreType.DMA((2,)),
            pltpu.SemaphoreType.DMA((3,)),
            pltpu.SemaphoreType.DMA((len(saved),)),
        ],
        compiler_params=pltpu.CompilerParams(
            collective_id=collective_id,
            has_side_effects=True,
            vmem_limit_bytes=60 * 1024 * 1024,
        ),
        name="forward_layer",
    )(tokens, memory, lengths, *vecs, *mats)
    return got[:n], got[n:]


class Deferred(Schedule):
    def __init__(self, plan, issue):
        super().__init__(list(plan), issue)
        self.made = set()

    def due(self):
        items, rest, held_back = [], [], set()
        for item in self.plan:
            when, unit, stage = item
            if unit in self.made and unit not in held_back and when <= self.now:
                items.append((unit, stage))
            else:
                held_back.add(unit)
                rest.append(item)
        self.plan = rest
        return items

    def finish(self, unit, last=99):
        late = [when for when, u, stage in self.plan if u == unit and stage <= last]
        if late:
            self.until(max(late))


def backward_pair(refs, accs, total_of, spans, length, scale, lanes):
    q_ref, k_ref, v_ref, g_ref = refs
    dk_acc, dv_acc = accs
    keys_all = k_ref.shape[0]
    half = (dk_acc.shape[1]) // 2
    for step, (start, size, keys) in enumerate(spans):
        part_rows = pl.ds(start, size)
        q2 = q_ref[part_rows, lanes]
        g2 = g_ref[part_rows, lanes]
        k2 = k_ref[pl.ds(0, keys), lanes]
        v2 = v_ref[pl.ds(0, keys), lanes]
        kt = k2.T
        dk, dv, dqt = None, None, []
        for head in (0, 1):
            qm = lane_half(q2, head, half)
            gm = lane_half(g2, head, half)
            raw = dot_nt(k2, qm)
            probs = jnp.exp2(raw * (scale * LOG2E) - total_of(head, start, size))
            if length is not None:
                key_pos = lax.broadcasted_iota(jnp.int32, raw.shape, 0)
                probs = jnp.where(key_pos <= limit_row(start, size, length), probs, 0.0)
            grad = dot_nt(v2, gm)
            part = probs * grad
            dot_row = jnp.sum(part, axis=0, keepdims=True)
            score = ((part - probs * dot_row) * scale).astype(jnp.bfloat16)
            dvh = dot_nn(probs.astype(jnp.bfloat16), gm)
            dkh = dot_nn(score, qm)
            dv = dvh if dv is None else dv + dvh
            dk = dkh if dk is None else dk + dkh
            dqt.append(dot_nn(kt[head * half : (head + 1) * half], score))
        q_ref[part_rows, lanes] = jnp.concatenate(dqt, axis=0).T.astype(jnp.bfloat16)
        if step == 0:
            dk_acc[pl.ds(0, keys), :] = dk
            dv_acc[pl.ds(0, keys), :] = dv
        else:
            dk_acc[pl.ds(0, keys), :] += dk
            dv_acc[pl.ds(0, keys), :] += dv
    every_key = pl.ds(0, keys_all)
    k_ref[every_key, lanes] = dk_acc[every_key, :].astype(jnp.bfloat16)
    v_ref[every_key, lanes] = dv_acc[every_key, :].astype(jnp.bfloat16)


BACK_INPUTS = ("dz", "tokens", "memory", "lengths")
BACK_INPUTS += ("q", "k", "v", "a", "total", "h1", "cq", "ck", "cv", "ca", "ctotal", "h2", "g", "rate")
BACK_INPUTS += ("wvec", "wq", "wk", "wv", "wck", "wcv", "wo", "wcq", "wco", "win", "wout")
MADE_AT = (5.0, 8.0, 11.0, 14.0, 21.0, 26.0, 31.0, 36.0, 44.0)
MADE_AT += (70.0, 72.0, 74.0, 88.0, 112.0, 114.0, 116.0, 128.0)
TALL_UNITS = 4
WIDE_HELD = 6
WIDE_BOXES = 3
TALL_BOXES = 2
SUM_SLOTS = 4


def ring_place(unit, n_wide):
    if unit < TALL_UNITS:
        return "tall", unit
    if unit < TALL_UNITS + n_wide:
        return "wide", unit - TALL_UNITS
    return "vec", 0


def backward_kernel(bits, orders, plan, outs_of, heads, *refs):
    count = len(bits)
    n_units = len(orders)
    n_wide = n_units - TALL_UNITS - 1
    given = dict(zip(BACK_INPUTS, refs[: len(BACK_INPUTS)]))
    refs = refs[len(BACK_INPUTS) :]
    tokens_grad, memory_grad = refs[:2]
    results = refs[2:13]
    refs = refs[13:]
    bdz, n, acc, dh, hb, wide_a, wide_b, stage_a, stage_b = refs[:9]
    held_tall, held_wide, box_tall, box_wide = refs[9:13]
    rest_tall, rest_wide = refs[13 : 13 + count - 1], refs[13 + count - 1 : 13 + 2 * (count - 1)]
    refs = refs[13 + 2 * (count - 1) :]
    vec_stage, vec_held = refs[:2]
    vec_boxes = refs[2 : 2 + count]
    refs = refs[2 + count :]
    sum_tall, sum_wide, sum_vec, vgrad, hgrad, table, vecs, tot, dk_acc, dv_acc = refs[:10]
    send_sem, recv_sem, own_sem, store_sem, load_sem, w_sem, credit = refs[10:]
    wides, stages = (wide_a, wide_b), (stage_a, stage_b)
    vgrad[...] = jnp.zeros_like(vgrad)
    mine = my_bits(bits)
    core = count - 1
    rows, width = bdz.shape
    every = (slice(None),) * count
    tall_stage = [None]

    loads = {}

    def load(name, source, target):
        loads[name] = pltpu.make_async_copy(source, target, load_sem.at[len(loads)])
        loads[name].start()

    load("dz", given["dz"], bdz)
    load("vecs", given["wvec"], vecs)
    load("h2", given["h2"], hb)
    greet(bits, mine)

    def held_of(unit):
        kind, i = ring_place(unit, n_wide)
        if kind == "vec":
            return vec_held
        return held_tall.at[i] if kind == "tall" else held_wide.at[i % WIDE_HELD]

    def stage_of(unit):
        kind, i = ring_place(unit, n_wide)
        if kind == "vec":
            return vec_stage
        return tall_stage[i % len(tall_stage)] if kind == "tall" else stages[i % len(stages)]

    def box_of(unit, stage):
        kind, i = ring_place(unit, n_wide)
        if kind == "vec":
            return vec_boxes[stage]
        if kind == "tall":
            return box_tall.at[i % TALL_BOXES] if stage == 0 else rest_tall[stage - 1].at[i]
        return box_wide.at[i % WIDE_BOXES] if stage == 0 else rest_wide[stage - 1].at[i]

    def own_copy(unit):
        half = stage_of(unit).at[(slice(None),) * core + (mine[core],)]
        return pltpu.make_async_copy(half, held_of(unit), own_sem.at[unit])

    def message(unit, stage):
        order = orders[unit]
        now = order[stage]
        where = []
        for b in range(count):
            if b == now:
                where.append(1 - mine[b])
            elif b in order[:stage]:
                where.append(mine[b])
            else:
                where.append(slice(None))
        if stage == 0:
            source = stage_of(unit).at[tuple(where)]
        else:
            source = held_of(unit).at[tuple(where[:core])]
        return pltpu.make_async_remote_copy(
            src_ref=source,
            dst_ref=box_of(unit, stage),
            send_sem=send_sem.at[unit, stage],
            recv_sem=recv_sem.at[unit, stage],
            device_id=partner(bits, mine, now),
            device_id_type=MESH_ID,
        )

    sent = set()
    copied = set()

    def own_ready(unit):
        if unit not in copied:
            copied.add(unit)
            own_copy(unit).wait()

    def drained(unit, stage):
        if (unit, stage) not in sent:
            sent.add((unit, stage))
            message(unit, stage).wait_send()

    def next_in_ring(unit):
        kind, i = ring_place(unit, n_wide)
        if kind == "tall":
            return i + TALL_BOXES < TALL_UNITS
        return kind == "wide" and i + WIDE_BOXES < n_wide

    def credit_of(unit):
        kind, i = ring_place(unit, n_wide)
        return credit.at[i % TALL_BOXES] if kind == "tall" else credit.at[TALL_BOXES + i % WIDE_BOXES]

    def add(unit, stage, target=None):
        order = orders[unit]
        message(unit, stage).wait_recv()
        if stage == 0:
            own_ready(unit)
        held, box = held_of(unit), box_of(unit, stage)
        open_bits = [b for b in range(count) if b not in order[: stage + 1]]
        blocks = 2 ** len(open_bits)

        def one(block, carry):
            where, spot = [], []
            for b in range(core):
                if b in open_bits:
                    digit = (block // 2 ** (len(open_bits) - 1 - open_bits.index(b))) % 2
                    where.append(digit)
                    spot.append(digit)
                else:
                    where.append(mine[b])
            where, spot = tuple(where), tuple(spot)
            if target is not None:
                total = held[where].astype(jnp.float32) + box[spot].astype(jnp.float32)
                target[...] = total
            else:
                held[where] = held[where] + box[spot]
            return carry

        if blocks == 1:
            one(0, 0)
        else:
            lax.fori_loop(0, blocks, one, 0)
        if stage == 0 and next_in_ring(unit):
            pl.semaphore_signal(
                credit_of(unit), inc=1, device_id=partner(bits, mine, core), device_id_type=MESH_ID
            )

    stored = {}

    def sum_of(unit):
        kind, i = ring_place(unit, n_wide)
        if kind == "vec":
            return sum_vec
        return sum_tall.at[i] if kind == "tall" else sum_wide.at[i % SUM_SLOTS]

    def store(unit):
        array, top, left = outs_of[unit]
        return pltpu.make_async_copy(
            sum_of(unit), results[array].at[top, left], store_sem.at[unit]
        )

    def end(unit):
        kind, i = ring_place(unit, n_wide)
        if kind == "wide":
            if i % SUM_SLOTS in stored:
                store(stored[i % SUM_SLOTS]).wait()
            stored[i % SUM_SLOTS] = unit
        add(unit, count - 1, sum_of(unit))
        store(unit).start()

    def issue(unit, stage):
        if stage == count:
            end(unit)
        else:
            add(unit, stage - 1)
            message(unit, stage).start()

    clock = Deferred(plan, issue)

    def made(unit):
        kind, i = ring_place(unit, n_wide)
        if kind == "wide" and i >= WIDE_HELD:
            clock.finish(unit - WIDE_HELD)
            for stage in range(1, count):
                drained(unit - WIDE_HELD, stage)
        own_copy(unit).start()
        ring = TALL_BOXES if kind == "tall" else WIDE_BOXES
        if kind != "vec" and i >= ring:
            clock.finish(unit - ring, 1)
            pl.semaphore_wait(credit_of(unit), 1)
        message(unit, 0).start()
        clock.made.add(unit)
        clock.spend(0.0)

    def stage_free(unit):
        kind, i = ring_place(unit, n_wide)
        depth = len(tall_stage) if kind == "tall" else len(stages)
        if i >= depth:
            own_ready(unit - depth)
            drained(unit - depth, 0)

    whole = every + (slice(None), slice(None))
    hidden = hgrad.shape[1]
    blocks = hidden // width
    names = [("win", every + (slice(None), slice(j * width, (j + 1) * width))) for j in range(blocks)]
    names += [(name, whole) for name in ("wco", "wcq", "wck", "wcv", "wo", "wq", "wk", "wv")]
    weights = [
        pltpu.make_async_copy(given[name].at[where], wides[i % 2], w_sem.at[i])
        for i, (name, where) in enumerate(names)
    ]
    weights[0].start()
    weights[1].start()

    def back_through(i, lhs, write, took=1.4):
        weights[i].wait()
        slot = wides[i % 2]

        def body(t):
            part = slot[t].reshape(width // 2, width)
            write(pl.ds(pl.multiple_of(t * (width // 2), width // 2), width // 2), dot_nt(lhs(), part))

        clock.loop(2, took / 2, body)
        if i + 2 < len(weights):
            weights[i + 2].start()

    def produce(unit, lhs, rhs, took=1.5):
        stage_free(unit)
        slot = stage_of(unit)
        half = width // 2

        def body(t):
            start = pl.multiple_of(t * half, half)
            cols = pl.ds(start, half)
            tile = dot_tn(lhs(), rhs(start, half)).astype(jnp.bfloat16)
            slot[every + (slice(None), cols)] = tile.reshape(slot.shape[:-1] + (half,))

        clock.loop(2, took / 2, body)
        made(unit)

    def column_sums(ref, rows_now, target, at):
        ones = jnp.ones((8, rows_now), jnp.bfloat16)
        target[pl.ds(at, 1), :] = dot_nn(ones, ref)[0:1]

    loads["vecs"].wait()
    unpack_table(vecs, table, bits, width)

    def vec(i):
        return table[pl.ds(i, 1), :]

    def norm_rows(source, gain, shift):
        def body(i):
            part = pl.ds(pl.multiple_of(i * ROWS_STEP, ROWS_STEP), ROWS_STEP)
            r = source[part, :].astype(jnp.float32)
            n[part, :] = normalize(r, vec(gain), vec(shift))[0].astype(jnp.bfloat16)

        clock.loop(rows // ROWS_STEP, 0.4, body)

    def norm_back(source, gain, base):
        vgrad[pl.ds(gain, 2), :] = jnp.zeros((2, width), jnp.float32)

        def body(i):
            part = pl.ds(pl.multiple_of(i * ROWS_STEP, ROWS_STEP), ROWS_STEP)
            r = source[part, :].astype(jnp.float32)
            _, unit_rows, inv_std = normalize(r, vec(gain), vec(gain))
            back, gain_sum, shift_sum = normalize_back(acc[part, :], unit_rows, inv_std, vec(gain))
            vgrad[pl.ds(gain, 1), :] += gain_sum
            vgrad[pl.ds(gain + 1, 1), :] += shift_sum
            total = base(part) + back
            dh[part, :] = total
            bdz[part, :] = total.astype(jnp.bfloat16)

        clock.loop(rows // ROWS_STEP, 0.8, body)

    def feed_phase(big, rate, wrow, tall_a):
        tall_stage[0] = tall_a
        load("g", given["g"], big)

        def rate_copy(j):
            cols = pl.ds(j * width, width)
            return pltpu.make_async_copy(given["rate"].at[:, cols], rate, load_sem.at[20 + j])

        def row_copy(j):
            return pltpu.make_async_copy(given["wout"].at[j // 2, j % 2], wrow, load_sem.at[24 + j])

        rate_copy(0).start()
        row_copy(0).start()
        loads["dz"].wait()
        loads["g"].wait()
        tall_cols = tall_a.shape[-1]
        for j in range(TALL_UNITS):
            stage_free(j)
            slot = stage_of(j)

            def body(t, j=j, slot=slot):
                part = big[:, pl.ds(pl.multiple_of(t * width, width), width)]
                tile = dot_tn(part, bdz[:, pl.ds(j * tall_cols, tall_cols)]).astype(jnp.bfloat16)
                slot[t // 2, t % 2] = tile.reshape(slot.shape[2:])

            clock.loop(4, 0.45, body)
            made(j)
        column_sums(bdz[...], rows, vgrad, 12)
        loads["h2"].wait()
        norm_rows(hb, 10, 11)
        for j in range(blocks):
            rate_copy(j).wait()
            row_copy(j).wait()
            half = width // 2

            def body(t, j=j):
                spot = pl.ds(pl.multiple_of(j * width + t * half, half), half)
                weight = wrow[t].reshape(half, width)
                slope = rate[:, pl.ds(pl.multiple_of(t * half, half), half)].astype(jnp.float32)
                big[:, spot] = (dot_nt(bdz[...], weight) * slope).astype(jnp.bfloat16)

            clock.loop(2, 0.8, body)
            if j + 1 < blocks:
                rate_copy(j + 1).start()
                row_copy(j + 1).start()
            block = pl.ds(j * width, width)
            hgrad[pl.ds(0, 1), block] = dot_nn(jnp.ones((8, rows), jnp.bfloat16), big[:, block])[0:1]
            produce(
                TALL_UNITS + j,
                lambda: n[...],
                lambda start, size, j=j: big[:, pl.ds(pl.multiple_of(j * width + start, size), size)],
            )

            def write(cols, value, j=j):
                top = pl.ds(0, rows)
                if j == 0:
                    acc[top, cols] = value
                else:
                    acc[top, cols] += value

            back_through(j, lambda j=j: big[:, pl.ds(j * width, width)], write)
        norm_back(hb, 10, lambda part: bdz[part, :].astype(jnp.float32))
        for unit in range(TALL_UNITS):
            own_ready(unit)
            drained(unit, 0)

    def attention_phase(bq, bk, bv, bg, mem, ba):
        load("h1", given["h1"], hb)
        load("ca", given["ca"], ba)
        load("cq", given["cq"], bq)
        load("ck", given["ck"], bk)
        load("cv", given["cv"], bv)
        load("ctotal", given["ctotal"], tot)
        load("memory", given["memory"], mem)

        def into(ref, size=rows):
            def write(cols, value):
                ref[pl.ds(0, size), cols] = value.astype(ref.dtype)

            return write

        def attend(keys, masked):
            pair = 2 * (width // heads)
            chunk = rows // 2
            spans = [(s, chunk, s + chunk if masked else keys) for s in range(0, rows, chunk)]
            key_rows = pl.ds(0, keys)
            refs_now = (bq, bk.at[key_rows], bv.at[key_rows], bg)

            def body(p):
                lanes = pl.ds(pl.multiple_of(p * pair, pair), pair)
                backward_pair(
                    refs_now,
                    (dk_acc, dv_acc),
                    lambda head, start, size: tot[p, pl.ds(head, 1), pl.ds(start, size)],
                    spans[::-1],
                    length if masked else None,
                    (width // heads) ** -0.5,
                    lanes,
                )

            clock.loop(heads // 2, 2.5, body)

        def picked(ref, size=rows):
            return lambda start, width_now: ref[pl.ds(0, size), pl.ds(start, width_now)]

        first = TALL_UNITS + blocks
        keys = mem.shape[0]
        length = given["lengths"][0]
        at = blocks
        back_through(at, lambda: bdz[...], into(bg))
        loads["ca"].wait()
        produce(first, lambda: ba[...], picked(bdz))
        column_sums(bdz[...], rows, vgrad, 9)
        for name in ("cq", "ck", "cv", "ctotal"):
            loads[name].wait()
        attend(keys, False)
        load("a", given["a"], ba)
        load("total", given["total"], tot)
        loads["h1"].wait()
        norm_rows(hb, 5, 6)
        produce(first + 1, lambda: n[...], picked(bq))
        loads["memory"].wait()
        produce(first + 2, lambda: mem[...], picked(bk, keys), 1.7)
        produce(first + 3, lambda: mem[...], picked(bv, keys), 1.7)
        column_sums(bq[...], rows, vgrad, 7)
        column_sums(bv[...], keys, vgrad, 8)
        back_through(at + 1, lambda: bq[...], into(acc))
        load("q", given["q"], bq)
        norm_back(hb, 5, lambda part: dh[part, :])
        back_through(at + 2, lambda: bk[...], into(acc, keys))

        def more(size):
            def write(cols, value):
                acc[pl.ds(0, size), cols] += value

            return write

        back_through(at + 3, lambda: bv[...], more(keys))
        put_memory = pltpu.make_async_copy(acc, memory_grad, load_sem.at[28])
        put_memory.start()
        top = pl.ds(0, rows)
        load("k", given["k"], bk.at[top])
        load("v", given["v"], bv.at[top])
        back_through(at + 4, lambda: bdz[...], into(bg))
        loads["a"].wait()
        produce(first + 4, lambda: ba[...], picked(bdz))
        column_sums(bdz[...], rows, vgrad, 4)
        for name in ("q", "k", "v", "total"):
            loads[name].wait()
        load("tokens", given["tokens"], ba)
        attend(rows, True)
        loads["tokens"].wait()
        norm_rows(ba, 0, 1)
        for i, ref in enumerate((bq, bk, bv)):
            produce(first + 5 + i, lambda: n[...], picked(ref))
        column_sums(bq[...], rows, vgrad, 2)
        column_sums(bv[top, :], rows, vgrad, 3)
        put_memory.wait()
        back_through(at + 5, lambda: bq[...], into(acc))
        back_through(at + 6, lambda: bk[top, :], more(rows))
        back_through(at + 7, lambda: bv[top, :], more(rows))
        norm_back(ba, 0, lambda part: dh[part, :])

    ff_dtype = jnp.bfloat16
    pl.run_scoped(
        feed_phase,
        pltpu.VMEM((rows, hidden), ff_dtype),
        pltpu.VMEM((rows, width), ff_dtype),
        pltpu.VMEM(given["wout"].shape[2:], ff_dtype),
        pltpu.VMEM((2,) * count + held_tall.shape[-2:], ff_dtype),
    )
    key_rows = given["memory"].shape[0]
    pl.run_scoped(
        attention_phase,
        pltpu.VMEM((rows, width), ff_dtype),
        pltpu.VMEM((key_rows, width), ff_dtype),
        pltpu.VMEM((key_rows, width), ff_dtype),
        pltpu.VMEM((rows, width), ff_dtype),
        pltpu.VMEM((key_rows, width), ff_dtype),
        pltpu.VMEM((rows, width), ff_dtype),
    )
    put_tokens = pltpu.make_async_copy(dh, tokens_grad, load_sem.at[29])
    put_tokens.start()
    devices = 2**count
    share = devices // (width // VEC_LANES)
    for d in range(devices):
        where = tuple((d >> (count - 1 - b)) & 1 for b in range(count))
        vec_stage[where] = vgrad[:, pl.ds(d // share * VEC_LANES, VEC_LANES)]
        vec_stage[where + (pl.ds(13, 1),)] = hgrad[:, pl.ds(d * VEC_LANES, VEC_LANES)]
    made(n_units - 1)
    clock.until(1e9)
    put_tokens.wait()
    waiting = set(stored.values()) | set(range(TALL_UNITS)) | {n_units - 1}
    for unit in range(n_units):
        if unit in waiting:
            store(unit).wait()
        for stage in range(count):
            drained(unit, stage)


def fused_backward(mesh, dz, tokens, memory, lengths, saved, gathered, heads, collective_id):
    bits = bit_table(mesh)
    count = len(bits)
    routes = route_orders(bits)
    rows, width = tokens.shape
    keys = memory.shape[0]
    shards = [w.shape[count:] for w in gathered[1:]]
    wide_block = shards[0]
    tall_rows = shards[9][0]
    hidden = shards[8][1]
    tall_cols = width * wide_block[0] // tall_rows
    tall_block = (tall_rows, tall_cols)
    pack = (VEC_ROWS, VEC_LANES)
    every = slice(None)
    outs_of = [(9, every, slice(c, c + tall_cols)) for c in range(0, width, tall_cols)]
    outs_of += [(8, every, slice(c, c + width)) for c in range(0, hidden, width)]
    outs_of += [(i, every, every) for i in (7, 6, 3, 4, 5, 0, 1, 2, 10)]
    n_units = len(outs_of)
    n_wide = n_units - TALL_UNITS - 1
    low = jnp.bfloat16
    sizes = [2 * wide_block[0] * wide_block[1]] * (n_units - 1) + [4 * pack[0] * pack[1]]
    orders = [routes[u % 2][::-1] for u in range(n_units)]
    sends, finish = plan_sends(bits, orders, sizes, False, 1000e3, MADE_AT)
    plan = [item for item in sends if item[2] > 0]
    plan = sorted(plan + [(when, unit, count) for unit, when in finish.items()])
    blocks = shards + [pack]
    scratch = [
        pltpu.VMEM((rows, width), low),
        pltpu.VMEM((rows, width), low),
        pltpu.VMEM((keys, width), jnp.float32),
        pltpu.VMEM((rows, width), jnp.float32),
        pltpu.VMEM((rows, width), jnp.float32),
    ]
    spots = (2,) * count
    scratch += [pltpu.VMEM(spots + wide_block, low)] * 4
    scratch += [
        pltpu.VMEM((TALL_UNITS,) + spots[1:] + tall_block, low),
        pltpu.VMEM((WIDE_HELD,) + spots[1:] + wide_block, low),
        pltpu.VMEM((TALL_BOXES,) + spots[1:] + tall_block, low),
        pltpu.VMEM((WIDE_BOXES,) + spots[1:] + wide_block, low),
    ]
    for number, block in ((TALL_UNITS, tall_block), (n_wide, wide_block)):
        for stage in range(1, count):
            scratch.append(pltpu.VMEM((number,) + (2,) * (count - 1 - stage) + block, low))
    scratch += [pltpu.VMEM(spots + pack, jnp.float32), pltpu.VMEM(spots[1:] + pack, jnp.float32)]
    for stage in range(count):
        scratch.append(pltpu.VMEM((2,) * (count - 1 - stage) + pack, jnp.float32))
    pair = 2 * (width // heads)
    scratch += [
        pltpu.VMEM((TALL_UNITS,) + tall_block, jnp.float32),
        pltpu.VMEM((SUM_SLOTS,) + wide_block, jnp.float32),
        pltpu.VMEM(pack, jnp.float32),
        pltpu.VMEM((VEC_ROWS, width), jnp.float32),
        pltpu.VMEM((1, hidden), jnp.float32),
        pltpu.VMEM((VEC_ROWS, width), jnp.float32),
        pltpu.VMEM(spots + pack, low),
        pltpu.VMEM((heads // 2, 2, rows), jnp.float32),
        pltpu.VMEM((keys, pair), jnp.float32),
        pltpu.VMEM((keys, pair), jnp.float32),
        pltpu.SemaphoreType.DMA((n_units, count)),
        pltpu.SemaphoreType.DMA((n_units, count)),
        pltpu.SemaphoreType.DMA((n_units,)),
        pltpu.SemaphoreType.DMA((n_units,)),
        pltpu.SemaphoreType.DMA((30,)),
        pltpu.SemaphoreType.DMA((12,)),
        pltpu.SemaphoreType.REGULAR((TALL_BOXES + WIDE_BOXES,)),
    ]
    hbm = pl.BlockSpec(memory_space=pltpu.HBM)
    return pl.pallas_call(
        functools.partial(backward_kernel, bits, orders, plan, outs_of, heads),
        out_shape=[
            jax.ShapeDtypeStruct((rows, width), jnp.float32),
            jax.ShapeDtypeStruct((keys, width), jnp.float32),
        ]
        + [jax.ShapeDtypeStruct(b, jnp.float32) for b in blocks],
        in_specs=[hbm, hbm, hbm, pl.BlockSpec(memory_space=pltpu.SMEM)]
        + [hbm] * (len(BACK_INPUTS) - 4),
        out_specs=[hbm] * (2 + len(blocks)),
        scratch_shapes=scratch,
        compiler_params=pltpu.CompilerParams(
            collective_id=collective_id,
            has_side_effects=True,
            vmem_limit_bytes=62 * 1024 * 1024,
        ),
        name="backward_layer",
    )(dz, tokens, memory, lengths, *saved, *gathered)


MATS_ORDER = (2, 4, 5, 13, 14, 7, 11, 16, 20, 22)
VECS = (0, 1, 3, 6, 8, 9, 10, 12, 15, 17, 18, 19, 23, 21)


def split_units(blocks):
    units = [(0, slice(None), slice(None))]
    for i, (rows, cols) in enumerate(blocks):
        base_rows, base_cols = min(rows, blocks[0][0]), min(cols, blocks[0][1])
        for top in range(0, rows, base_rows):
            for left in range(0, cols, base_cols):
                units.append(
                    (i + 1, slice(top, top + base_rows), slice(left, left + base_cols))
                )
    return units


def collect(*shards):
    return tuple(lax.all_gather(s, BOTH, axis=0, tiled=True) for s in shards)


def spread(*grads):
    return tuple(
        lax.psum_scatter(g.astype(jnp.float32), BOTH, scatter_dimension=0, tiled=True)
        for g in grads
    )


def own_vectors(block, position, shards):
    size = shards[0].shape[0]
    spot = position % (VEC_LANES // size)
    mine = lax.dynamic_slice(block, (0, spot * size), (VEC_ROWS, size))
    owned = [None] * len(shards)
    for row, i in enumerate(VECS[:-1]):
        owned[i] = mine[row]
    owned[VECS[-1]] = block[len(VECS) - 1]
    return owned


def on_device(
    mesh,
    tokens,
    memory,
    page_lengths,
    end_flags,
    out_grad,
    self_gain,
    self_shift,
    self_query,
    self_query_bias,
    self_key,
    self_value,
    self_value_bias,
    self_out,
    self_out_bias,
    cross_gain,
    cross_shift,
    cross_query,
    cross_query_bias,
    cross_key,
    cross_value,
    cross_value_bias,
    cross_out,
    cross_out_bias,
    feed_gain,
    feed_shift,
    feed_in,
    feed_in_bias,
    feed_out,
    feed_out_bias,
):
    page_count, page_len, width = tokens.shape
    mem_len = memory.shape[1]
    row_count = page_count * page_len
    lengths_now = jnp.where(end_flags == 1, 1, page_lengths)
    inputs = tokens.reshape(row_count, width).astype(jnp.float32)
    mem_rows = memory.reshape(page_count * mem_len, width)
    shard_set = (
        self_gain,
        self_shift,
        self_query,
        self_query_bias,
        self_key,
        self_value,
        self_value_bias,
        self_out,
        self_out_bias,
        cross_gain,
        cross_shift,
        cross_query,
        cross_query_bias,
        cross_key,
        cross_value,
        cross_value_bias,
        cross_out,
        cross_out_bias,
        feed_gain,
        feed_shift,
        feed_in,
        feed_in_bias,
        feed_out,
        feed_out_bias,
    )
    if can_route(mesh, self_query.shape[0]):
        mats = [shard_set[i] for i in MATS_ORDER]
        vecs = [shard_set[i] for i in VECS]
        gathered, saved = fused_forward(
            mesh, tokens[0], memory[0], lengths_now, mats, vecs, HEADS, 0
        )
        got = fused_backward(
            mesh, out_grad[0], tokens[0], memory[0], lengths_now, saved[:-1], gathered, HEADS, 1
        )
        position = lax.axis_index("dp") * mesh.shape["fsdp"] + lax.axis_index("fsdp")
        owned = own_vectors(got[-1], position, shard_set)
        for i, value in zip(MATS_ORDER, got[2:-1]):
            owned[i] = value
        return (saved[-1][None], got[0][None], got[1][None]) + tuple(owned)
    full_set = collect(*shard_set)
    (
        gain_one,
        shift_one,
        query_mat,
        query_vec,
        key_mat,
        value_mat,
        value_vec,
        out_mat,
        out_vec,
        gain_two,
        shift_two,
        cquery_mat,
        cquery_vec,
        ckey_mat,
        cvalue_mat,
        cvalue_vec,
        cout_mat,
        cout_vec,
        gain_three,
        shift_three,
        hidden_mat,
        hidden_vec,
        final_mat,
        final_vec,
    ) = full_set
    norm_of = lambda r, g, b: normalize(r, g.astype(jnp.float32), b.astype(jnp.float32))
    first_norm, first_unit, first_std = norm_of(inputs, gain_one, shift_one)
    first_low = first_norm.astype(jnp.bfloat16)
    query_low = (product(first_low, query_mat) + query_vec.astype(jnp.float32)).astype(jnp.bfloat16)
    key_low = product(first_low, key_mat).astype(jnp.bfloat16)
    value_low = (product(first_low, value_mat) + value_vec.astype(jnp.float32)).astype(jnp.bfloat16)
    query_pages = query_low.reshape(page_count, page_len, width)
    key_pages = key_low.reshape(page_count, page_len, width)
    value_pages = value_low.reshape(page_count, page_len, width)
    self_mixed, self_total = attend_fwd(
        query_pages, key_pages, value_pages, lengths_now, HEADS, 512
    )
    self_low = self_mixed.reshape(row_count, width)
    after_self = inputs + product(self_low, out_mat) + out_vec.astype(jnp.float32)
    second_norm, second_unit, second_std = normalize(
        after_self, gain_two.astype(jnp.float32), shift_two.astype(jnp.float32)
    )
    second_low = second_norm.astype(jnp.bfloat16)
    cquery_low = (product(second_low, cquery_mat) + cquery_vec.astype(jnp.float32)).astype(
        jnp.bfloat16
    )
    ckey_low = product(mem_rows, ckey_mat).astype(jnp.bfloat16)
    cvalue_low = (product(mem_rows, cvalue_mat) + cvalue_vec.astype(jnp.float32)).astype(
        jnp.bfloat16
    )
    cquery_pages = cquery_low.reshape(page_count, page_len, width)
    ckey_pages = ckey_low.reshape(page_count, mem_len, width)
    cvalue_pages = cvalue_low.reshape(page_count, mem_len, width)
    cross_mixed, cross_total = attend_fwd(
        cquery_pages, ckey_pages, cvalue_pages, None, HEADS, 512
    )
    cross_low = cross_mixed.reshape(row_count, width)
    after_cross = after_self + product(cross_low, cout_mat) + cout_vec.astype(jnp.float32)
    third_norm, third_unit, third_std = normalize(
        after_cross, gain_three.astype(jnp.float32), shift_three.astype(jnp.float32)
    )
    third_low = third_norm.astype(jnp.bfloat16)
    hidden_pre = product(third_low, hidden_mat) + hidden_vec.astype(jnp.float32)
    hidden_low, hidden_rate = gelu_parts(hidden_pre)
    hidden_low = hidden_low.astype(jnp.bfloat16)
    hidden_rate = hidden_rate.astype(jnp.bfloat16)
    result = after_cross + product(hidden_low, final_mat) + final_vec.astype(jnp.float32)
    layer_out = result.astype(jnp.bfloat16).reshape(page_count, page_len, width)
    second_norm, second_unit, second_std = norm_of(after_self, gain_two, shift_two)
    second_low = second_norm.astype(jnp.bfloat16)
    third_norm, third_unit, third_std = norm_of(after_cross, gain_three, shift_three)
    third_low = third_norm.astype(jnp.bfloat16)
    grad_rows = out_grad.reshape(row_count, width).astype(jnp.float32)
    final_grad = out_grad.reshape(row_count, width)
    grad_final_mat = product_tn(hidden_low, final_grad).astype(jnp.bfloat16)
    grad_final_vec = jnp.sum(final_grad.astype(jnp.float32), axis=0)
    hidden_grad = (product_nt(final_grad, final_mat) * hidden_rate.astype(jnp.float32)).astype(jnp.bfloat16)
    grad_hidden_mat = product_tn(third_low, hidden_grad).astype(jnp.bfloat16)
    grad_hidden_vec = jnp.sum(hidden_grad.astype(jnp.float32), axis=0)
    third_back, grad_gain_three, grad_shift_three = normalize_back(
        product_nt(hidden_grad, hidden_mat), third_unit, third_std, gain_three.astype(jnp.float32)
    )
    cross_grad_total = grad_rows + third_back
    cout_grad = cross_grad_total.astype(jnp.bfloat16)
    grad_cout_mat = product_tn(cross_low, cout_grad).astype(jnp.bfloat16)
    grad_cout_vec = jnp.sum(cout_grad.astype(jnp.float32), axis=0)
    cmix_grad = (
        product_nt(cout_grad, cout_mat).astype(jnp.bfloat16).reshape(page_count, page_len, width)
    )
    cquery_grad, ckey_grad, cvalue_grad = attend_bwd(
        cquery_pages, ckey_pages, cvalue_pages, cmix_grad, cross_total, None, HEADS, 512
    )
    cquery_grad = cquery_grad.reshape(row_count, width)
    ckey_grad = ckey_grad.reshape(page_count * mem_len, width)
    cvalue_grad = cvalue_grad.reshape(page_count * mem_len, width)
    grad_cquery_mat = product_tn(second_low, cquery_grad).astype(jnp.bfloat16)
    grad_cquery_vec = jnp.sum(cquery_grad.astype(jnp.float32), axis=0)
    grad_ckey_mat = product_tn(mem_rows, ckey_grad).astype(jnp.bfloat16)
    grad_cvalue_mat = product_tn(mem_rows, cvalue_grad).astype(jnp.bfloat16)
    grad_cvalue_vec = jnp.sum(cvalue_grad.astype(jnp.float32), axis=0)
    memory_grad = (product_nt(ckey_grad, ckey_mat) + product_nt(cvalue_grad, cvalue_mat)).reshape(
        page_count, mem_len, width
    )
    second_back, grad_gain_two, grad_shift_two = normalize_back(
        product_nt(cquery_grad, cquery_mat), second_unit, second_std, gain_two.astype(jnp.float32)
    )
    self_grad_total = cross_grad_total + second_back
    sout_grad = self_grad_total.astype(jnp.bfloat16)
    grad_out_mat = product_tn(self_low, sout_grad).astype(jnp.bfloat16)
    grad_out_vec = jnp.sum(sout_grad.astype(jnp.float32), axis=0)
    smix_grad = (
        product_nt(sout_grad, out_mat).astype(jnp.bfloat16).reshape(page_count, page_len, width)
    )
    query_grad, key_grad, value_grad = attend_bwd(
        query_pages, key_pages, value_pages, smix_grad, self_total, lengths_now, HEADS, 256
    )
    query_grad = query_grad.reshape(row_count, width)
    key_grad = key_grad.reshape(row_count, width)
    value_grad = value_grad.reshape(row_count, width)
    grad_query_mat = product_tn(first_low, query_grad).astype(jnp.bfloat16)
    grad_query_vec = jnp.sum(query_grad.astype(jnp.float32), axis=0)
    grad_key_mat = product_tn(first_low, key_grad).astype(jnp.bfloat16)
    grad_value_mat = product_tn(first_low, value_grad).astype(jnp.bfloat16)
    grad_value_vec = jnp.sum(value_grad.astype(jnp.float32), axis=0)
    first_in = (
        product_nt(query_grad, query_mat)
        + product_nt(key_grad, key_mat)
        + product_nt(value_grad, value_mat)
    )
    first_back, grad_gain_one, grad_shift_one = normalize_back(
        first_in, first_unit, first_std, gain_one.astype(jnp.float32)
    )
    tokens_grad = (self_grad_total + first_back).reshape(page_count, page_len, width)
    owned = spread(
        grad_gain_one[0],
        grad_shift_one[0],
        grad_query_mat,
        grad_query_vec,
        grad_key_mat,
        grad_value_mat,
        grad_value_vec,
        grad_out_mat,
        grad_out_vec,
        grad_gain_two[0],
        grad_shift_two[0],
        grad_cquery_mat,
        grad_cquery_vec,
        grad_ckey_mat,
        grad_cvalue_mat,
        grad_cvalue_vec,
        grad_cout_mat,
        grad_cout_vec,
        grad_gain_three[0],
        grad_shift_three[0],
        grad_hidden_mat,
        grad_hidden_vec,
        grad_final_mat,
        grad_final_vec,
    )
    return (layer_out, tokens_grad, memory_grad) + tuple(owned)


def solution(mesh):
    placed = (
        P(("dp", "fsdp"), None, None),
        P(("dp", "fsdp"), None, None),
        P(("dp", "fsdp")),
        P(("dp", "fsdp")),
        P(("dp", "fsdp"), None, None),
        P(("dp", "fsdp")),
        P(("dp", "fsdp")),
        P(("dp", "fsdp"), None),
        P(("dp", "fsdp")),
        P(("dp", "fsdp"), None),
        P(("dp", "fsdp"), None),
        P(("dp", "fsdp")),
        P(("dp", "fsdp"), None),
        P(("dp", "fsdp")),
        P(("dp", "fsdp")),
        P(("dp", "fsdp")),
        P(("dp", "fsdp"), None),
        P(("dp", "fsdp")),
        P(("dp", "fsdp"), None),
        P(("dp", "fsdp"), None),
        P(("dp", "fsdp")),
        P(("dp", "fsdp"), None),
        P(("dp", "fsdp")),
        P(("dp", "fsdp")),
        P(("dp", "fsdp")),
        P(("dp", "fsdp"), None),
        P(("dp", "fsdp")),
        P(("dp", "fsdp"), None),
        P(("dp", "fsdp")),
    )
    return jax.shard_map(
        functools.partial(on_device, mesh),
        mesh=mesh,
        in_specs=placed,
        out_specs=(
            P(("dp", "fsdp"), None, None),
            P(("dp", "fsdp"), None, None),
            P(("dp", "fsdp"), None, None),
            P(("dp", "fsdp")),
            P(("dp", "fsdp")),
            P(("dp", "fsdp"), None),
            P(("dp", "fsdp")),
            P(("dp", "fsdp"), None),
            P(("dp", "fsdp"), None),
            P(("dp", "fsdp")),
            P(("dp", "fsdp"), None),
            P(("dp", "fsdp")),
            P(("dp", "fsdp")),
            P(("dp", "fsdp")),
            P(("dp", "fsdp"), None),
            P(("dp", "fsdp")),
            P(("dp", "fsdp"), None),
            P(("dp", "fsdp"), None),
            P(("dp", "fsdp")),
            P(("dp", "fsdp"), None),
            P(("dp", "fsdp")),
            P(("dp", "fsdp")),
            P(("dp", "fsdp")),
            P(("dp", "fsdp"), None),
            P(("dp", "fsdp")),
            P(("dp", "fsdp"), None),
            P(("dp", "fsdp")),
        ),
        check_vma=False,
    )
```

```python
import functools

import jax
import jax.numpy as jnp
from jax import lax
from jax.experimental import pallas as pl
from jax.experimental.pallas import tpu as pltpu
from jax.sharding import PartitionSpec as P

HEADS = 16


EPSILON = 1e-05
ROOT_HALF = 0.7071067811865476
INV_ROOT_TWO_PI = 0.3989422804014327


def product(left, right):
    return jnp.dot(left, right, preferred_element_type=jnp.float32)


def product_tn(left, right):
    return lax.dot_general(
        left, right, (((0,), (0,)), ((), ())), preferred_element_type=jnp.float32
    )


def product_nt(left, right):
    return lax.dot_general(
        left, right, (((1,), (1,)), ((), ())), preferred_element_type=jnp.float32
    )


def normalize(rows_in, norm_gain, norm_shift):
    centered = rows_in - jnp.mean(rows_in, axis=-1, keepdims=True)
    inv_std = lax.rsqrt(jnp.mean(centered * centered, axis=-1, keepdims=True) + EPSILON)
    unit_rows = centered * inv_std
    return (unit_rows * norm_gain + norm_shift, unit_rows, inv_std)


def normalize_back(grad_norm, unit_rows, inv_std, norm_gain):
    scaled = grad_norm * norm_gain
    inner_part = (
        scaled
        - jnp.mean(scaled, axis=-1, keepdims=True)
        - unit_rows * jnp.mean(scaled * unit_rows, axis=-1, keepdims=True)
    )
    return (
        inner_part * inv_std,
        jnp.sum(grad_norm * unit_rows, axis=0, keepdims=True),
        jnp.sum(grad_norm, axis=0, keepdims=True),
    )


LOG2E = 1.4426950408889634
LN2 = 0.6931471805599453


def dot_nn(a, b):
    return jnp.dot(a, b, preferred_element_type=jnp.float32)


def dot_nt(a, b):
    return lax.dot_general(a, b, (((1,), (1,)), ((), ())), preferred_element_type=jnp.float32)


def dot_tn(a, b):
    return lax.dot_general(a, b, (((0,), (0,)), ((), ())), preferred_element_type=jnp.float32)


def lane_half(x, head, half):
    lane = lax.broadcasted_iota(jnp.int32, (1, x.shape[1]), 1)
    keep = (lane < half) if head == 0 else (lane >= half)
    return jnp.where(keep, x, jnp.zeros_like(x))


def causal_spans(rows, chunk):
    return [(start, chunk, start + chunk) for start in range(0, rows, chunk)]


def limit_row(start, width, length):
    pos = start + lax.broadcasted_iota(jnp.int32, (1, width), 1)
    return jnp.minimum(pos, length - 1)


def forward_pair(load_q, load_k, load_v, write, spans, length, scale):
    for start, size, keys in spans:
        q2 = load_q(start, size)
        k2 = load_k(0, keys)
        v2 = load_v(0, keys)
        half = q2.shape[1] // 2
        vt = v2.T
        outs, totals = [], []
        for head in (0, 1):
            raw = dot_nt(k2, lane_half(q2, head, half))
            if length is not None:
                key_pos = lax.broadcasted_iota(jnp.int32, raw.shape, 0)
                raw = jnp.where(key_pos <= limit_row(start, size, length), raw, -1e30)
            top = jnp.max(raw, axis=0, keepdims=True)
            expo = jnp.exp2((raw - top) * (scale * LOG2E))
            total = jnp.sum(expo, axis=0, keepdims=True)
            mixed = dot_nn(vt[head * half : (head + 1) * half], expo.astype(jnp.bfloat16))
            outs.append(mixed / total)
            totals.append(top * (scale * LOG2E) + jnp.log2(total))
        write(start, size, jnp.concatenate(outs, axis=0).T.astype(jnp.bfloat16), totals)


def fwd_kernel(masked, scale, chunk, *refs):
    if masked:
        len_ref, q_ref, k_ref, v_ref, a_ref, t_ref = refs
        length = len_ref[pl.program_id(0)]
    else:
        q_ref, k_ref, v_ref, a_ref, t_ref = refs
        length = None
    rows, keys = q_ref.shape[1], k_ref.shape[1]
    if masked:
        spans = causal_spans(rows, chunk)
    else:
        spans = [(s, chunk, keys) for s in range(0, rows, chunk)]

    def write(start, size, out, totals):
        a_ref[0, pl.ds(start, size), :] = out
        for head in (0, 1):
            t_ref[0, 0, pl.ds(head, 1), pl.ds(start, size)] = totals[head]

    forward_pair(
        lambda s, n: q_ref[0, pl.ds(s, n), :],
        lambda s, n: k_ref[0, pl.ds(s, n), :],
        lambda s, n: v_ref[0, pl.ds(s, n), :],
        write, spans, length, scale,
    )


def attend_fwd(q, k, v, lengths, heads, chunk=256):
    pages, rows, width = q.shape
    keys = k.shape[1]
    head = width // heads
    pairs = heads // 2
    masked = lengths is not None
    row_spec = pl.BlockSpec((1, rows, 2 * head), lambda p, h: (p, 0, h))
    key_spec = pl.BlockSpec((1, keys, 2 * head), lambda p, h: (p, 0, h))
    in_specs = [row_spec, key_spec, key_spec]
    args = [q, k, v]
    if masked:
        in_specs = [pl.BlockSpec(memory_space=pltpu.SMEM)] + in_specs
        args = [lengths] + args
    return pl.pallas_call(
        functools.partial(fwd_kernel, masked, head**-0.5, chunk),
        grid=(pages, pairs),
        in_specs=in_specs,
        out_specs=[row_spec, pl.BlockSpec((1, 1, 2, rows), lambda p, h: (p, h, 0, 0))],
        out_shape=[
            jax.ShapeDtypeStruct(q.shape, jnp.bfloat16),
            jax.ShapeDtypeStruct((pages, pairs, 2, rows), jnp.float32),
        ],
        compiler_params=pltpu.CompilerParams(vmem_limit_bytes=48 * 1024 * 1024),
        name="attend_forward",
    )(*args)


def bwd_kernel(masked, scale, chunk, *refs):
    if masked:
        len_ref, q_ref, k_ref, v_ref, g_ref, t_ref, dq_ref, dk_ref, dv_ref, dk_acc, dv_acc = refs
        length = len_ref[pl.program_id(0)]
    else:
        q_ref, k_ref, v_ref, g_ref, t_ref, dq_ref, dk_ref, dv_ref, dk_acc, dv_acc = refs
        length = None
    rows, keys_all = q_ref.shape[1], k_ref.shape[1]
    if masked:
        spans = causal_spans(rows, chunk)[::-1]
    else:
        spans = [(s, chunk, keys_all) for s in range(0, rows, chunk)]
    half = q_ref.shape[2] // 2
    for step, (start, size, keys) in enumerate(spans):
        q2 = q_ref[0, pl.ds(start, size), :]
        g2 = g_ref[0, pl.ds(start, size), :]
        k2 = k_ref[0, pl.ds(0, keys), :]
        v2 = v_ref[0, pl.ds(0, keys), :]
        kt = k2.T
        dk, dv, dqt = None, None, []
        for head in (0, 1):
            qm = lane_half(q2, head, half)
            gm = lane_half(g2, head, half)
            raw = dot_nt(k2, qm)
            total = t_ref[0, 0, pl.ds(head, 1), pl.ds(start, size)]
            probs = jnp.exp2(raw * (scale * LOG2E) - total)
            if length is not None:
                key_pos = lax.broadcasted_iota(jnp.int32, raw.shape, 0)
                probs = jnp.where(key_pos <= limit_row(start, size, length), probs, 0.0)
            grad = dot_nt(v2, gm)
            part = probs * grad
            dot_row = jnp.sum(part, axis=0, keepdims=True)
            score = ((part - probs * dot_row) * scale).astype(jnp.bfloat16)
            dvh = dot_nn(probs.astype(jnp.bfloat16), gm)
            dkh = dot_nn(score, qm)
            dv = dvh if dv is None else dv + dvh
            dk = dkh if dk is None else dk + dkh
            dqt.append(dot_nn(kt[head * half : (head + 1) * half], score))
        dq_ref[0, pl.ds(start, size), :] = jnp.concatenate(dqt, axis=0).T.astype(jnp.bfloat16)
        if step == 0:
            dk_acc[pl.ds(0, keys), :] = dk
            dv_acc[pl.ds(0, keys), :] = dv
        else:
            dk_acc[pl.ds(0, keys), :] += dk
            dv_acc[pl.ds(0, keys), :] += dv
    dk_ref[0] = dk_acc[...].astype(jnp.bfloat16)
    dv_ref[0] = dv_acc[...].astype(jnp.bfloat16)


def attend_bwd(q, k, v, g, totals, lengths, heads, chunk=256):
    pages, rows, width = q.shape
    keys = k.shape[1]
    head = width // heads
    pairs = heads // 2
    masked = lengths is not None
    row_spec = pl.BlockSpec((1, rows, 2 * head), lambda p, h: (p, 0, h))
    key_spec = pl.BlockSpec((1, keys, 2 * head), lambda p, h: (p, 0, h))
    total_spec = pl.BlockSpec((1, 1, 2, rows), lambda p, h: (p, h, 0, 0))
    in_specs = [row_spec, key_spec, key_spec, row_spec, total_spec]
    args = [q, k, v, g, totals]
    if masked:
        in_specs = [pl.BlockSpec(memory_space=pltpu.SMEM)] + in_specs
        args = [lengths] + args
    return pl.pallas_call(
        functools.partial(bwd_kernel, masked, head**-0.5, chunk),
        grid=(pages, pairs),
        in_specs=in_specs,
        out_specs=[row_spec, key_spec, key_spec],
        out_shape=[jax.ShapeDtypeStruct(a.shape, jnp.bfloat16) for a in (q, k, v)],
        scratch_shapes=[pltpu.VMEM((keys, 2 * head), jnp.float32)] * 2,
        compiler_params=pltpu.CompilerParams(vmem_limit_bytes=48 * 1024 * 1024),
        name="attend_backward",
    )(*args)


MESH_ID = pl.DeviceIdType.MESH
BOTH = ("dp", "fsdp")
CORE_RATE = 500e3
LINK_RATE = 92e3
HOP = 2.2
LAG = 8.0


def bit_table(mesh):
    bits = []
    for axis, name in enumerate(BOTH):
        step = mesh.shape[name] // 2
        while step >= 1:
            bits.append((axis, step))
            step //= 2
    return bits


def can_route(mesh, rows):
    sizes = [mesh.shape[name] for name in BOTH]
    return all(s & (s - 1) == 0 for s in sizes) and rows % 32 == 0


def route_orders(bits):
    outer = [i for i, (axis, _) in enumerate(bits) if axis == 0]
    inner = [i for i, (axis, _) in enumerate(bits) if axis == 1]
    middle, core = inner[:-1], inner[-1:]
    return (
        outer + middle + core,
        outer + middle[::-1] + core,
        middle[:1] + outer + middle[1:] + core,
        middle[-1:] + outer + middle[:-1] + core,
    )


def loads_of(bits, at, size):
    axis, step = bits[at]
    if axis == 1 and step == 1:
        return {"core": size / CORE_RATE}
    if axis == 1:
        return {f"inner{step}": 2 * size / LINK_RATE}
    loads = {"outer1": 2 * size / LINK_RATE}
    if step > 1:
        loads["outer2"] = 2 * size * step / LINK_RATE
    return loads


def plan_sends(bits, orders, sizes, growing, add_rate, begin=None):
    count = len(bits)
    ready = [(begin[unit] if begin else 0.0, unit, 0) for unit in range(len(orders))]
    free = {}
    plan = []
    arrive = {}
    while ready:
        choices = []
        for when, unit, stage in ready:
            scale = 2**stage if growing else 2 ** (count - 1 - stage)
            loads = loads_of(bits, orders[unit][stage], sizes[unit] * scale)
            start = max([when] + [free.get(link, 0.0) for link in loads])
            choices.append((round(start, 3), unit, -stage, when, scale))
        start, unit, stage, when, scale = min(choices)
        stage = -stage
        ready.remove((when, unit, stage))
        loads = loads_of(bits, orders[unit][stage], sizes[unit] * scale)
        for link, took in loads.items():
            free[link] = start + took
        plan.append((start, unit, stage))
        after = start + max(loads.values()) + HOP
        if add_rate:
            after += sizes[unit] * scale / add_rate
        if stage + 1 < count:
            ready.append((after, unit, stage + 1))
        else:
            arrive[unit] = after
    return sorted(plan), arrive


def my_bits(bits):
    place = (lax.axis_index("dp"), lax.axis_index("fsdp"))
    return [(place[axis] // step) % 2 for axis, step in bits]


def partner(bits, mine, at):
    place = [lax.axis_index("dp"), lax.axis_index("fsdp")]
    axis, step = bits[at]
    place[axis] = place[axis] + step * (1 - 2 * mine[at])
    return tuple(place)


def greet(bits, mine):
    barrier = pltpu.get_barrier_semaphore()
    for at in range(len(bits)):
        pl.semaphore_signal(
            barrier, inc=1, device_id=partner(bits, mine, at), device_id_type=MESH_ID
        )
    pl.semaphore_wait(barrier, len(bits))


def unit_shape(blocks, unit):
    array, rows, cols = unit
    block = blocks[array]
    return (len(range(*rows.indices(block[0]))), len(range(*cols.indices(block[1]))))


ERF_RATE = 0.3275911
ERF_TERMS = (0.254829592, -0.284496736, 1.421413741, -1.453152027, 1.061405429)


def gelu_parts(pre):
    bell = jnp.exp2(pre * pre * (-0.5 * LOG2E))
    arm = 1.0 / (1.0 + jnp.abs(pre) * (ERF_RATE * ROOT_HALF))
    series = ERF_TERMS[4]
    for term in ERF_TERMS[3::-1]:
        series = series * arm + term
    tail = 0.5 * series * arm * bell
    below = jnp.where(pre >= 0.0, 1.0 - tail, tail)
    return pre * below, below + pre * bell * INV_ROOT_TWO_PI


class Schedule:
    def __init__(self, plan, issue):
        self.plan = plan
        self.issue = issue
        self.at = 0
        self.now = 0.0

    def due(self):
        items = []
        while self.at < len(self.plan) and self.plan[self.at][0] <= self.now:
            items.append(self.plan[self.at][1:])
            self.at += 1
        return items

    def spend(self, took):
        self.now += took
        for unit, stage in self.due():
            self.issue(unit, stage)

    def until(self, when):
        self.now = max(self.now, when)
        for unit, stage in self.due():
            self.issue(unit, stage)

    def loop(self, count, took, body):
        buckets = []
        for _ in range(count):
            self.now += took
            buckets.append(self.due())

        def step(i, carry):
            body(i)
            for k, items in enumerate(buckets):
                if items:

                    @pl.when(i == k)
                    def _(items=items):
                        for unit, stage in items:
                            self.issue(unit, stage)

            return carry

        lax.fori_loop(0, count, step, 0)


ROWS_STEP = 128


N_VECS = 14
VEC_ROWS = 16
VEC_LANES = 128


def device_index(bits, mine):
    count = len(bits)
    return sum(mine[b] * 2 ** (count - 1 - b) for b in range(count))


def pack_vectors(loose, pack, spot, size):
    row = lax.broadcasted_iota(jnp.int32, (size, VEC_LANES), 0)
    lane = lax.broadcasted_iota(jnp.int32, (size, VEC_LANES), 1)
    place = (lane == row + size * spot).astype(jnp.float32)
    pieces = []
    for ref in loose[:-1]:
        pieces.append(dot_nn(ref[...].astype(jnp.float32).reshape(1, size), place))
    pieces.append(loose[-1][...].astype(jnp.float32).reshape(1, VEC_LANES))
    pieces.append(jnp.zeros((VEC_ROWS - len(pieces), VEC_LANES), jnp.float32))
    pack[...] = jnp.concatenate(pieces, axis=0).astype(pack.dtype)


def unpack_table(vecs, table, bits, width, hidden_row=None):
    count = len(bits)
    devices = 2**count
    share = devices * VEC_LANES // width
    spots = [tuple((d >> (count - 1 - b)) & 1 for b in range(count)) for d in range(devices)]
    for group in range(width // VEC_LANES):
        total = None
        for d in range(group * share, (group + 1) * share):
            block = vecs[spots[d]].astype(jnp.float32)
            total = block if total is None else total + block
        table[:, pl.ds(group * VEC_LANES, VEC_LANES)] = total
    if hidden_row is not None:
        for d in range(devices):
            block = vecs[spots[d]].astype(jnp.float32)
            hidden_row[pl.ds(0, 1), pl.ds(d * VEC_LANES, VEC_LANES)] = block[N_VECS - 1 : N_VECS]


def forward_kernel(bits, units, orders, plan, arrive, n_arrays, heads, *refs):
    count = len(bits)
    (tokens, memory, lengths), refs = refs[:3], refs[3:]
    loose, refs = refs[:N_VECS], refs[N_VECS:]
    sources, refs = refs[: n_arrays - 1], refs[n_arrays - 1 :]
    targets, refs = refs[:n_arrays], refs[n_arrays:]
    saved_names = ("q", "k", "v", "a", "total", "h1")
    saved_names += ("cq", "ck", "cv", "ca", "ctotal", "h2", "g", "slope")
    saved_names += ("n1", "n2", "n3", "out")
    saved = dict(zip(saved_names, refs[: len(saved_names)]))
    refs = refs[len(saved_names) :]
    x, mem, n, q, k, v, a, h, ck, cv, g, slope, tot, ctot = refs[:14]
    wide, tall = refs[14:16], refs[16:18]
    pack, vecs, table, hidden_row = refs[18:-6]
    last_wide = 8 + g.shape[1] // x.shape[1]
    last_weight = len(units) // 2
    send_sem, recv_sem, own_sem, in_sem, w_sem, out_sem = refs[-6:]
    mine = my_bits(bits)
    rows, width = x.shape
    devices = 2**count
    lanes_each = width // devices
    pack_vectors(loose, pack, device_index(bits, mine) % (VEC_LANES // lanes_each), lanes_each)
    sources = (pack,) + tuple(sources)
    own = [
        pltpu.make_async_copy(sources[i], targets[i].at[tuple(mine)], own_sem.at[i])
        for i in range(n_arrays)
    ]
    for copy in own:
        copy.start()
    load_x = pltpu.make_async_copy(tokens, x, in_sem.at[0])
    load_mem = pltpu.make_async_copy(memory, mem, in_sem.at[1])
    load_x.start()
    load_mem.start()
    greet(bits, mine)

    def message(unit, stage):
        array, top, left = units[unit]
        order = orders[unit]
        where = tuple(slice(None) if b in order[:stage] else mine[b] for b in range(count))
        place = targets[array].at[where + (top, left)]
        source = sources[array].at[top, left] if stage == 0 else place
        return pltpu.make_async_remote_copy(
            src_ref=source,
            dst_ref=place,
            send_sem=send_sem.at[unit, stage],
            recv_sem=recv_sem.at[unit, stage],
            device_id=partner(bits, mine, order[stage]),
            device_id_type=MESH_ID,
        )

    settled = set()

    def issue(unit, stage):
        array = units[unit][0]
        if stage > 0:
            if array not in settled:
                settled.add(array)
                own[array].wait()
            message(unit, stage - 1).wait_recv()
        message(unit, stage).start()

    clock = Schedule(plan, issue)
    every = (slice(None),) * count

    fetching = {}

    def parts_of(weight):
        return (0,) if weight == 0 else (2 * weight - 1, 2 * weight)

    def begin(weight):
        for unit in parts_of(weight):
            clock.until(arrive[unit] + LAG)
            message(unit, count - 1).wait_recv()
        array, _, left = units[parts_of(weight)[0]]
        if array not in settled:
            settled.add(array)
            own[array].wait()
        fetching[weight] = pltpu.make_async_copy(
            targets[array].at[every + (slice(None), left)], slot_of(weight), w_sem.at[weight]
        )
        fetching[weight].start()

    def slot_of(weight):
        if weight == 0:
            return vecs
        kind = wide if weight <= last_wide else tall
        return kind[weight % 2]

    def fetch(weight):
        if weight not in fetching:
            begin(weight)
        later = weight + 1
        if 0 < weight < last_weight and arrive[parts_of(later)[-1]] <= clock.now:
            begin(later)
        fetching[weight].wait()
        if weight > 0:
            clock.spend(0.6)
        return slot_of(weight)

    def times(lhs, slot, tile, write, took=1.4):
        depth = lhs.shape[1]
        tiles = slot.shape[-1] // tile

        def body(j):
            cols = pl.ds(pl.multiple_of(j * tile, tile), tile)
            weight = slot[every + (slice(None), cols)].reshape(depth, tile)
            write(cols, dot_nn(lhs[...], weight))

        clock.loop(tiles, took / tiles, body)

    def norm_into(gain, shift, source):
        def body(i):
            part = pl.ds(pl.multiple_of(i * ROWS_STEP, ROWS_STEP), ROWS_STEP)
            r = source[part, :].astype(jnp.float32)
            n[part, :] = normalize(r, gain, shift)[0].astype(jnp.bfloat16)

        clock.loop(rows // ROWS_STEP, 0.4, body)

    pending = {}

    def save(source, name):
        copy = pltpu.make_async_copy(source, saved[name], out_sem.at[saved_names.index(name)])
        copy.start()
        pending[name] = copy

    def saved_now(name):
        pending.pop(name).wait()

    def vec(i):
        return table[pl.ds(i, 1), :]

    clock.until(0.0)
    fetch(0)
    unpack_table(vecs, table, bits, width, hidden_row)
    load_x.wait()
    load_mem.wait()
    norm_into(vec(0), vec(1), x)
    save(n, "n1")
    length = lengths[0]

    def project(bias, target, extra=0):
        def write(cols, acc):
            if bias is not None:
                acc = acc + table[pl.ds(bias, 1), cols]
            target[:, cols] = acc.astype(target.dtype)

        return write

    def residual(bias, source):
        def write(cols, acc):
            h[:, cols] = source[:, cols].astype(jnp.float32) + acc + table[pl.ds(bias, 1), cols]

        return write

    def attend(q_ref, k_ref, v_ref, tot_ref, masked):
        keys = k_ref.shape[0]
        pair = 2 * (width // heads)

        def body(p):
            lanes = pl.ds(pl.multiple_of(p * pair, pair), pair)

            def write(start, size, out, totals):
                a[pl.ds(start, size), lanes] = out
                for head in (0, 1):
                    tot_ref[p, pl.ds(head, 1), pl.ds(start, size)] = totals[head]

            forward_pair(
                lambda s, m: q_ref[pl.ds(s, m), lanes],
                lambda s, m: k_ref[pl.ds(s, m), lanes],
                lambda s, m: v_ref[pl.ds(s, m), lanes],
                write,
                [(0, rows, keys)],
                length if masked else None,
                (width // heads) ** -0.5,
            )

        clock.loop(heads // 2, 1.4, body)

    for weight, target, bias in ((1, q, 2), (2, k, None), (3, v, 3)):
        times(n, fetch(weight), 512, project(bias, target))
    save(q, "q")
    save(k, "k")
    save(v, "v")
    attend(q, k, v, tot, True)
    save(a, "a")
    save(tot, "total")
    for weight, target, bias in ((4, ck, None), (5, cv, 8)):
        times(mem, fetch(weight), 512, project(bias, target), 1.9)
    save(ck, "ck")
    save(cv, "cv")
    times(a, fetch(6), 512, residual(4, x), 2.0)
    save(h, "h1")
    saved_now("n1")
    norm_into(vec(5), vec(6), h)
    save(n, "n2")
    saved_now("q")
    times(n, fetch(7), 512, project(7, q))
    save(q, "cq")
    saved_now("a")
    attend(q, ck, cv, ctot, False)
    save(a, "ca")
    save(ctot, "ctotal")
    saved_now("h1")
    times(a, fetch(8), 512, residual(9, h), 2.0)
    save(h, "h2")
    saved_now("n2")
    norm_into(vec(10), vec(11), h)
    save(n, "n3")
    block = width
    blocks = g.shape[1] // block
    for j in range(blocks):
        slot = fetch(9 + j)
        tile = 256

        def body(i, j=j, slot=slot):
            cols = pl.ds(pl.multiple_of(i * tile, tile), tile)
            spot = pl.ds(pl.multiple_of(j * block + i * tile, tile), tile)
            weight = slot[every + (slice(None), cols)].reshape(width, tile)
            for r in range(0, rows, ROWS_STEP):
                part = pl.ds(r, ROWS_STEP)
                pre = dot_nn(n[part, :], weight) + hidden_row[:, spot]
                low, rate = gelu_parts(pre)
                g[part, spot] = low.astype(jnp.bfloat16)
                slope[part, spot] = rate.astype(jnp.bfloat16)

        clock.loop(block // tile, 0.6, body)
    save(g, "g")
    save(slope, "slope")
    tall_cols = tall[0].shape[-1]
    for j in range(width // tall_cols):
        slot = fetch(9 + blocks + j)
        cols = pl.ds(j * tall_cols, tall_cols)
        weight = slot[...].reshape(g.shape[1], tall_cols)
        acc = dot_nn(g[...], weight)
        x[:, cols] = (h[:, cols] + acc + table[pl.ds(12, 1), cols]).astype(jnp.bfloat16)
        clock.spend(1.6)
    save(x, "out")
    clock.until(1e9)
    for copy in pending.values():
        copy.wait()
    for unit in range(len(units)):
        for stage in range(count):
            message(unit, stage).wait_send()


def fused_forward(mesh, tokens, memory, lengths, mats, vecs, heads, collective_id):
    bits = bit_table(mesh)
    routes = route_orders(bits)
    rows, width = tokens.shape
    keys = memory.shape[0]
    block = mats[0].shape
    pack = (VEC_ROWS, VEC_LANES)
    every = slice(None)
    whole = [(i, every) for i in range(1, 9)]
    hidden = mats[8].shape[1]
    for left in range(0, hidden, width):
        whole.append((9, slice(left, left + width)))
    tall_rows = mats[9].shape[0]
    tall_cols = width * block[0] // tall_rows
    for left in range(0, width, tall_cols):
        whole.append((10, slice(left, left + tall_cols)))
    units = [(0, every, every)]
    for array, cols in whole:
        half = mats[array - 1].shape[0] // 2
        units += [(array, slice(0, half), cols), (array, slice(half, 2 * half), cols)]
    blocks = [pack] + [m.shape for m in mats]
    shapes = [unit_shape(blocks, unit) for unit in units]
    sizes = [2 * s[0] * s[1] for s in shapes]
    orders = [routes[(u - 1) % 4] for u in range(len(units))]
    plan, arrive = plan_sends(bits, orders, sizes, True, None)
    n = len(blocks)
    spots = (2,) * len(bits)
    low = jnp.bfloat16
    wide_rows = jax.ShapeDtypeStruct((rows, width), low)
    wide_keys = jax.ShapeDtypeStruct((keys, width), low)
    full = jax.ShapeDtypeStruct((rows, width), jnp.float32)
    totals = jax.ShapeDtypeStruct((heads // 2, 2, rows), jnp.float32)
    ff = jax.ShapeDtypeStruct((rows, hidden), low)
    saved = [
        wide_rows, wide_rows, wide_rows, wide_rows, totals, full,
        wide_rows, wide_keys, wide_keys, wide_rows, totals, full, ff, ff,
        wide_rows, wide_rows, wide_rows, wide_rows,
    ]
    vm = lambda s: pltpu.VMEM(s.shape, s.dtype)
    sems = (len(units), len(bits))
    hbm = pl.BlockSpec(memory_space=pltpu.HBM)
    got = pl.pallas_call(
        functools.partial(forward_kernel, bits, units, orders, plan, arrive, n, heads),
        out_shape=[jax.ShapeDtypeStruct(spots + b, low) for b in blocks] + saved,
        in_specs=[hbm, hbm, pl.BlockSpec(memory_space=pltpu.SMEM)]
        + [pl.BlockSpec(memory_space=pltpu.VMEM)] * (len(vecs) + len(mats)),
        out_specs=[hbm] * (n + len(saved)),
        scratch_shapes=[
            vm(wide_rows), vm(wide_keys), vm(wide_rows), vm(wide_rows), vm(wide_rows),
            vm(wide_rows), vm(wide_rows), vm(full), vm(wide_keys), vm(wide_keys),
            vm(ff), vm(ff), vm(totals), vm(totals),
            pltpu.VMEM(spots + block, low),
            pltpu.VMEM(spots + block, low),
            pltpu.VMEM(spots + (tall_rows, tall_cols), low),
            pltpu.VMEM(spots + (tall_rows, tall_cols), low),
            pltpu.VMEM(pack, low),
            pltpu.VMEM(spots + pack, low),
            pltpu.VMEM((VEC_ROWS, width), jnp.float32),
            pltpu.VMEM((1, hidden), jnp.float32),
            pltpu.SemaphoreType.DMA(sems),
            pltpu.SemaphoreType.DMA(sems),
            pltpu.SemaphoreType.DMA((n,)),
            pltpu.SemaphoreType.DMA((2,)),
            pltpu.SemaphoreType.DMA((len(whole) + 1,)),
            pltpu.SemaphoreType.DMA((len(saved),)),
        ],
        compiler_params=pltpu.CompilerParams(
            collective_id=collective_id,
            has_side_effects=True,
            vmem_limit_bytes=60 * 1024 * 1024,
        ),
        name="forward_layer",
    )(tokens, memory, lengths, *vecs, *mats)
    return got[:n], got[n:]


class Deferred(Schedule):
    def __init__(self, plan, issue):
        super().__init__(list(plan), issue)
        self.made = set()

    def due(self):
        items, rest, held_back = [], [], set()
        for item in self.plan:
            when, unit, stage = item
            if unit in self.made and unit not in held_back and when <= self.now:
                items.append((unit, stage))
            else:
                held_back.add(unit)
                rest.append(item)
        self.plan = rest
        return items

    def finish(self, unit, last=99):
        late = [when for when, u, stage in self.plan if u == unit and stage <= last]
        if late:
            self.until(max(late))


def backward_pair(refs, accs, total_of, spans, length, scale, lanes):
    q_ref, k_ref, v_ref, g_ref = refs
    dk_acc, dv_acc = accs
    keys_all = k_ref.shape[0]
    half = (dk_acc.shape[1]) // 2
    for step, (start, size, keys) in enumerate(spans):
        part_rows = pl.ds(start, size)
        q2 = q_ref[part_rows, lanes]
        g2 = g_ref[part_rows, lanes]
        k2 = k_ref[pl.ds(0, keys), lanes]
        v2 = v_ref[pl.ds(0, keys), lanes]
        kt = k2.T
        dk, dv, dqt = None, None, []
        for head in (0, 1):
            qm = lane_half(q2, head, half)
            gm = lane_half(g2, head, half)
            raw = dot_nt(k2, qm)
            probs = jnp.exp2(raw * (scale * LOG2E) - total_of(head, start, size))
            if length is not None:
                key_pos = lax.broadcasted_iota(jnp.int32, raw.shape, 0)
                probs = jnp.where(key_pos <= limit_row(start, size, length), probs, 0.0)
            grad = dot_nt(v2, gm)
            part = probs * grad
            dot_row = jnp.sum(part, axis=0, keepdims=True)
            score = ((part - probs * dot_row) * scale).astype(jnp.bfloat16)
            dvh = dot_nn(probs.astype(jnp.bfloat16), gm)
            dkh = dot_nn(score, qm)
            dv = dvh if dv is None else dv + dvh
            dk = dkh if dk is None else dk + dkh
            dqt.append(dot_nn(kt[head * half : (head + 1) * half], score))
        q_ref[part_rows, lanes] = jnp.concatenate(dqt, axis=0).T.astype(jnp.bfloat16)
        if step == 0:
            dk_acc[pl.ds(0, keys), :] = dk
            dv_acc[pl.ds(0, keys), :] = dv
        else:
            dk_acc[pl.ds(0, keys), :] += dk
            dv_acc[pl.ds(0, keys), :] += dv
    every_key = pl.ds(0, keys_all)
    k_ref[every_key, lanes] = dk_acc[every_key, :].astype(jnp.bfloat16)
    v_ref[every_key, lanes] = dv_acc[every_key, :].astype(jnp.bfloat16)


BACK_INPUTS = ("dz", "tokens", "memory", "lengths")
BACK_INPUTS += ("q", "k", "v", "a", "total", "h1", "cq", "ck", "cv", "ca", "ctotal", "h2", "g", "rate")
BACK_INPUTS += ("n1", "n2", "n3")
BACK_INPUTS += ("wvec", "wq", "wk", "wv", "wck", "wcv", "wo", "wcq", "wco", "win", "wout")
TALL_PARTS = 8
WIDE_HELD = 11
WIDE_BOXES = 6
WIDE_STAGES = 4
SUM_SLOTS = 8


def backward_parts(width, hidden):
    half = width // 2
    parts = [(8, c) for c in range(0, hidden, half)]
    parts += [(7, 0), (7, half)]
    parts += [(i, c) for c in (0, half) for i in (6, 3, 4)]
    parts += [(5, 0), (5, half)]
    parts += [(i, c) for c in (0, half) for i in (0, 1, 2)]
    return parts


def made_times(n_wide):
    times = [6.0, 6.0, 9.0, 9.0, 12.0, 12.0, 15.0, 15.0]
    for first in (20.0, 25.5, 31.0, 36.5):
        times += [first, first + 1.0]
    times += [44.0, 45.0]
    times += [58.0, 59.0, 60.0, 73.0, 74.0, 75.0]
    times += [86.0, 87.0]
    times += [98.0, 99.0, 100.0, 112.0, 113.0, 114.0]
    return times + [124.0]


def backward_kernel(bits, orders, plan, begin, heads, *refs):
    count = len(bits)
    given = dict(zip(BACK_INPUTS, refs[: len(BACK_INPUTS)]))
    refs = refs[len(BACK_INPUTS) :]
    tokens_grad, memory_grad, keep_k, keep_v = refs[:4]
    results = refs[4:15]
    refs = refs[15:]
    bdz, n, acc, dh, hb, wide_a, wide_b = refs[:7]
    stages, held_tall, held_wide, box_tall, box_wide = refs[7:12]
    rest_tall, rest_wide = refs[12 : 12 + count - 1], refs[12 + count - 1 : 12 + 2 * (count - 1)]
    refs = refs[12 + 2 * (count - 1) :]
    vec_stage, vec_held = refs[:2]
    vec_boxes = refs[2 : 2 + count]
    refs = refs[2 + count :]
    sum_tall, sum_wide, sum_vec, vgrad, hgrad, table, vecs, tot, dk_acc, dv_acc = refs[:10]
    send_sem, recv_sem, store_sem, load_sem, w_sem, credit = refs[10:]
    wides = (wide_a, wide_b)
    mine = my_bits(bits)
    core = count - 1
    rows, width = bdz.shape
    half = width // 2
    hidden = hgrad.shape[1]
    every = (slice(None),) * count
    wide_parts = backward_parts(width, hidden)
    n_parts = len(orders)
    last = n_parts - 1
    tall_stage = [None, None]
    loads = {}

    def load(name, source, target):
        loads[name] = (source, target, len(loads))
        pltpu.make_async_copy(source, target, load_sem.at[len(loads) - 1]).start()

    def loaded(name):
        source, target, at = loads[name]
        pltpu.make_async_copy(source, target, load_sem.at[at]).wait()

    load("dz", given["dz"], bdz)
    load("vecs", given["wvec"], vecs)
    load("h2", given["h2"], hb)
    load("n3", given["n3"], n)
    vgrad[...] = jnp.zeros_like(vgrad)
    greet(bits, mine)

    def kind_of(part):
        if part < TALL_PARTS:
            return "tall"
        return "vec" if part == last else "wide"

    def lines_of(part):
        if kind_of(part) == "tall":
            height = held_tall.shape[-2] // 2
            return (pl.ds(part % 2 * height, height), slice(None))
        return (slice(None), slice(None))

    def held_of(part):
        kind = kind_of(part)
        if kind == "tall":
            return held_tall.at[part // 2]
        return vec_held if kind == "vec" else held_wide.at[(part - TALL_PARTS) % WIDE_HELD]

    def stage_of(part):
        kind = kind_of(part)
        if kind == "tall":
            return tall_stage[part // 2 % 2]
        return vec_stage if kind == "vec" else stages.at[(part - TALL_PARTS) % WIDE_STAGES]

    def box_of(part, step):
        kind = kind_of(part)
        if kind == "vec":
            return vec_boxes[step]
        if kind == "tall":
            return box_tall.at[part // 2 % 2] if step == 0 else rest_tall[step - 1].at[part // 2]
        i = part - TALL_PARTS
        return box_wide.at[i % WIDE_BOXES] if step == 0 else rest_wide[step - 1].at[i]

    def message(part, step):
        order = orders[part]
        now = order[step]
        lines = lines_of(part)
        where = []
        for b in range(count):
            if b == now:
                where.append(1 - mine[b])
            elif b in order[:step]:
                where.append(mine[b])
            else:
                where.append(slice(None))
        if step == 0:
            source = stage_of(part).at[tuple(where) + lines]
        else:
            source = held_of(part).at[tuple(where[:core]) + lines]
        return pltpu.make_async_remote_copy(
            src_ref=source,
            dst_ref=box_of(part, step).at[(slice(None),) * (core - step) + lines],
            send_sem=send_sem.at[part, step],
            recv_sem=recv_sem.at[part, step],
            device_id=partner(bits, mine, now),
            device_id_type=MESH_ID,
        )

    sent = set()

    def drained(part, step):
        if (part, step) not in sent:
            sent.add((part, step))
            message(part, step).wait_send()

    def credit_of(part):
        if kind_of(part) == "tall":
            return credit.at[part // 2 % 2]
        return credit.at[2 + (part - TALL_PARTS) % WIDE_BOXES]

    def box_used_again(part):
        if kind_of(part) == "tall":
            return part + 4 < TALL_PARTS
        return part != last and part + WIDE_BOXES < last

    def add(part, step, target=None):
        order, lines = orders[part], lines_of(part)
        message(part, step).wait_recv()
        held, box = held_of(part), box_of(part, step)
        own = stage_of(part) if step == 0 else None
        open_bits = [b for b in range(count) if b not in order[: step + 1]]
        looped = open_bits[:-2]

        def one(block, carry):
            where, spot = [], []
            for b in range(core):
                if b in looped:
                    digit = (block // 2 ** (len(looped) - 1 - looped.index(b))) % 2
                elif b in open_bits:
                    digit = slice(None)
                else:
                    digit = None
                where.append(mine[b] if digit is None else digit)
                if digit is not None:
                    spot.append(digit)
            source, where = tuple(where) + (mine[core],) + lines, tuple(where) + lines
            spot = tuple(spot) + lines
            if target is not None:
                target[...] = held[where].astype(jnp.float32) + box[spot].astype(jnp.float32)
            else:
                held[where] = (held[where] if own is None else own[source]) + box[spot]
            return carry

        if looped:
            lax.fori_loop(0, 2 ** len(looped), one, 0)
        else:
            one(0, 0)
        if step == 0 and box_used_again(part):
            pl.semaphore_signal(
                credit_of(part), inc=1, device_id=partner(bits, mine, core), device_id_type=MESH_ID
            )

    stored = {}

    def sum_of(part):
        kind = kind_of(part)
        if kind == "tall":
            return sum_tall.at[(part // 2,) + lines_of(part)]
        return sum_vec if kind == "vec" else sum_wide.at[(part - TALL_PARTS) % SUM_SLOTS]

    def store(part):
        kind = kind_of(part)
        if kind == "tall":
            cols = held_tall.shape[-1]
            target = results[9].at[lines_of(part)[0], pl.ds(part // 2 * cols, cols)]
        elif kind == "vec":
            target = results[10]
        else:
            array, left = wide_parts[part - TALL_PARTS]
            target = results[array].at[:, pl.ds(left, half)]
        return pltpu.make_async_copy(sum_of(part), target, store_sem.at[part])

    def issue(part, step):
        if step < count:
            add(part, step - 1)
            message(part, step).start()
            return
        slot = part if kind_of(part) != "wide" else -1 - (part - TALL_PARTS) % SUM_SLOTS
        if slot in stored:
            store(stored[slot]).wait()
        stored[slot] = part
        add(part, count - 1, sum_of(part))
        store(part).start()

    clock = Deferred(plan, issue)

    def room_for(part):
        kind = kind_of(part)
        back = 4 if kind == "tall" else WIDE_STAGES
        first = 0 if kind == "tall" else TALL_PARTS
        if part - back >= first:
            clock.finish(part - back, 1)
            drained(part - back, 0)
        if kind == "wide" and part - WIDE_HELD >= first:
            clock.finish(part - WIDE_HELD)
            for step in range(1, count):
                drained(part - WIDE_HELD, step)

    def made(part):
        kind = kind_of(part)
        if kind == "tall" and part >= 4 and part % 2 == 0:
            clock.finish(part - 4, 1)
            clock.finish(part - 3, 1)
            pl.semaphore_wait(credit_of(part), 2)
        if kind == "wide" and part - WIDE_BOXES >= TALL_PARTS:
            clock.finish(part - WIDE_BOXES, 1)
            pl.semaphore_wait(credit_of(part), 1)
        message(part, 0).start()
        clock.made.add(part)
        clock.now = max(clock.now, begin[part])
        clock.spend(0.0)

    blocks = hidden // width
    names = [("win", every + (slice(None), slice(j * width, (j + 1) * width))) for j in range(blocks)]
    whole = every + (slice(None), slice(None))
    names += [(name, whole) for name in ("wco", "wcq", "wo", "wq", "wk", "wv", "wck", "wcv")]
    weights = [
        pltpu.make_async_copy(given[name].at[where], wides[i % 2], w_sem.at[i])
        for i, (name, where) in enumerate(names)
    ]
    weights[0].start()
    weights[1].start()

    def back_through(i, lhs, write, took=1.1):
        weights[i].wait()
        slot = wides[i % 2]

        def body(t):
            part = slot[t].reshape(half, width)
            write(pl.ds(pl.multiple_of(t * half, half), half), dot_nt(lhs(), part))

        clock.loop(2, took / 2, body)
        if i + 2 < len(weights):
            weights[i + 2].start()

    def produce(part, lhs, rhs, took=0.75):
        room_for(part)
        slot = stage_of(part)
        slot[every + (slice(None), slice(None))] = (
            dot_tn(lhs, rhs).astype(jnp.bfloat16).reshape(slot.shape)
        )
        clock.spend(took)
        made(part)

    def column_sums(ref, rows_now, target, at):
        ones = jnp.ones((8, rows_now), jnp.bfloat16)
        target[pl.ds(at, 1), :] = dot_nn(ones, ref)[0:1]

    def vec(i):
        return table[pl.ds(i, 1), :]

    def norm_back(source, gain, base):
        def body(i):
            part = pl.ds(pl.multiple_of(i * ROWS_STEP, ROWS_STEP), ROWS_STEP)
            r = source[part, :].astype(jnp.float32)
            _, unit_rows, inv_std = normalize(r, vec(gain), vec(gain))
            back, gain_sum, shift_sum = normalize_back(acc[part, :], unit_rows, inv_std, vec(gain))
            vgrad[pl.ds(gain, 1), :] += gain_sum
            vgrad[pl.ds(gain + 1, 1), :] += shift_sum
            total = base(part) + back
            dh[part, :] = total
            bdz[part, :] = total.astype(jnp.bfloat16)

        clock.loop(rows // ROWS_STEP, 0.6, body)

    top = pl.ds(0, rows)
    first_half, second_half = pl.ds(0, half), pl.ds(half, half)
    halves = (first_half, second_half)

    def feed_phase(big, rate, wrow, tall_a, tall_b):
        tall_stage[:] = tall_a, tall_b
        load("g", given["g"], big)

        def rate_copy(j):
            cols = pl.ds(j * width, width)
            return pltpu.make_async_copy(given["rate"].at[:, cols], rate, load_sem.at[24 + j])

        def row_copy(j):
            return pltpu.make_async_copy(given["wout"].at[j // 2, j % 2], wrow, load_sem.at[28 + j])

        rate_copy(0).start()
        row_copy(0).start()
        loaded("dz")
        loaded("g")
        tall_cols = tall_a.shape[-1]
        for j in range(TALL_PARTS // 2):
            room_for(2 * j)
            room_for(2 * j + 1)
            slot = stage_of(2 * j)

            def body(t, j=j, slot=slot):
                part = big[:, pl.ds(pl.multiple_of(t * width, width), width)]
                tile = dot_tn(part, bdz[:, pl.ds(j * tall_cols, tall_cols)]).astype(jnp.bfloat16)
                slot[t // 2, t % 2] = tile.reshape(slot.shape[2:])

            clock.loop(4, 0.45, body)
            made(2 * j)
            made(2 * j + 1)
        column_sums(bdz[...], rows, vgrad, 12)
        loaded("n3")
        for j in range(blocks):
            rate_copy(j).wait()
            row_copy(j).wait()

            def body(t, j=j):
                spot = pl.ds(pl.multiple_of(j * width + t * half, half), half)
                weight = wrow[t].reshape(half, width)
                slope = rate[:, pl.ds(pl.multiple_of(t * half, half), half)].astype(jnp.float32)
                big[:, spot] = (dot_nt(bdz[...], weight) * slope).astype(jnp.bfloat16)

            clock.loop(2, 0.8, body)
            if j + 1 < blocks:
                rate_copy(j + 1).start()
                row_copy(j + 1).start()
            for h in (0, 1):
                produce(TALL_PARTS + 2 * j + h, n[...], big[:, pl.ds(j * width + h * half, half)])
            block = pl.ds(j * width, width)
            hgrad[pl.ds(0, 1), block] = dot_nn(jnp.ones((8, rows), jnp.bfloat16), big[:, block])[0:1]

            def write(cols, value, j=j):
                if j == 0:
                    acc[top, cols] = value
                else:
                    acc[top, cols] += value

            back_through(j, lambda j=j: big[:, pl.ds(j * width, width)], write)
        load("n2", given["n2"], n)
        loaded("vecs")
        unpack_table(vecs, table, bits, width)
        loaded("h2")
        norm_back(hb, 10, lambda part: bdz[part, :].astype(jnp.float32))
        for part in range(TALL_PARTS):
            clock.finish(part, 1)
            drained(part, 0)

    def attention_phase(bq, bk, bv, bg, mem, ba):
        load("ca", given["ca"], ba)
        load("cq", given["cq"], bq)
        load("ck", given["ck"], bk)
        load("cv", given["cv"], bv)
        load("ctotal", given["ctotal"], tot)
        load("memory", given["memory"], mem)
        load("h1", given["h1"], hb)

        def into(ref, size=rows):
            def write(cols, value):
                ref[pl.ds(0, size), cols] = value.astype(ref.dtype)

            return write

        def more(size):
            def write(cols, value):
                acc[pl.ds(0, size), cols] += value

            return write

        def attend(keys, masked, side):
            pair = 2 * (width // heads)
            pairs = heads // 4
            chunk = rows // 2
            spans = [(s, chunk, s + chunk if masked else keys) for s in range(0, rows, chunk)]
            key_rows = pl.ds(0, keys)
            refs_now = (bq, bk.at[key_rows], bv.at[key_rows], bg)

            def body(i):
                p = side * pairs + i
                lanes = pl.ds(pl.multiple_of(p * pair, pair), pair)
                backward_pair(
                    refs_now,
                    (dk_acc, dv_acc),
                    lambda head, start, size: tot[p, pl.ds(head, 1), pl.ds(start, size)],
                    spans[::-1],
                    length if masked else None,
                    (width // heads) ** -0.5,
                    lanes,
                )

            clock.loop(pairs, 1.9 if masked else 2.3, body)

        part = TALL_PARTS + 2 * blocks
        keys = mem.shape[0]
        length = given["lengths"][0]
        at = blocks
        back_through(at, lambda: bdz[...], into(bg))
        loaded("ca")
        for cols in halves:
            produce(part, ba[...], bdz[:, cols])
            part += 1
        column_sums(bdz[...], rows, vgrad, 9)
        load("a", given["a"], ba)
        for name in ("cq", "ck", "cv", "ctotal", "n2", "memory"):
            loaded(name)
        for side, cols in enumerate(halves):
            attend(keys, False, side)
            produce(part, n[...], bq[:, cols])
            produce(part + 1, mem[...], bk[:, cols], 0.85)
            produce(part + 2, mem[...], bv[:, cols], 0.85)
            part += 3
        load("total", given["total"], tot)
        load("n1", given["n1"], n)
        keeps = [
            pltpu.make_async_copy(bk, keep_k, load_sem.at[32]),
            pltpu.make_async_copy(bv, keep_v, load_sem.at[33]),
        ]
        for copy in keeps:
            copy.start()
        back_through(at + 1, lambda: bq[...], into(acc))
        column_sums(bq[...], rows, vgrad, 7)
        column_sums(bv[...], keys, vgrad, 8)
        load("q", given["q"], bq)
        for copy in keeps:
            copy.wait()
        load("k", given["k"], bk.at[top])
        load("v", given["v"], bv.at[top])
        loaded("h1")
        norm_back(hb, 5, lambda part: dh[part, :])
        back_through(at + 2, lambda: bdz[...], into(bg))
        loaded("a")
        for cols in halves:
            produce(part, ba[...], bdz[:, cols])
            part += 1
        column_sums(bdz[...], rows, vgrad, 4)
        load("tokens", given["tokens"], ba)
        for name in ("q", "k", "v", "total", "n1"):
            loaded(name)
        for side, cols in enumerate(halves):
            attend(rows, True, side)
            for i, ref in enumerate((bq, bk, bv)):
                produce(part + i, n[...], ref[top, cols])
            part += 3
        back_through(at + 3, lambda: bq[...], into(acc))
        back_through(at + 4, lambda: bk[top, :], more(rows))
        back_through(at + 5, lambda: bv[top, :], more(rows))
        column_sums(bq[...], rows, vgrad, 2)
        column_sums(bv[top, :], rows, vgrad, 3)
        load("keep_k", keep_k, bk)
        load("keep_v", keep_v, bv)
        loaded("tokens")
        norm_back(ba, 0, lambda part: dh[part, :])
        put_tokens = pltpu.make_async_copy(dh, tokens_grad, load_sem.at[34])
        put_tokens.start()
        devices = 2**count
        share = devices // (width // VEC_LANES)
        for d in range(devices):
            where = tuple((d >> (count - 1 - b)) & 1 for b in range(count))
            vec_stage[where] = vgrad[:, pl.ds(d // share * VEC_LANES, VEC_LANES)]
            vec_stage[where + (pl.ds(13, 1),)] = hgrad[:, pl.ds(d * VEC_LANES, VEC_LANES)]
        made(last)
        loaded("keep_k")
        loaded("keep_v")
        back_through(at + 6, lambda: bk[...], into(acc, keys))
        back_through(at + 7, lambda: bv[...], more(keys))
        put_memory = pltpu.make_async_copy(acc, memory_grad, load_sem.at[35])
        put_memory.start()
        clock.until(1e9)
        put_tokens.wait()
        put_memory.wait()

    low = jnp.bfloat16
    pl.run_scoped(
        feed_phase,
        pltpu.VMEM((rows, hidden), low),
        pltpu.VMEM((rows, width), low),
        pltpu.VMEM(given["wout"].shape[2:], low),
        pltpu.VMEM((2,) * count + held_tall.shape[-2:], low),
        pltpu.VMEM((2,) * count + held_tall.shape[-2:], low),
    )
    key_rows = given["memory"].shape[0]
    pl.run_scoped(
        attention_phase,
        pltpu.VMEM((rows, width), low),
        pltpu.VMEM((key_rows, width), low),
        pltpu.VMEM((key_rows, width), low),
        pltpu.VMEM((rows, width), low),
        pltpu.VMEM((key_rows, width), low),
        pltpu.VMEM((rows, width), low),
    )
    for part in stored.values():
        store(part).wait()
    for part in range(n_parts):
        for step in range(count):
            drained(part, step)


def fused_backward(mesh, dz, tokens, memory, lengths, saved, gathered, heads, collective_id):
    bits = bit_table(mesh)
    count = len(bits)
    routes = route_orders(bits)
    rows, width = tokens.shape
    keys = memory.shape[0]
    shards = [w.shape[count:] for w in gathered[1:]]
    wide_block = (shards[0][0], width // 2)
    tall_rows = shards[9][0]
    hidden = shards[8][1]
    tall_block = (tall_rows, 2 * width * shards[0][0] // tall_rows * 4 // TALL_PARTS)
    pack = (VEC_ROWS, VEC_LANES)
    n_wide = len(backward_parts(width, hidden))
    n_parts = TALL_PARTS + n_wide + 1
    low = jnp.bfloat16
    sizes = [2 * wide_block[0] * wide_block[1]] * (n_parts - 1) + [4 * pack[0] * pack[1]]
    orders = [routes[part % 4][::-1] for part in range(n_parts)]
    begin = made_times(n_wide)
    sends, finish = plan_sends(bits, orders, sizes, False, 2000e3, begin)
    plan = [item for item in sends if item[2] > 0]
    plan = sorted(plan + [(when, part, count) for part, when in finish.items()])
    blocks = shards + [pack]
    spots = (2,) * count
    scratch = [
        pltpu.VMEM((rows, width), low),
        pltpu.VMEM((rows, width), low),
        pltpu.VMEM((keys, width), jnp.float32),
        pltpu.VMEM((rows, width), jnp.float32),
        pltpu.VMEM((rows, width), jnp.float32),
        pltpu.VMEM(spots + shards[0], low),
        pltpu.VMEM(spots + shards[0], low),
        pltpu.VMEM((WIDE_STAGES,) + spots + wide_block, low),
        pltpu.VMEM((TALL_PARTS // 2,) + spots[1:] + tall_block, low),
        pltpu.VMEM((WIDE_HELD,) + spots[1:] + wide_block, low),
        pltpu.VMEM((2,) + spots[1:] + tall_block, low),
        pltpu.VMEM((WIDE_BOXES,) + spots[1:] + wide_block, low),
    ]
    for number, block in ((TALL_PARTS // 2, tall_block), (n_wide, wide_block)):
        for step in range(1, count):
            scratch.append(pltpu.VMEM((number,) + (2,) * (count - 1 - step) + block, low))
    scratch += [pltpu.VMEM(spots + pack, jnp.float32), pltpu.VMEM(spots[1:] + pack, jnp.float32)]
    for step in range(count):
        scratch.append(pltpu.VMEM((2,) * (count - 1 - step) + pack, jnp.float32))
    pair = 2 * (width // heads)
    scratch += [
        pltpu.VMEM((TALL_PARTS // 2,) + tall_block, jnp.float32),
        pltpu.VMEM((SUM_SLOTS,) + wide_block, jnp.float32),
        pltpu.VMEM(pack, jnp.float32),
        pltpu.VMEM((VEC_ROWS, width), jnp.float32),
        pltpu.VMEM((1, hidden), jnp.float32),
        pltpu.VMEM((VEC_ROWS, width), jnp.float32),
        pltpu.VMEM(spots + pack, low),
        pltpu.VMEM((heads // 2, 2, rows), jnp.float32),
        pltpu.VMEM((keys, pair), jnp.float32),
        pltpu.VMEM((keys, pair), jnp.float32),
        pltpu.SemaphoreType.DMA((n_parts, count)),
        pltpu.SemaphoreType.DMA((n_parts, count)),
        pltpu.SemaphoreType.DMA((n_parts,)),
        pltpu.SemaphoreType.DMA((36,)),
        pltpu.SemaphoreType.DMA((12,)),
        pltpu.SemaphoreType.REGULAR((2 + WIDE_BOXES,)),
    ]
    hbm = pl.BlockSpec(memory_space=pltpu.HBM)
    got = pl.pallas_call(
        functools.partial(backward_kernel, bits, orders, plan, begin, heads),
        out_shape=[
            jax.ShapeDtypeStruct((rows, width), jnp.float32),
            jax.ShapeDtypeStruct((keys, width), jnp.float32),
            jax.ShapeDtypeStruct((keys, width), low),
            jax.ShapeDtypeStruct((keys, width), low),
        ]
        + [jax.ShapeDtypeStruct(b, jnp.float32) for b in blocks],
        in_specs=[hbm, hbm, hbm, pl.BlockSpec(memory_space=pltpu.SMEM)]
        + [hbm] * (len(BACK_INPUTS) - 4),
        out_specs=[hbm] * (4 + len(blocks)),
        scratch_shapes=scratch,
        compiler_params=pltpu.CompilerParams(
            collective_id=collective_id,
            has_side_effects=True,
            vmem_limit_bytes=62 * 1024 * 1024,
        ),
        name="backward_layer",
    )(dz, tokens, memory, lengths, *saved, *gathered)
    return got[:2] + got[4:]


def place_kernel(count, pieces, *refs):
    sources, targets = refs[:count], refs[count : 2 * count]
    rooms, (in_sem, out_sem) = refs[2 * count : 3 * count], refs[3 * count :]
    moves = []
    for source, target, room in zip(sources, targets, rooms):
        height = source.shape[0]
        step = height // pieces // 8 * 8 if height > 64 * pieces else height
        top = 0
        while top < height:
            size = step if top + 2 * step <= height else height - top
            rows, at = pl.ds(top, size), len(moves)
            moves.append(
                (
                    pltpu.make_async_copy(source.at[rows], room.at[rows], in_sem.at[at]),
                    pltpu.make_async_copy(room.at[rows], target.at[rows], out_sem.at[at]),
                )
            )
            top += size
    for into, _ in moves:
        into.start()
    for into, out in moves:
        into.wait()
        out.start()
    for _, out in moves:
        out.wait()


def place_outputs(arrays):
    hbm = pl.BlockSpec(memory_space=pltpu.HBM)
    sems = (8 * len(arrays),)
    return pl.pallas_call(
        functools.partial(place_kernel, len(arrays), 4),
        out_shape=[jax.ShapeDtypeStruct(a.shape, a.dtype) for a in arrays],
        in_specs=[hbm] * len(arrays),
        out_specs=[hbm] * len(arrays),
        scratch_shapes=[pltpu.VMEM(a.shape, a.dtype) for a in arrays]
        + [pltpu.SemaphoreType.DMA(sems), pltpu.SemaphoreType.DMA(sems)],
        compiler_params=pltpu.CompilerParams(vmem_limit_bytes=32 * 1024 * 1024),
        name="place_outputs",
    )(*arrays)


MATS_ORDER = (2, 4, 5, 13, 14, 7, 11, 16, 20, 22)
VECS = (0, 1, 3, 6, 8, 9, 10, 12, 15, 17, 18, 19, 23, 21)


def split_units(blocks):
    units = [(0, slice(None), slice(None))]
    for i, (rows, cols) in enumerate(blocks):
        base_rows, base_cols = min(rows, blocks[0][0]), min(cols, blocks[0][1])
        for top in range(0, rows, base_rows):
            for left in range(0, cols, base_cols):
                units.append(
                    (i + 1, slice(top, top + base_rows), slice(left, left + base_cols))
                )
    return units


def collect(*shards):
    return tuple(lax.all_gather(s, BOTH, axis=0, tiled=True) for s in shards)


def spread(*grads):
    return tuple(
        lax.psum_scatter(g.astype(jnp.float32), BOTH, scatter_dimension=0, tiled=True)
        for g in grads
    )


def own_vectors(block, position, shards):
    size = shards[0].shape[0]
    spot = position % (VEC_LANES // size)
    mine = lax.dynamic_slice(block, (0, spot * size), (VEC_ROWS, size))
    owned = [None] * len(shards)
    for row, i in enumerate(VECS[:-1]):
        owned[i] = mine[row]
    owned[VECS[-1]] = block[len(VECS) - 1]
    return owned


def on_device(
    mesh,
    tokens,
    memory,
    page_lengths,
    end_flags,
    out_grad,
    self_gain,
    self_shift,
    self_query,
    self_query_bias,
    self_key,
    self_value,
    self_value_bias,
    self_out,
    self_out_bias,
    cross_gain,
    cross_shift,
    cross_query,
    cross_query_bias,
    cross_key,
    cross_value,
    cross_value_bias,
    cross_out,
    cross_out_bias,
    feed_gain,
    feed_shift,
    feed_in,
    feed_in_bias,
    feed_out,
    feed_out_bias,
):
    page_count, page_len, width = tokens.shape
    mem_len = memory.shape[1]
    row_count = page_count * page_len
    lengths_now = jnp.where(end_flags == 1, 1, page_lengths)
    inputs = tokens.reshape(row_count, width).astype(jnp.float32)
    mem_rows = memory.reshape(page_count * mem_len, width)
    shard_set = (
        self_gain,
        self_shift,
        self_query,
        self_query_bias,
        self_key,
        self_value,
        self_value_bias,
        self_out,
        self_out_bias,
        cross_gain,
        cross_shift,
        cross_query,
        cross_query_bias,
        cross_key,
        cross_value,
        cross_value_bias,
        cross_out,
        cross_out_bias,
        feed_gain,
        feed_shift,
        feed_in,
        feed_in_bias,
        feed_out,
        feed_out_bias,
    )
    if can_route(mesh, self_query.shape[0]):
        mats = [shard_set[i] for i in MATS_ORDER]
        vecs = [shard_set[i] for i in VECS]
        gathered, saved = fused_forward(
            mesh, tokens[0], memory[0], lengths_now, mats, vecs, HEADS, 0
        )
        got = fused_backward(
            mesh, out_grad[0], tokens[0], memory[0], lengths_now, saved[:-1], gathered, HEADS, 1
        )
        position = lax.axis_index("dp") * mesh.shape["fsdp"] + lax.axis_index("fsdp")
        owned = own_vectors(got[-1], position, shard_set)
        placed = place_outputs([saved[-1], got[0]] + list(got[2:-1]))
        for i, value in zip(MATS_ORDER, placed[2:]):
            owned[i] = value
        return (placed[0][None], placed[1][None], got[1][None]) + tuple(owned)
    full_set = collect(*shard_set)
    (
        gain_one,
        shift_one,
        query_mat,
        query_vec,
        key_mat,
        value_mat,
        value_vec,
        out_mat,
        out_vec,
        gain_two,
        shift_two,
        cquery_mat,
        cquery_vec,
        ckey_mat,
        cvalue_mat,
        cvalue_vec,
        cout_mat,
        cout_vec,
        gain_three,
        shift_three,
        hidden_mat,
        hidden_vec,
        final_mat,
        final_vec,
    ) = full_set
    norm_of = lambda r, g, b: normalize(r, g.astype(jnp.float32), b.astype(jnp.float32))
    first_norm, first_unit, first_std = norm_of(inputs, gain_one, shift_one)
    first_low = first_norm.astype(jnp.bfloat16)
    query_low = (product(first_low, query_mat) + query_vec.astype(jnp.float32)).astype(jnp.bfloat16)
    key_low = product(first_low, key_mat).astype(jnp.bfloat16)
    value_low = (product(first_low, value_mat) + value_vec.astype(jnp.float32)).astype(jnp.bfloat16)
    query_pages = query_low.reshape(page_count, page_len, width)
    key_pages = key_low.reshape(page_count, page_len, width)
    value_pages = value_low.reshape(page_count, page_len, width)
    self_mixed, self_total = attend_fwd(
        query_pages, key_pages, value_pages, lengths_now, HEADS, 512
    )
    self_low = self_mixed.reshape(row_count, width)
    after_self = inputs + product(self_low, out_mat) + out_vec.astype(jnp.float32)
    second_norm, second_unit, second_std = normalize(
        after_self, gain_two.astype(jnp.float32), shift_two.astype(jnp.float32)
    )
    second_low = second_norm.astype(jnp.bfloat16)
    cquery_low = (product(second_low, cquery_mat) + cquery_vec.astype(jnp.float32)).astype(
        jnp.bfloat16
    )
    ckey_low = product(mem_rows, ckey_mat).astype(jnp.bfloat16)
    cvalue_low = (product(mem_rows, cvalue_mat) + cvalue_vec.astype(jnp.float32)).astype(
        jnp.bfloat16
    )
    cquery_pages = cquery_low.reshape(page_count, page_len, width)
    ckey_pages = ckey_low.reshape(page_count, mem_len, width)
    cvalue_pages = cvalue_low.reshape(page_count, mem_len, width)
    cross_mixed, cross_total = attend_fwd(
        cquery_pages, ckey_pages, cvalue_pages, None, HEADS, 512
    )
    cross_low = cross_mixed.reshape(row_count, width)
    after_cross = after_self + product(cross_low, cout_mat) + cout_vec.astype(jnp.float32)
    third_norm, third_unit, third_std = normalize(
        after_cross, gain_three.astype(jnp.float32), shift_three.astype(jnp.float32)
    )
    third_low = third_norm.astype(jnp.bfloat16)
    hidden_pre = product(third_low, hidden_mat) + hidden_vec.astype(jnp.float32)
    hidden_low, hidden_rate = gelu_parts(hidden_pre)
    hidden_low = hidden_low.astype(jnp.bfloat16)
    hidden_rate = hidden_rate.astype(jnp.bfloat16)
    result = after_cross + product(hidden_low, final_mat) + final_vec.astype(jnp.float32)
    layer_out = result.astype(jnp.bfloat16).reshape(page_count, page_len, width)
    second_norm, second_unit, second_std = norm_of(after_self, gain_two, shift_two)
    second_low = second_norm.astype(jnp.bfloat16)
    third_norm, third_unit, third_std = norm_of(after_cross, gain_three, shift_three)
    third_low = third_norm.astype(jnp.bfloat16)
    grad_rows = out_grad.reshape(row_count, width).astype(jnp.float32)
    final_grad = out_grad.reshape(row_count, width)
    grad_final_mat = product_tn(hidden_low, final_grad).astype(jnp.bfloat16)
    grad_final_vec = jnp.sum(final_grad.astype(jnp.float32), axis=0)
    hidden_grad = (product_nt(final_grad, final_mat) * hidden_rate.astype(jnp.float32)).astype(jnp.bfloat16)
    grad_hidden_mat = product_tn(third_low, hidden_grad).astype(jnp.bfloat16)
    grad_hidden_vec = jnp.sum(hidden_grad.astype(jnp.float32), axis=0)
    third_back, grad_gain_three, grad_shift_three = normalize_back(
        product_nt(hidden_grad, hidden_mat), third_unit, third_std, gain_three.astype(jnp.float32)
    )
    cross_grad_total = grad_rows + third_back
    cout_grad = cross_grad_total.astype(jnp.bfloat16)
    grad_cout_mat = product_tn(cross_low, cout_grad).astype(jnp.bfloat16)
    grad_cout_vec = jnp.sum(cout_grad.astype(jnp.float32), axis=0)
    cmix_grad = (
        product_nt(cout_grad, cout_mat).astype(jnp.bfloat16).reshape(page_count, page_len, width)
    )
    cquery_grad, ckey_grad, cvalue_grad = attend_bwd(
        cquery_pages, ckey_pages, cvalue_pages, cmix_grad, cross_total, None, HEADS, 512
    )
    cquery_grad = cquery_grad.reshape(row_count, width)
    ckey_grad = ckey_grad.reshape(page_count * mem_len, width)
    cvalue_grad = cvalue_grad.reshape(page_count * mem_len, width)
    grad_cquery_mat = product_tn(second_low, cquery_grad).astype(jnp.bfloat16)
    grad_cquery_vec = jnp.sum(cquery_grad.astype(jnp.float32), axis=0)
    grad_ckey_mat = product_tn(mem_rows, ckey_grad).astype(jnp.bfloat16)
    grad_cvalue_mat = product_tn(mem_rows, cvalue_grad).astype(jnp.bfloat16)
    grad_cvalue_vec = jnp.sum(cvalue_grad.astype(jnp.float32), axis=0)
    memory_grad = (product_nt(ckey_grad, ckey_mat) + product_nt(cvalue_grad, cvalue_mat)).reshape(
        page_count, mem_len, width
    )
    second_back, grad_gain_two, grad_shift_two = normalize_back(
        product_nt(cquery_grad, cquery_mat), second_unit, second_std, gain_two.astype(jnp.float32)
    )
    self_grad_total = cross_grad_total + second_back
    sout_grad = self_grad_total.astype(jnp.bfloat16)
    grad_out_mat = product_tn(self_low, sout_grad).astype(jnp.bfloat16)
    grad_out_vec = jnp.sum(sout_grad.astype(jnp.float32), axis=0)
    smix_grad = (
        product_nt(sout_grad, out_mat).astype(jnp.bfloat16).reshape(page_count, page_len, width)
    )
    query_grad, key_grad, value_grad = attend_bwd(
        query_pages, key_pages, value_pages, smix_grad, self_total, lengths_now, HEADS, 256
    )
    query_grad = query_grad.reshape(row_count, width)
    key_grad = key_grad.reshape(row_count, width)
    value_grad = value_grad.reshape(row_count, width)
    grad_query_mat = product_tn(first_low, query_grad).astype(jnp.bfloat16)
    grad_query_vec = jnp.sum(query_grad.astype(jnp.float32), axis=0)
    grad_key_mat = product_tn(first_low, key_grad).astype(jnp.bfloat16)
    grad_value_mat = product_tn(first_low, value_grad).astype(jnp.bfloat16)
    grad_value_vec = jnp.sum(value_grad.astype(jnp.float32), axis=0)
    first_in = (
        product_nt(query_grad, query_mat)
        + product_nt(key_grad, key_mat)
        + product_nt(value_grad, value_mat)
    )
    first_back, grad_gain_one, grad_shift_one = normalize_back(
        first_in, first_unit, first_std, gain_one.astype(jnp.float32)
    )
    tokens_grad = (self_grad_total + first_back).reshape(page_count, page_len, width)
    owned = spread(
        grad_gain_one[0],
        grad_shift_one[0],
        grad_query_mat,
        grad_query_vec,
        grad_key_mat,
        grad_value_mat,
        grad_value_vec,
        grad_out_mat,
        grad_out_vec,
        grad_gain_two[0],
        grad_shift_two[0],
        grad_cquery_mat,
        grad_cquery_vec,
        grad_ckey_mat,
        grad_cvalue_mat,
        grad_cvalue_vec,
        grad_cout_mat,
        grad_cout_vec,
        grad_gain_three[0],
        grad_shift_three[0],
        grad_hidden_mat,
        grad_hidden_vec,
        grad_final_mat,
        grad_final_vec,
    )
    return (layer_out, tokens_grad, memory_grad) + tuple(owned)


def solution(mesh):
    placed = (
        P(("dp", "fsdp"), None, None),
        P(("dp", "fsdp"), None, None),
        P(("dp", "fsdp")),
        P(("dp", "fsdp")),
        P(("dp", "fsdp"), None, None),
        P(("dp", "fsdp")),
        P(("dp", "fsdp")),
        P(("dp", "fsdp"), None),
        P(("dp", "fsdp")),
        P(("dp", "fsdp"), None),
        P(("dp", "fsdp"), None),
        P(("dp", "fsdp")),
        P(("dp", "fsdp"), None),
        P(("dp", "fsdp")),
        P(("dp", "fsdp")),
        P(("dp", "fsdp")),
        P(("dp", "fsdp"), None),
        P(("dp", "fsdp")),
        P(("dp", "fsdp"), None),
        P(("dp", "fsdp"), None),
        P(("dp", "fsdp")),
        P(("dp", "fsdp"), None),
        P(("dp", "fsdp")),
        P(("dp", "fsdp")),
        P(("dp", "fsdp")),
        P(("dp", "fsdp"), None),
        P(("dp", "fsdp")),
        P(("dp", "fsdp"), None),
        P(("dp", "fsdp")),
    )
    return jax.shard_map(
        functools.partial(on_device, mesh),
        mesh=mesh,
        in_specs=placed,
        out_specs=(
            P(("dp", "fsdp"), None, None),
            P(("dp", "fsdp"), None, None),
            P(("dp", "fsdp"), None, None),
            P(("dp", "fsdp")),
            P(("dp", "fsdp")),
            P(("dp", "fsdp"), None),
            P(("dp", "fsdp")),
            P(("dp", "fsdp"), None),
            P(("dp", "fsdp"), None),
            P(("dp", "fsdp")),
            P(("dp", "fsdp"), None),
            P(("dp", "fsdp")),
            P(("dp", "fsdp")),
            P(("dp", "fsdp")),
            P(("dp", "fsdp"), None),
            P(("dp", "fsdp")),
            P(("dp", "fsdp"), None),
            P(("dp", "fsdp"), None),
            P(("dp", "fsdp")),
            P(("dp", "fsdp"), None),
            P(("dp", "fsdp")),
            P(("dp", "fsdp")),
            P(("dp", "fsdp")),
            P(("dp", "fsdp"), None),
            P(("dp", "fsdp")),
            P(("dp", "fsdp"), None),
            P(("dp", "fsdp")),
        ),
        check_vma=False,
    )
```

```python
import functools

import jax
import jax.numpy as jnp
from jax import lax
from jax.experimental import pallas as pl
from jax.experimental.pallas import tpu as pltpu
from jax.sharding import PartitionSpec as P

HEADS = 16


EPSILON = 1e-05
ROOT_HALF = 0.7071067811865476
INV_ROOT_TWO_PI = 0.3989422804014327


def product(left, right):
    return jnp.dot(left, right, preferred_element_type=jnp.float32)


def product_tn(left, right):
    return lax.dot_general(
        left, right, (((0,), (0,)), ((), ())), preferred_element_type=jnp.float32
    )


def product_nt(left, right):
    return lax.dot_general(
        left, right, (((1,), (1,)), ((), ())), preferred_element_type=jnp.float32
    )


def normalize(rows_in, norm_gain, norm_shift):
    centered = rows_in - jnp.mean(rows_in, axis=-1, keepdims=True)
    inv_std = lax.rsqrt(jnp.mean(centered * centered, axis=-1, keepdims=True) + EPSILON)
    unit_rows = centered * inv_std
    return (unit_rows * norm_gain + norm_shift, unit_rows, inv_std)


def normalize_back(grad_norm, unit_rows, inv_std, norm_gain):
    scaled = grad_norm * norm_gain
    inner_part = (
        scaled
        - jnp.mean(scaled, axis=-1, keepdims=True)
        - unit_rows * jnp.mean(scaled * unit_rows, axis=-1, keepdims=True)
    )
    return (
        inner_part * inv_std,
        jnp.sum(grad_norm * unit_rows, axis=0, keepdims=True),
        jnp.sum(grad_norm, axis=0, keepdims=True),
    )


LOG2E = 1.4426950408889634
LN2 = 0.6931471805599453


def dot_nn(a, b):
    return jnp.dot(a, b, preferred_element_type=jnp.float32)


def dot_nt(a, b):
    return lax.dot_general(a, b, (((1,), (1,)), ((), ())), preferred_element_type=jnp.float32)


def dot_tn(a, b):
    return lax.dot_general(a, b, (((0,), (0,)), ((), ())), preferred_element_type=jnp.float32)


def lane_half(x, head, half):
    lane = lax.broadcasted_iota(jnp.int32, (1, x.shape[1]), 1)
    keep = (lane < half) if head == 0 else (lane >= half)
    return jnp.where(keep, x, jnp.zeros_like(x))


def causal_spans(rows, chunk):
    return [(start, chunk, start + chunk) for start in range(0, rows, chunk)]


def limit_row(start, width, length):
    pos = start + lax.broadcasted_iota(jnp.int32, (1, width), 1)
    return jnp.minimum(pos, length - 1)


def forward_pair(load_q, load_k, load_v, write, spans, length, scale):
    for start, size, keys in spans:
        q2 = load_q(start, size)
        k2 = load_k(0, keys)
        v2 = load_v(0, keys)
        half = q2.shape[1] // 2
        vt = v2.T
        outs, totals = [], []
        for head in (0, 1):
            raw = dot_nt(k2, lane_half(q2, head, half))
            if length is not None:
                key_pos = lax.broadcasted_iota(jnp.int32, raw.shape, 0)
                raw = jnp.where(key_pos <= limit_row(start, size, length), raw, -1e30)
            top = jnp.max(raw, axis=0, keepdims=True)
            expo = jnp.exp2((raw - top) * (scale * LOG2E))
            total = jnp.sum(expo, axis=0, keepdims=True)
            mixed = dot_nn(vt[head * half : (head + 1) * half], expo.astype(jnp.bfloat16))
            outs.append(mixed / total)
            totals.append(top * (scale * LOG2E) + jnp.log2(total))
        write(start, size, jnp.concatenate(outs, axis=0).T.astype(jnp.bfloat16), totals)


def fwd_kernel(masked, scale, chunk, *refs):
    if masked:
        len_ref, q_ref, k_ref, v_ref, a_ref, t_ref = refs
        length = len_ref[pl.program_id(0)]
    else:
        q_ref, k_ref, v_ref, a_ref, t_ref = refs
        length = None
    rows, keys = q_ref.shape[1], k_ref.shape[1]
    if masked:
        spans = causal_spans(rows, chunk)
    else:
        spans = [(s, chunk, keys) for s in range(0, rows, chunk)]

    def write(start, size, out, totals):
        a_ref[0, pl.ds(start, size), :] = out
        for head in (0, 1):
            t_ref[0, 0, pl.ds(head, 1), pl.ds(start, size)] = totals[head]

    forward_pair(
        lambda s, n: q_ref[0, pl.ds(s, n), :],
        lambda s, n: k_ref[0, pl.ds(s, n), :],
        lambda s, n: v_ref[0, pl.ds(s, n), :],
        write, spans, length, scale,
    )


def attend_fwd(q, k, v, lengths, heads, chunk=256):
    pages, rows, width = q.shape
    keys = k.shape[1]
    head = width // heads
    pairs = heads // 2
    masked = lengths is not None
    row_spec = pl.BlockSpec((1, rows, 2 * head), lambda p, h: (p, 0, h))
    key_spec = pl.BlockSpec((1, keys, 2 * head), lambda p, h: (p, 0, h))
    in_specs = [row_spec, key_spec, key_spec]
    args = [q, k, v]
    if masked:
        in_specs = [pl.BlockSpec(memory_space=pltpu.SMEM)] + in_specs
        args = [lengths] + args
    return pl.pallas_call(
        functools.partial(fwd_kernel, masked, head**-0.5, chunk),
        grid=(pages, pairs),
        in_specs=in_specs,
        out_specs=[row_spec, pl.BlockSpec((1, 1, 2, rows), lambda p, h: (p, h, 0, 0))],
        out_shape=[
            jax.ShapeDtypeStruct(q.shape, jnp.bfloat16),
            jax.ShapeDtypeStruct((pages, pairs, 2, rows), jnp.float32),
        ],
        compiler_params=pltpu.CompilerParams(vmem_limit_bytes=48 * 1024 * 1024),
        name="attend_forward",
    )(*args)


def bwd_kernel(masked, scale, chunk, *refs):
    if masked:
        len_ref, q_ref, k_ref, v_ref, g_ref, t_ref, dq_ref, dk_ref, dv_ref, dk_acc, dv_acc = refs
        length = len_ref[pl.program_id(0)]
    else:
        q_ref, k_ref, v_ref, g_ref, t_ref, dq_ref, dk_ref, dv_ref, dk_acc, dv_acc = refs
        length = None
    rows, keys_all = q_ref.shape[1], k_ref.shape[1]
    if masked:
        spans = causal_spans(rows, chunk)[::-1]
    else:
        spans = [(s, chunk, keys_all) for s in range(0, rows, chunk)]
    half = q_ref.shape[2] // 2
    for step, (start, size, keys) in enumerate(spans):
        q2 = q_ref[0, pl.ds(start, size), :]
        g2 = g_ref[0, pl.ds(start, size), :]
        k2 = k_ref[0, pl.ds(0, keys), :]
        v2 = v_ref[0, pl.ds(0, keys), :]
        kt = k2.T
        dk, dv, dqt = None, None, []
        for head in (0, 1):
            qm = lane_half(q2, head, half)
            gm = lane_half(g2, head, half)
            raw = dot_nt(k2, qm)
            total = t_ref[0, 0, pl.ds(head, 1), pl.ds(start, size)]
            probs = jnp.exp2(raw * (scale * LOG2E) - total)
            if length is not None:
                key_pos = lax.broadcasted_iota(jnp.int32, raw.shape, 0)
                probs = jnp.where(key_pos <= limit_row(start, size, length), probs, 0.0)
            grad = dot_nt(v2, gm)
            part = probs * grad
            dot_row = jnp.sum(part, axis=0, keepdims=True)
            score = ((part - probs * dot_row) * scale).astype(jnp.bfloat16)
            dvh = dot_nn(probs.astype(jnp.bfloat16), gm)
            dkh = dot_nn(score, qm)
            dv = dvh if dv is None else dv + dvh
            dk = dkh if dk is None else dk + dkh
            dqt.append(dot_nn(kt[head * half : (head + 1) * half], score))
        dq_ref[0, pl.ds(start, size), :] = jnp.concatenate(dqt, axis=0).T.astype(jnp.bfloat16)
        if step == 0:
            dk_acc[pl.ds(0, keys), :] = dk
            dv_acc[pl.ds(0, keys), :] = dv
        else:
            dk_acc[pl.ds(0, keys), :] += dk
            dv_acc[pl.ds(0, keys), :] += dv
    dk_ref[0] = dk_acc[...].astype(jnp.bfloat16)
    dv_ref[0] = dv_acc[...].astype(jnp.bfloat16)


def attend_bwd(q, k, v, g, totals, lengths, heads, chunk=256):
    pages, rows, width = q.shape
    keys = k.shape[1]
    head = width // heads
    pairs = heads // 2
    masked = lengths is not None
    row_spec = pl.BlockSpec((1, rows, 2 * head), lambda p, h: (p, 0, h))
    key_spec = pl.BlockSpec((1, keys, 2 * head), lambda p, h: (p, 0, h))
    total_spec = pl.BlockSpec((1, 1, 2, rows), lambda p, h: (p, h, 0, 0))
    in_specs = [row_spec, key_spec, key_spec, row_spec, total_spec]
    args = [q, k, v, g, totals]
    if masked:
        in_specs = [pl.BlockSpec(memory_space=pltpu.SMEM)] + in_specs
        args = [lengths] + args
    return pl.pallas_call(
        functools.partial(bwd_kernel, masked, head**-0.5, chunk),
        grid=(pages, pairs),
        in_specs=in_specs,
        out_specs=[row_spec, key_spec, key_spec],
        out_shape=[jax.ShapeDtypeStruct(a.shape, jnp.bfloat16) for a in (q, k, v)],
        scratch_shapes=[pltpu.VMEM((keys, 2 * head), jnp.float32)] * 2,
        compiler_params=pltpu.CompilerParams(vmem_limit_bytes=48 * 1024 * 1024),
        name="attend_backward",
    )(*args)


MESH_ID = pl.DeviceIdType.MESH
BOTH = ("dp", "fsdp")
CORE_RATE = 500e3
LINK_RATE = 92e3
HOP = 3.1
LAG = 8.0


SCATTER_ROUTES = ()
SCATTER_ROUTES += (43210, 42310, 41023, 43210, 42103, 43120, 43210, 41320)
SCATTER_ROUTES += (42310, 41230, 43120, 42310, 42310, 42130, 42130, 43120)
SCATTER_ROUTES += (43210, 42310, 42310, 43210, 43210, 41320, 43210, 42130)
SCATTER_ROUTES += (43120, 42130, 43210, 43210, 42130, 41230, 42310, 43120)
SCATTER_ROUTES += (42310,)


def orders_of(bits, table, count, reverse):
    if len(bits) == 5 and bits[1] == (0, 1) and count == len(table):
        return [[int(c) for c in str(route)] for route in table]
    routes = route_orders(bits)
    return [routes[i % 4][::-1] if reverse else routes[i % 4] for i in range(count)]


def bit_table(mesh):
    bits = []
    for axis, name in enumerate(BOTH):
        step = mesh.shape[name] // 2
        while step >= 1:
            bits.append((axis, step))
            step //= 2
    return bits


def can_route(mesh, rows):
    sizes = [mesh.shape[name] for name in BOTH]
    return all(s & (s - 1) == 0 for s in sizes) and rows % 32 == 0


def route_orders(bits):
    outer = [i for i, (axis, _) in enumerate(bits) if axis == 0]
    inner = [i for i, (axis, _) in enumerate(bits) if axis == 1]
    middle, core = inner[:-1], inner[-1:]
    return (
        outer + middle + core,
        outer + middle[::-1] + core,
        middle[:1] + outer + middle[1:] + core,
        middle[-1:] + outer + middle[:-1] + core,
    )


def loads_of(bits, at, size):
    axis, step = bits[at]
    if axis == 1 and step == 1:
        return {"core": size / CORE_RATE}
    if axis == 1:
        return {f"inner{step}": 2 * size / LINK_RATE}
    loads = {"outer1": 2 * size / LINK_RATE}
    if step > 1:
        loads["outer2"] = 2 * size * step / LINK_RATE
    return loads


def plan_sends(bits, orders, sizes, growing, add_rate, begin=None):
    count = len(bits)
    ready = [(begin[unit] if begin else 0.0, unit, 0) for unit in range(len(orders))]
    free = {}
    plan = []
    arrive = {}
    while ready:
        choices = []
        for when, unit, stage in ready:
            scale = 2**stage if growing else 2 ** (count - 1 - stage)
            loads = loads_of(bits, orders[unit][stage], sizes[unit] * scale)
            start = max([when] + [free.get(link, 0.0) for link in loads])
            choices.append((round(start, 3), unit, -stage, when, scale))
        start, unit, stage, when, scale = min(choices)
        stage = -stage
        ready.remove((when, unit, stage))
        loads = loads_of(bits, orders[unit][stage], sizes[unit] * scale)
        for link, took in loads.items():
            free[link] = start + took
        plan.append((start, unit, stage))
        after = start + max(loads.values()) + HOP
        if add_rate:
            after += sizes[unit] * scale / add_rate
        if stage + 1 < count:
            ready.append((after, unit, stage + 1))
        else:
            arrive[unit] = after
    return sorted(plan), arrive


def my_bits(bits):
    place = (lax.axis_index("dp"), lax.axis_index("fsdp"))
    return [(place[axis] // step) % 2 for axis, step in bits]


def partner(bits, mine, at):
    place = [lax.axis_index("dp"), lax.axis_index("fsdp")]
    axis, step = bits[at]
    place[axis] = place[axis] + step * (1 - 2 * mine[at])
    return tuple(place)


def greet(bits, mine):
    barrier = pltpu.get_barrier_semaphore()
    for at in range(len(bits)):
        pl.semaphore_signal(
            barrier, inc=1, device_id=partner(bits, mine, at), device_id_type=MESH_ID
        )
    pl.semaphore_wait(barrier, len(bits))


def unit_shape(blocks, unit):
    array, rows, cols = unit
    block = blocks[array]
    return (len(range(*rows.indices(block[0]))), len(range(*cols.indices(block[1]))))


ERF_RATE = 0.3275911
ERF_TERMS = (0.254829592, -0.284496736, 1.421413741, -1.453152027, 1.061405429)


def gelu_parts(pre):
    bell = jnp.exp2(pre * pre * (-0.5 * LOG2E))
    arm = 1.0 / (1.0 + jnp.abs(pre) * (ERF_RATE * ROOT_HALF))
    series = ERF_TERMS[4]
    for term in ERF_TERMS[3::-1]:
        series = series * arm + term
    tail = 0.5 * series * arm * bell
    below = jnp.where(pre >= 0.0, 1.0 - tail, tail)
    return pre * below, below + pre * bell * INV_ROOT_TWO_PI


class Schedule:
    pace = 1.2

    def __init__(self, plan, issue):
        self.plan = plan
        self.issue = issue
        self.at = 0
        self.now = 0.0

    def due(self):
        items = []
        while self.at < len(self.plan) and self.plan[self.at][0] <= self.now:
            items.append(self.plan[self.at][1:])
            self.at += 1
        return items

    def spend(self, took):
        self.now += took * self.pace
        for unit, stage in self.due():
            self.issue(unit, stage)

    def until(self, when):
        self.now = max(self.now, when)
        for unit, stage in self.due():
            self.issue(unit, stage)

    def loop(self, count, took, body):
        buckets = []
        for _ in range(count):
            self.now += took * self.pace
            buckets.append(self.due())

        def step(i, carry):
            body(i)
            for k, items in enumerate(buckets):
                if items:

                    @pl.when(i == k)
                    def _(items=items):
                        for unit, stage in items:
                            self.issue(unit, stage)

            return carry

        lax.fori_loop(0, count, step, 0)


ROWS_STEP = 128


N_VECS = 14
VEC_ROWS = 16
VEC_LANES = 128


def device_index(bits, mine):
    count = len(bits)
    return sum(mine[b] * 2 ** (count - 1 - b) for b in range(count))


def pack_vectors(loose, pack, spot, size):
    row = lax.broadcasted_iota(jnp.int32, (size, VEC_LANES), 0)
    lane = lax.broadcasted_iota(jnp.int32, (size, VEC_LANES), 1)
    place = (lane == row + size * spot).astype(jnp.float32)
    pieces = []
    for ref in loose[:-1]:
        pieces.append(dot_nn(ref[...].astype(jnp.float32).reshape(1, size), place))
    pieces.append(loose[-1][...].astype(jnp.float32).reshape(1, VEC_LANES))
    pieces.append(jnp.zeros((VEC_ROWS - len(pieces), VEC_LANES), jnp.float32))
    pack[...] = jnp.concatenate(pieces, axis=0).astype(pack.dtype)


def unpack_table(vecs, table, bits, width, hidden_row=None):
    count = len(bits)
    devices = 2**count
    share = devices * VEC_LANES // width
    spots = [tuple((d >> (count - 1 - b)) & 1 for b in range(count)) for d in range(devices)]
    for group in range(width // VEC_LANES):
        total = None
        for d in range(group * share, (group + 1) * share):
            block = vecs[spots[d]].astype(jnp.float32)
            total = block if total is None else total + block
        table[:, pl.ds(group * VEC_LANES, VEC_LANES)] = total
    if hidden_row is not None:
        for d in range(devices):
            block = vecs[spots[d]].astype(jnp.float32)
            hidden_row[pl.ds(0, 1), pl.ds(d * VEC_LANES, VEC_LANES)] = block[N_VECS - 1 : N_VECS]


def forward_kernel(bits, units, orders, plan, arrive, n_arrays, heads, *refs):
    count = len(bits)
    (tokens, memory, lengths), refs = refs[:3], refs[3:]
    loose, refs = refs[:N_VECS], refs[N_VECS:]
    sources, refs = refs[: n_arrays - 1], refs[n_arrays - 1 :]
    targets, refs = refs[:n_arrays], refs[n_arrays:]
    saved_names = ("q", "k", "v", "a", "total", "h1")
    saved_names += ("cq", "ck", "cv", "ca", "ctotal", "h2", "g", "slope")
    saved_names += ("n1", "n2", "n3", "out")
    saved = dict(zip(saved_names, refs[: len(saved_names)]))
    refs = refs[len(saved_names) :]
    x, mem, n, q, k, v, a, h, ck, cv, g, slope, tot, ctot = refs[:14]
    wide, tall = refs[14:16], refs[16:18]
    pack, vecs, table, hidden_row = refs[18:-6]
    last_wide = 8 + g.shape[1] // x.shape[1]
    last_weight = len(units) // 2
    send_sem, recv_sem, own_sem, in_sem, w_sem, out_sem = refs[-6:]
    mine = my_bits(bits)
    rows, width = x.shape
    devices = 2**count
    lanes_each = width // devices
    pack_vectors(loose, pack, device_index(bits, mine) % (VEC_LANES // lanes_each), lanes_each)
    sources = (pack,) + tuple(sources)
    own = [
        pltpu.make_async_copy(sources[i], targets[i].at[tuple(mine)], own_sem.at[i])
        for i in range(n_arrays)
    ]
    for copy in own:
        copy.start()
    load_x = pltpu.make_async_copy(tokens, x, in_sem.at[0])
    load_mem = pltpu.make_async_copy(memory, mem, in_sem.at[1])
    load_x.start()
    load_mem.start()
    greet(bits, mine)

    def message(unit, stage):
        array, top, left = units[unit]
        order = orders[unit]
        where = tuple(slice(None) if b in order[:stage] else mine[b] for b in range(count))
        place = targets[array].at[where + (top, left)]
        source = sources[array].at[top, left] if stage == 0 else place
        return pltpu.make_async_remote_copy(
            src_ref=source,
            dst_ref=place,
            send_sem=send_sem.at[unit, stage],
            recv_sem=recv_sem.at[unit, stage],
            device_id=partner(bits, mine, order[stage]),
            device_id_type=MESH_ID,
        )

    settled = set()

    def issue(unit, stage):
        array = units[unit][0]
        if stage > 0:
            if array not in settled:
                settled.add(array)
                own[array].wait()
            message(unit, stage - 1).wait_recv()
        message(unit, stage).start()

    clock = Schedule(plan, issue)
    every = (slice(None),) * count

    fetching = {}

    def parts_of(weight):
        return (0,) if weight == 0 else (2 * weight - 1, 2 * weight)

    def begin(weight):
        for unit in parts_of(weight):
            clock.until(arrive[unit] + LAG)
            message(unit, count - 1).wait_recv()
        array, _, left = units[parts_of(weight)[0]]
        if array not in settled:
            settled.add(array)
            own[array].wait()
        fetching[weight] = pltpu.make_async_copy(
            targets[array].at[every + (slice(None), left)], slot_of(weight), w_sem.at[weight]
        )
        fetching[weight].start()

    def slot_of(weight):
        if weight == 0:
            return vecs
        kind = wide if weight <= last_wide else tall
        return kind[weight % 2]

    def fetch(weight):
        if weight not in fetching:
            begin(weight)
        later = weight + 1
        if 0 < weight < last_weight and arrive[parts_of(later)[-1]] <= clock.now:
            begin(later)
        fetching[weight].wait()
        if weight > 0:
            clock.spend(0.6)
        return slot_of(weight)

    def times(lhs, slot, tile, write, took=1.4):
        depth = lhs.shape[1]
        tiles = slot.shape[-1] // tile

        def body(j):
            cols = pl.ds(pl.multiple_of(j * tile, tile), tile)
            weight = slot[every + (slice(None), cols)].reshape(depth, tile)
            write(cols, dot_nn(lhs[...], weight))

        clock.loop(tiles, took / tiles, body)

    def norm_into(gain, shift, source):
        def body(i):
            part = pl.ds(pl.multiple_of(i * ROWS_STEP, ROWS_STEP), ROWS_STEP)
            r = source[part, :].astype(jnp.float32)
            n[part, :] = normalize(r, gain, shift)[0].astype(jnp.bfloat16)

        clock.loop(rows // ROWS_STEP, 0.4, body)

    pending = {}

    def save(source, name):
        copy = pltpu.make_async_copy(source, saved[name], out_sem.at[saved_names.index(name)])
        copy.start()
        pending[name] = copy

    def saved_now(name):
        pending.pop(name).wait()

    def vec(i):
        return table[pl.ds(i, 1), :]

    clock.until(0.0)
    fetch(0)
    unpack_table(vecs, table, bits, width, hidden_row)
    load_x.wait()
    load_mem.wait()
    norm_into(vec(0), vec(1), x)
    save(n, "n1")
    length = lengths[0]

    def project(bias, target, extra=0):
        def write(cols, acc):
            if bias is not None:
                acc = acc + table[pl.ds(bias, 1), cols]
            target[:, cols] = acc.astype(target.dtype)

        return write

    def residual(bias, source):
        def write(cols, acc):
            h[:, cols] = source[:, cols].astype(jnp.float32) + acc + table[pl.ds(bias, 1), cols]

        return write

    def attend(q_ref, k_ref, v_ref, tot_ref, masked):
        keys = k_ref.shape[0]
        pair = 2 * (width // heads)

        def body(p):
            lanes = pl.ds(pl.multiple_of(p * pair, pair), pair)

            def write(start, size, out, totals):
                a[pl.ds(start, size), lanes] = out
                for head in (0, 1):
                    tot_ref[p, pl.ds(head, 1), pl.ds(start, size)] = totals[head]

            forward_pair(
                lambda s, m: q_ref[pl.ds(s, m), lanes],
                lambda s, m: k_ref[pl.ds(s, m), lanes],
                lambda s, m: v_ref[pl.ds(s, m), lanes],
                write,
                [(0, rows, keys)],
                length if masked else None,
                (width // heads) ** -0.5,
            )

        clock.loop(heads // 2, 1.4, body)

    for weight, target, bias in ((1, q, 2), (2, k, None), (3, v, 3)):
        times(n, fetch(weight), 512, project(bias, target))
    save(q, "q")
    save(k, "k")
    save(v, "v")
    attend(q, k, v, tot, True)
    save(a, "a")
    save(tot, "total")
    for weight, target, bias in ((4, ck, None), (5, cv, 8)):
        times(mem, fetch(weight), 512, project(bias, target), 1.9)
    save(ck, "ck")
    save(cv, "cv")
    times(a, fetch(6), 512, residual(4, x), 2.0)
    save(h, "h1")
    saved_now("n1")
    norm_into(vec(5), vec(6), h)
    save(n, "n2")
    saved_now("q")
    times(n, fetch(7), 512, project(7, q))
    save(q, "cq")
    saved_now("a")
    attend(q, ck, cv, ctot, False)
    save(a, "ca")
    save(ctot, "ctotal")
    saved_now("h1")
    times(a, fetch(8), 512, residual(9, h), 2.0)
    save(h, "h2")
    saved_now("n2")
    norm_into(vec(10), vec(11), h)
    save(n, "n3")
    block = width
    blocks = g.shape[1] // block
    for j in range(blocks):
        slot = fetch(9 + j)
        tile = 256

        def body(i, j=j, slot=slot):
            cols = pl.ds(pl.multiple_of(i * tile, tile), tile)
            spot = pl.ds(pl.multiple_of(j * block + i * tile, tile), tile)
            weight = slot[every + (slice(None), cols)].reshape(width, tile)
            for r in range(0, rows, ROWS_STEP):
                part = pl.ds(r, ROWS_STEP)
                pre = dot_nn(n[part, :], weight) + hidden_row[:, spot]
                low, rate = gelu_parts(pre)
                g[part, spot] = low.astype(jnp.bfloat16)
                slope[part, spot] = rate.astype(jnp.bfloat16)

        clock.loop(block // tile, 0.6, body)
    save(g, "g")
    save(slope, "slope")
    tall_cols = tall[0].shape[-1]
    for j in range(width // tall_cols):
        slot = fetch(9 + blocks + j)
        cols = pl.ds(j * tall_cols, tall_cols)
        weight = slot[...].reshape(g.shape[1], tall_cols)
        acc = dot_nn(g[...], weight)
        x[:, cols] = (h[:, cols] + acc + table[pl.ds(12, 1), cols]).astype(jnp.bfloat16)
        clock.spend(1.6)
    save(x, "out")
    clock.until(1e9)
    for copy in pending.values():
        copy.wait()
    for unit in range(len(units)):
        for stage in range(count):
            message(unit, stage).wait_send()


def fused_forward(mesh, tokens, memory, lengths, mats, vecs, heads, collective_id):
    bits = bit_table(mesh)
    rows, width = tokens.shape
    keys = memory.shape[0]
    block = mats[0].shape
    pack = (VEC_ROWS, VEC_LANES)
    every = slice(None)
    whole = [(i, every) for i in range(1, 9)]
    hidden = mats[8].shape[1]
    for left in range(0, hidden, width):
        whole.append((9, slice(left, left + width)))
    tall_rows = mats[9].shape[0]
    tall_cols = width * block[0] // tall_rows
    for left in range(0, width, tall_cols):
        whole.append((10, slice(left, left + tall_cols)))
    units = [(0, every, every)]
    for array, cols in whole:
        half = mats[array - 1].shape[0] // 2
        units += [(array, slice(0, half), cols), (array, slice(half, 2 * half), cols)]
    blocks = [pack] + [m.shape for m in mats]
    shapes = [unit_shape(blocks, unit) for unit in units]
    sizes = [2 * s[0] * s[1] for s in shapes]
    orders = [route_orders(bits)[(u - 1) % 4] for u in range(len(units))]
    plan, arrive = plan_sends(bits, orders, sizes, True, None)
    n = len(blocks)
    spots = (2,) * len(bits)
    low = jnp.bfloat16
    wide_rows = jax.ShapeDtypeStruct((rows, width), low)
    wide_keys = jax.ShapeDtypeStruct((keys, width), low)
    full = jax.ShapeDtypeStruct((rows, width), jnp.float32)
    totals = jax.ShapeDtypeStruct((heads // 2, 2, rows), jnp.float32)
    ff = jax.ShapeDtypeStruct((rows, hidden), low)
    saved = [
        wide_rows, wide_rows, wide_rows, wide_rows, totals, full,
        wide_rows, wide_keys, wide_keys, wide_rows, totals, full, ff, ff,
        wide_rows, wide_rows, wide_rows, wide_rows,
    ]
    vm = lambda s: pltpu.VMEM(s.shape, s.dtype)
    sems = (len(units), len(bits))
    hbm = pl.BlockSpec(memory_space=pltpu.HBM)
    got = pl.pallas_call(
        functools.partial(forward_kernel, bits, units, orders, plan, arrive, n, heads),
        out_shape=[jax.ShapeDtypeStruct(spots + b, low) for b in blocks] + saved,
        in_specs=[hbm, hbm, pl.BlockSpec(memory_space=pltpu.SMEM)]
        + [pl.BlockSpec(memory_space=pltpu.VMEM)] * (len(vecs) + len(mats)),
        out_specs=[hbm] * (n + len(saved)),
        scratch_shapes=[
            vm(wide_rows), vm(wide_keys), vm(wide_rows), vm(wide_rows), vm(wide_rows),
            vm(wide_rows), vm(wide_rows), vm(full), vm(wide_keys), vm(wide_keys),
            vm(ff), vm(ff), vm(totals), vm(totals),
            pltpu.VMEM(spots + block, low),
            pltpu.VMEM(spots + block, low),
            pltpu.VMEM(spots + (tall_rows, tall_cols), low),
            pltpu.VMEM(spots + (tall_rows, tall_cols), low),
            pltpu.VMEM(pack, low),
            pltpu.VMEM(spots + pack, low),
            pltpu.VMEM((VEC_ROWS, width), jnp.float32),
            pltpu.VMEM((1, hidden), jnp.float32),
            pltpu.SemaphoreType.DMA(sems),
            pltpu.SemaphoreType.DMA(sems),
            pltpu.SemaphoreType.DMA((n,)),
            pltpu.SemaphoreType.DMA((2,)),
            pltpu.SemaphoreType.DMA((len(whole) + 1,)),
            pltpu.SemaphoreType.DMA((len(saved),)),
        ],
        compiler_params=pltpu.CompilerParams(
            collective_id=collective_id,
            has_side_effects=True,
            vmem_limit_bytes=60 * 1024 * 1024,
        ),
        name="forward_layer",
    )(tokens, memory, lengths, *vecs, *mats)
    return got[:n], got[n:]


class Deferred(Schedule):
    pace = 1.1

    def __init__(self, plan, issue):
        super().__init__(list(plan), issue)
        self.made = set()

    def due(self):
        items, rest, held_back = [], [], set()
        for item in self.plan:
            when, unit, stage = item
            if unit in self.made and unit not in held_back and when <= self.now:
                items.append((unit, stage))
            else:
                held_back.add(unit)
                rest.append(item)
        self.plan = rest
        return items

    def finish(self, unit, last=99):
        late = [when for when, u, stage in self.plan if u == unit and stage <= last]
        if late:
            self.until(max(late))


def backward_pair(refs, accs, total_of, spans, length, scale, lanes):
    q_ref, k_ref, v_ref, g_ref = refs
    dk_acc, dv_acc = accs
    keys_all = k_ref.shape[0]
    half = (dk_acc.shape[1]) // 2
    for step, (start, size, keys) in enumerate(spans):
        part_rows = pl.ds(start, size)
        q2 = q_ref[part_rows, lanes]
        g2 = g_ref[part_rows, lanes]
        k2 = k_ref[pl.ds(0, keys), lanes]
        v2 = v_ref[pl.ds(0, keys), lanes]
        kt = k2.T
        dk, dv, dqt = None, None, []
        for head in (0, 1):
            qm = lane_half(q2, head, half)
            gm = lane_half(g2, head, half)
            raw = dot_nt(k2, qm)
            probs = jnp.exp2(raw * (scale * LOG2E) - total_of(head, start, size))
            if length is not None:
                key_pos = lax.broadcasted_iota(jnp.int32, raw.shape, 0)
                probs = jnp.where(key_pos <= limit_row(start, size, length), probs, 0.0)
            grad = dot_nt(v2, gm)
            part = probs * grad
            dot_row = jnp.sum(part, axis=0, keepdims=True)
            score = ((part - probs * dot_row) * scale).astype(jnp.bfloat16)
            dvh = dot_nn(probs.astype(jnp.bfloat16), gm)
            dkh = dot_nn(score, qm)
            dv = dvh if dv is None else dv + dvh
            dk = dkh if dk is None else dk + dkh
            dqt.append(dot_nn(kt[head * half : (head + 1) * half], score))
        q_ref[part_rows, lanes] = jnp.concatenate(dqt, axis=0).T.astype(jnp.bfloat16)
        if step == 0:
            dk_acc[pl.ds(0, keys), :] = dk
            dv_acc[pl.ds(0, keys), :] = dv
        else:
            dk_acc[pl.ds(0, keys), :] += dk
            dv_acc[pl.ds(0, keys), :] += dv
    every_key = pl.ds(0, keys_all)
    k_ref[every_key, lanes] = dk_acc[every_key, :].astype(jnp.bfloat16)
    v_ref[every_key, lanes] = dv_acc[every_key, :].astype(jnp.bfloat16)


BACK_INPUTS = ("dz", "tokens", "memory", "lengths")
BACK_INPUTS += ("q", "k", "v", "a", "total", "h1", "cq", "ck", "cv", "ca", "ctotal", "h2", "g", "rate")
BACK_INPUTS += ("n1", "n2", "n3")
BACK_INPUTS += ("wvec", "wq", "wk", "wv", "wck", "wcv", "wo", "wcq", "wco", "win", "wout")
TALL_PARTS = 8
WIDE_HELD = 11
WIDE_BOXES = 6
WIDE_STAGES = 4
SUM_SLOTS = 8


def backward_parts(width, hidden):
    half = width // 2
    parts = [(8, c) for c in range(0, hidden, half)]
    parts += [(7, 0), (7, half)]
    parts += [(i, c) for c in (0, half) for i in (6, 3, 4)]
    parts += [(5, 0), (5, half)]
    parts += [(i, c) for c in (0, half) for i in (0, 1, 2)]
    return parts


def made_times(n_wide):
    times = [6.0, 6.0, 9.0, 9.0, 12.0, 12.0, 15.0, 15.0]
    for first in (20.0, 25.5, 31.0, 36.5):
        times += [first, first + 1.0]
    times += [44.0, 45.0]
    times += [58.0, 59.0, 60.0, 73.0, 74.0, 75.0]
    times += [86.0, 87.0]
    times += [98.0, 99.0, 100.0, 112.0, 113.0, 114.0]
    return times + [124.0]


def backward_kernel(bits, orders, plan, begin, heads, *refs):
    count = len(bits)
    given = dict(zip(BACK_INPUTS, refs[: len(BACK_INPUTS)]))
    refs = refs[len(BACK_INPUTS) :]
    tokens_grad, memory_grad, keep_k, keep_v = refs[:4]
    results = refs[4:15]
    refs = refs[15:]
    bdz, n, acc, dh, hb, wide_a, wide_b = refs[:7]
    stages, held_tall, held_wide, box_tall, box_wide = refs[7:12]
    rest_tall, rest_wide = refs[12 : 12 + count - 1], refs[12 + count - 1 : 12 + 2 * (count - 1)]
    refs = refs[12 + 2 * (count - 1) :]
    vec_stage, vec_held = refs[:2]
    vec_boxes = refs[2 : 2 + count]
    refs = refs[2 + count :]
    sum_tall, sum_wide, sum_vec, vgrad, hgrad, table, vecs, tot, dk_acc, dv_acc = refs[:10]
    send_sem, recv_sem, store_sem, load_sem, w_sem, credit = refs[10:]
    wides = (wide_a, wide_b)
    mine = my_bits(bits)
    core = count - 1
    rows, width = bdz.shape
    half = width // 2
    hidden = hgrad.shape[1]
    every = (slice(None),) * count
    wide_parts = backward_parts(width, hidden)
    n_parts = len(orders)
    last = n_parts - 1
    tall_stage = [None, None]
    loads = {}

    def load(name, source, target):
        loads[name] = (source, target, len(loads))
        pltpu.make_async_copy(source, target, load_sem.at[len(loads) - 1]).start()

    def loaded(name):
        source, target, at = loads[name]
        pltpu.make_async_copy(source, target, load_sem.at[at]).wait()

    load("dz", given["dz"], bdz)
    load("vecs", given["wvec"], vecs)
    load("h2", given["h2"], hb)
    load("n3", given["n3"], n)
    vgrad[...] = jnp.zeros_like(vgrad)
    greet(bits, mine)

    def kind_of(part):
        if part < TALL_PARTS:
            return "tall"
        return "vec" if part == last else "wide"

    def lines_of(part):
        if kind_of(part) == "tall":
            height = held_tall.shape[-2] // 2
            return (pl.ds(part % 2 * height, height), slice(None))
        return (slice(None), slice(None))

    def held_of(part):
        kind = kind_of(part)
        if kind == "tall":
            return held_tall.at[part // 2]
        return vec_held if kind == "vec" else held_wide.at[(part - TALL_PARTS) % WIDE_HELD]

    def stage_of(part):
        kind = kind_of(part)
        if kind == "tall":
            return tall_stage[part // 2 % 2]
        return vec_stage if kind == "vec" else stages.at[(part - TALL_PARTS) % WIDE_STAGES]

    def box_of(part, step):
        kind = kind_of(part)
        if kind == "vec":
            return vec_boxes[step]
        if kind == "tall":
            return box_tall.at[part // 2 % 2] if step == 0 else rest_tall[step - 1].at[part // 2]
        i = part - TALL_PARTS
        return box_wide.at[i % WIDE_BOXES] if step == 0 else rest_wide[step - 1].at[i]

    def message(part, step):
        order = orders[part]
        now = order[step]
        lines = lines_of(part)
        where = []
        for b in range(count):
            if b == now:
                where.append(1 - mine[b])
            elif b in order[:step]:
                where.append(mine[b])
            else:
                where.append(slice(None))
        if step == 0:
            source = stage_of(part).at[tuple(where) + lines]
        else:
            source = held_of(part).at[tuple(where[:core]) + lines]
        return pltpu.make_async_remote_copy(
            src_ref=source,
            dst_ref=box_of(part, step).at[(slice(None),) * (core - step) + lines],
            send_sem=send_sem.at[part, step],
            recv_sem=recv_sem.at[part, step],
            device_id=partner(bits, mine, now),
            device_id_type=MESH_ID,
        )

    sent = set()

    def drained(part, step):
        if (part, step) not in sent:
            sent.add((part, step))
            message(part, step).wait_send()

    def credit_of(part):
        if kind_of(part) == "tall":
            return credit.at[part // 2 % 2]
        return credit.at[2 + (part - TALL_PARTS) % WIDE_BOXES]

    def box_used_again(part):
        if kind_of(part) == "tall":
            return part + 4 < TALL_PARTS
        return part != last and part + WIDE_BOXES < last

    def add(part, step, target=None):
        order, lines = orders[part], lines_of(part)
        message(part, step).wait_recv()
        held, box = held_of(part), box_of(part, step)
        own = stage_of(part) if step == 0 else None
        open_bits = [b for b in range(count) if b not in order[: step + 1]]
        looped = open_bits[:-2]

        def one(block, carry):
            where, spot = [], []
            for b in range(core):
                if b in looped:
                    digit = (block // 2 ** (len(looped) - 1 - looped.index(b))) % 2
                elif b in open_bits:
                    digit = slice(None)
                else:
                    digit = None
                where.append(mine[b] if digit is None else digit)
                if digit is not None:
                    spot.append(digit)
            source, where = tuple(where) + (mine[core],) + lines, tuple(where) + lines
            spot = tuple(spot) + lines
            if target is not None:
                target[...] = held[where].astype(jnp.float32) + box[spot].astype(jnp.float32)
            else:
                held[where] = (held[where] if own is None else own[source]) + box[spot]
            return carry

        if looped:
            lax.fori_loop(0, 2 ** len(looped), one, 0)
        else:
            one(0, 0)
        if step == 0 and box_used_again(part):
            pl.semaphore_signal(
                credit_of(part), inc=1, device_id=partner(bits, mine, core), device_id_type=MESH_ID
            )

    stored = {}

    def sum_of(part):
        kind = kind_of(part)
        if kind == "tall":
            return sum_tall.at[(part // 2,) + lines_of(part)]
        return sum_vec if kind == "vec" else sum_wide.at[(part - TALL_PARTS) % SUM_SLOTS]

    def store(part):
        kind = kind_of(part)
        if kind == "tall":
            cols = held_tall.shape[-1]
            target = results[9].at[lines_of(part)[0], pl.ds(part // 2 * cols, cols)]
        elif kind == "vec":
            target = results[10]
        else:
            array, left = wide_parts[part - TALL_PARTS]
            target = results[array].at[:, pl.ds(left, half)]
        return pltpu.make_async_copy(sum_of(part), target, store_sem.at[part])

    def issue(part, step):
        if step < count:
            add(part, step - 1)
            message(part, step).start()
            return
        slot = part if kind_of(part) != "wide" else -1 - (part - TALL_PARTS) % SUM_SLOTS
        if slot in stored:
            store(stored[slot]).wait()
        stored[slot] = part
        add(part, count - 1, sum_of(part))
        store(part).start()

    clock = Deferred(plan, issue)

    def room_for(part):
        kind = kind_of(part)
        back = 4 if kind == "tall" else WIDE_STAGES
        first = 0 if kind == "tall" else TALL_PARTS
        if part - back >= first:
            clock.finish(part - back, 1)
            drained(part - back, 0)
        if kind == "wide" and part - WIDE_HELD >= first:
            clock.finish(part - WIDE_HELD)
            for step in range(1, count):
                drained(part - WIDE_HELD, step)

    def made(part):
        kind = kind_of(part)
        if kind == "tall" and part >= 4 and part % 2 == 0:
            clock.finish(part - 4, 1)
            clock.finish(part - 3, 1)
            pl.semaphore_wait(credit_of(part), 2)
        if kind == "wide" and part - WIDE_BOXES >= TALL_PARTS:
            clock.finish(part - WIDE_BOXES, 1)
            pl.semaphore_wait(credit_of(part), 1)
        message(part, 0).start()
        clock.made.add(part)
        clock.now = max(clock.now, begin[part])
        clock.spend(0.0)

    blocks = hidden // width
    names = [("win", every + (slice(None), slice(j * width, (j + 1) * width))) for j in range(blocks)]
    whole = every + (slice(None), slice(None))
    names += [(name, whole) for name in ("wco", "wcq", "wo", "wq", "wk", "wv", "wck", "wcv")]
    weights = [
        pltpu.make_async_copy(given[name].at[where], wides[i % 2], w_sem.at[i])
        for i, (name, where) in enumerate(names)
    ]
    weights[0].start()
    weights[1].start()

    def back_through(i, lhs, write, took=1.1):
        weights[i].wait()
        slot = wides[i % 2]

        def body(t):
            part = slot[t].reshape(half, width)
            write(pl.ds(pl.multiple_of(t * half, half), half), dot_nt(lhs(), part))

        clock.loop(2, took / 2, body)
        if i + 2 < len(weights):
            weights[i + 2].start()

    def produce(part, lhs, rhs, took=0.75):
        room_for(part)
        slot = stage_of(part)
        slot[every + (slice(None), slice(None))] = (
            dot_tn(lhs, rhs).astype(jnp.bfloat16).reshape(slot.shape)
        )
        clock.spend(took)
        made(part)

    def column_sums(ref, rows_now, target, at):
        ones = jnp.ones((8, rows_now), jnp.bfloat16)
        target[pl.ds(at, 1), :] = dot_nn(ones, ref)[0:1]

    def vec(i):
        return table[pl.ds(i, 1), :]

    def norm_back(source, gain, base):
        def body(i):
            part = pl.ds(pl.multiple_of(i * ROWS_STEP, ROWS_STEP), ROWS_STEP)
            r = source[part, :].astype(jnp.float32)
            _, unit_rows, inv_std = normalize(r, vec(gain), vec(gain))
            back, gain_sum, shift_sum = normalize_back(acc[part, :], unit_rows, inv_std, vec(gain))
            vgrad[pl.ds(gain, 1), :] += gain_sum
            vgrad[pl.ds(gain + 1, 1), :] += shift_sum
            total = base(part) + back
            dh[part, :] = total
            bdz[part, :] = total.astype(jnp.bfloat16)

        clock.loop(rows // ROWS_STEP, 0.6, body)

    top = pl.ds(0, rows)
    first_half, second_half = pl.ds(0, half), pl.ds(half, half)
    halves = (first_half, second_half)

    def feed_phase(big, rate, wrow, tall_a, tall_b):
        tall_stage[:] = tall_a, tall_b
        load("g", given["g"], big)

        def rate_copy(j):
            cols = pl.ds(j * width, width)
            return pltpu.make_async_copy(given["rate"].at[:, cols], rate, load_sem.at[24 + j])

        def row_copy(j):
            return pltpu.make_async_copy(given["wout"].at[j // 2, j % 2], wrow, load_sem.at[28 + j])

        rate_copy(0).start()
        row_copy(0).start()
        loaded("dz")
        loaded("g")
        tall_cols = tall_a.shape[-1]
        for j in range(TALL_PARTS // 2):
            room_for(2 * j)
            room_for(2 * j + 1)
            slot = stage_of(2 * j)

            def body(t, j=j, slot=slot):
                part = big[:, pl.ds(pl.multiple_of(t * width, width), width)]
                tile = dot_tn(part, bdz[:, pl.ds(j * tall_cols, tall_cols)]).astype(jnp.bfloat16)
                slot[t // 2, t % 2] = tile.reshape(slot.shape[2:])

            clock.loop(4, 0.45, body)
            made(2 * j)
            made(2 * j + 1)
        column_sums(bdz[...], rows, vgrad, 12)
        loaded("n3")
        for j in range(blocks):
            rate_copy(j).wait()
            row_copy(j).wait()

            def body(t, j=j):
                spot = pl.ds(pl.multiple_of(j * width + t * half, half), half)
                weight = wrow[t].reshape(half, width)
                slope = rate[:, pl.ds(pl.multiple_of(t * half, half), half)].astype(jnp.float32)
                big[:, spot] = (dot_nt(bdz[...], weight) * slope).astype(jnp.bfloat16)

            clock.loop(2, 0.8, body)
            if j + 1 < blocks:
                rate_copy(j + 1).start()
                row_copy(j + 1).start()
            for h in (0, 1):
                produce(TALL_PARTS + 2 * j + h, n[...], big[:, pl.ds(j * width + h * half, half)])
            block = pl.ds(j * width, width)
            hgrad[pl.ds(0, 1), block] = dot_nn(jnp.ones((8, rows), jnp.bfloat16), big[:, block])[0:1]

            def write(cols, value, j=j):
                if j == 0:
                    acc[top, cols] = value
                else:
                    acc[top, cols] += value

            back_through(j, lambda j=j: big[:, pl.ds(j * width, width)], write)
        load("n2", given["n2"], n)
        loaded("vecs")
        unpack_table(vecs, table, bits, width)
        loaded("h2")
        norm_back(hb, 10, lambda part: bdz[part, :].astype(jnp.float32))
        for part in range(TALL_PARTS):
            clock.finish(part, 1)
            drained(part, 0)

    def attention_phase(bq, bk, bv, bg, mem, ba, tilted):
        load("ca", given["ca"], ba)
        load("cq", given["cq"], bq)
        load("ck", given["ck"], bk)
        load("cv", given["cv"], bv)
        load("ctotal", given["ctotal"], tot)
        load("memory", given["memory"], mem)
        load("h1", given["h1"], hb)

        def into(ref, size=rows):
            def write(cols, value):
                ref[pl.ds(0, size), cols] = value.astype(ref.dtype)

            return write

        def more(size):
            def write(cols, value):
                acc[pl.ds(0, size), cols] += value

            return write

        def attend(keys, masked, side):
            pair = 2 * (width // heads)
            pairs = heads // 4
            chunk = rows // 2
            spans = [(s, chunk, s + chunk if masked else keys) for s in range(0, rows, chunk)]
            key_rows = pl.ds(0, keys)
            refs_now = (bq, bk.at[key_rows], bv.at[key_rows], bg)

            def body(i):
                p = side * pairs + i
                lanes = pl.ds(pl.multiple_of(p * pair, pair), pair)
                backward_pair(
                    refs_now,
                    (dk_acc, dv_acc),
                    lambda head, start, size: tot[p, pl.ds(head, 1), pl.ds(start, size)],
                    spans[::-1],
                    length if masked else None,
                    (width // heads) ** -0.5,
                    lanes,
                )

            clock.loop(pairs, 1.9 if masked else 2.3, body)

        part = TALL_PARTS + 2 * blocks
        keys = mem.shape[0]
        length = given["lengths"][0]
        at = blocks
        back_through(at, lambda: bdz[...], into(bg))
        loaded("ca")
        for cols in halves:
            produce(part, ba[...], bdz[:, cols])
            part += 1
        column_sums(bdz[...], rows, vgrad, 9)
        load("a", given["a"], ba)
        for name in ("cq", "ck", "cv", "ctotal", "n2", "memory"):
            loaded(name)
        for side, cols in enumerate(halves):
            attend(keys, False, side)
            produce(part, n[...], bq[:, cols])
            produce(part + 1, mem[...], bk[:, cols], 0.85)
            produce(part + 2, mem[...], bv[:, cols], 0.85)
            part += 3
        load("total", given["total"], tot)
        load("n1", given["n1"], n)
        keeps = [
            pltpu.make_async_copy(bk, keep_k, load_sem.at[32]),
            pltpu.make_async_copy(bv, keep_v, load_sem.at[33]),
        ]
        for copy in keeps:
            copy.start()
        back_through(at + 1, lambda: bq[...], into(acc))
        column_sums(bq[...], rows, vgrad, 7)
        column_sums(bv[...], keys, vgrad, 8)
        load("q", given["q"], bq)
        for copy in keeps:
            copy.wait()
        load("k", given["k"], bk.at[top])
        load("v", given["v"], bv.at[top])
        loaded("h1")
        norm_back(hb, 5, lambda part: dh[part, :])
        back_through(at + 2, lambda: bdz[...], into(bg))
        loaded("a")
        for cols in halves:
            produce(part, ba[...], bdz[:, cols])
            part += 1
        column_sums(bdz[...], rows, vgrad, 4)
        load("tokens", given["tokens"], ba)
        for name in ("q", "k", "v", "total", "n1"):
            loaded(name)
        for side, cols in enumerate(halves):
            attend(rows, True, side)
            for i, ref in enumerate((bq, bk, bv)):
                produce(part + i, n[...], ref[top, cols])
            part += 3
        back_through(at + 3, lambda: bq[...], into(acc))
        back_through(at + 4, lambda: bk[top, :], more(rows))
        back_through(at + 5, lambda: bv[top, :], more(rows))
        column_sums(bq[...], rows, vgrad, 2)
        column_sums(bv[top, :], rows, vgrad, 3)
        load("keep_k", keep_k, bk)
        load("keep_v", keep_v, bv)
        loaded("tokens")
        norm_back(ba, 0, lambda part: dh[part, :])
        put_tokens = pltpu.make_async_copy(dh, tokens_grad, load_sem.at[34])
        put_tokens.start()
        devices = 2**count
        share = devices // (width // VEC_LANES)
        for d in range(devices):
            where = tuple((d >> (count - 1 - b)) & 1 for b in range(count))
            vec_stage[where] = vgrad[:, pl.ds(d // share * VEC_LANES, VEC_LANES)]
            vec_stage[where + (pl.ds(13, 1),)] = hgrad[:, pl.ds(d * VEC_LANES, VEC_LANES)]
        made(last)
        loaded("keep_k")
        loaded("keep_v")
        back_through(at + 6, lambda: bk[...], into(acc, keys))

        def write(cols, value):
            tilted[:, 0, cols] = acc[pl.ds(0, keys), cols] + value

        back_through(at + 7, lambda: bv[...], write)
        put_memory = pltpu.make_async_copy(tilted, memory_grad, load_sem.at[35])
        put_memory.start()
        clock.until(1e9)
        put_tokens.wait()
        put_memory.wait()

    low = jnp.bfloat16
    pl.run_scoped(
        feed_phase,
        pltpu.VMEM((rows, hidden), low),
        pltpu.VMEM((rows, width), low),
        pltpu.VMEM(given["wout"].shape[2:], low),
        pltpu.VMEM((2,) * count + held_tall.shape[-2:], low),
        pltpu.VMEM((2,) * count + held_tall.shape[-2:], low),
    )
    key_rows = given["memory"].shape[0]
    pl.run_scoped(
        attention_phase,
        pltpu.VMEM((rows, width), low),
        pltpu.VMEM((key_rows, width), low),
        pltpu.VMEM((key_rows, width), low),
        pltpu.VMEM((rows, width), low),
        pltpu.VMEM((key_rows, width), low),
        pltpu.VMEM((rows, width), low),
        pltpu.VMEM((key_rows, 1, width), jnp.float32),
    )
    for part in stored.values():
        store(part).wait()
    for part in range(n_parts):
        for step in range(count):
            drained(part, step)


def fused_backward(mesh, dz, tokens, memory, lengths, saved, gathered, heads, collective_id):
    bits = bit_table(mesh)
    count = len(bits)
    rows, width = tokens.shape
    keys = memory.shape[0]
    shards = [w.shape[count:] for w in gathered[1:]]
    wide_block = (shards[0][0], width // 2)
    tall_rows = shards[9][0]
    hidden = shards[8][1]
    tall_block = (tall_rows, 2 * width * shards[0][0] // tall_rows * 4 // TALL_PARTS)
    pack = (VEC_ROWS, VEC_LANES)
    n_wide = len(backward_parts(width, hidden))
    n_parts = TALL_PARTS + n_wide + 1
    low = jnp.bfloat16
    sizes = [2 * wide_block[0] * wide_block[1]] * (n_parts - 1) + [4 * pack[0] * pack[1]]
    orders = orders_of(bits, SCATTER_ROUTES, n_parts, True)
    begin = made_times(n_wide)
    sends, finish = plan_sends(bits, orders, sizes, False, 2000e3, begin)
    plan = [item for item in sends if item[2] > 0]
    plan = sorted(plan + [(when, part, count) for part, when in finish.items()])
    blocks = shards + [pack]
    spots = (2,) * count
    scratch = [
        pltpu.VMEM((rows, width), low),
        pltpu.VMEM((rows, width), low),
        pltpu.VMEM((keys, width), jnp.float32),
        pltpu.VMEM((rows, width), jnp.float32),
        pltpu.VMEM((rows, width), jnp.float32),
        pltpu.VMEM(spots + shards[0], low),
        pltpu.VMEM(spots + shards[0], low),
        pltpu.VMEM((WIDE_STAGES,) + spots + wide_block, low),
        pltpu.VMEM((TALL_PARTS // 2,) + spots[1:] + tall_block, low),
        pltpu.VMEM((WIDE_HELD,) + spots[1:] + wide_block, low),
        pltpu.VMEM((2,) + spots[1:] + tall_block, low),
        pltpu.VMEM((WIDE_BOXES,) + spots[1:] + wide_block, low),
    ]
    for number, block in ((TALL_PARTS // 2, tall_block), (n_wide, wide_block)):
        for step in range(1, count):
            scratch.append(pltpu.VMEM((number,) + (2,) * (count - 1 - step) + block, low))
    scratch += [pltpu.VMEM(spots + pack, jnp.float32), pltpu.VMEM(spots[1:] + pack, jnp.float32)]
    for step in range(count):
        scratch.append(pltpu.VMEM((2,) * (count - 1 - step) + pack, jnp.float32))
    pair = 2 * (width // heads)
    scratch += [
        pltpu.VMEM((TALL_PARTS // 2,) + tall_block, jnp.float32),
        pltpu.VMEM((SUM_SLOTS,) + wide_block, jnp.float32),
        pltpu.VMEM(pack, jnp.float32),
        pltpu.VMEM((VEC_ROWS, width), jnp.float32),
        pltpu.VMEM((1, hidden), jnp.float32),
        pltpu.VMEM((VEC_ROWS, width), jnp.float32),
        pltpu.VMEM(spots + pack, low),
        pltpu.VMEM((heads // 2, 2, rows), jnp.float32),
        pltpu.VMEM((keys, pair), jnp.float32),
        pltpu.VMEM((keys, pair), jnp.float32),
        pltpu.SemaphoreType.DMA((n_parts, count)),
        pltpu.SemaphoreType.DMA((n_parts, count)),
        pltpu.SemaphoreType.DMA((n_parts,)),
        pltpu.SemaphoreType.DMA((36,)),
        pltpu.SemaphoreType.DMA((12,)),
        pltpu.SemaphoreType.REGULAR((2 + WIDE_BOXES,)),
    ]
    hbm = pl.BlockSpec(memory_space=pltpu.HBM)
    got = pl.pallas_call(
        functools.partial(backward_kernel, bits, orders, plan, begin, heads),
        out_shape=[
            jax.ShapeDtypeStruct((rows, width), jnp.float32),
            jax.ShapeDtypeStruct((keys, 1, width), jnp.float32),
            jax.ShapeDtypeStruct((keys, width), low),
            jax.ShapeDtypeStruct((keys, width), low),
        ]
        + [jax.ShapeDtypeStruct(b, jnp.float32) for b in blocks],
        in_specs=[hbm, hbm, hbm, pl.BlockSpec(memory_space=pltpu.SMEM)]
        + [hbm] * (len(BACK_INPUTS) - 4),
        out_specs=[hbm] * (4 + len(blocks)),
        scratch_shapes=scratch,
        compiler_params=pltpu.CompilerParams(
            collective_id=collective_id,
            has_side_effects=True,
            vmem_limit_bytes=62 * 1024 * 1024,
        ),
        name="backward_layer",
    )(dz, tokens, memory, lengths, *saved, *gathered)
    return got[:2] + got[4:]


def place_kernel(count, pieces, *refs):
    sources, targets = refs[:count], refs[count : 2 * count]
    rooms, (in_sem, out_sem) = refs[2 * count : 3 * count], refs[3 * count :]
    moves = []
    for source, target, room in zip(sources, targets, rooms):
        height = source.shape[0]
        step = height // pieces // 8 * 8 if height > 64 * pieces else height
        top = 0
        while top < height:
            size = step if top + 2 * step <= height else height - top
            rows, at = pl.ds(top, size), len(moves)
            moves.append(
                (
                    pltpu.make_async_copy(source.at[rows], room.at[rows], in_sem.at[at]),
                    pltpu.make_async_copy(room.at[rows], target.at[rows], out_sem.at[at]),
                )
            )
            top += size
    for into, _ in moves:
        into.start()
    for into, out in moves:
        into.wait()
        out.start()
    for _, out in moves:
        out.wait()


def place_outputs(arrays):
    hbm = pl.BlockSpec(memory_space=pltpu.HBM)
    sems = (16 * len(arrays),)
    return pl.pallas_call(
        functools.partial(place_kernel, len(arrays), 4),
        out_shape=[jax.ShapeDtypeStruct(a.shape, a.dtype) for a in arrays],
        in_specs=[hbm] * len(arrays),
        out_specs=[hbm] * len(arrays),
        scratch_shapes=[pltpu.VMEM(a.shape, a.dtype) for a in arrays]
        + [pltpu.SemaphoreType.DMA(sems), pltpu.SemaphoreType.DMA(sems)],
        compiler_params=pltpu.CompilerParams(vmem_limit_bytes=62 * 1024 * 1024),
        name="place_outputs",
    )(*arrays)


MATS_ORDER = (2, 4, 5, 13, 14, 7, 11, 16, 20, 22)
VECS = (0, 1, 3, 6, 8, 9, 10, 12, 15, 17, 18, 19, 23, 21)


def split_units(blocks):
    units = [(0, slice(None), slice(None))]
    for i, (rows, cols) in enumerate(blocks):
        base_rows, base_cols = min(rows, blocks[0][0]), min(cols, blocks[0][1])
        for top in range(0, rows, base_rows):
            for left in range(0, cols, base_cols):
                units.append(
                    (i + 1, slice(top, top + base_rows), slice(left, left + base_cols))
                )
    return units


def collect(*shards):
    return tuple(lax.all_gather(s, BOTH, axis=0, tiled=True) for s in shards)


def spread(*grads):
    return tuple(
        lax.psum_scatter(g.astype(jnp.float32), BOTH, scatter_dimension=0, tiled=True)
        for g in grads
    )


def own_vectors(block, position, shards):
    size = shards[0].shape[0]
    spot = position % (VEC_LANES // size)
    mine = lax.dynamic_slice(block, (0, spot * size), (VEC_ROWS, size))
    owned = [None] * len(shards)
    for row, i in enumerate(VECS[:-1]):
        owned[i] = mine[row]
    owned[VECS[-1]] = block[len(VECS) - 1]
    return owned


def on_device(
    mesh,
    tokens,
    memory,
    page_lengths,
    end_flags,
    out_grad,
    self_gain,
    self_shift,
    self_query,
    self_query_bias,
    self_key,
    self_value,
    self_value_bias,
    self_out,
    self_out_bias,
    cross_gain,
    cross_shift,
    cross_query,
    cross_query_bias,
    cross_key,
    cross_value,
    cross_value_bias,
    cross_out,
    cross_out_bias,
    feed_gain,
    feed_shift,
    feed_in,
    feed_in_bias,
    feed_out,
    feed_out_bias,
):
    page_count, page_len, width = tokens.shape
    mem_len = memory.shape[1]
    row_count = page_count * page_len
    lengths_now = jnp.where(end_flags == 1, 1, page_lengths)
    inputs = tokens.reshape(row_count, width).astype(jnp.float32)
    mem_rows = memory.reshape(page_count * mem_len, width)
    shard_set = (
        self_gain,
        self_shift,
        self_query,
        self_query_bias,
        self_key,
        self_value,
        self_value_bias,
        self_out,
        self_out_bias,
        cross_gain,
        cross_shift,
        cross_query,
        cross_query_bias,
        cross_key,
        cross_value,
        cross_value_bias,
        cross_out,
        cross_out_bias,
        feed_gain,
        feed_shift,
        feed_in,
        feed_in_bias,
        feed_out,
        feed_out_bias,
    )
    if can_route(mesh, self_query.shape[0]):
        mats = [shard_set[i] for i in MATS_ORDER]
        vecs = [shard_set[i] for i in VECS]
        gathered, saved = fused_forward(
            mesh, tokens[0], memory[0], lengths_now, mats, vecs, HEADS, 0
        )
        got = fused_backward(
            mesh, out_grad[0], tokens[0], memory[0], lengths_now, saved[:-1], gathered, HEADS, 1
        )
        position = lax.axis_index("dp") * mesh.shape["fsdp"] + lax.axis_index("fsdp")
        owned = own_vectors(got[-1], position, shard_set)
        placed = place_outputs([saved[-1]] + list(got[:-1]))
        for i, value in zip(MATS_ORDER, placed[3:]):
            owned[i] = value
        return (placed[0][None], placed[1][None], placed[2].transpose(1, 0, 2)) + tuple(owned)
    full_set = collect(*shard_set)
    (
        gain_one,
        shift_one,
        query_mat,
        query_vec,
        key_mat,
        value_mat,
        value_vec,
        out_mat,
        out_vec,
        gain_two,
        shift_two,
        cquery_mat,
        cquery_vec,
        ckey_mat,
        cvalue_mat,
        cvalue_vec,
        cout_mat,
        cout_vec,
        gain_three,
        shift_three,
        hidden_mat,
        hidden_vec,
        final_mat,
        final_vec,
    ) = full_set
    norm_of = lambda r, g, b: normalize(r, g.astype(jnp.float32), b.astype(jnp.float32))
    first_norm, first_unit, first_std = norm_of(inputs, gain_one, shift_one)
    first_low = first_norm.astype(jnp.bfloat16)
    query_low = (product(first_low, query_mat) + query_vec.astype(jnp.float32)).astype(jnp.bfloat16)
    key_low = product(first_low, key_mat).astype(jnp.bfloat16)
    value_low = (product(first_low, value_mat) + value_vec.astype(jnp.float32)).astype(jnp.bfloat16)
    query_pages = query_low.reshape(page_count, page_len, width)
    key_pages = key_low.reshape(page_count, page_len, width)
    value_pages = value_low.reshape(page_count, page_len, width)
    self_mixed, self_total = attend_fwd(
        query_pages, key_pages, value_pages, lengths_now, HEADS, 512
    )
    self_low = self_mixed.reshape(row_count, width)
    after_self = inputs + product(self_low, out_mat) + out_vec.astype(jnp.float32)
    second_norm, second_unit, second_std = normalize(
        after_self, gain_two.astype(jnp.float32), shift_two.astype(jnp.float32)
    )
    second_low = second_norm.astype(jnp.bfloat16)
    cquery_low = (product(second_low, cquery_mat) + cquery_vec.astype(jnp.float32)).astype(
        jnp.bfloat16
    )
    ckey_low = product(mem_rows, ckey_mat).astype(jnp.bfloat16)
    cvalue_low = (product(mem_rows, cvalue_mat) + cvalue_vec.astype(jnp.float32)).astype(
        jnp.bfloat16
    )
    cquery_pages = cquery_low.reshape(page_count, page_len, width)
    ckey_pages = ckey_low.reshape(page_count, mem_len, width)
    cvalue_pages = cvalue_low.reshape(page_count, mem_len, width)
    cross_mixed, cross_total = attend_fwd(
        cquery_pages, ckey_pages, cvalue_pages, None, HEADS, 512
    )
    cross_low = cross_mixed.reshape(row_count, width)
    after_cross = after_self + product(cross_low, cout_mat) + cout_vec.astype(jnp.float32)
    third_norm, third_unit, third_std = normalize(
        after_cross, gain_three.astype(jnp.float32), shift_three.astype(jnp.float32)
    )
    third_low = third_norm.astype(jnp.bfloat16)
    hidden_pre = product(third_low, hidden_mat) + hidden_vec.astype(jnp.float32)
    hidden_low, hidden_rate = gelu_parts(hidden_pre)
    hidden_low = hidden_low.astype(jnp.bfloat16)
    hidden_rate = hidden_rate.astype(jnp.bfloat16)
    result = after_cross + product(hidden_low, final_mat) + final_vec.astype(jnp.float32)
    layer_out = result.astype(jnp.bfloat16).reshape(page_count, page_len, width)
    second_norm, second_unit, second_std = norm_of(after_self, gain_two, shift_two)
    second_low = second_norm.astype(jnp.bfloat16)
    third_norm, third_unit, third_std = norm_of(after_cross, gain_three, shift_three)
    third_low = third_norm.astype(jnp.bfloat16)
    grad_rows = out_grad.reshape(row_count, width).astype(jnp.float32)
    final_grad = out_grad.reshape(row_count, width)
    grad_final_mat = product_tn(hidden_low, final_grad).astype(jnp.bfloat16)
    grad_final_vec = jnp.sum(final_grad.astype(jnp.float32), axis=0)
    hidden_grad = (product_nt(final_grad, final_mat) * hidden_rate.astype(jnp.float32)).astype(jnp.bfloat16)
    grad_hidden_mat = product_tn(third_low, hidden_grad).astype(jnp.bfloat16)
    grad_hidden_vec = jnp.sum(hidden_grad.astype(jnp.float32), axis=0)
    third_back, grad_gain_three, grad_shift_three = normalize_back(
        product_nt(hidden_grad, hidden_mat), third_unit, third_std, gain_three.astype(jnp.float32)
    )
    cross_grad_total = grad_rows + third_back
    cout_grad = cross_grad_total.astype(jnp.bfloat16)
    grad_cout_mat = product_tn(cross_low, cout_grad).astype(jnp.bfloat16)
    grad_cout_vec = jnp.sum(cout_grad.astype(jnp.float32), axis=0)
    cmix_grad = (
        product_nt(cout_grad, cout_mat).astype(jnp.bfloat16).reshape(page_count, page_len, width)
    )
    cquery_grad, ckey_grad, cvalue_grad = attend_bwd(
        cquery_pages, ckey_pages, cvalue_pages, cmix_grad, cross_total, None, HEADS, 512
    )
    cquery_grad = cquery_grad.reshape(row_count, width)
    ckey_grad = ckey_grad.reshape(page_count * mem_len, width)
    cvalue_grad = cvalue_grad.reshape(page_count * mem_len, width)
    grad_cquery_mat = product_tn(second_low, cquery_grad).astype(jnp.bfloat16)
    grad_cquery_vec = jnp.sum(cquery_grad.astype(jnp.float32), axis=0)
    grad_ckey_mat = product_tn(mem_rows, ckey_grad).astype(jnp.bfloat16)
    grad_cvalue_mat = product_tn(mem_rows, cvalue_grad).astype(jnp.bfloat16)
    grad_cvalue_vec = jnp.sum(cvalue_grad.astype(jnp.float32), axis=0)
    memory_grad = (product_nt(ckey_grad, ckey_mat) + product_nt(cvalue_grad, cvalue_mat)).reshape(
        page_count, mem_len, width
    )
    second_back, grad_gain_two, grad_shift_two = normalize_back(
        product_nt(cquery_grad, cquery_mat), second_unit, second_std, gain_two.astype(jnp.float32)
    )
    self_grad_total = cross_grad_total + second_back
    sout_grad = self_grad_total.astype(jnp.bfloat16)
    grad_out_mat = product_tn(self_low, sout_grad).astype(jnp.bfloat16)
    grad_out_vec = jnp.sum(sout_grad.astype(jnp.float32), axis=0)
    smix_grad = (
        product_nt(sout_grad, out_mat).astype(jnp.bfloat16).reshape(page_count, page_len, width)
    )
    query_grad, key_grad, value_grad = attend_bwd(
        query_pages, key_pages, value_pages, smix_grad, self_total, lengths_now, HEADS, 256
    )
    query_grad = query_grad.reshape(row_count, width)
    key_grad = key_grad.reshape(row_count, width)
    value_grad = value_grad.reshape(row_count, width)
    grad_query_mat = product_tn(first_low, query_grad).astype(jnp.bfloat16)
    grad_query_vec = jnp.sum(query_grad.astype(jnp.float32), axis=0)
    grad_key_mat = product_tn(first_low, key_grad).astype(jnp.bfloat16)
    grad_value_mat = product_tn(first_low, value_grad).astype(jnp.bfloat16)
    grad_value_vec = jnp.sum(value_grad.astype(jnp.float32), axis=0)
    first_in = (
        product_nt(query_grad, query_mat)
        + product_nt(key_grad, key_mat)
        + product_nt(value_grad, value_mat)
    )
    first_back, grad_gain_one, grad_shift_one = normalize_back(
        first_in, first_unit, first_std, gain_one.astype(jnp.float32)
    )
    tokens_grad = (self_grad_total + first_back).reshape(page_count, page_len, width)
    owned = spread(
        grad_gain_one[0],
        grad_shift_one[0],
        grad_query_mat,
        grad_query_vec,
        grad_key_mat,
        grad_value_mat,
        grad_value_vec,
        grad_out_mat,
        grad_out_vec,
        grad_gain_two[0],
        grad_shift_two[0],
        grad_cquery_mat,
        grad_cquery_vec,
        grad_ckey_mat,
        grad_cvalue_mat,
        grad_cvalue_vec,
        grad_cout_mat,
        grad_cout_vec,
        grad_gain_three[0],
        grad_shift_three[0],
        grad_hidden_mat,
        grad_hidden_vec,
        grad_final_mat,
        grad_final_vec,
    )
    return (layer_out, tokens_grad, memory_grad) + tuple(owned)


def solution(mesh):
    placed = (
        P(("dp", "fsdp"), None, None),
        P(("dp", "fsdp"), None, None),
        P(("dp", "fsdp")),
        P(("dp", "fsdp")),
        P(("dp", "fsdp"), None, None),
        P(("dp", "fsdp")),
        P(("dp", "fsdp")),
        P(("dp", "fsdp"), None),
        P(("dp", "fsdp")),
        P(("dp", "fsdp"), None),
        P(("dp", "fsdp"), None),
        P(("dp", "fsdp")),
        P(("dp", "fsdp"), None),
        P(("dp", "fsdp")),
        P(("dp", "fsdp")),
        P(("dp", "fsdp")),
        P(("dp", "fsdp"), None),
        P(("dp", "fsdp")),
        P(("dp", "fsdp"), None),
        P(("dp", "fsdp"), None),
        P(("dp", "fsdp")),
        P(("dp", "fsdp"), None),
        P(("dp", "fsdp")),
        P(("dp", "fsdp")),
        P(("dp", "fsdp")),
        P(("dp", "fsdp"), None),
        P(("dp", "fsdp")),
        P(("dp", "fsdp"), None),
        P(("dp", "fsdp")),
    )
    return jax.shard_map(
        functools.partial(on_device, mesh),
        mesh=mesh,
        in_specs=placed,
        out_specs=(
            P(("dp", "fsdp"), None, None),
            P(("dp", "fsdp"), None, None),
            P(("dp", "fsdp"), None, None),
            P(("dp", "fsdp")),
            P(("dp", "fsdp")),
            P(("dp", "fsdp"), None),
            P(("dp", "fsdp")),
            P(("dp", "fsdp"), None),
            P(("dp", "fsdp"), None),
            P(("dp", "fsdp")),
            P(("dp", "fsdp"), None),
            P(("dp", "fsdp")),
            P(("dp", "fsdp")),
            P(("dp", "fsdp")),
            P(("dp", "fsdp"), None),
            P(("dp", "fsdp")),
            P(("dp", "fsdp"), None),
            P(("dp", "fsdp"), None),
            P(("dp", "fsdp")),
            P(("dp", "fsdp"), None),
            P(("dp", "fsdp")),
            P(("dp", "fsdp")),
            P(("dp", "fsdp")),
            P(("dp", "fsdp"), None),
            P(("dp", "fsdp")),
            P(("dp", "fsdp"), None),
            P(("dp", "fsdp")),
        ),
        check_vma=False,
    )
```

```python
import functools

import jax
import jax.numpy as jnp
from jax import lax
from jax.experimental import pallas as pl
from jax.experimental.pallas import tpu as pltpu
from jax.sharding import PartitionSpec as P

HEADS = 16


EPSILON = 1e-05
ROOT_HALF = 0.7071067811865476
INV_ROOT_TWO_PI = 0.3989422804014327


def product(left, right):
    return jnp.dot(left, right, preferred_element_type=jnp.float32)


def product_tn(left, right):
    return lax.dot_general(
        left, right, (((0,), (0,)), ((), ())), preferred_element_type=jnp.float32
    )


def product_nt(left, right):
    return lax.dot_general(
        left, right, (((1,), (1,)), ((), ())), preferred_element_type=jnp.float32
    )


def normalize(rows_in, norm_gain, norm_shift):
    centered = rows_in - jnp.mean(rows_in, axis=-1, keepdims=True)
    inv_std = lax.rsqrt(jnp.mean(centered * centered, axis=-1, keepdims=True) + EPSILON)
    unit_rows = centered * inv_std
    return (unit_rows * norm_gain + norm_shift, unit_rows, inv_std)


def normalize_back(grad_norm, unit_rows, inv_std, norm_gain):
    scaled = grad_norm * norm_gain
    inner_part = (
        scaled
        - jnp.mean(scaled, axis=-1, keepdims=True)
        - unit_rows * jnp.mean(scaled * unit_rows, axis=-1, keepdims=True)
    )
    return (
        inner_part * inv_std,
        jnp.sum(grad_norm * unit_rows, axis=0, keepdims=True),
        jnp.sum(grad_norm, axis=0, keepdims=True),
    )


LOG2E = 1.4426950408889634
LN2 = 0.6931471805599453


def dot_nn(a, b):
    return jnp.dot(a, b, preferred_element_type=jnp.float32)


def dot_nt(a, b):
    return lax.dot_general(a, b, (((1,), (1,)), ((), ())), preferred_element_type=jnp.float32)


def dot_tn(a, b):
    return lax.dot_general(a, b, (((0,), (0,)), ((), ())), preferred_element_type=jnp.float32)


def lane_half(x, head, half):
    lane = lax.broadcasted_iota(jnp.int32, (1, x.shape[1]), 1)
    keep = (lane < half) if head == 0 else (lane >= half)
    return jnp.where(keep, x, jnp.zeros_like(x))


def causal_spans(rows, chunk):
    return [(start, chunk, start + chunk) for start in range(0, rows, chunk)]


def limit_row(start, width, length):
    pos = start + lax.broadcasted_iota(jnp.int32, (1, width), 1)
    return jnp.minimum(pos, length - 1)


def forward_pair(load_q, load_k, load_v, write, spans, length, scale):
    for start, size, keys in spans:
        q2 = load_q(start, size)
        k2 = load_k(0, keys)
        v2 = load_v(0, keys)
        half = q2.shape[1] // 2
        vt = v2.T
        outs, totals = [], []
        for head in (0, 1):
            raw = dot_nt(k2, lane_half(q2, head, half))
            if length is not None:
                key_pos = lax.broadcasted_iota(jnp.int32, raw.shape, 0)
                raw = jnp.where(key_pos <= limit_row(start, size, length), raw, -1e30)
            top = jnp.max(raw, axis=0, keepdims=True)
            expo = jnp.exp2((raw - top) * (scale * LOG2E))
            total = jnp.sum(expo, axis=0, keepdims=True)
            mixed = dot_nn(vt[head * half : (head + 1) * half], expo.astype(jnp.bfloat16))
            outs.append(mixed / total)
            totals.append(top * (scale * LOG2E) + jnp.log2(total))
        write(start, size, jnp.concatenate(outs, axis=0).T.astype(jnp.bfloat16), totals)


def fwd_kernel(masked, scale, chunk, *refs):
    if masked:
        len_ref, q_ref, k_ref, v_ref, a_ref, t_ref = refs
        length = len_ref[pl.program_id(0)]
    else:
        q_ref, k_ref, v_ref, a_ref, t_ref = refs
        length = None
    rows, keys = q_ref.shape[1], k_ref.shape[1]
    if masked:
        spans = causal_spans(rows, chunk)
    else:
        spans = [(s, chunk, keys) for s in range(0, rows, chunk)]

    def write(start, size, out, totals):
        a_ref[0, pl.ds(start, size), :] = out
        for head in (0, 1):
            t_ref[0, 0, pl.ds(head, 1), pl.ds(start, size)] = totals[head]

    forward_pair(
        lambda s, n: q_ref[0, pl.ds(s, n), :],
        lambda s, n: k_ref[0, pl.ds(s, n), :],
        lambda s, n: v_ref[0, pl.ds(s, n), :],
        write, spans, length, scale,
    )


def attend_fwd(q, k, v, lengths, heads, chunk=256):
    pages, rows, width = q.shape
    keys = k.shape[1]
    head = width // heads
    pairs = heads // 2
    masked = lengths is not None
    row_spec = pl.BlockSpec((1, rows, 2 * head), lambda p, h: (p, 0, h))
    key_spec = pl.BlockSpec((1, keys, 2 * head), lambda p, h: (p, 0, h))
    in_specs = [row_spec, key_spec, key_spec]
    args = [q, k, v]
    if masked:
        in_specs = [pl.BlockSpec(memory_space=pltpu.SMEM)] + in_specs
        args = [lengths] + args
    return pl.pallas_call(
        functools.partial(fwd_kernel, masked, head**-0.5, chunk),
        grid=(pages, pairs),
        in_specs=in_specs,
        out_specs=[row_spec, pl.BlockSpec((1, 1, 2, rows), lambda p, h: (p, h, 0, 0))],
        out_shape=[
            jax.ShapeDtypeStruct(q.shape, jnp.bfloat16),
            jax.ShapeDtypeStruct((pages, pairs, 2, rows), jnp.float32),
        ],
        compiler_params=pltpu.CompilerParams(vmem_limit_bytes=48 * 1024 * 1024),
        name="attend_forward",
    )(*args)


def bwd_kernel(masked, scale, chunk, *refs):
    if masked:
        len_ref, q_ref, k_ref, v_ref, g_ref, t_ref, dq_ref, dk_ref, dv_ref, dk_acc, dv_acc = refs
        length = len_ref[pl.program_id(0)]
    else:
        q_ref, k_ref, v_ref, g_ref, t_ref, dq_ref, dk_ref, dv_ref, dk_acc, dv_acc = refs
        length = None
    rows, keys_all = q_ref.shape[1], k_ref.shape[1]
    if masked:
        spans = causal_spans(rows, chunk)[::-1]
    else:
        spans = [(s, chunk, keys_all) for s in range(0, rows, chunk)]
    half = q_ref.shape[2] // 2
    for step, (start, size, keys) in enumerate(spans):
        q2 = q_ref[0, pl.ds(start, size), :]
        g2 = g_ref[0, pl.ds(start, size), :]
        k2 = k_ref[0, pl.ds(0, keys), :]
        v2 = v_ref[0, pl.ds(0, keys), :]
        kt = k2.T
        dk, dv, dqt = None, None, []
        for head in (0, 1):
            qm = lane_half(q2, head, half)
            gm = lane_half(g2, head, half)
            raw = dot_nt(k2, qm)
            total = t_ref[0, 0, pl.ds(head, 1), pl.ds(start, size)]
            probs = jnp.exp2(raw * (scale * LOG2E) - total)
            if length is not None:
                key_pos = lax.broadcasted_iota(jnp.int32, raw.shape, 0)
                probs = jnp.where(key_pos <= limit_row(start, size, length), probs, 0.0)
            grad = dot_nt(v2, gm)
            part = probs * grad
            dot_row = jnp.sum(part, axis=0, keepdims=True)
            score = ((part - probs * dot_row) * scale).astype(jnp.bfloat16)
            dvh = dot_nn(probs.astype(jnp.bfloat16), gm)
            dkh = dot_nn(score, qm)
            dv = dvh if dv is None else dv + dvh
            dk = dkh if dk is None else dk + dkh
            dqt.append(dot_nn(kt[head * half : (head + 1) * half], score))
        dq_ref[0, pl.ds(start, size), :] = jnp.concatenate(dqt, axis=0).T.astype(jnp.bfloat16)
        if step == 0:
            dk_acc[pl.ds(0, keys), :] = dk
            dv_acc[pl.ds(0, keys), :] = dv
        else:
            dk_acc[pl.ds(0, keys), :] += dk
            dv_acc[pl.ds(0, keys), :] += dv
    dk_ref[0] = dk_acc[...].astype(jnp.bfloat16)
    dv_ref[0] = dv_acc[...].astype(jnp.bfloat16)


def attend_bwd(q, k, v, g, totals, lengths, heads, chunk=256):
    pages, rows, width = q.shape
    keys = k.shape[1]
    head = width // heads
    pairs = heads // 2
    masked = lengths is not None
    row_spec = pl.BlockSpec((1, rows, 2 * head), lambda p, h: (p, 0, h))
    key_spec = pl.BlockSpec((1, keys, 2 * head), lambda p, h: (p, 0, h))
    total_spec = pl.BlockSpec((1, 1, 2, rows), lambda p, h: (p, h, 0, 0))
    in_specs = [row_spec, key_spec, key_spec, row_spec, total_spec]
    args = [q, k, v, g, totals]
    if masked:
        in_specs = [pl.BlockSpec(memory_space=pltpu.SMEM)] + in_specs
        args = [lengths] + args
    return pl.pallas_call(
        functools.partial(bwd_kernel, masked, head**-0.5, chunk),
        grid=(pages, pairs),
        in_specs=in_specs,
        out_specs=[row_spec, key_spec, key_spec],
        out_shape=[jax.ShapeDtypeStruct(a.shape, jnp.bfloat16) for a in (q, k, v)],
        scratch_shapes=[pltpu.VMEM((keys, 2 * head), jnp.float32)] * 2,
        compiler_params=pltpu.CompilerParams(vmem_limit_bytes=48 * 1024 * 1024),
        name="attend_backward",
    )(*args)


MESH_ID = pl.DeviceIdType.MESH
BOTH = ("dp", "fsdp")
CORE_RATE = 500e3
LINK_RATE = 92e3
HOP = 3.1
LAG = 8.0


SCATTER_ROUTES = ()
SCATTER_ROUTES += (43210, 42310, 41023, 43210, 42103, 43120, 43210, 41320)
SCATTER_ROUTES += (42310, 41230, 43120, 42310, 42310, 42130, 42130, 43120)
SCATTER_ROUTES += (43210, 42310, 42310, 43210, 43210, 41320, 43210, 42130)
SCATTER_ROUTES += (43120, 42130, 43210, 43210, 42130, 41230, 42310, 43120)
SCATTER_ROUTES += (42310,)


def orders_of(bits, table, count, reverse):
    if len(bits) == 5 and bits[1] == (0, 1) and count == len(table):
        return [[int(c) for c in str(route)] for route in table]
    routes = route_orders(bits)
    return [routes[i % 4][::-1] if reverse else routes[i % 4] for i in range(count)]


def bit_table(mesh):
    bits = []
    for axis, name in enumerate(BOTH):
        step = mesh.shape[name] // 2
        while step >= 1:
            bits.append((axis, step))
            step //= 2
    return bits


def can_route(mesh, rows):
    sizes = [mesh.shape[name] for name in BOTH]
    return all(s & (s - 1) == 0 for s in sizes) and rows % 32 == 0


def route_orders(bits):
    outer = [i for i, (axis, _) in enumerate(bits) if axis == 0]
    inner = [i for i, (axis, _) in enumerate(bits) if axis == 1]
    middle, core = inner[:-1], inner[-1:]
    return (
        outer + middle + core,
        outer + middle[::-1] + core,
        middle[:1] + outer + middle[1:] + core,
        middle[-1:] + outer + middle[:-1] + core,
    )


def loads_of(bits, at, size):
    axis, step = bits[at]
    if axis == 1 and step == 1:
        return {"core": size / CORE_RATE}
    if axis == 1:
        return {f"inner{step}": 2 * size / LINK_RATE}
    loads = {"outer1": 2 * size / LINK_RATE}
    if step > 1:
        loads["outer2"] = 2 * size * step / LINK_RATE
    return loads


def plan_sends(bits, orders, sizes, growing, add_rate, begin=None):
    count = len(bits)
    ready = [(begin[unit] if begin else 0.0, unit, 0) for unit in range(len(orders))]
    free = {}
    plan = []
    arrive = {}
    while ready:
        choices = []
        for when, unit, stage in ready:
            scale = 2**stage if growing else 2 ** (count - 1 - stage)
            loads = loads_of(bits, orders[unit][stage], sizes[unit] * scale)
            start = max([when] + [free.get(link, 0.0) for link in loads])
            choices.append((round(start, 3), unit, -stage, when, scale))
        start, unit, stage, when, scale = min(choices)
        stage = -stage
        ready.remove((when, unit, stage))
        loads = loads_of(bits, orders[unit][stage], sizes[unit] * scale)
        for link, took in loads.items():
            free[link] = start + took
        plan.append((start, unit, stage))
        after = start + max(loads.values()) + HOP
        if add_rate:
            after += sizes[unit] * scale / add_rate
        if stage + 1 < count:
            ready.append((after, unit, stage + 1))
        else:
            arrive[unit] = after
    return sorted(plan), arrive


def my_bits(bits):
    place = (lax.axis_index("dp"), lax.axis_index("fsdp"))
    return [(place[axis] // step) % 2 for axis, step in bits]


def partner(bits, mine, at):
    place = [lax.axis_index("dp"), lax.axis_index("fsdp")]
    axis, step = bits[at]
    place[axis] = place[axis] + step * (1 - 2 * mine[at])
    return tuple(place)


def greet(bits, mine):
    barrier = pltpu.get_barrier_semaphore()
    for at in range(len(bits)):
        pl.semaphore_signal(
            barrier, inc=1, device_id=partner(bits, mine, at), device_id_type=MESH_ID
        )
    pl.semaphore_wait(barrier, len(bits))


def unit_shape(blocks, unit):
    array, rows, cols = unit
    block = blocks[array]
    return (len(range(*rows.indices(block[0]))), len(range(*cols.indices(block[1]))))


ERF_RATE = 0.3275911
ERF_TERMS = (0.254829592, -0.284496736, 1.421413741, -1.453152027, 1.061405429)


def gelu_parts(pre):
    bell = jnp.exp2(pre * pre * (-0.5 * LOG2E))
    arm = 1.0 / (1.0 + jnp.abs(pre) * (ERF_RATE * ROOT_HALF))
    series = ERF_TERMS[4]
    for term in ERF_TERMS[3::-1]:
        series = series * arm + term
    tail = 0.5 * series * arm * bell
    below = jnp.where(pre >= 0.0, 1.0 - tail, tail)
    return pre * below, below + pre * bell * INV_ROOT_TWO_PI


class Schedule:
    pace = 1.2

    def __init__(self, plan, issue):
        self.plan = plan
        self.issue = issue
        self.at = 0
        self.now = 0.0

    def due(self):
        items = []
        while self.at < len(self.plan) and self.plan[self.at][0] <= self.now:
            items.append(self.plan[self.at][1:])
            self.at += 1
        return items

    def spend(self, took):
        self.now += took * self.pace
        for unit, stage in self.due():
            self.issue(unit, stage)

    def until(self, when):
        self.now = max(self.now, when)
        for unit, stage in self.due():
            self.issue(unit, stage)

    def loop(self, count, took, body):
        buckets = []
        for _ in range(count):
            self.now += took * self.pace
            buckets.append(self.due())

        def step(i, carry):
            body(i)
            for k, items in enumerate(buckets):
                if items:

                    @pl.when(i == k)
                    def _(items=items):
                        for unit, stage in items:
                            self.issue(unit, stage)

            return carry

        lax.fori_loop(0, count, step, 0)


ROWS_STEP = 128


N_VECS = 14
VEC_ROWS = 16
VEC_LANES = 128


def device_index(bits, mine):
    count = len(bits)
    return sum(mine[b] * 2 ** (count - 1 - b) for b in range(count))


def pack_vectors(loose, pack, spot, size):
    row = lax.broadcasted_iota(jnp.int32, (size, VEC_LANES), 0)
    lane = lax.broadcasted_iota(jnp.int32, (size, VEC_LANES), 1)
    place = (lane == row + size * spot).astype(jnp.float32)
    pieces = []
    for ref in loose[:-1]:
        pieces.append(dot_nn(ref[...].astype(jnp.float32).reshape(1, size), place))
    pieces.append(loose[-1][...].astype(jnp.float32).reshape(1, VEC_LANES))
    pieces.append(jnp.zeros((VEC_ROWS - len(pieces), VEC_LANES), jnp.float32))
    pack[...] = jnp.concatenate(pieces, axis=0).astype(pack.dtype)


def unpack_table(vecs, table, bits, width, hidden_row=None):
    count = len(bits)
    devices = 2**count
    share = devices * VEC_LANES // width
    spots = [tuple((d >> (count - 1 - b)) & 1 for b in range(count)) for d in range(devices)]
    for group in range(width // VEC_LANES):
        total = None
        for d in range(group * share, (group + 1) * share):
            block = vecs[spots[d]].astype(jnp.float32)
            total = block if total is None else total + block
        table[:, pl.ds(group * VEC_LANES, VEC_LANES)] = total
    if hidden_row is not None:
        for d in range(devices):
            block = vecs[spots[d]].astype(jnp.float32)
            hidden_row[pl.ds(0, 1), pl.ds(d * VEC_LANES, VEC_LANES)] = block[N_VECS - 1 : N_VECS]


def forward_kernel(bits, units, orders, plan, arrive, n_arrays, heads, *refs):
    count = len(bits)
    (tokens, memory, lengths), refs = refs[:3], refs[3:]
    loose, refs = refs[:N_VECS], refs[N_VECS:]
    sources, refs = refs[: n_arrays - 1], refs[n_arrays - 1 :]
    targets, refs = refs[:n_arrays], refs[n_arrays:]
    saved_names = ("q", "k", "v", "a", "total", "h1")
    saved_names += ("cq", "ck", "cv", "ca", "ctotal", "h2", "g", "slope")
    saved_names += ("n1", "n2", "n3", "out")
    saved = dict(zip(saved_names, refs[: len(saved_names)]))
    refs = refs[len(saved_names) :]
    x, mem, n, q, k, v, a, h, ck, cv, g, slope, tot, ctot = refs[:14]
    wide, tall = refs[14:16], refs[16:18]
    pack, vecs, table, hidden_row = refs[18:-6]
    last_wide = 8 + g.shape[1] // x.shape[1]
    last_weight = len(units) // 2
    send_sem, recv_sem, own_sem, in_sem, w_sem, out_sem = refs[-6:]
    mine = my_bits(bits)
    rows, width = x.shape
    devices = 2**count
    lanes_each = width // devices
    pack_vectors(loose, pack, device_index(bits, mine) % (VEC_LANES // lanes_each), lanes_each)
    sources = (pack,) + tuple(sources)
    own = [
        pltpu.make_async_copy(sources[i], targets[i].at[tuple(mine)], own_sem.at[i])
        for i in range(n_arrays)
    ]
    for copy in own:
        copy.start()
    load_x = pltpu.make_async_copy(tokens, x, in_sem.at[0])
    load_mem = pltpu.make_async_copy(memory, mem, in_sem.at[1])
    load_x.start()
    load_mem.start()
    greet(bits, mine)

    def message(unit, stage):
        array, top, left = units[unit]
        order = orders[unit]
        where = tuple(slice(None) if b in order[:stage] else mine[b] for b in range(count))
        place = targets[array].at[where + (top, left)]
        source = sources[array].at[top, left] if stage == 0 else place
        return pltpu.make_async_remote_copy(
            src_ref=source,
            dst_ref=place,
            send_sem=send_sem.at[unit, stage],
            recv_sem=recv_sem.at[unit, stage],
            device_id=partner(bits, mine, order[stage]),
            device_id_type=MESH_ID,
        )

    settled = set()

    def issue(unit, stage):
        array = units[unit][0]
        if stage > 0:
            if array not in settled:
                settled.add(array)
                own[array].wait()
            message(unit, stage - 1).wait_recv()
        message(unit, stage).start()

    clock = Schedule(plan, issue)
    every = (slice(None),) * count

    fetching = {}

    def parts_of(weight):
        return (0,) if weight == 0 else (2 * weight - 1, 2 * weight)

    def begin(weight):
        for unit in parts_of(weight):
            clock.until(arrive[unit] + LAG)
            message(unit, count - 1).wait_recv()
        array, _, left = units[parts_of(weight)[0]]
        if array not in settled:
            settled.add(array)
            own[array].wait()
        fetching[weight] = pltpu.make_async_copy(
            targets[array].at[every + (slice(None), left)], slot_of(weight), w_sem.at[weight]
        )
        fetching[weight].start()

    def slot_of(weight):
        if weight == 0:
            return vecs
        kind = wide if weight <= last_wide else tall
        return kind[weight % 2]

    def fetch(weight):
        if weight not in fetching:
            begin(weight)
        later = weight + 1
        if 0 < weight < last_weight and arrive[parts_of(later)[-1]] <= clock.now:
            begin(later)
        fetching[weight].wait()
        if weight > 0:
            clock.spend(0.6)
        return slot_of(weight)

    def times(lhs, slot, tile, write, took=1.4):
        depth = lhs.shape[1]
        tiles = slot.shape[-1] // tile

        def body(j):
            cols = pl.ds(pl.multiple_of(j * tile, tile), tile)
            weight = slot[every + (slice(None), cols)].reshape(depth, tile)
            write(cols, dot_nn(lhs[...], weight))

        clock.loop(tiles, took / tiles, body)

    def norm_into(gain, shift, source):
        def body(i):
            part = pl.ds(pl.multiple_of(i * ROWS_STEP, ROWS_STEP), ROWS_STEP)
            r = source[part, :].astype(jnp.float32)
            n[part, :] = normalize(r, gain, shift)[0].astype(jnp.bfloat16)

        clock.loop(rows // ROWS_STEP, 0.4, body)

    pending = {}

    def save(source, name):
        copy = pltpu.make_async_copy(source, saved[name], out_sem.at[saved_names.index(name)])
        copy.start()
        pending[name] = copy

    def saved_now(name):
        pending.pop(name).wait()

    def vec(i):
        return table[pl.ds(i, 1), :]

    clock.until(0.0)
    fetch(0)
    unpack_table(vecs, table, bits, width, hidden_row)
    load_x.wait()
    load_mem.wait()
    norm_into(vec(0), vec(1), x)
    save(n, "n1")
    length = lengths[0]

    def project(bias, target, extra=0):
        def write(cols, acc):
            if bias is not None:
                acc = acc + table[pl.ds(bias, 1), cols]
            target[:, cols] = acc.astype(target.dtype)

        return write

    def residual(bias, source):
        def write(cols, acc):
            h[:, cols] = source[:, cols].astype(jnp.float32) + acc + table[pl.ds(bias, 1), cols]

        return write

    def attend(q_ref, k_ref, v_ref, tot_ref, masked):
        keys = k_ref.shape[0]
        pair = 2 * (width // heads)

        def body(p):
            lanes = pl.ds(pl.multiple_of(p * pair, pair), pair)

            def write(start, size, out, totals):
                a[pl.ds(start, size), lanes] = out
                for head in (0, 1):
                    tot_ref[p, pl.ds(head, 1), pl.ds(start, size)] = totals[head]

            forward_pair(
                lambda s, m: q_ref[pl.ds(s, m), lanes],
                lambda s, m: k_ref[pl.ds(s, m), lanes],
                lambda s, m: v_ref[pl.ds(s, m), lanes],
                write,
                [(0, rows, keys)],
                length if masked else None,
                (width // heads) ** -0.5,
            )

        clock.loop(heads // 2, 1.4, body)

    for weight, target, bias in ((1, q, 2), (2, k, None), (3, v, 3)):
        times(n, fetch(weight), 512, project(bias, target))
    save(q, "q")
    save(k, "k")
    save(v, "v")
    attend(q, k, v, tot, True)
    save(a, "a")
    save(tot, "total")
    for weight, target, bias in ((4, ck, None), (5, cv, 8)):
        times(mem, fetch(weight), 512, project(bias, target), 1.9)
    save(ck, "ck")
    save(cv, "cv")
    times(a, fetch(6), 512, residual(4, x), 2.0)
    save(h, "h1")
    saved_now("n1")
    norm_into(vec(5), vec(6), h)
    save(n, "n2")
    saved_now("q")
    times(n, fetch(7), 512, project(7, q))
    save(q, "cq")
    saved_now("a")
    attend(q, ck, cv, ctot, False)
    save(a, "ca")
    save(ctot, "ctotal")
    saved_now("h1")
    times(a, fetch(8), 512, residual(9, h), 2.0)
    save(h, "h2")
    saved_now("n2")
    norm_into(vec(10), vec(11), h)
    save(n, "n3")
    block = width
    blocks = g.shape[1] // block
    for j in range(blocks):
        slot = fetch(9 + j)
        tile = 256

        def body(i, j=j, slot=slot):
            cols = pl.ds(pl.multiple_of(i * tile, tile), tile)
            spot = pl.ds(pl.multiple_of(j * block + i * tile, tile), tile)
            weight = slot[every + (slice(None), cols)].reshape(width, tile)
            for r in range(0, rows, ROWS_STEP):
                part = pl.ds(r, ROWS_STEP)
                pre = dot_nn(n[part, :], weight) + hidden_row[:, spot]
                low, rate = gelu_parts(pre)
                g[part, spot] = low.astype(jnp.bfloat16)
                slope[part, spot] = rate.astype(jnp.bfloat16)

        clock.loop(block // tile, 0.6, body)
    save(g, "g")
    save(slope, "slope")
    tall_cols = tall[0].shape[-1]
    for j in range(width // tall_cols):
        slot = fetch(9 + blocks + j)
        cols = pl.ds(j * tall_cols, tall_cols)
        weight = slot[...].reshape(g.shape[1], tall_cols)
        acc = dot_nn(g[...], weight)
        x[:, cols] = (h[:, cols] + acc + table[pl.ds(12, 1), cols]).astype(jnp.bfloat16)
        clock.spend(1.6)
    save(x, "out")
    clock.until(1e9)
    for copy in pending.values():
        copy.wait()
    for unit in range(len(units)):
        for stage in range(count):
            message(unit, stage).wait_send()


def fused_forward(mesh, tokens, memory, lengths, mats, vecs, heads, collective_id):
    bits = bit_table(mesh)
    rows, width = tokens.shape
    keys = memory.shape[0]
    block = mats[0].shape
    pack = (VEC_ROWS, VEC_LANES)
    every = slice(None)
    whole = [(i, every) for i in range(1, 9)]
    hidden = mats[8].shape[1]
    for left in range(0, hidden, width):
        whole.append((9, slice(left, left + width)))
    tall_rows = mats[9].shape[0]
    tall_cols = width * block[0] // tall_rows
    for left in range(0, width, tall_cols):
        whole.append((10, slice(left, left + tall_cols)))
    units = [(0, every, every)]
    for array, cols in whole:
        half = mats[array - 1].shape[0] // 2
        units += [(array, slice(0, half), cols), (array, slice(half, 2 * half), cols)]
    blocks = [pack] + [m.shape for m in mats]
    shapes = [unit_shape(blocks, unit) for unit in units]
    sizes = [2 * s[0] * s[1] for s in shapes]
    orders = [route_orders(bits)[(u - 1) % 4] for u in range(len(units))]
    plan, arrive = plan_sends(bits, orders, sizes, True, None)
    n = len(blocks)
    spots = (2,) * len(bits)
    low = jnp.bfloat16
    wide_rows = jax.ShapeDtypeStruct((rows, width), low)
    wide_keys = jax.ShapeDtypeStruct((keys, width), low)
    full = jax.ShapeDtypeStruct((rows, width), jnp.float32)
    totals = jax.ShapeDtypeStruct((heads // 2, 2, rows), jnp.float32)
    ff = jax.ShapeDtypeStruct((rows, hidden), low)
    saved = [
        wide_rows, wide_rows, wide_rows, wide_rows, totals, full,
        wide_rows, wide_keys, wide_keys, wide_rows, totals, full, ff, ff,
        wide_rows, wide_rows, wide_rows, wide_rows,
    ]
    vm = lambda s: pltpu.VMEM(s.shape, s.dtype)
    sems = (len(units), len(bits))
    hbm = pl.BlockSpec(memory_space=pltpu.HBM)
    got = pl.pallas_call(
        functools.partial(forward_kernel, bits, units, orders, plan, arrive, n, heads),
        out_shape=[jax.ShapeDtypeStruct(spots + b, low) for b in blocks] + saved,
        in_specs=[hbm, hbm, pl.BlockSpec(memory_space=pltpu.SMEM)]
        + [pl.BlockSpec(memory_space=pltpu.VMEM)] * (len(vecs) + len(mats)),
        out_specs=[hbm] * (n + len(saved)),
        scratch_shapes=[
            vm(wide_rows), vm(wide_keys), vm(wide_rows), vm(wide_rows), vm(wide_rows),
            vm(wide_rows), vm(wide_rows), vm(full), vm(wide_keys), vm(wide_keys),
            vm(ff), vm(ff), vm(totals), vm(totals),
            pltpu.VMEM(spots + block, low),
            pltpu.VMEM(spots + block, low),
            pltpu.VMEM(spots + (tall_rows, tall_cols), low),
            pltpu.VMEM(spots + (tall_rows, tall_cols), low),
            pltpu.VMEM(pack, low),
            pltpu.VMEM(spots + pack, low),
            pltpu.VMEM((VEC_ROWS, width), jnp.float32),
            pltpu.VMEM((1, hidden), jnp.float32),
            pltpu.SemaphoreType.DMA(sems),
            pltpu.SemaphoreType.DMA(sems),
            pltpu.SemaphoreType.DMA((n,)),
            pltpu.SemaphoreType.DMA((2,)),
            pltpu.SemaphoreType.DMA((len(whole) + 1,)),
            pltpu.SemaphoreType.DMA((len(saved),)),
        ],
        compiler_params=pltpu.CompilerParams(
            collective_id=collective_id,
            has_side_effects=True,
            vmem_limit_bytes=60 * 1024 * 1024,
        ),
        name="forward_layer",
    )(tokens, memory, lengths, *vecs, *mats)
    return got[:n], got[n:]


class Deferred(Schedule):
    pace = 1.1

    def __init__(self, plan, issue):
        super().__init__(list(plan), issue)
        self.made = set()

    def due(self):
        items, rest, held_back = [], [], set()
        for item in self.plan:
            when, unit, stage = item
            if unit in self.made and unit not in held_back and when <= self.now:
                items.append((unit, stage))
            else:
                held_back.add(unit)
                rest.append(item)
        self.plan = rest
        return items

    def finish(self, unit, last=99):
        late = [when for when, u, stage in self.plan if u == unit and stage <= last]
        if late:
            self.until(max(late))


def backward_pair(refs, accs, total_of, spans, length, scale, lanes):
    q_ref, k_ref, v_ref, g_ref = refs
    dk_acc, dv_acc = accs
    keys_all = k_ref.shape[0]
    half = (dk_acc.shape[1]) // 2
    for step, (start, size, keys) in enumerate(spans):
        part_rows = pl.ds(start, size)
        q2 = q_ref[part_rows, lanes]
        g2 = g_ref[part_rows, lanes]
        k2 = k_ref[pl.ds(0, keys), lanes]
        v2 = v_ref[pl.ds(0, keys), lanes]
        kt = k2.T
        dk, dv, dqt = None, None, []
        for head in (0, 1):
            qm = lane_half(q2, head, half)
            gm = lane_half(g2, head, half)
            raw = dot_nt(k2, qm)
            probs = jnp.exp2(raw * (scale * LOG2E) - total_of(head, start, size))
            if length is not None:
                key_pos = lax.broadcasted_iota(jnp.int32, raw.shape, 0)
                probs = jnp.where(key_pos <= limit_row(start, size, length), probs, 0.0)
            grad = dot_nt(v2, gm)
            part = probs * grad
            dot_row = jnp.sum(part, axis=0, keepdims=True)
            score = ((part - probs * dot_row) * scale).astype(jnp.bfloat16)
            dvh = dot_nn(probs.astype(jnp.bfloat16), gm)
            dkh = dot_nn(score, qm)
            dv = dvh if dv is None else dv + dvh
            dk = dkh if dk is None else dk + dkh
            dqt.append(dot_nn(kt[head * half : (head + 1) * half], score))
        q_ref[part_rows, lanes] = jnp.concatenate(dqt, axis=0).T.astype(jnp.bfloat16)
        if step == 0:
            dk_acc[pl.ds(0, keys), :] = dk
            dv_acc[pl.ds(0, keys), :] = dv
        else:
            dk_acc[pl.ds(0, keys), :] += dk
            dv_acc[pl.ds(0, keys), :] += dv
    every_key = pl.ds(0, keys_all)
    k_ref[every_key, lanes] = dk_acc[every_key, :].astype(jnp.bfloat16)
    v_ref[every_key, lanes] = dv_acc[every_key, :].astype(jnp.bfloat16)


BACK_INPUTS = ("dz", "tokens", "memory", "lengths")
BACK_INPUTS += ("q", "k", "v", "a", "total", "h1", "cq", "ck", "cv", "ca", "ctotal", "h2", "g", "rate")
BACK_INPUTS += ("n1", "n2", "n3")
BACK_INPUTS += ("wvec", "wq", "wk", "wv", "wck", "wcv", "wo", "wcq", "wco", "win", "wout")
TALL_PARTS = 8
WIDE_HELD = 11
WIDE_BOXES = 6
WIDE_STAGES = 4
SUM_SLOTS = 8


def backward_parts(width, hidden):
    half = width // 2
    parts = [(8, c) for c in range(0, hidden, half)]
    parts += [(7, 0), (7, half)]
    parts += [(i, c) for c in (0, half) for i in (6, 3, 4)]
    parts += [(5, 0), (5, half)]
    parts += [(i, c) for c in (0, half) for i in (0, 1, 2)]
    return parts


def made_times(n_wide):
    times = [6.0, 6.0, 9.0, 9.0, 12.0, 12.0, 15.0, 15.0]
    for first in (20.0, 25.5, 31.0, 36.5):
        times += [first, first + 1.0]
    times += [44.0, 45.0]
    times += [58.0, 59.0, 60.0, 73.0, 74.0, 75.0]
    times += [86.0, 87.0]
    times += [98.0, 99.0, 100.0, 112.0, 113.0, 114.0]
    return times + [124.0]


def backward_kernel(bits, orders, plan, begin, heads, *refs):
    count = len(bits)
    given = dict(zip(BACK_INPUTS, refs[: len(BACK_INPUTS)]))
    refs = refs[len(BACK_INPUTS) :]
    tokens_grad, memory_grad, keep_k, keep_v = refs[:4]
    results = refs[4:15]
    refs = refs[15:]
    bdz, n, acc, dh, hb, wide_a, wide_b = refs[:7]
    stages, held_tall, held_wide, box_tall, box_wide = refs[7:12]
    rest_tall, rest_wide = refs[12 : 12 + count - 1], refs[12 + count - 1 : 12 + 2 * (count - 1)]
    refs = refs[12 + 2 * (count - 1) :]
    vec_stage, vec_held = refs[:2]
    vec_boxes = refs[2 : 2 + count]
    refs = refs[2 + count :]
    sum_tall, sum_wide, sum_vec, vgrad, hgrad, table, vecs, tot, dk_acc, dv_acc = refs[:10]
    send_sem, recv_sem, store_sem, load_sem, w_sem, credit = refs[10:]
    wides = (wide_a, wide_b)
    mine = my_bits(bits)
    core = count - 1
    rows, width = bdz.shape
    half = width // 2
    hidden = hgrad.shape[1]
    every = (slice(None),) * count
    wide_parts = backward_parts(width, hidden)
    n_parts = len(orders)
    last = n_parts - 1
    tall_stage = [None, None]
    loads = {}

    def load(name, source, target):
        loads[name] = (source, target, len(loads))
        pltpu.make_async_copy(source, target, load_sem.at[len(loads) - 1]).start()

    def loaded(name):
        source, target, at = loads[name]
        pltpu.make_async_copy(source, target, load_sem.at[at]).wait()

    load("dz", given["dz"], bdz)
    load("vecs", given["wvec"], vecs)
    load("h2", given["h2"], hb)
    load("n3", given["n3"], n)
    vgrad[...] = jnp.zeros_like(vgrad)
    greet(bits, mine)

    def kind_of(part):
        if part < TALL_PARTS:
            return "tall"
        return "vec" if part == last else "wide"

    def lines_of(part):
        if kind_of(part) == "tall":
            height = held_tall.shape[-2] // 2
            return (pl.ds(part % 2 * height, height), slice(None))
        return (slice(None), slice(None))

    def held_of(part):
        kind = kind_of(part)
        if kind == "tall":
            return held_tall.at[part // 2]
        return vec_held if kind == "vec" else held_wide.at[(part - TALL_PARTS) % WIDE_HELD]

    def stage_of(part):
        kind = kind_of(part)
        if kind == "tall":
            return tall_stage[part // 2 % 2]
        return vec_stage if kind == "vec" else stages.at[(part - TALL_PARTS) % WIDE_STAGES]

    def box_of(part, step):
        kind = kind_of(part)
        if kind == "vec":
            return vec_boxes[step]
        if kind == "tall":
            return box_tall.at[part // 2 % 2] if step == 0 else rest_tall[step - 1].at[part // 2]
        i = part - TALL_PARTS
        return box_wide.at[i % WIDE_BOXES] if step == 0 else rest_wide[step - 1].at[i]

    def message(part, step):
        order = orders[part]
        now = order[step]
        lines = lines_of(part)
        where = []
        for b in range(count):
            if b == now:
                where.append(1 - mine[b])
            elif b in order[:step]:
                where.append(mine[b])
            else:
                where.append(slice(None))
        if step == 0:
            source = stage_of(part).at[tuple(where) + lines]
        else:
            source = held_of(part).at[tuple(where[:core]) + lines]
        return pltpu.make_async_remote_copy(
            src_ref=source,
            dst_ref=box_of(part, step).at[(slice(None),) * (core - step) + lines],
            send_sem=send_sem.at[part, step],
            recv_sem=recv_sem.at[part, step],
            device_id=partner(bits, mine, now),
            device_id_type=MESH_ID,
        )

    sent = set()

    def drained(part, step):
        if (part, step) not in sent:
            sent.add((part, step))
            message(part, step).wait_send()

    def credit_of(part):
        if kind_of(part) == "tall":
            return credit.at[part // 2 % 2]
        return credit.at[2 + (part - TALL_PARTS) % WIDE_BOXES]

    def box_used_again(part):
        if kind_of(part) == "tall":
            return part + 4 < TALL_PARTS
        return part != last and part + WIDE_BOXES < last

    def add(part, step, target=None):
        order, lines = orders[part], lines_of(part)
        message(part, step).wait_recv()
        held, box = held_of(part), box_of(part, step)
        own = stage_of(part) if step == 0 else None
        open_bits = [b for b in range(count) if b not in order[: step + 1]]
        looped = open_bits[:-2]

        def one(block, carry):
            where, spot = [], []
            for b in range(core):
                if b in looped:
                    digit = (block // 2 ** (len(looped) - 1 - looped.index(b))) % 2
                elif b in open_bits:
                    digit = slice(None)
                else:
                    digit = None
                where.append(mine[b] if digit is None else digit)
                if digit is not None:
                    spot.append(digit)
            source, where = tuple(where) + (mine[core],) + lines, tuple(where) + lines
            spot = tuple(spot) + lines
            if target is not None:
                target[...] = held[where].astype(jnp.float32) + box[spot].astype(jnp.float32)
            else:
                held[where] = (held[where] if own is None else own[source]) + box[spot]
            return carry

        if looped:
            lax.fori_loop(0, 2 ** len(looped), one, 0)
        else:
            one(0, 0)
        if step == 0 and box_used_again(part):
            pl.semaphore_signal(
                credit_of(part), inc=1, device_id=partner(bits, mine, core), device_id_type=MESH_ID
            )

    stored = {}

    def sum_of(part):
        kind = kind_of(part)
        if kind == "tall":
            return sum_tall.at[(part // 2,) + lines_of(part)]
        return sum_vec if kind == "vec" else sum_wide.at[(part - TALL_PARTS) % SUM_SLOTS]

    def store(part):
        kind = kind_of(part)
        if kind == "tall":
            cols = held_tall.shape[-1]
            target = results[9].at[lines_of(part)[0], pl.ds(part // 2 * cols, cols)]
        elif kind == "vec":
            target = results[10]
        else:
            array, left = wide_parts[part - TALL_PARTS]
            target = results[array].at[:, pl.ds(left, half)]
        return pltpu.make_async_copy(sum_of(part), target, store_sem.at[part])

    def issue(part, step):
        if step < count:
            add(part, step - 1)
            message(part, step).start()
            return
        slot = part if kind_of(part) != "wide" else -1 - (part - TALL_PARTS) % SUM_SLOTS
        if slot in stored:
            store(stored[slot]).wait()
        stored[slot] = part
        add(part, count - 1, sum_of(part))
        store(part).start()

    clock = Deferred(plan, issue)

    def room_for(part):
        kind = kind_of(part)
        back = 4 if kind == "tall" else WIDE_STAGES
        first = 0 if kind == "tall" else TALL_PARTS
        if part - back >= first:
            clock.finish(part - back, 1)
            drained(part - back, 0)
        if kind == "wide" and part - WIDE_HELD >= first:
            clock.finish(part - WIDE_HELD)
            for step in range(1, count):
                drained(part - WIDE_HELD, step)

    def made(part):
        kind = kind_of(part)
        if kind == "tall" and part >= 4 and part % 2 == 0:
            clock.finish(part - 4, 1)
            clock.finish(part - 3, 1)
            pl.semaphore_wait(credit_of(part), 2)
        if kind == "wide" and part - WIDE_BOXES >= TALL_PARTS:
            clock.finish(part - WIDE_BOXES, 1)
            pl.semaphore_wait(credit_of(part), 1)
        message(part, 0).start()
        clock.made.add(part)
        clock.now = max(clock.now, begin[part])
        clock.spend(0.0)

    blocks = hidden // width
    names = [("win", every + (slice(None), slice(j * width, (j + 1) * width))) for j in range(blocks)]
    whole = every + (slice(None), slice(None))
    names += [(name, whole) for name in ("wco", "wcq", "wo", "wq", "wk", "wv", "wck", "wcv")]
    weights = [
        pltpu.make_async_copy(given[name].at[where], wides[i % 2], w_sem.at[i])
        for i, (name, where) in enumerate(names)
    ]
    weights[0].start()
    weights[1].start()

    def back_through(i, lhs, write, took=1.1):
        weights[i].wait()
        slot = wides[i % 2]

        def body(t):
            part = slot[t].reshape(half, width)
            write(pl.ds(pl.multiple_of(t * half, half), half), dot_nt(lhs(), part))

        clock.loop(2, took / 2, body)
        if i + 2 < len(weights):
            weights[i + 2].start()

    def produce(part, lhs, rhs, took=0.75):
        room_for(part)
        slot = stage_of(part)
        slot[every + (slice(None), slice(None))] = (
            dot_tn(lhs, rhs).astype(jnp.bfloat16).reshape(slot.shape)
        )
        clock.spend(took)
        made(part)

    def column_sums(ref, rows_now, target, at):
        ones = jnp.ones((8, rows_now), jnp.bfloat16)
        target[pl.ds(at, 1), :] = dot_nn(ones, ref)[0:1]

    def vec(i):
        return table[pl.ds(i, 1), :]

    def norm_back(source, gain, base):
        def body(i):
            part = pl.ds(pl.multiple_of(i * ROWS_STEP, ROWS_STEP), ROWS_STEP)
            r = source[part, :].astype(jnp.float32)
            _, unit_rows, inv_std = normalize(r, vec(gain), vec(gain))
            back, gain_sum, shift_sum = normalize_back(acc[part, :], unit_rows, inv_std, vec(gain))
            vgrad[pl.ds(gain, 1), :] += gain_sum
            vgrad[pl.ds(gain + 1, 1), :] += shift_sum
            total = base(part) + back
            dh[part, :] = total
            bdz[part, :] = total.astype(jnp.bfloat16)

        clock.loop(rows // ROWS_STEP, 0.6, body)

    top = pl.ds(0, rows)
    first_half, second_half = pl.ds(0, half), pl.ds(half, half)
    halves = (first_half, second_half)

    def feed_phase(big, rate, wrow, tall_a, tall_b):
        tall_stage[:] = tall_a, tall_b
        load("g", given["g"], big)

        def rate_copy(j):
            cols = pl.ds(j * width, width)
            return pltpu.make_async_copy(given["rate"].at[:, cols], rate, load_sem.at[24 + j])

        def row_copy(j):
            return pltpu.make_async_copy(given["wout"].at[j // 2, j % 2], wrow, load_sem.at[28 + j])

        rate_copy(0).start()
        row_copy(0).start()
        loaded("dz")
        loaded("g")
        tall_cols = tall_a.shape[-1]
        for j in range(TALL_PARTS // 2):
            room_for(2 * j)
            room_for(2 * j + 1)
            slot = stage_of(2 * j)

            def body(t, j=j, slot=slot):
                part = big[:, pl.ds(pl.multiple_of(t * width, width), width)]
                tile = dot_tn(part, bdz[:, pl.ds(j * tall_cols, tall_cols)]).astype(jnp.bfloat16)
                slot[t // 2, t % 2] = tile.reshape(slot.shape[2:])

            clock.loop(4, 0.45, body)
            made(2 * j)
            made(2 * j + 1)
        column_sums(bdz[...], rows, vgrad, 12)
        loaded("n3")
        for j in range(blocks):
            rate_copy(j).wait()
            row_copy(j).wait()

            def body(t, j=j):
                spot = pl.ds(pl.multiple_of(j * width + t * half, half), half)
                weight = wrow[t].reshape(half, width)
                slope = rate[:, pl.ds(pl.multiple_of(t * half, half), half)].astype(jnp.float32)
                big[:, spot] = (dot_nt(bdz[...], weight) * slope).astype(jnp.bfloat16)

            clock.loop(2, 0.8, body)
            if j + 1 < blocks:
                rate_copy(j + 1).start()
                row_copy(j + 1).start()
            for h in (0, 1):
                produce(TALL_PARTS + 2 * j + h, n[...], big[:, pl.ds(j * width + h * half, half)])
            block = pl.ds(j * width, width)
            hgrad[pl.ds(0, 1), block] = dot_nn(jnp.ones((8, rows), jnp.bfloat16), big[:, block])[0:1]

            def write(cols, value, j=j):
                if j == 0:
                    acc[top, cols] = value
                else:
                    acc[top, cols] += value

            back_through(j, lambda j=j: big[:, pl.ds(j * width, width)], write)
        load("n2", given["n2"], n)
        loaded("vecs")
        unpack_table(vecs, table, bits, width)
        loaded("h2")
        norm_back(hb, 10, lambda part: bdz[part, :].astype(jnp.float32))
        for part in range(TALL_PARTS):
            clock.finish(part, 1)
            drained(part, 0)

    def attention_phase(bq, bk, bv, bg, mem, ba, tilted):
        load("ca", given["ca"], ba)
        load("cq", given["cq"], bq)
        load("ck", given["ck"], bk)
        load("cv", given["cv"], bv)
        load("ctotal", given["ctotal"], tot)
        load("memory", given["memory"], mem)
        load("h1", given["h1"], hb)

        def into(ref, size=rows):
            def write(cols, value):
                ref[pl.ds(0, size), cols] = value.astype(ref.dtype)

            return write

        def more(size):
            def write(cols, value):
                acc[pl.ds(0, size), cols] += value

            return write

        def attend(keys, masked, side):
            pair = 2 * (width // heads)
            pairs = heads // 4
            chunk = rows // 2
            spans = [(s, chunk, s + chunk if masked else keys) for s in range(0, rows, chunk)]
            key_rows = pl.ds(0, keys)
            refs_now = (bq, bk.at[key_rows], bv.at[key_rows], bg)

            def body(i):
                p = side * pairs + i
                lanes = pl.ds(pl.multiple_of(p * pair, pair), pair)
                backward_pair(
                    refs_now,
                    (dk_acc, dv_acc),
                    lambda head, start, size: tot[p, pl.ds(head, 1), pl.ds(start, size)],
                    spans[::-1],
                    length if masked else None,
                    (width // heads) ** -0.5,
                    lanes,
                )

            clock.loop(pairs, 1.9 if masked else 2.3, body)

        part = TALL_PARTS + 2 * blocks
        keys = mem.shape[0]
        length = given["lengths"][0]
        at = blocks
        back_through(at, lambda: bdz[...], into(bg))
        loaded("ca")
        for cols in halves:
            produce(part, ba[...], bdz[:, cols])
            part += 1
        column_sums(bdz[...], rows, vgrad, 9)
        load("a", given["a"], ba)
        for name in ("cq", "ck", "cv", "ctotal", "n2", "memory"):
            loaded(name)
        for side, cols in enumerate(halves):
            attend(keys, False, side)
            produce(part, n[...], bq[:, cols])
            produce(part + 1, mem[...], bk[:, cols], 0.85)
            produce(part + 2, mem[...], bv[:, cols], 0.85)
            part += 3
        load("total", given["total"], tot)
        load("n1", given["n1"], n)
        keeps = [
            pltpu.make_async_copy(bk, keep_k, load_sem.at[32]),
            pltpu.make_async_copy(bv, keep_v, load_sem.at[33]),
        ]
        for copy in keeps:
            copy.start()
        back_through(at + 1, lambda: bq[...], into(acc))
        column_sums(bq[...], rows, vgrad, 7)
        column_sums(bv[...], keys, vgrad, 8)
        load("q", given["q"], bq)
        for copy in keeps:
            copy.wait()
        load("k", given["k"], bk.at[top])
        load("v", given["v"], bv.at[top])
        loaded("h1")
        norm_back(hb, 5, lambda part: dh[part, :])
        back_through(at + 2, lambda: bdz[...], into(bg))
        loaded("a")
        for cols in halves:
            produce(part, ba[...], bdz[:, cols])
            part += 1
        column_sums(bdz[...], rows, vgrad, 4)
        load("tokens", given["tokens"], ba)
        for name in ("q", "k", "v", "total", "n1"):
            loaded(name)
        for side, cols in enumerate(halves):
            attend(rows, True, side)
            for i, ref in enumerate((bq, bk, bv)):
                produce(part + i, n[...], ref[top, cols])
            part += 3
        back_through(at + 3, lambda: bq[...], into(acc))
        back_through(at + 4, lambda: bk[top, :], more(rows))
        back_through(at + 5, lambda: bv[top, :], more(rows))
        column_sums(bq[...], rows, vgrad, 2)
        column_sums(bv[top, :], rows, vgrad, 3)
        load("keep_k", keep_k, bk)
        load("keep_v", keep_v, bv)
        loaded("tokens")
        norm_back(ba, 0, lambda part: dh[part, :])
        put_tokens = pltpu.make_async_copy(dh, tokens_grad, load_sem.at[34])
        put_tokens.start()
        devices = 2**count
        share = devices // (width // VEC_LANES)
        for d in range(devices):
            where = tuple((d >> (count - 1 - b)) & 1 for b in range(count))
            vec_stage[where] = vgrad[:, pl.ds(d // share * VEC_LANES, VEC_LANES)]
            vec_stage[where + (pl.ds(13, 1),)] = hgrad[:, pl.ds(d * VEC_LANES, VEC_LANES)]
        made(last)
        loaded("keep_k")
        loaded("keep_v")
        back_through(at + 6, lambda: bk[...], into(acc, keys))

        def write(cols, value):
            tilted[:, 0, cols] = acc[pl.ds(0, keys), cols] + value

        back_through(at + 7, lambda: bv[...], write)
        put_memory = pltpu.make_async_copy(tilted, memory_grad, load_sem.at[35])
        put_memory.start()
        clock.until(1e9)
        put_tokens.wait()
        put_memory.wait()

    low = jnp.bfloat16
    pl.run_scoped(
        feed_phase,
        pltpu.VMEM((rows, hidden), low),
        pltpu.VMEM((rows, width), low),
        pltpu.VMEM(given["wout"].shape[2:], low),
        pltpu.VMEM((2,) * count + held_tall.shape[-2:], low),
        pltpu.VMEM((2,) * count + held_tall.shape[-2:], low),
    )
    key_rows = given["memory"].shape[0]
    pl.run_scoped(
        attention_phase,
        pltpu.VMEM((rows, width), low),
        pltpu.VMEM((key_rows, width), low),
        pltpu.VMEM((key_rows, width), low),
        pltpu.VMEM((rows, width), low),
        pltpu.VMEM((key_rows, width), low),
        pltpu.VMEM((rows, width), low),
        pltpu.VMEM((key_rows, 1, width), jnp.float32),
    )
    for part in stored.values():
        store(part).wait()
    for part in range(n_parts):
        for step in range(count):
            drained(part, step)


def fused_backward(mesh, dz, tokens, memory, lengths, saved, gathered, heads, collective_id):
    bits = bit_table(mesh)
    count = len(bits)
    rows, width = tokens.shape
    keys = memory.shape[0]
    shards = [w.shape[count:] for w in gathered[1:]]
    wide_block = (shards[0][0], width // 2)
    tall_rows = shards[9][0]
    hidden = shards[8][1]
    tall_block = (tall_rows, 2 * width * shards[0][0] // tall_rows * 4 // TALL_PARTS)
    pack = (VEC_ROWS, VEC_LANES)
    n_wide = len(backward_parts(width, hidden))
    n_parts = TALL_PARTS + n_wide + 1
    low = jnp.bfloat16
    sizes = [2 * wide_block[0] * wide_block[1]] * (n_parts - 1) + [4 * pack[0] * pack[1]]
    orders = orders_of(bits, SCATTER_ROUTES, n_parts, True)
    begin = made_times(n_wide)
    sends, finish = plan_sends(bits, orders, sizes, False, 2000e3, begin)
    plan = [item for item in sends if item[2] > 0]
    plan = sorted(plan + [(when, part, count) for part, when in finish.items()])
    blocks = shards + [pack]
    spots = (2,) * count
    scratch = [
        pltpu.VMEM((rows, width), low),
        pltpu.VMEM((rows, width), low),
        pltpu.VMEM((keys, width), jnp.float32),
        pltpu.VMEM((rows, width), jnp.float32),
        pltpu.VMEM((rows, width), jnp.float32),
        pltpu.VMEM(spots + shards[0], low),
        pltpu.VMEM(spots + shards[0], low),
        pltpu.VMEM((WIDE_STAGES,) + spots + wide_block, low),
        pltpu.VMEM((TALL_PARTS // 2,) + spots[1:] + tall_block, low),
        pltpu.VMEM((WIDE_HELD,) + spots[1:] + wide_block, low),
        pltpu.VMEM((2,) + spots[1:] + tall_block, low),
        pltpu.VMEM((WIDE_BOXES,) + spots[1:] + wide_block, low),
    ]
    for number, block in ((TALL_PARTS // 2, tall_block), (n_wide, wide_block)):
        for step in range(1, count):
            scratch.append(pltpu.VMEM((number,) + (2,) * (count - 1 - step) + block, low))
    scratch += [pltpu.VMEM(spots + pack, jnp.float32), pltpu.VMEM(spots[1:] + pack, jnp.float32)]
    for step in range(count):
        scratch.append(pltpu.VMEM((2,) * (count - 1 - step) + pack, jnp.float32))
    pair = 2 * (width // heads)
    scratch += [
        pltpu.VMEM((TALL_PARTS // 2,) + tall_block, jnp.float32),
        pltpu.VMEM((SUM_SLOTS,) + wide_block, jnp.float32),
        pltpu.VMEM(pack, jnp.float32),
        pltpu.VMEM((VEC_ROWS, width), jnp.float32),
        pltpu.VMEM((1, hidden), jnp.float32),
        pltpu.VMEM((VEC_ROWS, width), jnp.float32),
        pltpu.VMEM(spots + pack, low),
        pltpu.VMEM((heads // 2, 2, rows), jnp.float32),
        pltpu.VMEM((keys, pair), jnp.float32),
        pltpu.VMEM((keys, pair), jnp.float32),
        pltpu.SemaphoreType.DMA((n_parts, count)),
        pltpu.SemaphoreType.DMA((n_parts, count)),
        pltpu.SemaphoreType.DMA((n_parts,)),
        pltpu.SemaphoreType.DMA((36,)),
        pltpu.SemaphoreType.DMA((12,)),
        pltpu.SemaphoreType.REGULAR((2 + WIDE_BOXES,)),
    ]
    hbm = pl.BlockSpec(memory_space=pltpu.HBM)
    got = pl.pallas_call(
        functools.partial(backward_kernel, bits, orders, plan, begin, heads),
        out_shape=[
            jax.ShapeDtypeStruct((rows, width), jnp.float32),
            jax.ShapeDtypeStruct((keys, 1, width), jnp.float32),
            jax.ShapeDtypeStruct((keys, width), low),
            jax.ShapeDtypeStruct((keys, width), low),
        ]
        + [jax.ShapeDtypeStruct(b, jnp.float32) for b in blocks],
        in_specs=[hbm, hbm, hbm, pl.BlockSpec(memory_space=pltpu.SMEM)]
        + [hbm] * (len(BACK_INPUTS) - 4),
        out_specs=[hbm] * (4 + len(blocks)),
        scratch_shapes=scratch,
        compiler_params=pltpu.CompilerParams(
            collective_id=collective_id,
            has_side_effects=True,
            vmem_limit_bytes=62 * 1024 * 1024,
        ),
        name="backward_layer",
    )(dz, tokens, memory, lengths, *saved, *gathered)
    return got[:2] + got[4:]


def place_kernel(count, pieces, *refs):
    sources, targets = refs[:count], refs[count : 2 * count]
    rooms, (in_sem, out_sem) = refs[2 * count : 3 * count], refs[3 * count :]
    moves = []
    for source, target, room in zip(sources, targets, rooms):
        height = source.shape[0]
        step = height
        top = 0
        while top < height:
            size = step if top + 2 * step <= height else height - top
            rows, at = pl.ds(top, size), len(moves)
            moves.append(
                (
                    pltpu.make_async_copy(source.at[rows], room.at[rows], in_sem.at[at]),
                    pltpu.make_async_copy(room.at[rows], target.at[rows], out_sem.at[at]),
                )
            )
            top += size
    for into, _ in moves:
        into.start()
    for into, out in moves:
        into.wait()
        out.start()
    for _, out in moves:
        out.wait()


def place_outputs(arrays):
    hbm = pl.BlockSpec(memory_space=pltpu.HBM)
    sems = (sum(1 if a.shape[0] > 256 else 1 for a in arrays),)
    return pl.pallas_call(
        functools.partial(place_kernel, len(arrays), 1),
        out_shape=[jax.ShapeDtypeStruct(a.shape, a.dtype) for a in arrays],
        in_specs=[hbm] * len(arrays),
        out_specs=[hbm] * len(arrays),
        scratch_shapes=[pltpu.VMEM(a.shape, a.dtype) for a in arrays]
        + [pltpu.SemaphoreType.DMA(sems), pltpu.SemaphoreType.DMA(sems)],
        compiler_params=pltpu.CompilerParams(vmem_limit_bytes=62 * 1024 * 1024),
        name="place_outputs",
    )(*arrays)


MATS_ORDER = (2, 4, 5, 13, 14, 7, 11, 16, 20, 22)
VECS = (0, 1, 3, 6, 8, 9, 10, 12, 15, 17, 18, 19, 23, 21)


def split_units(blocks):
    units = [(0, slice(None), slice(None))]
    for i, (rows, cols) in enumerate(blocks):
        base_rows, base_cols = min(rows, blocks[0][0]), min(cols, blocks[0][1])
        for top in range(0, rows, base_rows):
            for left in range(0, cols, base_cols):
                units.append(
                    (i + 1, slice(top, top + base_rows), slice(left, left + base_cols))
                )
    return units


def collect(*shards):
    return tuple(lax.all_gather(s, BOTH, axis=0, tiled=True) for s in shards)


def spread(*grads):
    return tuple(
        lax.psum_scatter(g.astype(jnp.float32), BOTH, scatter_dimension=0, tiled=True)
        for g in grads
    )


def own_vectors(block, position, shards):
    size = shards[0].shape[0]
    spot = position % (VEC_LANES // size)
    mine = lax.dynamic_slice(block, (0, spot * size), (VEC_ROWS, size))
    owned = [None] * len(shards)
    for row, i in enumerate(VECS[:-1]):
        owned[i] = mine[row]
    owned[VECS[-1]] = block[len(VECS) - 1]
    return owned


def on_device(
    mesh,
    tokens,
    memory,
    page_lengths,
    end_flags,
    out_grad,
    self_gain,
    self_shift,
    self_query,
    self_query_bias,
    self_key,
    self_value,
    self_value_bias,
    self_out,
    self_out_bias,
    cross_gain,
    cross_shift,
    cross_query,
    cross_query_bias,
    cross_key,
    cross_value,
    cross_value_bias,
    cross_out,
    cross_out_bias,
    feed_gain,
    feed_shift,
    feed_in,
    feed_in_bias,
    feed_out,
    feed_out_bias,
):
    page_count, page_len, width = tokens.shape
    mem_len = memory.shape[1]
    row_count = page_count * page_len
    lengths_now = jnp.where(end_flags == 1, 1, page_lengths)
    inputs = tokens.reshape(row_count, width).astype(jnp.float32)
    mem_rows = memory.reshape(page_count * mem_len, width)
    shard_set = (
        self_gain,
        self_shift,
        self_query,
        self_query_bias,
        self_key,
        self_value,
        self_value_bias,
        self_out,
        self_out_bias,
        cross_gain,
        cross_shift,
        cross_query,
        cross_query_bias,
        cross_key,
        cross_value,
        cross_value_bias,
        cross_out,
        cross_out_bias,
        feed_gain,
        feed_shift,
        feed_in,
        feed_in_bias,
        feed_out,
        feed_out_bias,
    )
    if can_route(mesh, self_query.shape[0]):
        mats = [shard_set[i] for i in MATS_ORDER]
        vecs = [shard_set[i] for i in VECS]
        gathered, saved = fused_forward(
            mesh, tokens[0], memory[0], lengths_now, mats, vecs, HEADS, 0
        )
        got = fused_backward(
            mesh, out_grad[0], tokens[0], memory[0], lengths_now, saved[:-1], gathered, HEADS, 1
        )
        position = lax.axis_index("dp") * mesh.shape["fsdp"] + lax.axis_index("fsdp")
        owned = own_vectors(got[-1], position, shard_set)
        placed = place_outputs([saved[-1]] + list(got[:-1]))
        for i, value in zip(MATS_ORDER, placed[3:]):
            owned[i] = value
        return (placed[0][None], placed[1][None], placed[2].transpose(1, 0, 2)) + tuple(owned)
    full_set = collect(*shard_set)
    (
        gain_one,
        shift_one,
        query_mat,
        query_vec,
        key_mat,
        value_mat,
        value_vec,
        out_mat,
        out_vec,
        gain_two,
        shift_two,
        cquery_mat,
        cquery_vec,
        ckey_mat,
        cvalue_mat,
        cvalue_vec,
        cout_mat,
        cout_vec,
        gain_three,
        shift_three,
        hidden_mat,
        hidden_vec,
        final_mat,
        final_vec,
    ) = full_set
    norm_of = lambda r, g, b: normalize(r, g.astype(jnp.float32), b.astype(jnp.float32))
    first_norm, first_unit, first_std = norm_of(inputs, gain_one, shift_one)
    first_low = first_norm.astype(jnp.bfloat16)
    query_low = (product(first_low, query_mat) + query_vec.astype(jnp.float32)).astype(jnp.bfloat16)
    key_low = product(first_low, key_mat).astype(jnp.bfloat16)
    value_low = (product(first_low, value_mat) + value_vec.astype(jnp.float32)).astype(jnp.bfloat16)
    query_pages = query_low.reshape(page_count, page_len, width)
    key_pages = key_low.reshape(page_count, page_len, width)
    value_pages = value_low.reshape(page_count, page_len, width)
    self_mixed, self_total = attend_fwd(
        query_pages, key_pages, value_pages, lengths_now, HEADS, 512
    )
    self_low = self_mixed.reshape(row_count, width)
    after_self = inputs + product(self_low, out_mat) + out_vec.astype(jnp.float32)
    second_norm, second_unit, second_std = normalize(
        after_self, gain_two.astype(jnp.float32), shift_two.astype(jnp.float32)
    )
    second_low = second_norm.astype(jnp.bfloat16)
    cquery_low = (product(second_low, cquery_mat) + cquery_vec.astype(jnp.float32)).astype(
        jnp.bfloat16
    )
    ckey_low = product(mem_rows, ckey_mat).astype(jnp.bfloat16)
    cvalue_low = (product(mem_rows, cvalue_mat) + cvalue_vec.astype(jnp.float32)).astype(
        jnp.bfloat16
    )
    cquery_pages = cquery_low.reshape(page_count, page_len, width)
    ckey_pages = ckey_low.reshape(page_count, mem_len, width)
    cvalue_pages = cvalue_low.reshape(page_count, mem_len, width)
    cross_mixed, cross_total = attend_fwd(
        cquery_pages, ckey_pages, cvalue_pages, None, HEADS, 512
    )
    cross_low = cross_mixed.reshape(row_count, width)
    after_cross = after_self + product(cross_low, cout_mat) + cout_vec.astype(jnp.float32)
    third_norm, third_unit, third_std = normalize(
        after_cross, gain_three.astype(jnp.float32), shift_three.astype(jnp.float32)
    )
    third_low = third_norm.astype(jnp.bfloat16)
    hidden_pre = product(third_low, hidden_mat) + hidden_vec.astype(jnp.float32)
    hidden_low, hidden_rate = gelu_parts(hidden_pre)
    hidden_low = hidden_low.astype(jnp.bfloat16)
    hidden_rate = hidden_rate.astype(jnp.bfloat16)
    result = after_cross + product(hidden_low, final_mat) + final_vec.astype(jnp.float32)
    layer_out = result.astype(jnp.bfloat16).reshape(page_count, page_len, width)
    second_norm, second_unit, second_std = norm_of(after_self, gain_two, shift_two)
    second_low = second_norm.astype(jnp.bfloat16)
    third_norm, third_unit, third_std = norm_of(after_cross, gain_three, shift_three)
    third_low = third_norm.astype(jnp.bfloat16)
    grad_rows = out_grad.reshape(row_count, width).astype(jnp.float32)
    final_grad = out_grad.reshape(row_count, width)
    grad_final_mat = product_tn(hidden_low, final_grad).astype(jnp.bfloat16)
    grad_final_vec = jnp.sum(final_grad.astype(jnp.float32), axis=0)
    hidden_grad = (product_nt(final_grad, final_mat) * hidden_rate.astype(jnp.float32)).astype(jnp.bfloat16)
    grad_hidden_mat = product_tn(third_low, hidden_grad).astype(jnp.bfloat16)
    grad_hidden_vec = jnp.sum(hidden_grad.astype(jnp.float32), axis=0)
    third_back, grad_gain_three, grad_shift_three = normalize_back(
        product_nt(hidden_grad, hidden_mat), third_unit, third_std, gain_three.astype(jnp.float32)
    )
    cross_grad_total = grad_rows + third_back
    cout_grad = cross_grad_total.astype(jnp.bfloat16)
    grad_cout_mat = product_tn(cross_low, cout_grad).astype(jnp.bfloat16)
    grad_cout_vec = jnp.sum(cout_grad.astype(jnp.float32), axis=0)
    cmix_grad = (
        product_nt(cout_grad, cout_mat).astype(jnp.bfloat16).reshape(page_count, page_len, width)
    )
    cquery_grad, ckey_grad, cvalue_grad = attend_bwd(
        cquery_pages, ckey_pages, cvalue_pages, cmix_grad, cross_total, None, HEADS, 512
    )
    cquery_grad = cquery_grad.reshape(row_count, width)
    ckey_grad = ckey_grad.reshape(page_count * mem_len, width)
    cvalue_grad = cvalue_grad.reshape(page_count * mem_len, width)
    grad_cquery_mat = product_tn(second_low, cquery_grad).astype(jnp.bfloat16)
    grad_cquery_vec = jnp.sum(cquery_grad.astype(jnp.float32), axis=0)
    grad_ckey_mat = product_tn(mem_rows, ckey_grad).astype(jnp.bfloat16)
    grad_cvalue_mat = product_tn(mem_rows, cvalue_grad).astype(jnp.bfloat16)
    grad_cvalue_vec = jnp.sum(cvalue_grad.astype(jnp.float32), axis=0)
    memory_grad = (product_nt(ckey_grad, ckey_mat) + product_nt(cvalue_grad, cvalue_mat)).reshape(
        page_count, mem_len, width
    )
    second_back, grad_gain_two, grad_shift_two = normalize_back(
        product_nt(cquery_grad, cquery_mat), second_unit, second_std, gain_two.astype(jnp.float32)
    )
    self_grad_total = cross_grad_total + second_back
    sout_grad = self_grad_total.astype(jnp.bfloat16)
    grad_out_mat = product_tn(self_low, sout_grad).astype(jnp.bfloat16)
    grad_out_vec = jnp.sum(sout_grad.astype(jnp.float32), axis=0)
    smix_grad = (
        product_nt(sout_grad, out_mat).astype(jnp.bfloat16).reshape(page_count, page_len, width)
    )
    query_grad, key_grad, value_grad = attend_bwd(
        query_pages, key_pages, value_pages, smix_grad, self_total, lengths_now, HEADS, 256
    )
    query_grad = query_grad.reshape(row_count, width)
    key_grad = key_grad.reshape(row_count, width)
    value_grad = value_grad.reshape(row_count, width)
    grad_query_mat = product_tn(first_low, query_grad).astype(jnp.bfloat16)
    grad_query_vec = jnp.sum(query_grad.astype(jnp.float32), axis=0)
    grad_key_mat = product_tn(first_low, key_grad).astype(jnp.bfloat16)
    grad_value_mat = product_tn(first_low, value_grad).astype(jnp.bfloat16)
    grad_value_vec = jnp.sum(value_grad.astype(jnp.float32), axis=0)
    first_in = (
        product_nt(query_grad, query_mat)
        + product_nt(key_grad, key_mat)
        + product_nt(value_grad, value_mat)
    )
    first_back, grad_gain_one, grad_shift_one = normalize_back(
        first_in, first_unit, first_std, gain_one.astype(jnp.float32)
    )
    tokens_grad = (self_grad_total + first_back).reshape(page_count, page_len, width)
    owned = spread(
        grad_gain_one[0],
        grad_shift_one[0],
        grad_query_mat,
        grad_query_vec,
        grad_key_mat,
        grad_value_mat,
        grad_value_vec,
        grad_out_mat,
        grad_out_vec,
        grad_gain_two[0],
        grad_shift_two[0],
        grad_cquery_mat,
        grad_cquery_vec,
        grad_ckey_mat,
        grad_cvalue_mat,
        grad_cvalue_vec,
        grad_cout_mat,
        grad_cout_vec,
        grad_gain_three[0],
        grad_shift_three[0],
        grad_hidden_mat,
        grad_hidden_vec,
        grad_final_mat,
        grad_final_vec,
    )
    return (layer_out, tokens_grad, memory_grad) + tuple(owned)


def solution(mesh):
    placed = (
        P(("dp", "fsdp"), None, None),
        P(("dp", "fsdp"), None, None),
        P(("dp", "fsdp")),
        P(("dp", "fsdp")),
        P(("dp", "fsdp"), None, None),
        P(("dp", "fsdp")),
        P(("dp", "fsdp")),
        P(("dp", "fsdp"), None),
        P(("dp", "fsdp")),
        P(("dp", "fsdp"), None),
        P(("dp", "fsdp"), None),
        P(("dp", "fsdp")),
        P(("dp", "fsdp"), None),
        P(("dp", "fsdp")),
        P(("dp", "fsdp")),
        P(("dp", "fsdp")),
        P(("dp", "fsdp"), None),
        P(("dp", "fsdp")),
        P(("dp", "fsdp"), None),
        P(("dp", "fsdp"), None),
        P(("dp", "fsdp")),
        P(("dp", "fsdp"), None),
        P(("dp", "fsdp")),
        P(("dp", "fsdp")),
        P(("dp", "fsdp")),
        P(("dp", "fsdp"), None),
        P(("dp", "fsdp")),
        P(("dp", "fsdp"), None),
        P(("dp", "fsdp")),
    )
    return jax.shard_map(
        functools.partial(on_device, mesh),
        mesh=mesh,
        in_specs=placed,
        out_specs=(
            P(("dp", "fsdp"), None, None),
            P(("dp", "fsdp"), None, None),
            P(("dp", "fsdp"), None, None),
            P(("dp", "fsdp")),
            P(("dp", "fsdp")),
            P(("dp", "fsdp"), None),
            P(("dp", "fsdp")),
            P(("dp", "fsdp"), None),
            P(("dp", "fsdp"), None),
            P(("dp", "fsdp")),
            P(("dp", "fsdp"), None),
            P(("dp", "fsdp")),
            P(("dp", "fsdp")),
            P(("dp", "fsdp")),
            P(("dp", "fsdp"), None),
            P(("dp", "fsdp")),
            P(("dp", "fsdp"), None),
            P(("dp", "fsdp"), None),
            P(("dp", "fsdp")),
            P(("dp", "fsdp"), None),
            P(("dp", "fsdp")),
            P(("dp", "fsdp")),
            P(("dp", "fsdp")),
            P(("dp", "fsdp"), None),
            P(("dp", "fsdp")),
            P(("dp", "fsdp"), None),
            P(("dp", "fsdp")),
        ),
        check_vma=False,
    )
```
